128 devices in a mesh: fsdp: 16 (over z_hi, y, core), ctx: 8 (over z_lo, x).
Axes of the slice: x: 4, y: 4, z: 4 (z_hi: 2, z_lo: 2; z = z_hi * 2 + z_lo), core: 2. Of those that a mesh axis runs over, the one named last changes fastest.
Arguments:
- tokens: bfloat16 [16, 2048, 1024], P('fsdp', 'ctx'), may hold values from -6 to 6
- first_value: bfloat16 [16, 2048, 1024], P('fsdp', 'ctx'), may hold values from -6 to 6
- query_weight: bfloat16 [1024, 1024], P('fsdp'), may hold values from -0.1875 to 0.1875
- key_weight: bfloat16 [1024, 1024], P('fsdp'), may hold values from -0.1875 to 0.1875
- value_weight: bfloat16 [1024, 1024], P('fsdp'), may hold values from -0.1875 to 0.1875
- out_weight: bfloat16 [1024, 1024], P('fsdp'), may hold values from -1.5 to 1.5
- gate_weight: bfloat16 [1024, 2816], P('fsdp'), may hold values from -0.1875 to 0.1875
- up_weight: bfloat16 [1024, 2816], P('fsdp'), may hold values from -0.1875 to 0.1875
- down_weight: bfloat16 [2816, 1024], P('fsdp'), may hold values from -0.109375 to 0.109375
- prenorm_gain: bfloat16 [1024], P('fsdp'), may hold values from 0.5 to 1.5
- midnorm_gain: bfloat16 [1024], P('fsdp'), may hold values from 0.5 to 1.5
- cotangent: bfloat16 [16, 2048, 1024], P('fsdp', 'ctx'), may hold values from -6 to 6
- lengths: int32 [16], replicated, may hold values from 1 to 2048, 22528 in all
- assignment: int32 [16], replicated, may hold values from 0 to 15, each once
Outputs:
- layer_out: bfloat16 [16, 2048, 1024], P('fsdp', 'ctx')
- tokens_grad: float32 [16, 2048, 1024], P('fsdp', 'ctx')
- first_grad: float32 [16, 2048, 1024], P('fsdp', 'ctx')
- query_grad: float32 [1024, 1024], P('fsdp')
- key_grad: float32 [1024, 1024], P('fsdp')
- value_grad: float32 [1024, 1024], P('fsdp')
- out_grad: float32 [1024, 1024], P('fsdp')
- gate_grad: float32 [1024, 2816], P('fsdp')
- up_grad: float32 [1024, 2816], P('fsdp')
- down_grad: float32 [2816, 1024], P('fsdp')
- prenorm_grad: float32 [1024], P('fsdp')
- midnorm_grad: float32 [1024], P('fsdp')
The draws below stay inside these ranges and needn't reach their ends.
Inputs may be any that keep to these rules, and one draw needn't show every extreme that they name: lengths of the sequences sum to 22528; the longest is exactly 2048. `assignment`: each sequence stands in exactly one slot.
All inputs are finite; a program needn't handle non-finite values.
Results may differ from the reference program's by a relative error of at most 0.025.
Values may be sent and summed in bfloat16 or wider, within the bound.
No kernel may reach another device: no remote copies, remote signals or barrier semaphores. Data moves between devices by JAX's collectives and lax.ppermute only.
A program may use at most 256 MiB of HBM per device.

```python
import math
import jax
import jax.numpy as jnp
import numpy as np
from jax import lax

D = 1024
H = 16
HD = 64
FF = 2816
SLOT_LEN = 2048
SLOTS = 16
TOTAL_LEN = 22528


def block_levels(key, extent, cuts, smallest, high):
    factor_of = 1.0
    for dim, blocks in cuts:
        heights = jax.random.uniform(jax.random.fold_in(jax.random.fold_in(key, 6), dim), (blocks,), jnp.float32, smallest / len(cuts), high / len(cuts))
        factor_of = factor_of * jnp.repeat(jnp.exp(heights), extent[dim] // blocks).reshape((-1,) + (1,) * (len(extent) - 1 - dim))
    return factor_of


def length_profile(number_of, total, most, slope):
    weights = [(1 << 20) // math.isqrt(grade ** slope) + 1 for grade in range(2, number_of + 1)]
    surplus, counts = total - most - (number_of - 1), [1] * (number_of - 1)
    while surplus > 0:
        free = [i for i in range(number_of - 1) if counts[i] < most]
        mass, budget = sum([weights[i] for i in free]), surplus
        for i in free:
            more = min(most - counts[i], max(1, budget * weights[i] // mass), surplus)
            counts[i] = counts[i] + more
            surplus = surplus - more
    return np.array([most] + counts)


def ragged_sizes(stream_key, count, total, bound, skew):
    if count == 2:
        one = jax.random.randint(stream_key, (), max(1, total - bound), min(bound, total - 1) + 1)
        return jnp.stack([one, total - one])
    tallies = jnp.asarray(length_profile(count, total, bound, skew), jnp.int32)
    couples = (count - 1) // 2
    giver, receiver = tallies[1:1 + 2 * couples:2], tallies[2:2 + 2 * couples:2]
    slack = jnp.minimum(giver - 1, bound - receiver)
    moved = jax.random.randint(jax.random.fold_in(stream_key, 1), (couples,), 0, 1 << 20) % (slack + 1)
    tallies = tallies.at[1:1 + 2 * couples:2].set(giver - moved).at[2:2 + 2 * couples:2].set(receiver + moved)
    return tallies[jax.random.permutation(jax.random.fold_in(stream_key, 2), count)]


def bell_draw(key, extent, spread, most, cuts=(), held_as=jnp.bfloat16):
    array = jax.random.normal(key, extent, jnp.float32) * spread
    if len(cuts) > 0:
        array = block_levels(key, extent, cuts, -0.22, 0.18) * array
    return jnp.clip(array, min=-most, max=most).astype(held_as)


def setup_inputs(seed: int = 0) -> dict:
    arg_keys = jax.random.split(jax.random.key(seed), 15)
    return {
        "tokens": bell_draw(arg_keys[0], (SLOTS, SLOT_LEN, D), 1.0, 6.0, ((0, 16), (1, 8))),
        "first_value": bell_draw(arg_keys[1], (SLOTS, SLOT_LEN, D), 1.0, 6.0, ((0, 16), (1, 8))),
        "query_weight": bell_draw(arg_keys[2], (D, D), D ** -0.5, 0.1875, ((0, 16),)),
        "key_weight": bell_draw(arg_keys[3], (D, D), D ** -0.5, 0.1875, ((0, 16),)),
        "value_weight": bell_draw(arg_keys[4], (D, D), D ** -0.5, 0.1875, ((0, 16),)),
        "out_weight": bell_draw(arg_keys[5], (D, D), (D // 64) ** -0.5, 1.5, ((0, 16),)),
        "gate_weight": bell_draw(arg_keys[6], (D, FF), D ** -0.5, 0.1875, ((0, 16),)),
        "up_weight": bell_draw(arg_keys[7], (D, FF), D ** -0.5, 0.1875, ((0, 16),)),
        "down_weight": bell_draw(arg_keys[8], (FF, D), FF ** -0.5, 0.109375, ((0, 16),)),
        "prenorm_gain": jnp.clip(1.0 + 0.1 * jax.random.normal(arg_keys[9], (D,), jnp.float32), 0.5, 1.5).astype(jnp.bfloat16),
        "midnorm_gain": jnp.clip(1.0 + 0.1 * jax.random.normal(arg_keys[10], (D,), jnp.float32), 0.5, 1.5).astype(jnp.bfloat16),
        "cotangent": bell_draw(arg_keys[11], (SLOTS, SLOT_LEN, D), 1.0, 6.0, ((0, 16), (1, 8))),
        "lengths": ragged_sizes(arg_keys[12], SLOTS, TOTAL_LEN, SLOT_LEN, 2).astype(jnp.int32),
        "assignment": jax.random.permutation(arg_keys[13], SLOTS).astype(jnp.int32),
    }


EPS = 1e-06
MASKED = -1e+30

@jax.custom_vjp
def low(v):
    return lax.optimization_barrier(v.astype(jnp.bfloat16)).astype(jnp.float32)

@jax.custom_vjp
def low_back(v):
    return v

def low_keep(v):
    return (low(v), None)

def low_pass(kept, grad):
    return (grad,)

def back_keep(v):
    return (v, None)

def back_low(kept, grad):
    return (low(grad),)
low.defvjp(low_keep, low_pass)
low_back.defvjp(back_keep, back_low)

def matmul_high(left, right):
    return jnp.dot(left, right, precision=lax.Precision.HIGHEST, preferred_element_type=jnp.float32)

def rms_scale(value_rows, gain):
    inverse = lax.rsqrt(lax.optimization_barrier(jnp.mean(value_rows * value_rows, axis=-1, keepdims=True)) + EPS)
    return value_rows * inverse * gain

def rope_tables(positions, half):
    freq = jnp.exp(jnp.arange(half, dtype=jnp.int32).astype(jnp.float32) * (-math.log(10000.0) / half))
    angle = positions.astype(jnp.float32)[:, None] * freq[None, :]
    return (jnp.cos(angle), jnp.sin(angle))

def rotate(value_rows, cosine, sine):
    half = value_rows.shape[-1] // 2
    first = value_rows[..., :half]
    second = value_rows[..., half:]
    return jnp.concatenate([first * cosine - second * sine, second * cosine + first * sine], axis=-1)

def layer(row_tokens, row_first, params, length):
    query_mat, key_mat, value_mat, out_mat, gate_mat, upper_mat, down_mat, gain_one, gain_two = params
    span = row_tokens.shape[0]
    places = jnp.arange(span, dtype=jnp.int32)
    valid = places < length
    cosine, sine = rope_tables(places, HD // 2)
    cosine = cosine[:, None, :]
    sine = sine[:, None, :]
    normed = low(rms_scale(row_tokens, gain_one))
    query = low_back(matmul_high(normed, query_mat)).reshape(span, H, HD)
    keyed = low_back(matmul_high(normed, key_mat)).reshape(span, H, HD)
    own_value = low_back(matmul_high(normed, value_mat))
    query_rotated_rows = low(rotate(query, cosine, sine))
    key_rot = low(rotate(keyed, cosine, sine))
    value_mix = low(0.5 * own_value + 0.5 * row_first).reshape(span, H, HD)
    scores = jnp.einsum('qhd,khd->hqk', query_rotated_rows, key_rot, precision=lax.Precision.HIGHEST) * HD ** (-0.5)
    scores = low_back(scores)
    allowed = (places[None, :] <= places[:, None]) & valid[None, :]
    scores = jnp.where(allowed[None], scores, MASKED)
    shares = low(jax.nn.softmax(scores, axis=-1))
    mixed = jnp.einsum('hqk,khd->qhd', shares, value_mix, precision=lax.Precision.HIGHEST)
    mixed = low(low_back(mixed)).reshape(span, D)
    middle = row_tokens + low_back(matmul_high(mixed, out_mat))
    normed_two = low(rms_scale(middle, gain_two))
    gate = low_back(matmul_high(normed_two, gate_mat))
    upper = low_back(matmul_high(normed_two, upper_mat))
    hidden = low(jax.nn.silu(gate) * upper)
    branch = low_back(matmul_high(hidden, down_mat))
    return jnp.where(valid[:, None], middle + branch, 0.0)

def reference(tokens, first_value, query_weight, key_weight, value_weight, out_weight, gate_weight, up_weight, down_weight, prenorm_gain, midnorm_gain, cotangent, lengths, assignment):
    slot_lengths = lengths[assignment]
    params = tuple((item.astype(jnp.float32) for item in (query_weight, key_weight, value_weight, out_weight, gate_weight, up_weight, down_weight, prenorm_gain, midnorm_gain)))

    def one_slot(totals, item):
        row_tokens, row_first, row_cot, length = item

        def forward(tokens_in, first_in, params_in):
            return layer(tokens_in, first_in, params_in, length)
        result, pull = jax.vjp(forward, row_tokens.astype(jnp.float32), row_first.astype(jnp.float32), params)
        tokens_back, first_back, params_back = pull(row_cot.astype(jnp.float32))
        totals = jax.tree.map(jnp.add, totals, params_back)
        return (totals, (result.astype(jnp.bfloat16), tokens_back, first_back))
    zeros = tuple((jnp.zeros(item.shape, jnp.float32) for item in params))
    totals, outputs = lax.scan(one_slot, zeros, (tokens, first_value, cotangent, slot_lengths))
    layer_out, tokens_grad, first_grad = outputs
    return (layer_out, tokens_grad, first_grad, totals[0], totals[1], totals[2], totals[3], totals[4], totals[5], totals[6], totals[7], totals[8])
```

```python
import math

import jax
import jax.numpy as jnp
from jax import lax
from jax.sharding import PartitionSpec as P

H = 16


EPS = 1e-06
MASKED = -1e30
GAIN_ROWS = 16


def rope_tables(positions, half):
    freq = jnp.exp(
        jnp.arange(half, dtype=jnp.int32).astype(jnp.float32) * (-math.log(10000.0) / half)
    )
    angle = positions.astype(jnp.float32)[:, None] * freq[None, :]
    return (jnp.cos(angle), jnp.sin(angle))


def rotate(value_rows, cosine, sine):
    half = value_rows.shape[-1] // 2
    first = value_rows[..., :half]
    second = value_rows[..., half:]
    return jnp.concatenate(
        [first * cosine - second * sine, second * cosine + first * sine], axis=-1
    )


def norm_apply(value_rows, gain):
    inverse = lax.rsqrt(jnp.mean(value_rows * value_rows, axis=-1, keepdims=True) + EPS)
    return (value_rows * inverse * gain, inverse)


def norm_back(value_rows, inverse, gain, upstream):
    scaled = upstream * gain
    gain_part = jnp.sum(upstream * value_rows * inverse, axis=(0, 1))
    inner = jnp.mean(scaled * value_rows, axis=-1, keepdims=True)
    return (inverse * scaled - value_rows * inverse * inverse * inverse * inner, gain_part)


def gain_block(first, second, width, leading=()):
    pad_cols = width - first.shape[-1] - second.shape[-1]
    row = jnp.concatenate(
        [first, second, jnp.zeros(leading + (pad_cols,), first.dtype)], axis=-1
    )
    row = row[..., None, :]
    pads = [(0, 0)] * len(leading) + [(0, GAIN_ROWS - 1), (0, 0)]
    return jnp.pad(row, pads)


def body(
    tokens,
    first_value,
    query_weight,
    key_weight,
    value_weight,
    out_weight,
    gate_weight,
    up_weight,
    down_weight,
    prenorm_gain,
    midnorm_gain,
    cotangent,
    lengths,
    assignment,
):
    slots, rows, width = tokens.shape
    head_count = H
    head_dim = width // head_count
    score_scale = head_dim ** (-0.5)
    n_fsdp = lax.axis_size("fsdp")
    n_ctx = lax.axis_size("ctx")
    total_len = rows * n_ctx
    w_rows = query_weight.shape[0]
    g_len = prenorm_gain.shape[0]
    ff = gate_weight.shape[1]
    d_rows = down_weight.shape[0]

    slot_count = assignment.shape[0]
    chosen = assignment[:, None] == jnp.arange(slot_count, dtype=jnp.int32)[None, :]
    lengths_all = jnp.sum(jnp.where(chosen, lengths[None, :], 0), axis=1)
    slot_lengths = lax.dynamic_slice_in_dim(lengths_all, lax.axis_index("fsdp") * slots, slots)
    query_places = lax.axis_index("ctx") * rows + jnp.arange(rows, dtype=jnp.int32)
    key_places = jnp.arange(total_len, dtype=jnp.int32)
    valid = query_places[None, :] < slot_lengths[:, None]
    allowed = (key_places[None, None, :] <= query_places[None, :, None]) & (
        key_places[None, None, :] < slot_lengths[:, None, None]
    )
    cosine, sine = rope_tables(query_places, head_dim // 2)
    cos_rows = cosine[None, :, None, :]
    sin_rows = sine[None, :, None, :]
    valid_wide = valid[:, :, None]

    attn_pack = jnp.concatenate(
        [query_weight, key_weight, value_weight, out_weight,
         gain_block(prenorm_gain, midnorm_gain, width)],
        axis=0,
    )
    attn_all = lax.all_gather(attn_pack, "fsdp", axis=0, tiled=False)

    def attn_part(i):
        return attn_all[:, i * w_rows:(i + 1) * w_rows, :].reshape(n_fsdp * w_rows, width)

    query_mat, key_mat, value_mat, out_mat = (attn_part(i) for i in range(4))
    prenorm_full = attn_all[:, 4 * w_rows, 0:g_len].reshape(n_fsdp * g_len)
    midnorm_full = attn_all[:, 4 * w_rows, g_len:2 * g_len].reshape(n_fsdp * g_len)

    mlp_pack = jnp.concatenate(
        [gate_weight, up_weight, down_weight.reshape(w_rows, ff)], axis=1
    )
    mlp_all = lax.all_gather(mlp_pack, "fsdp", axis=0, tiled=False)
    gate_mat = mlp_all[:, :, 0:ff].reshape(n_fsdp * w_rows, ff)
    upper_mat = mlp_all[:, :, ff:2 * ff].reshape(n_fsdp * w_rows, ff)
    down_mat = mlp_all[:, :, 2 * ff:].reshape(n_fsdp, d_rows, width).reshape(n_fsdp * d_rows, width)

    tokens_wide = tokens.astype(jnp.float32)
    first_wide = first_value.astype(jnp.float32)
    normed, inverse = norm_apply(tokens_wide, prenorm_full.astype(jnp.float32))
    normed_low = normed.astype(jnp.bfloat16)
    query = jnp.dot(normed_low, query_mat, preferred_element_type=jnp.float32)
    keyed = jnp.dot(normed_low, key_mat, preferred_element_type=jnp.float32)
    own_value = jnp.dot(normed_low, value_mat, preferred_element_type=jnp.float32)
    heads_shape = query.shape[:2] + (head_count, head_dim)
    query_rotated_rows = rotate(query.reshape(heads_shape), cos_rows, sin_rows).astype(jnp.bfloat16)
    key_rot = (
        rotate(keyed.reshape(heads_shape), cos_rows, sin_rows)
        .astype(jnp.bfloat16)
        .reshape(query.shape)
    )
    value_mix = (0.5 * own_value + 0.5 * first_wide).astype(jnp.bfloat16)

    kv_all = lax.all_gather(
        jnp.concatenate([key_rot, value_mix], axis=-1), "ctx", axis=1, tiled=True
    )
    key_rows_per_head = kv_all[..., :width].reshape(slots, total_len, head_count, head_dim)
    value_rows_per_head = kv_all[..., width:].reshape(slots, total_len, head_count, head_dim)

    scores = (
        jnp.einsum(
            "biuv,bfuv->buif",
            query_rotated_rows,
            key_rows_per_head,
            preferred_element_type=jnp.float32,
        )
        * score_scale
    )
    scores = jnp.where(allowed[:, None], scores, MASKED)
    peak = jnp.max(scores, axis=-1, keepdims=True)
    raised = jnp.exp(scores - peak)
    denominator = jnp.sum(raised, axis=-1, keepdims=True)
    shares = raised / denominator
    attention_share_narrow = shares.astype(jnp.bfloat16)
    mixed = jnp.einsum(
        "ytjo,yotv->yjtv",
        attention_share_narrow,
        value_rows_per_head,
        preferred_element_type=jnp.float32,
    )
    mixed_low = mixed.astype(jnp.bfloat16).reshape(slots, rows, width)

    middle = tokens_wide + jnp.dot(mixed_low, out_mat, preferred_element_type=jnp.float32)
    normed_two, inverse_two = norm_apply(middle, midnorm_full.astype(jnp.float32))
    normed_two = normed_two.astype(jnp.bfloat16)
    gate = jnp.dot(normed_two, gate_mat, preferred_element_type=jnp.float32)
    upper = jnp.dot(normed_two, upper_mat, preferred_element_type=jnp.float32)
    hidden = (jax.nn.silu(gate) * upper).astype(jnp.bfloat16)
    branch = jnp.dot(hidden, down_mat, preferred_element_type=jnp.float32)
    layer_out = jnp.where(valid_wide, middle + branch, 0.0).astype(jnp.bfloat16)

    cot_wide = jnp.where(valid_wide, cotangent.astype(jnp.float32), 0.0)
    cot_low = cot_wide.astype(jnp.bfloat16)
    down_total = jnp.einsum("srf,sre->fe", hidden, cot_low, preferred_element_type=jnp.float32)
    hidden_back = jnp.einsum("sre,fe->srf", cot_low, down_mat, preferred_element_type=jnp.float32)
    sigma = jax.nn.sigmoid(gate)
    gate_back = (hidden_back * upper * sigma * (1.0 + gate * (1.0 - sigma))).astype(jnp.bfloat16)
    upper_back = (hidden_back * gate * sigma).astype(jnp.bfloat16)
    gate_total = jnp.einsum(
        "srd,srf->df", normed_two, gate_back, preferred_element_type=jnp.float32
    )
    upper_total = jnp.einsum(
        "srd,srf->df", normed_two, upper_back, preferred_element_type=jnp.float32
    )
    normed_two_back = jnp.einsum(
        "srf,df->srd", gate_back, gate_mat, preferred_element_type=jnp.float32
    )
    normed_two_back = normed_two_back + jnp.einsum(
        "srf,df->srd", upper_back, upper_mat, preferred_element_type=jnp.float32
    )
    middle_norm_back, midnorm_total = norm_back(
        middle, inverse_two, midnorm_full.astype(jnp.float32), normed_two_back
    )
    middle_back = cot_wide + middle_norm_back
    middle_low = middle_back.astype(jnp.bfloat16)
    out_total = jnp.einsum("srd,sre->de", mixed_low, middle_low, preferred_element_type=jnp.float32)

    mlp_grads = jnp.concatenate(
        [
            gate_total.reshape(n_fsdp, w_rows, ff),
            upper_total.reshape(n_fsdp, w_rows, ff),
            down_total.reshape(n_fsdp, d_rows, width).reshape(n_fsdp, w_rows, ff),
            out_total.reshape(n_fsdp, w_rows, width),
        ],
        axis=2,
    ).astype(jnp.bfloat16)
    mlp_share = lax.psum_scatter(mlp_grads, "fsdp", scatter_dimension=0, tiled=False)

    blended_value_gradient = jnp.einsum(
        "sre,de->srd", middle_low, out_mat, preferred_element_type=jnp.float32
    ).astype(jnp.bfloat16)
    blended_value_gradient = blended_value_gradient.reshape(slots, rows, head_count, head_dim)
    prob_back = jnp.einsum(
        "biuv,bfuv->buif",
        blended_value_gradient,
        value_rows_per_head,
        preferred_element_type=jnp.float32,
    )
    inner = jnp.sum(shares * prob_back, axis=-1, keepdims=True)
    score_gradient = (shares * (prob_back - inner)).astype(jnp.bfloat16)
    query_rot_back = (
        jnp.einsum(
            "ytjo,yotv->yjtv", score_gradient, key_rows_per_head, preferred_element_type=jnp.float32
        )
        * score_scale
    )
    key_part = (
        jnp.einsum(
            "xtfk,xfty->kxty",
            score_gradient,
            query_rotated_rows,
            preferred_element_type=jnp.float32,
        )
        * score_scale
    )
    value_part = jnp.einsum(
        "xtfk,xfty->kxty",
        attention_share_narrow,
        blended_value_gradient,
        preferred_element_type=jnp.float32,
    )
    key_value = lax.psum_scatter(
        jnp.concatenate(
            [key_part.reshape(total_len, slots, width), value_part.reshape(total_len, slots, width)],
            axis=-1,
        ).astype(jnp.bfloat16),
        "ctx",
        scatter_dimension=0,
        tiled=True,
    ).astype(jnp.float32)
    key_value = jnp.swapaxes(key_value, 0, 1)
    key_rot_back = key_value[..., :width].reshape(slots, rows, head_count, head_dim)
    value_mix_back = key_value[..., width:]
    first_grad = 0.5 * value_mix_back
    query_back = (
        rotate(query_rot_back, cos_rows, -sin_rows).reshape(slots, rows, width).astype(jnp.bfloat16)
    )
    key_back = (
        rotate(key_rot_back, cos_rows, -sin_rows).reshape(slots, rows, width).astype(jnp.bfloat16)
    )
    value_back = (0.5 * value_mix_back).astype(jnp.bfloat16)
    query_total = jnp.einsum(
        "srd,sre->de", normed_low, query_back, preferred_element_type=jnp.float32
    )
    key_total = jnp.einsum("srd,sre->de", normed_low, key_back, preferred_element_type=jnp.float32)
    value_total = jnp.einsum(
        "srd,sre->de", normed_low, value_back, preferred_element_type=jnp.float32
    )
    normed_back = jnp.einsum(
        "sre,de->srd", query_back, query_mat, preferred_element_type=jnp.float32
    )
    normed_back = normed_back + jnp.einsum(
        "sre,de->srd", key_back, key_mat, preferred_element_type=jnp.float32
    )
    normed_back = normed_back + jnp.einsum(
        "sre,de->srd", value_back, value_mat, preferred_element_type=jnp.float32
    )
    tokens_norm_back, prenorm_total = norm_back(
        tokens_wide, inverse, prenorm_full.astype(jnp.float32), normed_back
    )
    tokens_grad = middle_back + tokens_norm_back

    attn_grads = jnp.concatenate(
        [
            query_total.reshape(n_fsdp, w_rows, width),
            key_total.reshape(n_fsdp, w_rows, width),
            value_total.reshape(n_fsdp, w_rows, width),
            gain_block(
                prenorm_total.reshape(n_fsdp, g_len),
                midnorm_total.reshape(n_fsdp, g_len),
                width,
                leading=(n_fsdp,),
            ),
        ],
        axis=1,
    ).astype(jnp.bfloat16)
    attn_share = lax.psum_scatter(attn_grads, "fsdp", scatter_dimension=0, tiled=False)

    attn_share, mlp_share = lax.psum((attn_share, mlp_share), "ctx")
    attn_share = attn_share.astype(jnp.float32)
    mlp_share = mlp_share.astype(jnp.float32)

    def attn_grad(i):
        return attn_share[i * w_rows:(i + 1) * w_rows]

    query_grad, key_grad, value_grad = (attn_grad(i) for i in range(3))
    prenorm_grad = attn_share[3 * w_rows, 0:g_len]
    midnorm_grad = attn_share[3 * w_rows, g_len:2 * g_len]
    gate_grad = mlp_share[:, 0:ff]
    up_grad = mlp_share[:, ff:2 * ff]
    down_grad = mlp_share[:, 2 * ff:3 * ff].reshape(d_rows, width)
    out_grad = mlp_share[:, 3 * ff:]
    return (
        layer_out,
        tokens_grad,
        first_grad,
        query_grad,
        key_grad,
        value_grad,
        out_grad,
        gate_grad,
        up_grad,
        down_grad,
        prenorm_grad,
        midnorm_grad,
    )


def solution(mesh):
    placed = (
        P("fsdp", "ctx", None),
        P("fsdp", "ctx", None),
        P("fsdp", None),
        P("fsdp", None),
        P("fsdp", None),
        P("fsdp", None),
        P("fsdp", None),
        P("fsdp", None),
        P("fsdp", None),
        P("fsdp"),
        P("fsdp"),
        P("fsdp", "ctx", None),
        P(),
        P(),
    )
    return jax.shard_map(
        body,
        mesh=mesh,
        in_specs=placed,
        out_specs=(
            P("fsdp", "ctx", None),
            P("fsdp", "ctx", None),
            P("fsdp", "ctx", None),
            P("fsdp", None),
            P("fsdp", None),
            P("fsdp", None),
            P("fsdp", None),
            P("fsdp", None),
            P("fsdp", None),
            P("fsdp", None),
            P("fsdp"),
            P("fsdp"),
        ),
        check_vma=False,
    )
```

```python
import functools
import math

import jax
import jax.numpy as jnp
from jax import lax
from jax.experimental import pallas as pl
from jax.experimental.pallas import tpu as pltpu
from jax.sharding import PartitionSpec as P

H = 16


EPS = 1e-06
MASKED = -1e30
GAIN_ROWS = 16


HEAD_BLOCK = 128
NT_DIMS = (((1,), (1,)), ((), ()))
TN_DIMS = (((0,), (0,)), ((), ()))


def attention_shares(query, keys, first_row, slot_len, scale):
    scores = lax.dot_general(query, keys, NT_DIMS, preferred_element_type=jnp.float32) * scale
    shape = scores.shape
    query_pos = first_row + lax.broadcasted_iota(jnp.int32, shape, 0)
    key_pos = lax.broadcasted_iota(jnp.int32, shape, 1)
    allowed = (key_pos <= query_pos) & (key_pos < slot_len)
    scores = jnp.where(allowed, scores, MASKED)
    peak = jnp.max(scores, axis=-1, keepdims=True)
    raised = jnp.exp(scores - peak)
    denominator = jnp.sum(raised, axis=-1, keepdims=True)
    return raised / denominator


def attn_fwd_kernel(head_dim, scale, meta_ref, q_ref, k_ref, v_ref, o_ref):
    first_row = meta_ref[0]
    slot_len = meta_ref[1]
    for j in range(q_ref.shape[1] // head_dim):
        cols = slice(j * head_dim, (j + 1) * head_dim)
        shares = attention_shares(q_ref[:, cols], k_ref[:, cols], first_row, slot_len, scale)
        mixed = jnp.dot(
            shares.astype(jnp.bfloat16), v_ref[:, cols], preferred_element_type=jnp.float32
        )
        o_ref[:, cols] = mixed.astype(o_ref.dtype)


def attn_bwd_kernel(head_dim, scale, meta_ref, q_ref, k_ref, v_ref, do_ref, dq_ref, dk_ref, dv_ref):
    first_row = meta_ref[0]
    slot_len = meta_ref[1]
    for j in range(q_ref.shape[1] // head_dim):
        cols = slice(j * head_dim, (j + 1) * head_dim)
        query = q_ref[:, cols]
        keys = k_ref[:, cols]
        back = do_ref[:, cols]
        shares = attention_shares(query, keys, first_row, slot_len, scale)
        prob_back = lax.dot_general(back, v_ref[:, cols], NT_DIMS, preferred_element_type=jnp.float32)
        inner = jnp.sum(shares * prob_back, axis=-1, keepdims=True)
        score_back = (shares * (prob_back - inner)).astype(jnp.bfloat16)
        dq_ref[:, cols] = (
            jnp.dot(score_back, keys, preferred_element_type=jnp.float32) * scale
        )
        dk_ref[:, cols] = (
            lax.dot_general(score_back, query, TN_DIMS, preferred_element_type=jnp.float32) * scale
        ).astype(dk_ref.dtype)
        dv_ref[:, cols] = lax.dot_general(
            shares.astype(jnp.bfloat16), back, TN_DIMS, preferred_element_type=jnp.float32
        ).astype(dv_ref.dtype)


def attention_forward(meta, query_rows, kv_rows, head_dim, scale):
    rows, width = query_rows.shape
    keys = kv_rows.shape[0]
    blocks = width // HEAD_BLOCK
    return pl.pallas_call(
        functools.partial(attn_fwd_kernel, head_dim, scale),
        out_shape=jax.ShapeDtypeStruct((rows, width), jnp.bfloat16),
        grid_spec=pltpu.PrefetchScalarGridSpec(
            num_scalar_prefetch=1,
            grid=(blocks,),
            in_specs=[
                pl.BlockSpec((rows, HEAD_BLOCK), lambda h, m: (0, h)),
                pl.BlockSpec((keys, HEAD_BLOCK), lambda h, m: (0, h)),
                pl.BlockSpec((keys, HEAD_BLOCK), lambda h, m: (0, h + blocks)),
            ],
            out_specs=pl.BlockSpec((rows, HEAD_BLOCK), lambda h, m: (0, h)),
        ),
        compiler_params=pltpu.CompilerParams(
            dimension_semantics=("arbitrary",), vmem_limit_bytes=48 * 1024 * 1024
        ),
        cost_estimate=pl.CostEstimate(
            flops=4 * rows * keys * width,
            transcendentals=rows * keys * (width // head_dim),
            bytes_accessed=2 * (2 * rows * width + 2 * keys * width),
        ),
    )(meta, query_rows, kv_rows, kv_rows)


def attention_backward(meta, query_rows, kv_rows, back_rows, head_dim, scale):
    rows, width = query_rows.shape
    keys = kv_rows.shape[0]
    blocks = width // HEAD_BLOCK
    return pl.pallas_call(
        functools.partial(attn_bwd_kernel, head_dim, scale),
        out_shape=(
            jax.ShapeDtypeStruct((rows, width), jnp.float32),
            jax.ShapeDtypeStruct((keys, width), jnp.bfloat16),
            jax.ShapeDtypeStruct((keys, width), jnp.bfloat16),
        ),
        grid_spec=pltpu.PrefetchScalarGridSpec(
            num_scalar_prefetch=1,
            grid=(blocks,),
            in_specs=[
                pl.BlockSpec((rows, HEAD_BLOCK), lambda h, m: (0, h)),
                pl.BlockSpec((keys, HEAD_BLOCK), lambda h, m: (0, h)),
                pl.BlockSpec((keys, HEAD_BLOCK), lambda h, m: (0, h + blocks)),
                pl.BlockSpec((rows, HEAD_BLOCK), lambda h, m: (0, h)),
            ],
            out_specs=[
                pl.BlockSpec((rows, HEAD_BLOCK), lambda h, m: (0, h)),
                pl.BlockSpec((keys, HEAD_BLOCK), lambda h, m: (0, h)),
                pl.BlockSpec((keys, HEAD_BLOCK), lambda h, m: (0, h)),
            ],
        ),
        compiler_params=pltpu.CompilerParams(
            dimension_semantics=("arbitrary",), vmem_limit_bytes=48 * 1024 * 1024
        ),
        cost_estimate=pl.CostEstimate(
            flops=10 * rows * keys * width,
            transcendentals=rows * keys * (width // head_dim),
            bytes_accessed=2 * (3 * rows * width + 4 * keys * width) + 4 * rows * width,
        ),
    )(meta, query_rows, kv_rows, kv_rows, back_rows)


def rope_tables(positions, half):
    freq = jnp.exp(
        jnp.arange(half, dtype=jnp.int32).astype(jnp.float32) * (-math.log(10000.0) / half)
    )
    angle = positions.astype(jnp.float32)[:, None] * freq[None, :]
    return (jnp.cos(angle), jnp.sin(angle))


def rotate(value_rows, cosine, sine):
    half = value_rows.shape[-1] // 2
    first = value_rows[..., :half]
    second = value_rows[..., half:]
    return jnp.concatenate(
        [first * cosine - second * sine, second * cosine + first * sine], axis=-1
    )


def norm_apply(value_rows, gain):
    inverse = lax.rsqrt(jnp.mean(value_rows * value_rows, axis=-1, keepdims=True) + EPS)
    return (value_rows * inverse * gain, inverse)


def norm_back(value_rows, inverse, gain, upstream):
    scaled = upstream * gain
    gain_part = jnp.sum(upstream * value_rows * inverse, axis=(0, 1))
    inner = jnp.mean(scaled * value_rows, axis=-1, keepdims=True)
    return (inverse * scaled - value_rows * inverse * inverse * inverse * inner, gain_part)


def gain_block(first, second, width, leading=()):
    pad_cols = width - first.shape[-1] - second.shape[-1]
    row = jnp.concatenate(
        [first, second, jnp.zeros(leading + (pad_cols,), first.dtype)], axis=-1
    )
    row = row[..., None, :]
    pads = [(0, 0)] * len(leading) + [(0, GAIN_ROWS - 1), (0, 0)]
    return jnp.pad(row, pads)


def body(
    tokens,
    first_value,
    query_weight,
    key_weight,
    value_weight,
    out_weight,
    gate_weight,
    up_weight,
    down_weight,
    prenorm_gain,
    midnorm_gain,
    cotangent,
    lengths,
    assignment,
):
    slots, rows, width = tokens.shape
    assert slots == 1
    head_count = H
    head_dim = width // head_count
    score_scale = head_dim ** (-0.5)
    n_fsdp = lax.axis_size("fsdp")
    n_ctx = lax.axis_size("ctx")
    total_len = rows * n_ctx
    w_rows = query_weight.shape[0]
    g_len = prenorm_gain.shape[0]
    ff = gate_weight.shape[1]
    d_rows = down_weight.shape[0]

    slot_count = assignment.shape[0]
    chosen = assignment[:, None] == jnp.arange(slot_count, dtype=jnp.int32)[None, :]
    lengths_all = jnp.sum(jnp.where(chosen, lengths[None, :], 0), axis=1)
    slot_lengths = lax.dynamic_slice_in_dim(lengths_all, lax.axis_index("fsdp") * slots, slots)
    query_places = lax.axis_index("ctx") * rows + jnp.arange(rows, dtype=jnp.int32)
    valid = query_places[None, :] < slot_lengths[:, None]
    cosine, sine = rope_tables(query_places, head_dim // 2)
    cos_rows = cosine[None, :, None, :]
    sin_rows = sine[None, :, None, :]
    valid_wide = valid[:, :, None]

    attn_pack = jnp.concatenate(
        [query_weight, key_weight, value_weight, out_weight,
         gain_block(prenorm_gain, midnorm_gain, width)],
        axis=0,
    )
    attn_all = lax.all_gather(attn_pack, "fsdp", axis=0, tiled=False)

    def attn_part(i):
        return attn_all[:, i * w_rows:(i + 1) * w_rows, :].reshape(n_fsdp * w_rows, width)

    query_mat, key_mat, value_mat, out_mat = (attn_part(i) for i in range(4))
    prenorm_full = attn_all[:, 4 * w_rows, 0:g_len].reshape(n_fsdp * g_len)
    midnorm_full = attn_all[:, 4 * w_rows, g_len:2 * g_len].reshape(n_fsdp * g_len)

    mlp_pack = jnp.concatenate(
        [gate_weight, up_weight, down_weight.reshape(w_rows, ff)], axis=1
    )
    mlp_all = lax.all_gather(mlp_pack, "fsdp", axis=0, tiled=False)
    gate_mat = mlp_all[:, :, 0:ff].reshape(n_fsdp * w_rows, ff)
    upper_mat = mlp_all[:, :, ff:2 * ff].reshape(n_fsdp * w_rows, ff)
    down_mat = mlp_all[:, :, 2 * ff:].reshape(n_fsdp, d_rows, width).reshape(n_fsdp * d_rows, width)

    tokens_wide = tokens.astype(jnp.float32)
    first_wide = first_value.astype(jnp.float32)
    normed, inverse = norm_apply(tokens_wide, prenorm_full.astype(jnp.float32))
    normed_low = normed.astype(jnp.bfloat16)
    query = jnp.dot(normed_low, query_mat, preferred_element_type=jnp.float32)
    keyed = jnp.dot(normed_low, key_mat, preferred_element_type=jnp.float32)
    own_value = jnp.dot(normed_low, value_mat, preferred_element_type=jnp.float32)
    heads_shape = query.shape[:2] + (head_count, head_dim)
    query_rotated_rows = rotate(query.reshape(heads_shape), cos_rows, sin_rows).astype(jnp.bfloat16)
    key_rot = (
        rotate(keyed.reshape(heads_shape), cos_rows, sin_rows)
        .astype(jnp.bfloat16)
        .reshape(query.shape)
    )
    value_mix = (0.5 * own_value + 0.5 * first_wide).astype(jnp.bfloat16)

    kv_all = lax.all_gather(
        jnp.concatenate([key_rot, value_mix], axis=-1), "ctx", axis=1, tiled=True
    ).reshape(total_len, 2 * width)
    meta = jnp.stack([lax.axis_index("ctx") * rows, slot_lengths[0]]).astype(jnp.int32)
    query_flat = query_rotated_rows.reshape(rows, width)
    mixed_low = attention_forward(
        meta, query_flat, kv_all, head_dim, score_scale
    ).reshape(slots, rows, width)

    middle = tokens_wide + jnp.dot(mixed_low, out_mat, preferred_element_type=jnp.float32)
    normed_two, inverse_two = norm_apply(middle, midnorm_full.astype(jnp.float32))
    normed_two = normed_two.astype(jnp.bfloat16)
    gate = jnp.dot(normed_two, gate_mat, preferred_element_type=jnp.float32)
    upper = jnp.dot(normed_two, upper_mat, preferred_element_type=jnp.float32)
    hidden = (jax.nn.silu(gate) * upper).astype(jnp.bfloat16)
    branch = jnp.dot(hidden, down_mat, preferred_element_type=jnp.float32)
    layer_out = jnp.where(valid_wide, middle + branch, 0.0).astype(jnp.bfloat16)

    cot_wide = jnp.where(valid_wide, cotangent.astype(jnp.float32), 0.0)
    cot_low = cot_wide.astype(jnp.bfloat16)
    down_total = jnp.einsum("srf,sre->fe", hidden, cot_low, preferred_element_type=jnp.float32)
    hidden_back = jnp.einsum("sre,fe->srf", cot_low, down_mat, preferred_element_type=jnp.float32)
    sigma = jax.nn.sigmoid(gate)
    gate_back = (hidden_back * upper * sigma * (1.0 + gate * (1.0 - sigma))).astype(jnp.bfloat16)
    upper_back = (hidden_back * gate * sigma).astype(jnp.bfloat16)
    gate_total = jnp.einsum(
        "srd,srf->df", normed_two, gate_back, preferred_element_type=jnp.float32
    )
    upper_total = jnp.einsum(
        "srd,srf->df", normed_two, upper_back, preferred_element_type=jnp.float32
    )
    normed_two_back = jnp.einsum(
        "srf,df->srd", gate_back, gate_mat, preferred_element_type=jnp.float32
    )
    normed_two_back = normed_two_back + jnp.einsum(
        "srf,df->srd", upper_back, upper_mat, preferred_element_type=jnp.float32
    )
    middle_norm_back, midnorm_total = norm_back(
        middle, inverse_two, midnorm_full.astype(jnp.float32), normed_two_back
    )
    middle_back = cot_wide + middle_norm_back
    middle_low = middle_back.astype(jnp.bfloat16)
    out_total = jnp.einsum("srd,sre->de", mixed_low, middle_low, preferred_element_type=jnp.float32)

    mlp_grads = jnp.concatenate(
        [
            gate_total.reshape(n_fsdp, w_rows, ff),
            upper_total.reshape(n_fsdp, w_rows, ff),
            down_total.reshape(n_fsdp, d_rows, width).reshape(n_fsdp, w_rows, ff),
            out_total.reshape(n_fsdp, w_rows, width),
        ],
        axis=2,
    ).astype(jnp.bfloat16)
    mlp_share = lax.psum_scatter(mlp_grads, "fsdp", scatter_dimension=0, tiled=False)

    blended_value_gradient = jnp.einsum(
        "sre,de->srd", middle_low, out_mat, preferred_element_type=jnp.float32
    ).astype(jnp.bfloat16)
    query_rot_back, key_part, value_part = attention_backward(
        meta, query_flat, kv_all, blended_value_gradient.reshape(rows, width), head_dim, score_scale
    )
    query_rot_back = query_rot_back.reshape(slots, rows, head_count, head_dim)
    key_value = lax.psum_scatter(
        jnp.stack([key_part, value_part]), "ctx", scatter_dimension=1, tiled=True
    ).astype(jnp.float32)
    key_rot_back = key_value[0].reshape(slots, rows, head_count, head_dim)
    value_mix_back = key_value[1].reshape(slots, rows, width)
    first_grad = 0.5 * value_mix_back
    query_back = (
        rotate(query_rot_back, cos_rows, -sin_rows).reshape(slots, rows, width).astype(jnp.bfloat16)
    )
    key_back = (
        rotate(key_rot_back, cos_rows, -sin_rows).reshape(slots, rows, width).astype(jnp.bfloat16)
    )
    value_back = (0.5 * value_mix_back).astype(jnp.bfloat16)
    query_total = jnp.einsum(
        "srd,sre->de", normed_low, query_back, preferred_element_type=jnp.float32
    )
    key_total = jnp.einsum("srd,sre->de", normed_low, key_back, preferred_element_type=jnp.float32)
    value_total = jnp.einsum(
        "srd,sre->de", normed_low, value_back, preferred_element_type=jnp.float32
    )
    normed_back = jnp.einsum(
        "sre,de->srd", query_back, query_mat, preferred_element_type=jnp.float32
    )
    normed_back = normed_back + jnp.einsum(
        "sre,de->srd", key_back, key_mat, preferred_element_type=jnp.float32
    )
    normed_back = normed_back + jnp.einsum(
        "sre,de->srd", value_back, value_mat, preferred_element_type=jnp.float32
    )
    tokens_norm_back, prenorm_total = norm_back(
        tokens_wide, inverse, prenorm_full.astype(jnp.float32), normed_back
    )
    tokens_grad = middle_back + tokens_norm_back

    attn_grads = jnp.concatenate(
        [
            query_total.reshape(n_fsdp, w_rows, width),
            key_total.reshape(n_fsdp, w_rows, width),
            value_total.reshape(n_fsdp, w_rows, width),
            gain_block(
                prenorm_total.reshape(n_fsdp, g_len),
                midnorm_total.reshape(n_fsdp, g_len),
                width,
                leading=(n_fsdp,),
            ),
        ],
        axis=1,
    ).astype(jnp.bfloat16)
    attn_share = lax.psum_scatter(attn_grads, "fsdp", scatter_dimension=0, tiled=False)

    attn_share, mlp_share = lax.psum((attn_share, mlp_share), "ctx")
    attn_share = attn_share.astype(jnp.float32)
    mlp_share = mlp_share.astype(jnp.float32)

    def attn_grad(i):
        return attn_share[i * w_rows:(i + 1) * w_rows]

    query_grad, key_grad, value_grad = (attn_grad(i) for i in range(3))
    prenorm_grad = attn_share[3 * w_rows, 0:g_len]
    midnorm_grad = attn_share[3 * w_rows, g_len:2 * g_len]
    gate_grad = mlp_share[:, 0:ff]
    up_grad = mlp_share[:, ff:2 * ff]
    down_grad = mlp_share[:, 2 * ff:3 * ff].reshape(d_rows, width)
    out_grad = mlp_share[:, 3 * ff:]
    return (
        layer_out,
        tokens_grad,
        first_grad,
        query_grad,
        key_grad,
        value_grad,
        out_grad,
        gate_grad,
        up_grad,
        down_grad,
        prenorm_grad,
        midnorm_grad,
    )


def solution(mesh):
    placed = (
        P("fsdp", "ctx", None),
        P("fsdp", "ctx", None),
        P("fsdp", None),
        P("fsdp", None),
        P("fsdp", None),
        P("fsdp", None),
        P("fsdp", None),
        P("fsdp", None),
        P("fsdp", None),
        P("fsdp"),
        P("fsdp"),
        P("fsdp", "ctx", None),
        P(),
        P(),
    )
    return jax.shard_map(
        body,
        mesh=mesh,
        in_specs=placed,
        out_specs=(
            P("fsdp", "ctx", None),
            P("fsdp", "ctx", None),
            P("fsdp", "ctx", None),
            P("fsdp", None),
            P("fsdp", None),
            P("fsdp", None),
            P("fsdp", None),
            P("fsdp", None),
            P("fsdp", None),
            P("fsdp", None),
            P("fsdp"),
            P("fsdp"),
        ),
        check_vma=False,
    )
```

```python
import functools
import math

import jax
import jax.numpy as jnp
from jax import lax
from jax.experimental import pallas as pl
from jax.experimental.pallas import tpu as pltpu
from jax.sharding import PartitionSpec as P

H = 16


EPS = 1e-06
MASKED = -1e30
GAIN_ROWS = 16


HEAD_BLOCK = 128
NT_DIMS = (((1,), (1,)), ((), ()))
TN_DIMS = (((0,), (0,)), ((), ()))


def attention_shares(query, keys, first_row, slot_len, scale):
    scores = lax.dot_general(query, keys, NT_DIMS, preferred_element_type=jnp.float32) * scale
    shape = scores.shape
    rows = query.shape[0]
    query_pos = first_row + lax.broadcasted_iota(jnp.int32, shape, 0)
    key_row = lax.broadcasted_iota(jnp.int32, shape, 1)
    key_pos = first_row + key_row - 2 * rows * (key_row // rows)
    allowed = (key_pos >= 0) & (key_pos <= query_pos) & (key_pos < slot_len)
    scores = jnp.where(allowed, scores, MASKED)
    peak = jnp.max(scores, axis=-1, keepdims=True)
    raised = jnp.exp(scores - peak)
    denominator = jnp.sum(raised, axis=-1, keepdims=True)
    return raised / denominator


def attn_fwd_kernel(head_dim, scale, meta_ref, q_ref, k_ref, v_ref, o_ref):
    first_row = meta_ref[0]
    slot_len = meta_ref[1]
    for j in range(q_ref.shape[1] // head_dim):
        cols = slice(j * head_dim, (j + 1) * head_dim)
        shares = attention_shares(q_ref[:, cols], k_ref[:, cols], first_row, slot_len, scale)
        mixed = jnp.dot(
            shares.astype(jnp.bfloat16), v_ref[:, cols], preferred_element_type=jnp.float32
        )
        o_ref[:, cols] = mixed.astype(o_ref.dtype)


def attn_bwd_kernel(head_dim, scale, meta_ref, q_ref, k_ref, v_ref, do_ref, dq_ref, dkv_ref):
    first_row = meta_ref[0]
    slot_len = meta_ref[1]
    for j in range(q_ref.shape[1] // head_dim):
        cols = slice(j * head_dim, (j + 1) * head_dim)
        query = q_ref[:, cols]
        keys = k_ref[:, cols]
        back = do_ref[:, cols]
        shares = attention_shares(query, keys, first_row, slot_len, scale)
        prob_back = lax.dot_general(back, v_ref[:, cols], NT_DIMS, preferred_element_type=jnp.float32)
        inner = jnp.sum(shares * prob_back, axis=-1, keepdims=True)
        score_back = (shares * (prob_back - inner)).astype(jnp.bfloat16)
        dq_ref[:, cols] = (
            jnp.dot(score_back, keys, preferred_element_type=jnp.float32) * scale
        )
        dkv_ref[:, cols] = (
            lax.dot_general(score_back, query, TN_DIMS, preferred_element_type=jnp.float32) * scale
        ).astype(dkv_ref.dtype)
        half = q_ref.shape[1]
        dkv_ref[:, half + j * head_dim:half + (j + 1) * head_dim] = lax.dot_general(
            shares.astype(jnp.bfloat16), back, TN_DIMS, preferred_element_type=jnp.float32
        ).astype(dkv_ref.dtype)


def attention_forward(meta, query_rows, kv_rows, head_dim, scale):
    rows, width = query_rows.shape
    keys = kv_rows.shape[0]
    blocks = width // HEAD_BLOCK
    return pl.pallas_call(
        functools.partial(attn_fwd_kernel, head_dim, scale),
        out_shape=jax.ShapeDtypeStruct((rows, width), jnp.bfloat16),
        grid_spec=pltpu.PrefetchScalarGridSpec(
            num_scalar_prefetch=1,
            grid=(blocks,),
            in_specs=[
                pl.BlockSpec((rows, HEAD_BLOCK), lambda h, m: (0, h)),
                pl.BlockSpec((keys, HEAD_BLOCK), lambda h, m: (0, h)),
                pl.BlockSpec((keys, HEAD_BLOCK), lambda h, m: (0, h + blocks)),
            ],
            out_specs=pl.BlockSpec((rows, HEAD_BLOCK), lambda h, m: (0, h)),
        ),
        compiler_params=pltpu.CompilerParams(
            dimension_semantics=("arbitrary",), vmem_limit_bytes=48 * 1024 * 1024
        ),
        cost_estimate=pl.CostEstimate(
            flops=4 * rows * keys * width,
            transcendentals=rows * keys * (width // head_dim),
            bytes_accessed=2 * (2 * rows * width + 2 * keys * width),
        ),
    )(meta, query_rows, kv_rows, kv_rows)


def attention_backward(meta, query_rows, kv_rows, back_rows, head_dim, scale):
    rows, width = query_rows.shape
    keys = kv_rows.shape[0]
    blocks = width // HEAD_BLOCK
    return pl.pallas_call(
        functools.partial(attn_bwd_kernel, head_dim, scale),
        out_shape=(
            jax.ShapeDtypeStruct((rows, width), jnp.float32),
            jax.ShapeDtypeStruct((keys, 2 * width), jnp.bfloat16),
        ),
        grid_spec=pltpu.PrefetchScalarGridSpec(
            num_scalar_prefetch=1,
            grid=(blocks,),
            in_specs=[
                pl.BlockSpec((rows, HEAD_BLOCK), lambda h, m: (0, h)),
                pl.BlockSpec((keys, HEAD_BLOCK), lambda h, m: (0, h)),
                pl.BlockSpec((keys, HEAD_BLOCK), lambda h, m: (0, h + blocks)),
                pl.BlockSpec((rows, HEAD_BLOCK), lambda h, m: (0, h)),
            ],
            out_specs=[
                pl.BlockSpec((rows, HEAD_BLOCK), lambda h, m: (0, h)),
                pl.BlockSpec((keys, 2 * HEAD_BLOCK), lambda h, m: (0, h)),
            ],
        ),
        compiler_params=pltpu.CompilerParams(
            dimension_semantics=("arbitrary",), vmem_limit_bytes=48 * 1024 * 1024
        ),
        cost_estimate=pl.CostEstimate(
            flops=10 * rows * keys * width,
            transcendentals=rows * keys * (width // head_dim),
            bytes_accessed=2 * (3 * rows * width + 4 * keys * width) + 4 * rows * width,
        ),
    )(meta, query_rows, kv_rows, kv_rows, back_rows)


def rope_tables(positions, half):
    freq = jnp.exp(
        jnp.arange(half, dtype=jnp.int32).astype(jnp.float32) * (-math.log(10000.0) / half)
    )
    angle = positions.astype(jnp.float32)[:, None] * freq[None, :]
    return (jnp.cos(angle), jnp.sin(angle))


def rotate(value_rows, cosine, sine):
    half = value_rows.shape[-1] // 2
    first = value_rows[..., :half]
    second = value_rows[..., half:]
    return jnp.concatenate(
        [first * cosine - second * sine, second * cosine + first * sine], axis=-1
    )


def norm_apply(value_rows, gain):
    inverse = lax.rsqrt(jnp.mean(value_rows * value_rows, axis=-1, keepdims=True) + EPS)
    return (value_rows * inverse * gain, inverse)


def norm_back(value_rows, inverse, gain, upstream):
    scaled = upstream * gain
    gain_part = jnp.sum(upstream * value_rows * inverse, axis=(0, 1))
    inner = jnp.mean(scaled * value_rows, axis=-1, keepdims=True)
    return (inverse * scaled - value_rows * inverse * inverse * inverse * inner, gain_part)


def gain_block(first, second, width, leading=()):
    pad_cols = width - first.shape[-1] - second.shape[-1]
    row = jnp.concatenate(
        [first, second, jnp.zeros(leading + (pad_cols,), first.dtype)], axis=-1
    )
    row = row[..., None, :]
    pads = [(0, 0)] * len(leading) + [(0, GAIN_ROWS - 1), (0, 0)]
    return jnp.pad(row, pads)


def ctx_allreduce(part, n_ctx):
    total = part
    step = 1
    while step < n_ctx:
        other = lax.ppermute(total, "ctx", [(j, j ^ step) for j in range(n_ctx)])
        total = (total.astype(jnp.float32) + other.astype(jnp.float32)).astype(jnp.bfloat16)
        step *= 2
    return total.astype(jnp.float32)


def body(
    tokens,
    first_value,
    query_weight,
    key_weight,
    value_weight,
    out_weight,
    gate_weight,
    up_weight,
    down_weight,
    prenorm_gain,
    midnorm_gain,
    cotangent,
    lengths,
    assignment,
):
    slots, rows, width = tokens.shape
    assert slots == 1
    head_count = H
    head_dim = width // head_count
    score_scale = head_dim ** (-0.5)
    n_fsdp = lax.axis_size("fsdp")
    n_ctx = lax.axis_size("ctx")
    total_len = rows * n_ctx
    w_rows = query_weight.shape[0]
    g_len = prenorm_gain.shape[0]
    ff = gate_weight.shape[1]
    d_rows = down_weight.shape[0]

    slot_count = assignment.shape[0]
    chosen = assignment[:, None] == jnp.arange(slot_count, dtype=jnp.int32)[None, :]
    lengths_all = jnp.sum(jnp.where(chosen, lengths[None, :], 0), axis=1)
    slot_lengths = lax.dynamic_slice_in_dim(lengths_all, lax.axis_index("fsdp") * slots, slots)
    query_places = lax.axis_index("ctx") * rows + jnp.arange(rows, dtype=jnp.int32)
    valid = query_places[None, :] < slot_lengths[:, None]
    cosine, sine = rope_tables(query_places, head_dim // 2)
    cos_rows = cosine[None, :, None, :]
    sin_rows = sine[None, :, None, :]
    valid_wide = valid[:, :, None]

    attn_pack = jnp.concatenate(
        [query_weight, key_weight, value_weight, out_weight,
         gain_block(prenorm_gain, midnorm_gain, width)],
        axis=0,
    )
    attn_all = lax.all_gather(attn_pack, "fsdp", axis=0, tiled=False)

    def attn_part(i):
        return attn_all[:, i * w_rows:(i + 1) * w_rows, :].reshape(n_fsdp * w_rows, width)

    query_mat, key_mat, value_mat, out_mat = (attn_part(i) for i in range(4))
    prenorm_full = attn_all[:, 4 * w_rows, 0:g_len].reshape(n_fsdp * g_len)
    midnorm_full = attn_all[:, 4 * w_rows, g_len:2 * g_len].reshape(n_fsdp * g_len)

    mlp_pack = jnp.concatenate(
        [gate_weight, up_weight, down_weight.reshape(w_rows, ff)], axis=1
    )
    mlp_all = lax.all_gather(mlp_pack, "fsdp", axis=0, tiled=False)
    gate_mat = mlp_all[:, :, 0:ff].reshape(n_fsdp * w_rows, ff)
    upper_mat = mlp_all[:, :, ff:2 * ff].reshape(n_fsdp * w_rows, ff)
    down_mat = mlp_all[:, :, 2 * ff:].reshape(n_fsdp, d_rows, width).reshape(n_fsdp * d_rows, width)

    tokens_wide = tokens.astype(jnp.float32)
    first_wide = first_value.astype(jnp.float32)
    normed, inverse = norm_apply(tokens_wide, prenorm_full.astype(jnp.float32))
    normed_low = normed.astype(jnp.bfloat16)
    query = jnp.dot(normed_low, query_mat, preferred_element_type=jnp.float32)
    keyed = jnp.dot(normed_low, key_mat, preferred_element_type=jnp.float32)
    own_value = jnp.dot(normed_low, value_mat, preferred_element_type=jnp.float32)
    heads_shape = query.shape[:2] + (head_count, head_dim)
    query_rotated_rows = rotate(query.reshape(heads_shape), cos_rows, sin_rows).astype(jnp.bfloat16)
    key_rot = (
        rotate(keyed.reshape(heads_shape), cos_rows, sin_rows)
        .astype(jnp.bfloat16)
        .reshape(query.shape)
    )
    value_mix = (0.5 * own_value + 0.5 * first_wide).astype(jnp.bfloat16)

    kv_own = jnp.concatenate([key_rot, value_mix], axis=-1).reshape(rows, 2 * width)
    kv_all = jnp.concatenate(
        [kv_own]
        + [
            lax.ppermute(kv_own, "ctx", [(j, j + b) for j in range(n_ctx - b)])
            for b in range(1, n_ctx)
        ],
        axis=0,
    )
    meta = jnp.stack([lax.axis_index("ctx") * rows, slot_lengths[0]]).astype(jnp.int32)
    query_flat = query_rotated_rows.reshape(rows, width)
    mixed_low = attention_forward(
        meta, query_flat, kv_all, head_dim, score_scale
    ).reshape(slots, rows, width)

    middle = tokens_wide + jnp.dot(mixed_low, out_mat, preferred_element_type=jnp.float32)
    normed_two, inverse_two = norm_apply(middle, midnorm_full.astype(jnp.float32))
    normed_two = normed_two.astype(jnp.bfloat16)
    gate = jnp.dot(normed_two, gate_mat, preferred_element_type=jnp.float32)
    upper = jnp.dot(normed_two, upper_mat, preferred_element_type=jnp.float32)
    hidden = (jax.nn.silu(gate) * upper).astype(jnp.bfloat16)
    branch = jnp.dot(hidden, down_mat, preferred_element_type=jnp.float32)
    layer_out = jnp.where(valid_wide, middle + branch, 0.0).astype(jnp.bfloat16)

    cot_wide = jnp.where(valid_wide, cotangent.astype(jnp.float32), 0.0)
    cot_low = cot_wide.astype(jnp.bfloat16)
    down_total = jnp.einsum("srf,sre->fe", hidden, cot_low, preferred_element_type=jnp.float32)
    hidden_back = jnp.einsum("sre,fe->srf", cot_low, down_mat, preferred_element_type=jnp.float32)
    sigma = jax.nn.sigmoid(gate)
    gate_back = (hidden_back * upper * sigma * (1.0 + gate * (1.0 - sigma))).astype(jnp.bfloat16)
    upper_back = (hidden_back * gate * sigma).astype(jnp.bfloat16)
    gate_total = jnp.einsum(
        "srd,srf->df", normed_two, gate_back, preferred_element_type=jnp.float32
    )
    upper_total = jnp.einsum(
        "srd,srf->df", normed_two, upper_back, preferred_element_type=jnp.float32
    )
    normed_two_back = jnp.einsum(
        "srf,df->srd", gate_back, gate_mat, preferred_element_type=jnp.float32
    )
    normed_two_back = normed_two_back + jnp.einsum(
        "srf,df->srd", upper_back, upper_mat, preferred_element_type=jnp.float32
    )
    middle_norm_back, midnorm_total = norm_back(
        middle, inverse_two, midnorm_full.astype(jnp.float32), normed_two_back
    )
    middle_back = cot_wide + middle_norm_back
    middle_low = middle_back.astype(jnp.bfloat16)
    out_total = jnp.einsum("srd,sre->de", mixed_low, middle_low, preferred_element_type=jnp.float32)

    mlp_grads = jnp.concatenate(
        [
            gate_total.reshape(n_fsdp, w_rows, ff),
            upper_total.reshape(n_fsdp, w_rows, ff),
            down_total.reshape(n_fsdp, d_rows, width).reshape(n_fsdp, w_rows, ff),
            out_total.reshape(n_fsdp, w_rows, width),
        ],
        axis=2,
    ).astype(jnp.bfloat16)
    mlp_share = lax.psum_scatter(mlp_grads, "fsdp", scatter_dimension=0, tiled=False)

    blended_value_gradient = jnp.einsum(
        "sre,de->srd", middle_low, out_mat, preferred_element_type=jnp.float32
    ).astype(jnp.bfloat16)
    query_rot_back, kv_back = attention_backward(
        meta, query_flat, kv_all, blended_value_gradient.reshape(rows, width), head_dim, score_scale
    )
    query_rot_back = query_rot_back.reshape(slots, rows, head_count, head_dim)
    kv_back = kv_back.reshape(n_ctx, rows, 2 * width)
    key_value = kv_back[0].astype(jnp.float32)
    for b_shift in range(1, n_ctx):
        key_value = key_value + lax.ppermute(
            kv_back[b_shift], "ctx", [(j, j - b_shift) for j in range(b_shift, n_ctx)]
        ).astype(jnp.float32)
    key_value = key_value.reshape(rows, width // HEAD_BLOCK, 2, HEAD_BLOCK)
    key_rot_back = key_value[:, :, 0, :].reshape(slots, rows, head_count, head_dim)
    value_mix_back = key_value[:, :, 1, :].reshape(slots, rows, width)
    first_grad = 0.5 * value_mix_back
    query_back = (
        rotate(query_rot_back, cos_rows, -sin_rows).reshape(slots, rows, width).astype(jnp.bfloat16)
    )
    key_back = (
        rotate(key_rot_back, cos_rows, -sin_rows).reshape(slots, rows, width).astype(jnp.bfloat16)
    )
    value_back = (0.5 * value_mix_back).astype(jnp.bfloat16)
    query_total = jnp.einsum(
        "srd,sre->de", normed_low, query_back, preferred_element_type=jnp.float32
    )
    key_total = jnp.einsum("srd,sre->de", normed_low, key_back, preferred_element_type=jnp.float32)
    value_total = jnp.einsum(
        "srd,sre->de", normed_low, value_back, preferred_element_type=jnp.float32
    )
    normed_back = jnp.einsum(
        "sre,de->srd", query_back, query_mat, preferred_element_type=jnp.float32
    )
    normed_back = normed_back + jnp.einsum(
        "sre,de->srd", key_back, key_mat, preferred_element_type=jnp.float32
    )
    normed_back = normed_back + jnp.einsum(
        "sre,de->srd", value_back, value_mat, preferred_element_type=jnp.float32
    )
    tokens_norm_back, prenorm_total = norm_back(
        tokens_wide, inverse, prenorm_full.astype(jnp.float32), normed_back
    )
    tokens_grad = middle_back + tokens_norm_back

    attn_grads = jnp.concatenate(
        [
            query_total.reshape(n_fsdp, w_rows, width),
            key_total.reshape(n_fsdp, w_rows, width),
            value_total.reshape(n_fsdp, w_rows, width),
            gain_block(
                prenorm_total.reshape(n_fsdp, g_len),
                midnorm_total.reshape(n_fsdp, g_len),
                width,
                leading=(n_fsdp,),
            ),
        ],
        axis=1,
    ).astype(jnp.bfloat16)
    attn_grads, mlp_share = lax.optimization_barrier((attn_grads, mlp_share))
    mlp_share = ctx_allreduce(mlp_share, n_ctx)
    attn_share = lax.psum_scatter(attn_grads, "fsdp", scatter_dimension=0, tiled=False)
    attn_share = ctx_allreduce(attn_share, n_ctx)

    def attn_grad(i):
        return attn_share[i * w_rows:(i + 1) * w_rows]

    query_grad, key_grad, value_grad = (attn_grad(i) for i in range(3))
    prenorm_grad = attn_share[3 * w_rows, 0:g_len]
    midnorm_grad = attn_share[3 * w_rows, g_len:2 * g_len]
    gate_grad = mlp_share[:, 0:ff]
    up_grad = mlp_share[:, ff:2 * ff]
    down_grad = mlp_share[:, 2 * ff:3 * ff].reshape(d_rows, width)
    out_grad = mlp_share[:, 3 * ff:]
    return (
        layer_out,
        tokens_grad,
        first_grad,
        query_grad,
        key_grad,
        value_grad,
        out_grad,
        gate_grad,
        up_grad,
        down_grad,
        prenorm_grad,
        midnorm_grad,
    )


def solution(mesh):
    placed = (
        P("fsdp", "ctx", None),
        P("fsdp", "ctx", None),
        P("fsdp", None),
        P("fsdp", None),
        P("fsdp", None),
        P("fsdp", None),
        P("fsdp", None),
        P("fsdp", None),
        P("fsdp", None),
        P("fsdp"),
        P("fsdp"),
        P("fsdp", "ctx", None),
        P(),
        P(),
    )
    return jax.shard_map(
        body,
        mesh=mesh,
        in_specs=placed,
        out_specs=(
            P("fsdp", "ctx", None),
            P("fsdp", "ctx", None),
            P("fsdp", "ctx", None),
            P("fsdp", None),
            P("fsdp", None),
            P("fsdp", None),
            P("fsdp", None),
            P("fsdp", None),
            P("fsdp", None),
            P("fsdp", None),
            P("fsdp"),
            P("fsdp"),
        ),
        check_vma=False,
    )
```

```python
import functools
import math

import jax
import jax.numpy as jnp
from jax import lax
from jax.experimental import pallas as pl
from jax.experimental.pallas import tpu as pltpu
from jax.sharding import PartitionSpec as P

H = 16


EPS = 1e-06
MASKED = -1e30
GAIN_ROWS = 16


HEAD_BLOCK = 128
NT_DIMS = (((1,), (1,)), ((), ()))
TN_DIMS = (((0,), (0,)), ((), ()))


def attention_shares(query, keys, first_row, slot_len, scale):
    scores = lax.dot_general(query, keys, NT_DIMS, preferred_element_type=jnp.float32) * scale
    shape = scores.shape
    rows = query.shape[0]
    query_pos = first_row + lax.broadcasted_iota(jnp.int32, shape, 0)
    key_row = lax.broadcasted_iota(jnp.int32, shape, 1)
    key_pos = first_row + key_row - 2 * rows * (key_row // rows)
    allowed = (key_pos >= 0) & (key_pos <= query_pos) & (key_pos < slot_len)
    scores = jnp.where(allowed, scores, MASKED)
    peak = jnp.max(scores, axis=-1, keepdims=True)
    raised = jnp.exp(scores - peak)
    denominator = jnp.sum(raised, axis=-1, keepdims=True)
    return raised / denominator


def attn_fwd_kernel(head_dim, scale, meta_ref, q_ref, k_ref, v_ref, o_ref):
    first_row = meta_ref[0]
    slot_len = meta_ref[1]
    for j in range(q_ref.shape[1] // head_dim):
        cols = slice(j * head_dim, (j + 1) * head_dim)
        shares = attention_shares(q_ref[:, cols], k_ref[:, cols], first_row, slot_len, scale)
        mixed = jnp.dot(
            shares.astype(jnp.bfloat16), v_ref[:, cols], preferred_element_type=jnp.float32
        )
        o_ref[:, cols] = mixed.astype(o_ref.dtype)


def attn_bwd_kernel(head_dim, scale, meta_ref, q_ref, k_ref, v_ref, do_ref, dq_ref, dkv_ref):
    first_row = meta_ref[0]
    slot_len = meta_ref[1]
    for j in range(q_ref.shape[1] // head_dim):
        cols = slice(j * head_dim, (j + 1) * head_dim)
        query = q_ref[:, cols]
        keys = k_ref[:, cols]
        back = do_ref[:, cols]
        shares = attention_shares(query, keys, first_row, slot_len, scale)
        prob_back = lax.dot_general(back, v_ref[:, cols], NT_DIMS, preferred_element_type=jnp.float32)
        inner = jnp.sum(shares * prob_back, axis=-1, keepdims=True)
        score_back = (shares * (prob_back - inner)).astype(jnp.bfloat16)
        dq_ref[:, cols] = (
            jnp.dot(score_back, keys, preferred_element_type=jnp.float32) * scale
        )
        dkv_ref[:, cols] = (
            lax.dot_general(score_back, query, TN_DIMS, preferred_element_type=jnp.float32) * scale
        ).astype(dkv_ref.dtype)
        half = q_ref.shape[1]
        dkv_ref[:, half + j * head_dim:half + (j + 1) * head_dim] = lax.dot_general(
            shares.astype(jnp.bfloat16), back, TN_DIMS, preferred_element_type=jnp.float32
        ).astype(dkv_ref.dtype)


def attention_forward(meta, query_rows, kv_rows, head_dim, scale):
    rows, width = query_rows.shape
    keys = kv_rows.shape[0]
    blocks = width // HEAD_BLOCK
    return pl.pallas_call(
        functools.partial(attn_fwd_kernel, head_dim, scale),
        out_shape=jax.ShapeDtypeStruct((rows, width), jnp.bfloat16),
        grid_spec=pltpu.PrefetchScalarGridSpec(
            num_scalar_prefetch=1,
            grid=(blocks,),
            in_specs=[
                pl.BlockSpec((rows, HEAD_BLOCK), lambda h, m: (0, h)),
                pl.BlockSpec((keys, HEAD_BLOCK), lambda h, m: (0, h)),
                pl.BlockSpec((keys, HEAD_BLOCK), lambda h, m: (0, h + blocks)),
            ],
            out_specs=pl.BlockSpec((rows, HEAD_BLOCK), lambda h, m: (0, h)),
        ),
        compiler_params=pltpu.CompilerParams(
            dimension_semantics=("arbitrary",), vmem_limit_bytes=48 * 1024 * 1024
        ),
        cost_estimate=pl.CostEstimate(
            flops=4 * rows * keys * width,
            transcendentals=rows * keys * (width // head_dim),
            bytes_accessed=2 * (2 * rows * width + 2 * keys * width),
        ),
    )(meta, query_rows, kv_rows, kv_rows)


def attention_backward(meta, query_rows, kv_rows, back_rows, head_dim, scale):
    rows, width = query_rows.shape
    keys = kv_rows.shape[0]
    blocks = width // HEAD_BLOCK
    return pl.pallas_call(
        functools.partial(attn_bwd_kernel, head_dim, scale),
        out_shape=(
            jax.ShapeDtypeStruct((rows, width), jnp.float32),
            jax.ShapeDtypeStruct((keys, 2 * width), jnp.bfloat16),
        ),
        grid_spec=pltpu.PrefetchScalarGridSpec(
            num_scalar_prefetch=1,
            grid=(blocks,),
            in_specs=[
                pl.BlockSpec((rows, HEAD_BLOCK), lambda h, m: (0, h)),
                pl.BlockSpec((keys, HEAD_BLOCK), lambda h, m: (0, h)),
                pl.BlockSpec((keys, HEAD_BLOCK), lambda h, m: (0, h + blocks)),
                pl.BlockSpec((rows, HEAD_BLOCK), lambda h, m: (0, h)),
            ],
            out_specs=[
                pl.BlockSpec((rows, HEAD_BLOCK), lambda h, m: (0, h)),
                pl.BlockSpec((keys, 2 * HEAD_BLOCK), lambda h, m: (0, h)),
            ],
        ),
        compiler_params=pltpu.CompilerParams(
            dimension_semantics=("arbitrary",), vmem_limit_bytes=48 * 1024 * 1024
        ),
        cost_estimate=pl.CostEstimate(
            flops=10 * rows * keys * width,
            transcendentals=rows * keys * (width // head_dim),
            bytes_accessed=2 * (3 * rows * width + 4 * keys * width) + 4 * rows * width,
        ),
    )(meta, query_rows, kv_rows, kv_rows, back_rows)


def rope_tables(positions, half):
    freq = jnp.exp(
        jnp.arange(half, dtype=jnp.int32).astype(jnp.float32) * (-math.log(10000.0) / half)
    )
    angle = positions.astype(jnp.float32)[:, None] * freq[None, :]
    return (jnp.cos(angle), jnp.sin(angle))


def rotate(value_rows, cosine, sine):
    half = value_rows.shape[-1] // 2
    first = value_rows[..., :half]
    second = value_rows[..., half:]
    return jnp.concatenate(
        [first * cosine - second * sine, second * cosine + first * sine], axis=-1
    )


def norm_apply(value_rows, gain):
    inverse = lax.rsqrt(jnp.mean(value_rows * value_rows, axis=-1, keepdims=True) + EPS)
    return (value_rows * inverse * gain, inverse)


def norm_back(value_rows, inverse, gain, upstream):
    scaled = upstream * gain
    gain_part = jnp.sum(upstream * value_rows * inverse, axis=(0, 1))
    inner = jnp.mean(scaled * value_rows, axis=-1, keepdims=True)
    return (inverse * scaled - value_rows * inverse * inverse * inverse * inner, gain_part)


def gain_block(first, second, width, leading=()):
    pad_cols = width - first.shape[-1] - second.shape[-1]
    row = jnp.concatenate(
        [first, second, jnp.zeros(leading + (pad_cols,), first.dtype)], axis=-1
    )
    row = row[..., None, :]
    pads = [(0, 0)] * len(leading) + [(0, GAIN_ROWS - 1), (0, 0)]
    return jnp.pad(row, pads)


def ctx_allreduce(part, n_ctx):
    total = part
    step = 1
    while step < n_ctx:
        other = lax.ppermute(total, "ctx", [(j, j ^ step) for j in range(n_ctx)])
        total = (total.astype(jnp.float32) + other.astype(jnp.float32)).astype(jnp.bfloat16)
        step *= 2
    return total.astype(jnp.float32)


def body(
    tokens,
    first_value,
    query_weight,
    key_weight,
    value_weight,
    out_weight,
    gate_weight,
    up_weight,
    down_weight,
    prenorm_gain,
    midnorm_gain,
    cotangent,
    lengths,
    assignment,
):
    slots, rows, width = tokens.shape
    assert slots == 1
    head_count = H
    head_dim = width // head_count
    score_scale = head_dim ** (-0.5)
    n_fsdp = lax.axis_size("fsdp")
    n_ctx = lax.axis_size("ctx")
    total_len = rows * n_ctx
    w_rows = query_weight.shape[0]
    g_len = prenorm_gain.shape[0]
    ff = gate_weight.shape[1]
    d_rows = down_weight.shape[0]

    slot_count = assignment.shape[0]
    chosen = assignment[:, None] == jnp.arange(slot_count, dtype=jnp.int32)[None, :]
    lengths_all = jnp.sum(jnp.where(chosen, lengths[None, :], 0), axis=1)
    slot_lengths = lax.dynamic_slice_in_dim(lengths_all, lax.axis_index("fsdp") * slots, slots)
    query_places = lax.axis_index("ctx") * rows + jnp.arange(rows, dtype=jnp.int32)
    valid = query_places[None, :] < slot_lengths[:, None]
    cosine, sine = rope_tables(query_places, head_dim // 2)
    cos_rows = cosine[None, :, None, :]
    sin_rows = sine[None, :, None, :]
    valid_wide = valid[:, :, None]

    attn_pack = jnp.concatenate(
        [query_weight, key_weight, value_weight, out_weight,
         gain_block(prenorm_gain, midnorm_gain, width)],
        axis=0,
    )
    attn_all = lax.all_gather(attn_pack, "fsdp", axis=0, tiled=False)

    def attn_part(i):
        return attn_all[:, i * w_rows:(i + 1) * w_rows, :].reshape(n_fsdp * w_rows, width)

    query_mat, key_mat, value_mat, out_mat = (attn_part(i) for i in range(4))
    prenorm_full = attn_all[:, 4 * w_rows, 0:g_len].reshape(n_fsdp * g_len)
    midnorm_full = attn_all[:, 4 * w_rows, g_len:2 * g_len].reshape(n_fsdp * g_len)

    mlp_pack = jnp.concatenate(
        [gate_weight, up_weight, down_weight.reshape(w_rows, ff)], axis=1
    )
    mlp_all = lax.all_gather(mlp_pack, "fsdp", axis=0, tiled=False)
    gate_mat = mlp_all[:, :, 0:ff].reshape(n_fsdp * w_rows, ff)
    upper_mat = mlp_all[:, :, ff:2 * ff].reshape(n_fsdp * w_rows, ff)
    down_mat = mlp_all[:, :, 2 * ff:].reshape(n_fsdp, d_rows, width).reshape(n_fsdp * d_rows, width)

    raw_own = jnp.concatenate([tokens, first_value], axis=-1).reshape(rows, 2 * width)
    raw_all = jnp.concatenate(
        [raw_own]
        + [
            lax.ppermute(raw_own, "ctx", [(j, j + b) for j in range(n_ctx - b)])
            for b in range(1, n_ctx)
        ],
        axis=0,
    )
    block_of = jnp.arange(total_len, dtype=jnp.int32) // rows
    key_places = (
        (lax.axis_index("ctx") - block_of) * rows + jnp.arange(total_len, dtype=jnp.int32) % rows
    )
    key_cos, key_sin = rope_tables(key_places, head_dim // 2)

    tokens_wide = tokens.astype(jnp.float32)
    normed_all, inverse_all = norm_apply(
        raw_all[:, :width].astype(jnp.float32), prenorm_full.astype(jnp.float32)
    )
    normed_all = normed_all.astype(jnp.bfloat16)
    normed_low = normed_all[:rows].reshape(slots, rows, width)
    inverse = inverse_all[:rows].reshape(slots, rows, 1)
    query = jnp.dot(normed_low, query_mat, preferred_element_type=jnp.float32)
    keyed = jnp.dot(normed_all, key_mat, preferred_element_type=jnp.float32)
    own_value = jnp.dot(normed_all, value_mat, preferred_element_type=jnp.float32)
    heads_shape = query.shape[:2] + (head_count, head_dim)
    query_rotated_rows = rotate(query.reshape(heads_shape), cos_rows, sin_rows).astype(jnp.bfloat16)
    key_rot = (
        rotate(
            keyed.reshape(total_len, head_count, head_dim), key_cos[:, None, :], key_sin[:, None, :]
        )
        .astype(jnp.bfloat16)
        .reshape(total_len, width)
    )
    value_mix = (0.5 * own_value + 0.5 * raw_all[:, width:].astype(jnp.float32)).astype(jnp.bfloat16)
    kv_all = jnp.concatenate([key_rot, value_mix], axis=-1)
    meta = jnp.stack([lax.axis_index("ctx") * rows, slot_lengths[0]]).astype(jnp.int32)
    query_flat = query_rotated_rows.reshape(rows, width)
    mixed_low = attention_forward(
        meta, query_flat, kv_all, head_dim, score_scale
    ).reshape(slots, rows, width)

    middle = tokens_wide + jnp.dot(mixed_low, out_mat, preferred_element_type=jnp.float32)
    normed_two, inverse_two = norm_apply(middle, midnorm_full.astype(jnp.float32))
    normed_two = normed_two.astype(jnp.bfloat16)
    gate = jnp.dot(normed_two, gate_mat, preferred_element_type=jnp.float32)
    upper = jnp.dot(normed_two, upper_mat, preferred_element_type=jnp.float32)
    hidden = (jax.nn.silu(gate) * upper).astype(jnp.bfloat16)
    branch = jnp.dot(hidden, down_mat, preferred_element_type=jnp.float32)
    layer_out = jnp.where(valid_wide, middle + branch, 0.0).astype(jnp.bfloat16)

    cot_wide = jnp.where(valid_wide, cotangent.astype(jnp.float32), 0.0)
    cot_low = cot_wide.astype(jnp.bfloat16)
    down_total = jnp.einsum("srf,sre->fe", hidden, cot_low, preferred_element_type=jnp.float32)
    hidden_back = jnp.einsum("sre,fe->srf", cot_low, down_mat, preferred_element_type=jnp.float32)
    sigma = jax.nn.sigmoid(gate)
    gate_back = (hidden_back * upper * sigma * (1.0 + gate * (1.0 - sigma))).astype(jnp.bfloat16)
    upper_back = (hidden_back * gate * sigma).astype(jnp.bfloat16)
    gate_total = jnp.einsum(
        "srd,srf->df", normed_two, gate_back, preferred_element_type=jnp.float32
    )
    upper_total = jnp.einsum(
        "srd,srf->df", normed_two, upper_back, preferred_element_type=jnp.float32
    )
    normed_two_back = jnp.einsum(
        "srf,df->srd", gate_back, gate_mat, preferred_element_type=jnp.float32
    )
    normed_two_back = normed_two_back + jnp.einsum(
        "srf,df->srd", upper_back, upper_mat, preferred_element_type=jnp.float32
    )
    middle_norm_back, midnorm_total = norm_back(
        middle, inverse_two, midnorm_full.astype(jnp.float32), normed_two_back
    )
    middle_back = cot_wide + middle_norm_back
    middle_low = middle_back.astype(jnp.bfloat16)
    out_total = jnp.einsum("srd,sre->de", mixed_low, middle_low, preferred_element_type=jnp.float32)

    mlp_grads = jnp.concatenate(
        [
            gate_total.reshape(n_fsdp, w_rows, ff),
            upper_total.reshape(n_fsdp, w_rows, ff),
            down_total.reshape(n_fsdp, d_rows, width).reshape(n_fsdp, w_rows, ff),
            out_total.reshape(n_fsdp, w_rows, width),
        ],
        axis=2,
    ).astype(jnp.bfloat16)
    mlp_share = lax.psum_scatter(mlp_grads, "fsdp", scatter_dimension=0, tiled=False)

    blended_value_gradient = jnp.einsum(
        "sre,de->srd", middle_low, out_mat, preferred_element_type=jnp.float32
    ).astype(jnp.bfloat16)
    query_rot_back, kv_back = attention_backward(
        meta, query_flat, kv_all, blended_value_gradient.reshape(rows, width), head_dim, score_scale
    )
    query_rot_back = query_rot_back.reshape(slots, rows, head_count, head_dim)
    kv_back = kv_back.reshape(n_ctx, rows, 2 * width)
    key_value = kv_back[0].astype(jnp.float32)
    for b_shift in range(1, n_ctx):
        key_value = key_value + lax.ppermute(
            kv_back[b_shift], "ctx", [(j, j - b_shift) for j in range(b_shift, n_ctx)]
        ).astype(jnp.float32)
    key_value = key_value.reshape(rows, width // HEAD_BLOCK, 2, HEAD_BLOCK)
    key_rot_back = key_value[:, :, 0, :].reshape(slots, rows, head_count, head_dim)
    value_mix_back = key_value[:, :, 1, :].reshape(slots, rows, width)
    first_grad = 0.5 * value_mix_back
    query_back = (
        rotate(query_rot_back, cos_rows, -sin_rows).reshape(slots, rows, width).astype(jnp.bfloat16)
    )
    key_back = (
        rotate(key_rot_back, cos_rows, -sin_rows).reshape(slots, rows, width).astype(jnp.bfloat16)
    )
    value_back = (0.5 * value_mix_back).astype(jnp.bfloat16)
    query_total = jnp.einsum(
        "srd,sre->de", normed_low, query_back, preferred_element_type=jnp.float32
    )
    key_total = jnp.einsum("srd,sre->de", normed_low, key_back, preferred_element_type=jnp.float32)
    value_total = jnp.einsum(
        "srd,sre->de", normed_low, value_back, preferred_element_type=jnp.float32
    )
    normed_back = jnp.einsum(
        "sre,de->srd", query_back, query_mat, preferred_element_type=jnp.float32
    )
    normed_back = normed_back + jnp.einsum(
        "sre,de->srd", key_back, key_mat, preferred_element_type=jnp.float32
    )
    normed_back = normed_back + jnp.einsum(
        "sre,de->srd", value_back, value_mat, preferred_element_type=jnp.float32
    )
    tokens_norm_back, prenorm_total = norm_back(
        tokens_wide, inverse, prenorm_full.astype(jnp.float32), normed_back
    )
    tokens_grad = middle_back + tokens_norm_back

    attn_grads = jnp.concatenate(
        [
            query_total.reshape(n_fsdp, w_rows, width),
            key_total.reshape(n_fsdp, w_rows, width),
            value_total.reshape(n_fsdp, w_rows, width),
            gain_block(
                prenorm_total.reshape(n_fsdp, g_len),
                midnorm_total.reshape(n_fsdp, g_len),
                width,
                leading=(n_fsdp,),
            ),
        ],
        axis=1,
    ).astype(jnp.bfloat16)
    attn_grads, mlp_share = lax.optimization_barrier((attn_grads, mlp_share))
    mlp_share = ctx_allreduce(mlp_share, n_ctx)
    attn_share = lax.psum_scatter(attn_grads, "fsdp", scatter_dimension=0, tiled=False)
    attn_share = ctx_allreduce(attn_share, n_ctx)

    def attn_grad(i):
        return attn_share[i * w_rows:(i + 1) * w_rows]

    query_grad, key_grad, value_grad = (attn_grad(i) for i in range(3))
    prenorm_grad = attn_share[3 * w_rows, 0:g_len]
    midnorm_grad = attn_share[3 * w_rows, g_len:2 * g_len]
    gate_grad = mlp_share[:, 0:ff]
    up_grad = mlp_share[:, ff:2 * ff]
    down_grad = mlp_share[:, 2 * ff:3 * ff].reshape(d_rows, width)
    out_grad = mlp_share[:, 3 * ff:]
    return (
        layer_out,
        tokens_grad,
        first_grad,
        query_grad,
        key_grad,
        value_grad,
        out_grad,
        gate_grad,
        up_grad,
        down_grad,
        prenorm_grad,
        midnorm_grad,
    )


def solution(mesh):
    placed = (
        P("fsdp", "ctx", None),
        P("fsdp", "ctx", None),
        P("fsdp", None),
        P("fsdp", None),
        P("fsdp", None),
        P("fsdp", None),
        P("fsdp", None),
        P("fsdp", None),
        P("fsdp", None),
        P("fsdp"),
        P("fsdp"),
        P("fsdp", "ctx", None),
        P(),
        P(),
    )
    return jax.shard_map(
        body,
        mesh=mesh,
        in_specs=placed,
        out_specs=(
            P("fsdp", "ctx", None),
            P("fsdp", "ctx", None),
            P("fsdp", "ctx", None),
            P("fsdp", None),
            P("fsdp", None),
            P("fsdp", None),
            P("fsdp", None),
            P("fsdp", None),
            P("fsdp", None),
            P("fsdp", None),
            P("fsdp"),
            P("fsdp"),
        ),
        check_vma=False,
    )
```

```python
import functools
import math

import jax
import jax.numpy as jnp
from jax import lax
from jax.experimental import pallas as pl
from jax.experimental.pallas import tpu as pltpu
from jax.sharding import PartitionSpec as P

H = 16


EPS = 1e-06
MASKED = -1e30
GAIN_ROWS = 16


HEAD_BLOCK = 128
NT_DIMS = (((1,), (1,)), ((), ()))
TN_DIMS = (((0,), (0,)), ((), ()))


def attention_shares(query, keys, first_row, slot_len, scale):
    scores = lax.dot_general(query, keys, NT_DIMS, preferred_element_type=jnp.float32) * scale
    shape = scores.shape
    query_pos = first_row + lax.broadcasted_iota(jnp.int32, shape, 0)
    key_pos = lax.broadcasted_iota(jnp.int32, shape, 1)
    allowed = (key_pos <= query_pos) & (key_pos < slot_len)
    scores = jnp.where(allowed, scores, MASKED)
    peak = jnp.max(scores, axis=-1, keepdims=True)
    raised = jnp.exp(scores - peak)
    denominator = jnp.sum(raised, axis=-1, keepdims=True)
    return raised / denominator


def attn_fwd_kernel(head_dim, scale, meta_ref, q_ref, k_ref, v_ref, o_ref):
    first_row = meta_ref[0]
    slot_len = meta_ref[1]
    for j in range(q_ref.shape[1] // head_dim):
        cols = slice(j * head_dim, (j + 1) * head_dim)
        shares = attention_shares(q_ref[:, cols], k_ref[:, cols], first_row, slot_len, scale)
        mixed = jnp.dot(
            shares.astype(jnp.bfloat16), v_ref[:, cols], preferred_element_type=jnp.float32
        )
        o_ref[:, cols] = mixed.astype(o_ref.dtype)


def attn_bwd_kernel(head_dim, scale, meta_ref, q_ref, k_ref, v_ref, do_ref, dq_ref, dkv_ref):
    first_row = meta_ref[0]
    slot_len = meta_ref[1]
    for j in range(q_ref.shape[1] // head_dim):
        cols = slice(j * head_dim, (j + 1) * head_dim)
        query = q_ref[:, cols]
        keys = k_ref[:, cols]
        back = do_ref[:, cols]
        shares = attention_shares(query, keys, first_row, slot_len, scale)
        prob_back = lax.dot_general(back, v_ref[:, cols], NT_DIMS, preferred_element_type=jnp.float32)
        inner = jnp.sum(shares * prob_back, axis=-1, keepdims=True)
        score_back = (shares * (prob_back - inner)).astype(jnp.bfloat16)
        dq_ref[:, cols] = (
            jnp.dot(score_back, keys, preferred_element_type=jnp.float32) * scale
        )
        dkv_ref[:, cols] = (
            lax.dot_general(score_back, query, TN_DIMS, preferred_element_type=jnp.float32) * scale
        ).astype(dkv_ref.dtype)
        half = q_ref.shape[1]
        dkv_ref[:, half + j * head_dim:half + (j + 1) * head_dim] = lax.dot_general(
            shares.astype(jnp.bfloat16), back, TN_DIMS, preferred_element_type=jnp.float32
        ).astype(dkv_ref.dtype)


def attention_forward(meta, query_rows, kv_rows, head_dim, scale):
    rows, width = query_rows.shape
    keys = kv_rows.shape[0]
    blocks = width // HEAD_BLOCK
    return pl.pallas_call(
        functools.partial(attn_fwd_kernel, head_dim, scale),
        out_shape=jax.ShapeDtypeStruct((rows, width), jnp.bfloat16),
        grid_spec=pltpu.PrefetchScalarGridSpec(
            num_scalar_prefetch=1,
            grid=(blocks,),
            in_specs=[
                pl.BlockSpec((rows, HEAD_BLOCK), lambda h, m: (0, h)),
                pl.BlockSpec((keys, HEAD_BLOCK), lambda h, m: (0, h)),
                pl.BlockSpec((keys, HEAD_BLOCK), lambda h, m: (0, h + blocks)),
            ],
            out_specs=pl.BlockSpec((rows, HEAD_BLOCK), lambda h, m: (0, h)),
        ),
        compiler_params=pltpu.CompilerParams(
            dimension_semantics=("arbitrary",), vmem_limit_bytes=48 * 1024 * 1024
        ),
        cost_estimate=pl.CostEstimate(
            flops=4 * rows * keys * width,
            transcendentals=rows * keys * (width // head_dim),
            bytes_accessed=2 * (2 * rows * width + 2 * keys * width),
        ),
    )(meta, query_rows, kv_rows, kv_rows)


def attention_backward(meta, query_rows, kv_rows, back_rows, head_dim, scale):
    rows, width = query_rows.shape
    keys = kv_rows.shape[0]
    blocks = width // HEAD_BLOCK
    return pl.pallas_call(
        functools.partial(attn_bwd_kernel, head_dim, scale),
        out_shape=(
            jax.ShapeDtypeStruct((rows, width), jnp.float32),
            jax.ShapeDtypeStruct((keys, 2 * width), jnp.bfloat16),
        ),
        grid_spec=pltpu.PrefetchScalarGridSpec(
            num_scalar_prefetch=1,
            grid=(blocks,),
            in_specs=[
                pl.BlockSpec((rows, HEAD_BLOCK), lambda h, m: (0, h)),
                pl.BlockSpec((keys, HEAD_BLOCK), lambda h, m: (0, h)),
                pl.BlockSpec((keys, HEAD_BLOCK), lambda h, m: (0, h + blocks)),
                pl.BlockSpec((rows, HEAD_BLOCK), lambda h, m: (0, h)),
            ],
            out_specs=[
                pl.BlockSpec((rows, HEAD_BLOCK), lambda h, m: (0, h)),
                pl.BlockSpec((keys, 2 * HEAD_BLOCK), lambda h, m: (0, h)),
            ],
        ),
        compiler_params=pltpu.CompilerParams(
            dimension_semantics=("arbitrary",), vmem_limit_bytes=48 * 1024 * 1024
        ),
        cost_estimate=pl.CostEstimate(
            flops=10 * rows * keys * width,
            transcendentals=rows * keys * (width // head_dim),
            bytes_accessed=2 * (3 * rows * width + 4 * keys * width) + 4 * rows * width,
        ),
    )(meta, query_rows, kv_rows, kv_rows, back_rows)


def rope_tables(positions, half):
    freq = jnp.exp(
        jnp.arange(half, dtype=jnp.int32).astype(jnp.float32) * (-math.log(10000.0) / half)
    )
    angle = positions.astype(jnp.float32)[:, None] * freq[None, :]
    return (jnp.cos(angle), jnp.sin(angle))


def rotate(value_rows, cosine, sine):
    half = value_rows.shape[-1] // 2
    first = value_rows[..., :half]
    second = value_rows[..., half:]
    return jnp.concatenate(
        [first * cosine - second * sine, second * cosine + first * sine], axis=-1
    )


def norm_apply(value_rows, gain):
    inverse = lax.rsqrt(jnp.mean(value_rows * value_rows, axis=-1, keepdims=True) + EPS)
    return (value_rows * inverse * gain, inverse)


def norm_back(value_rows, inverse, gain, upstream):
    scaled = upstream * gain
    gain_part = jnp.sum(upstream * value_rows * inverse, axis=(0, 1))
    inner = jnp.mean(scaled * value_rows, axis=-1, keepdims=True)
    return (inverse * scaled - value_rows * inverse * inverse * inverse * inner, gain_part)


def gain_block(first, second, width, leading=()):
    pad_cols = width - first.shape[-1] - second.shape[-1]
    row = jnp.concatenate(
        [first, second, jnp.zeros(leading + (pad_cols,), first.dtype)], axis=-1
    )
    row = row[..., None, :]
    pads = [(0, 0)] * len(leading) + [(0, GAIN_ROWS - 1), (0, 0)]
    return jnp.pad(row, pads)


def ctx_allreduce(part, n_ctx):
    total = part
    step = 1
    while step < n_ctx:
        other = lax.ppermute(total, "ctx", [(j, j ^ step) for j in range(n_ctx)])
        total = (total.astype(jnp.float32) + other.astype(jnp.float32)).astype(jnp.bfloat16)
        step *= 2
    return total.astype(jnp.float32)


def body(
    tokens,
    first_value,
    query_weight,
    key_weight,
    value_weight,
    out_weight,
    gate_weight,
    up_weight,
    down_weight,
    prenorm_gain,
    midnorm_gain,
    cotangent,
    lengths,
    assignment,
):
    slots, rows, width = tokens.shape
    assert slots == 1
    head_count = H
    head_dim = width // head_count
    score_scale = head_dim ** (-0.5)
    n_fsdp = lax.axis_size("fsdp")
    n_ctx = lax.axis_size("ctx")
    total_len = rows * n_ctx
    w_rows = query_weight.shape[0]
    g_len = prenorm_gain.shape[0]
    ff = gate_weight.shape[1]
    d_rows = down_weight.shape[0]

    slot_count = assignment.shape[0]
    chosen = assignment[:, None] == jnp.arange(slot_count, dtype=jnp.int32)[None, :]
    lengths_all = jnp.sum(jnp.where(chosen, lengths[None, :], 0), axis=1)
    slot_lengths = lax.dynamic_slice_in_dim(lengths_all, lax.axis_index("fsdp") * slots, slots)
    query_places = lax.axis_index("ctx") * rows + jnp.arange(rows, dtype=jnp.int32)
    valid = query_places[None, :] < slot_lengths[:, None]
    cosine, sine = rope_tables(query_places, head_dim // 2)
    cos_rows = cosine[None, :, None, :]
    sin_rows = sine[None, :, None, :]
    valid_wide = valid[:, :, None]

    attn_pack = jnp.concatenate(
        [query_weight, key_weight, value_weight, out_weight,
         gain_block(prenorm_gain, midnorm_gain, width)],
        axis=0,
    )
    attn_all = lax.all_gather(attn_pack, "fsdp", axis=0, tiled=False)

    def attn_part(i):
        return attn_all[:, i * w_rows:(i + 1) * w_rows, :].reshape(n_fsdp * w_rows, width)

    query_mat, key_mat, value_mat, out_mat = (attn_part(i) for i in range(4))
    prenorm_full = attn_all[:, 4 * w_rows, 0:g_len].reshape(n_fsdp * g_len)
    midnorm_full = attn_all[:, 4 * w_rows, g_len:2 * g_len].reshape(n_fsdp * g_len)

    mlp_pack = jnp.concatenate(
        [gate_weight, up_weight, down_weight.reshape(w_rows, ff)], axis=1
    )
    mlp_all = lax.all_gather(mlp_pack, "fsdp", axis=0, tiled=False)
    gate_mat = mlp_all[:, :, 0:ff].reshape(n_fsdp * w_rows, ff)
    upper_mat = mlp_all[:, :, ff:2 * ff].reshape(n_fsdp * w_rows, ff)
    down_mat = mlp_all[:, :, 2 * ff:].reshape(n_fsdp, d_rows, width).reshape(n_fsdp * d_rows, width)

    tokens_wide = tokens.astype(jnp.float32)
    first_wide = first_value.astype(jnp.float32)
    normed, inverse = norm_apply(tokens_wide, prenorm_full.astype(jnp.float32))
    normed_low = normed.astype(jnp.bfloat16)
    query = jnp.dot(normed_low, query_mat, preferred_element_type=jnp.float32)
    keyed = jnp.dot(normed_low, key_mat, preferred_element_type=jnp.float32)
    own_value = jnp.dot(normed_low, value_mat, preferred_element_type=jnp.float32)
    heads_shape = query.shape[:2] + (head_count, head_dim)
    query_rotated_rows = rotate(query.reshape(heads_shape), cos_rows, sin_rows).astype(jnp.bfloat16)
    key_rot = (
        rotate(keyed.reshape(heads_shape), cos_rows, sin_rows)
        .astype(jnp.bfloat16)
        .reshape(query.shape)
    )
    value_mix = (0.5 * own_value + 0.5 * first_wide).astype(jnp.bfloat16)

    kv_own = jnp.concatenate([key_rot, value_mix], axis=-1).reshape(rows, 2 * width)
    kv_all = lax.all_to_all(
        jnp.broadcast_to(kv_own[None], (n_ctx, rows, 2 * width)), "ctx", 0, 0, tiled=False
    ).reshape(total_len, 2 * width)
    meta = jnp.stack([lax.axis_index("ctx") * rows, slot_lengths[0]]).astype(jnp.int32)
    query_flat = query_rotated_rows.reshape(rows, width)
    mixed_low = attention_forward(
        meta, query_flat, kv_all, head_dim, score_scale
    ).reshape(slots, rows, width)

    middle = tokens_wide + jnp.dot(mixed_low, out_mat, preferred_element_type=jnp.float32)
    normed_two, inverse_two = norm_apply(middle, midnorm_full.astype(jnp.float32))
    normed_two = normed_two.astype(jnp.bfloat16)
    gate = jnp.dot(normed_two, gate_mat, preferred_element_type=jnp.float32)
    upper = jnp.dot(normed_two, upper_mat, preferred_element_type=jnp.float32)
    hidden = (jax.nn.silu(gate) * upper).astype(jnp.bfloat16)
    branch = jnp.dot(hidden, down_mat, preferred_element_type=jnp.float32)
    layer_out = jnp.where(valid_wide, middle + branch, 0.0).astype(jnp.bfloat16)

    cot_wide = jnp.where(valid_wide, cotangent.astype(jnp.float32), 0.0)
    cot_low = cot_wide.astype(jnp.bfloat16)
    down_total = jnp.einsum("srf,sre->fe", hidden, cot_low, preferred_element_type=jnp.float32)
    hidden_back = jnp.einsum("sre,fe->srf", cot_low, down_mat, preferred_element_type=jnp.float32)
    sigma = jax.nn.sigmoid(gate)
    gate_back = (hidden_back * upper * sigma * (1.0 + gate * (1.0 - sigma))).astype(jnp.bfloat16)
    upper_back = (hidden_back * gate * sigma).astype(jnp.bfloat16)
    gate_total = jnp.einsum(
        "srd,srf->df", normed_two, gate_back, preferred_element_type=jnp.float32
    )
    upper_total = jnp.einsum(
        "srd,srf->df", normed_two, upper_back, preferred_element_type=jnp.float32
    )
    normed_two_back = jnp.einsum(
        "srf,df->srd", gate_back, gate_mat, preferred_element_type=jnp.float32
    )
    normed_two_back = normed_two_back + jnp.einsum(
        "srf,df->srd", upper_back, upper_mat, preferred_element_type=jnp.float32
    )
    middle_norm_back, midnorm_total = norm_back(
        middle, inverse_two, midnorm_full.astype(jnp.float32), normed_two_back
    )
    middle_back = cot_wide + middle_norm_back
    middle_low = middle_back.astype(jnp.bfloat16)
    out_total = jnp.einsum("srd,sre->de", mixed_low, middle_low, preferred_element_type=jnp.float32)

    mlp_grads = jnp.concatenate(
        [
            gate_total.reshape(n_fsdp, w_rows, ff),
            upper_total.reshape(n_fsdp, w_rows, ff),
            down_total.reshape(n_fsdp, d_rows, width).reshape(n_fsdp, w_rows, ff),
            out_total.reshape(n_fsdp, w_rows, width),
        ],
        axis=2,
    ).astype(jnp.bfloat16)
    mlp_share = lax.psum_scatter(mlp_grads, "fsdp", scatter_dimension=0, tiled=False)

    blended_value_gradient = jnp.einsum(
        "sre,de->srd", middle_low, out_mat, preferred_element_type=jnp.float32
    ).astype(jnp.bfloat16)
    query_rot_back, kv_back = attention_backward(
        meta, query_flat, kv_all, blended_value_gradient.reshape(rows, width), head_dim, score_scale
    )
    query_rot_back = query_rot_back.reshape(slots, rows, head_count, head_dim)
    key_value = jnp.sum(
        lax.all_to_all(kv_back.reshape(n_ctx, rows, 2 * width), "ctx", 0, 0, tiled=False).astype(
            jnp.float32
        ),
        axis=0,
    )
    key_value = key_value.reshape(rows, width // HEAD_BLOCK, 2, HEAD_BLOCK)
    key_rot_back = key_value[:, :, 0, :].reshape(slots, rows, head_count, head_dim)
    value_mix_back = key_value[:, :, 1, :].reshape(slots, rows, width)
    first_grad = 0.5 * value_mix_back
    query_back = (
        rotate(query_rot_back, cos_rows, -sin_rows).reshape(slots, rows, width).astype(jnp.bfloat16)
    )
    key_back = (
        rotate(key_rot_back, cos_rows, -sin_rows).reshape(slots, rows, width).astype(jnp.bfloat16)
    )
    value_back = (0.5 * value_mix_back).astype(jnp.bfloat16)
    query_total = jnp.einsum(
        "srd,sre->de", normed_low, query_back, preferred_element_type=jnp.float32
    )
    key_total = jnp.einsum("srd,sre->de", normed_low, key_back, preferred_element_type=jnp.float32)
    value_total = jnp.einsum(
        "srd,sre->de", normed_low, value_back, preferred_element_type=jnp.float32
    )
    normed_back = jnp.einsum(
        "sre,de->srd", query_back, query_mat, preferred_element_type=jnp.float32
    )
    normed_back = normed_back + jnp.einsum(
        "sre,de->srd", key_back, key_mat, preferred_element_type=jnp.float32
    )
    normed_back = normed_back + jnp.einsum(
        "sre,de->srd", value_back, value_mat, preferred_element_type=jnp.float32
    )
    tokens_norm_back, prenorm_total = norm_back(
        tokens_wide, inverse, prenorm_full.astype(jnp.float32), normed_back
    )
    tokens_grad = middle_back + tokens_norm_back

    attn_grads = jnp.concatenate(
        [
            query_total.reshape(n_fsdp, w_rows, width),
            key_total.reshape(n_fsdp, w_rows, width),
            value_total.reshape(n_fsdp, w_rows, width),
            gain_block(
                prenorm_total.reshape(n_fsdp, g_len),
                midnorm_total.reshape(n_fsdp, g_len),
                width,
                leading=(n_fsdp,),
            ),
        ],
        axis=1,
    ).astype(jnp.bfloat16)
    attn_grads, mlp_share = lax.optimization_barrier((attn_grads, mlp_share))
    mlp_share = ctx_allreduce(mlp_share, n_ctx)
    attn_share = lax.psum_scatter(attn_grads, "fsdp", scatter_dimension=0, tiled=False)
    attn_share = ctx_allreduce(attn_share, n_ctx)

    def attn_grad(i):
        return attn_share[i * w_rows:(i + 1) * w_rows]

    query_grad, key_grad, value_grad = (attn_grad(i) for i in range(3))
    prenorm_grad = attn_share[3 * w_rows, 0:g_len]
    midnorm_grad = attn_share[3 * w_rows, g_len:2 * g_len]
    gate_grad = mlp_share[:, 0:ff]
    up_grad = mlp_share[:, ff:2 * ff]
    down_grad = mlp_share[:, 2 * ff:3 * ff].reshape(d_rows, width)
    out_grad = mlp_share[:, 3 * ff:]
    return (
        layer_out,
        tokens_grad,
        first_grad,
        query_grad,
        key_grad,
        value_grad,
        out_grad,
        gate_grad,
        up_grad,
        down_grad,
        prenorm_grad,
        midnorm_grad,
    )


def solution(mesh):
    placed = (
        P("fsdp", "ctx", None),
        P("fsdp", "ctx", None),
        P("fsdp", None),
        P("fsdp", None),
        P("fsdp", None),
        P("fsdp", None),
        P("fsdp", None),
        P("fsdp", None),
        P("fsdp", None),
        P("fsdp"),
        P("fsdp"),
        P("fsdp", "ctx", None),
        P(),
        P(),
    )
    return jax.shard_map(
        body,
        mesh=mesh,
        in_specs=placed,
        out_specs=(
            P("fsdp", "ctx", None),
            P("fsdp", "ctx", None),
            P("fsdp", "ctx", None),
            P("fsdp", None),
            P("fsdp", None),
            P("fsdp", None),
            P("fsdp", None),
            P("fsdp", None),
            P("fsdp", None),
            P("fsdp", None),
            P("fsdp"),
            P("fsdp"),
        ),
        check_vma=False,
    )
```

```python
import functools
import math

import jax
import jax.numpy as jnp
from jax import lax
from jax.experimental import pallas as pl
from jax.experimental.pallas import tpu as pltpu
from jax.sharding import PartitionSpec as P

H = 16


EPS = 1e-06
MASKED = -1e30
GAIN_ROWS = 16


HEAD_BLOCK = 128
NT_DIMS = (((1,), (1,)), ((), ()))
TN_DIMS = (((0,), (0,)), ((), ()))


def attention_shares(query, keys, first_row, slot_len, scale):
    scores = lax.dot_general(query, keys, NT_DIMS, preferred_element_type=jnp.float32) * scale
    shape = scores.shape
    query_pos = first_row + lax.broadcasted_iota(jnp.int32, shape, 0)
    key_pos = lax.broadcasted_iota(jnp.int32, shape, 1)
    allowed = (key_pos <= query_pos) & (key_pos < slot_len)
    scores = jnp.where(allowed, scores, MASKED)
    peak = jnp.max(scores, axis=-1, keepdims=True)
    raised = jnp.exp(scores - peak)
    denominator = jnp.sum(raised, axis=-1, keepdims=True)
    return raised / denominator


def attn_fwd_kernel(head_dim, scale, meta_ref, q_ref, k_ref, v_ref, o_ref):
    first_row = meta_ref[0]
    slot_len = meta_ref[1]
    for j in range(q_ref.shape[1] // head_dim):
        cols = slice(j * head_dim, (j + 1) * head_dim)
        shares = attention_shares(q_ref[:, cols], k_ref[:, cols], first_row, slot_len, scale)
        mixed = jnp.dot(
            shares.astype(jnp.bfloat16), v_ref[:, cols], preferred_element_type=jnp.float32
        )
        o_ref[:, cols] = mixed.astype(o_ref.dtype)


def attn_bwd_kernel(head_dim, scale, meta_ref, q_ref, k_ref, v_ref, do_ref, dq_ref, dkv_ref):
    first_row = meta_ref[0]
    slot_len = meta_ref[1]
    for j in range(q_ref.shape[1] // head_dim):
        cols = slice(j * head_dim, (j + 1) * head_dim)
        query = q_ref[:, cols]
        keys = k_ref[:, cols]
        back = do_ref[:, cols]
        shares = attention_shares(query, keys, first_row, slot_len, scale)
        prob_back = lax.dot_general(back, v_ref[:, cols], NT_DIMS, preferred_element_type=jnp.float32)
        inner = jnp.sum(shares * prob_back, axis=-1, keepdims=True)
        score_back = (shares * (prob_back - inner)).astype(jnp.bfloat16)
        dq_ref[:, cols] = (
            jnp.dot(score_back, keys, preferred_element_type=jnp.float32) * scale
        )
        dkv_ref[:, cols] = (
            lax.dot_general(score_back, query, TN_DIMS, preferred_element_type=jnp.float32) * scale
        ).astype(dkv_ref.dtype)
        half = q_ref.shape[1]
        dkv_ref[:, half + j * head_dim:half + (j + 1) * head_dim] = lax.dot_general(
            shares.astype(jnp.bfloat16), back, TN_DIMS, preferred_element_type=jnp.float32
        ).astype(dkv_ref.dtype)


def attention_forward(meta, query_rows, kv_rows, head_dim, scale):
    rows, width = query_rows.shape
    keys = kv_rows.shape[0]
    blocks = width // HEAD_BLOCK
    return pl.pallas_call(
        functools.partial(attn_fwd_kernel, head_dim, scale),
        out_shape=jax.ShapeDtypeStruct((rows, width), jnp.bfloat16),
        grid_spec=pltpu.PrefetchScalarGridSpec(
            num_scalar_prefetch=1,
            grid=(blocks,),
            in_specs=[
                pl.BlockSpec((rows, HEAD_BLOCK), lambda h, m: (0, h)),
                pl.BlockSpec((keys, HEAD_BLOCK), lambda h, m: (0, h)),
                pl.BlockSpec((keys, HEAD_BLOCK), lambda h, m: (0, h + blocks)),
            ],
            out_specs=pl.BlockSpec((rows, HEAD_BLOCK), lambda h, m: (0, h)),
        ),
        compiler_params=pltpu.CompilerParams(
            dimension_semantics=("arbitrary",), vmem_limit_bytes=48 * 1024 * 1024
        ),
        cost_estimate=pl.CostEstimate(
            flops=4 * rows * keys * width,
            transcendentals=rows * keys * (width // head_dim),
            bytes_accessed=2 * (2 * rows * width + 2 * keys * width),
        ),
    )(meta, query_rows, kv_rows, kv_rows)


def attention_backward(meta, query_rows, kv_rows, back_rows, head_dim, scale):
    rows, width = query_rows.shape
    keys = kv_rows.shape[0]
    blocks = width // HEAD_BLOCK
    return pl.pallas_call(
        functools.partial(attn_bwd_kernel, head_dim, scale),
        out_shape=(
            jax.ShapeDtypeStruct((rows, width), jnp.float32),
            jax.ShapeDtypeStruct((keys, 2 * width), jnp.bfloat16),
        ),
        grid_spec=pltpu.PrefetchScalarGridSpec(
            num_scalar_prefetch=1,
            grid=(blocks,),
            in_specs=[
                pl.BlockSpec((rows, HEAD_BLOCK), lambda h, m: (0, h)),
                pl.BlockSpec((keys, HEAD_BLOCK), lambda h, m: (0, h)),
                pl.BlockSpec((keys, HEAD_BLOCK), lambda h, m: (0, h + blocks)),
                pl.BlockSpec((rows, HEAD_BLOCK), lambda h, m: (0, h)),
            ],
            out_specs=[
                pl.BlockSpec((rows, HEAD_BLOCK), lambda h, m: (0, h)),
                pl.BlockSpec((keys, 2 * HEAD_BLOCK), lambda h, m: (0, h)),
            ],
        ),
        compiler_params=pltpu.CompilerParams(
            dimension_semantics=("arbitrary",), vmem_limit_bytes=48 * 1024 * 1024
        ),
        cost_estimate=pl.CostEstimate(
            flops=10 * rows * keys * width,
            transcendentals=rows * keys * (width // head_dim),
            bytes_accessed=2 * (3 * rows * width + 4 * keys * width) + 4 * rows * width,
        ),
    )(meta, query_rows, kv_rows, kv_rows, back_rows)


def rope_tables(positions, half):
    freq = jnp.exp(
        jnp.arange(half, dtype=jnp.int32).astype(jnp.float32) * (-math.log(10000.0) / half)
    )
    angle = positions.astype(jnp.float32)[:, None] * freq[None, :]
    return (jnp.cos(angle), jnp.sin(angle))


def rotate(value_rows, cosine, sine):
    half = value_rows.shape[-1] // 2
    first = value_rows[..., :half]
    second = value_rows[..., half:]
    return jnp.concatenate(
        [first * cosine - second * sine, second * cosine + first * sine], axis=-1
    )


def norm_apply(value_rows, gain):
    inverse = lax.rsqrt(jnp.mean(value_rows * value_rows, axis=-1, keepdims=True) + EPS)
    return (value_rows * inverse * gain, inverse)


def norm_back(value_rows, inverse, gain, upstream):
    scaled = upstream * gain
    gain_part = jnp.sum(upstream * value_rows * inverse, axis=(0, 1))
    inner = jnp.mean(scaled * value_rows, axis=-1, keepdims=True)
    return (inverse * scaled - value_rows * inverse * inverse * inverse * inner, gain_part)


def gain_block(first, second, width, leading=()):
    pad_cols = width - first.shape[-1] - second.shape[-1]
    row = jnp.concatenate(
        [first, second, jnp.zeros(leading + (pad_cols,), first.dtype)], axis=-1
    )
    row = row[..., None, :]
    pads = [(0, 0)] * len(leading) + [(0, GAIN_ROWS - 1), (0, 0)]
    return jnp.pad(row, pads)


def ctx_allreduce(part, n_ctx):
    total = part
    step = 1
    while step < n_ctx:
        other = lax.ppermute(total, "ctx", [(j, j ^ step) for j in range(n_ctx)])
        total = (total.astype(jnp.float32) + other.astype(jnp.float32)).astype(jnp.bfloat16)
        step *= 2
    return total.astype(jnp.float32)


def body(
    tokens,
    first_value,
    query_weight,
    key_weight,
    value_weight,
    out_weight,
    gate_weight,
    up_weight,
    down_weight,
    prenorm_gain,
    midnorm_gain,
    cotangent,
    lengths,
    assignment,
):
    slots, rows, width = tokens.shape
    assert slots == 1
    head_count = H
    head_dim = width // head_count
    score_scale = head_dim ** (-0.5)
    n_fsdp = lax.axis_size("fsdp")
    n_ctx = lax.axis_size("ctx")
    total_len = rows * n_ctx
    w_rows = query_weight.shape[0]
    g_len = prenorm_gain.shape[0]
    ff = gate_weight.shape[1]
    d_rows = down_weight.shape[0]

    slot_count = assignment.shape[0]
    chosen = assignment[:, None] == jnp.arange(slot_count, dtype=jnp.int32)[None, :]
    lengths_all = jnp.sum(jnp.where(chosen, lengths[None, :], 0), axis=1)
    slot_lengths = lax.dynamic_slice_in_dim(lengths_all, lax.axis_index("fsdp") * slots, slots)
    query_places = lax.axis_index("ctx") * rows + jnp.arange(rows, dtype=jnp.int32)
    valid = query_places[None, :] < slot_lengths[:, None]
    cosine, sine = rope_tables(query_places, head_dim // 2)
    cos_rows = cosine[None, :, None, :]
    sin_rows = sine[None, :, None, :]
    valid_wide = valid[:, :, None]

    attn_pack = jnp.concatenate(
        [query_weight, key_weight, value_weight, out_weight,
         gain_block(prenorm_gain, midnorm_gain, width)],
        axis=0,
    )
    attn_all = lax.all_gather(attn_pack, "fsdp", axis=0, tiled=False)

    def attn_part(i):
        return attn_all[:, i * w_rows:(i + 1) * w_rows, :].reshape(n_fsdp * w_rows, width)

    query_mat, key_mat, value_mat, out_mat = (attn_part(i) for i in range(4))
    prenorm_full = attn_all[:, 4 * w_rows, 0:g_len].reshape(n_fsdp * g_len)
    midnorm_full = attn_all[:, 4 * w_rows, g_len:2 * g_len].reshape(n_fsdp * g_len)

    mlp_pack = jnp.concatenate(
        [gate_weight, up_weight, down_weight.reshape(w_rows, ff)], axis=1
    )
    mlp_all = lax.all_gather(mlp_pack, "fsdp", axis=0, tiled=False)
    gate_mat = mlp_all[:, :, 0:ff].reshape(n_fsdp * w_rows, ff)
    upper_mat = mlp_all[:, :, ff:2 * ff].reshape(n_fsdp * w_rows, ff)
    down_mat = mlp_all[:, :, 2 * ff:].reshape(n_fsdp, d_rows, width).reshape(n_fsdp * d_rows, width)

    tokens_wide = tokens.astype(jnp.float32)
    first_wide = first_value.astype(jnp.float32)
    normed, inverse = norm_apply(tokens_wide, prenorm_full.astype(jnp.float32))
    normed_low = normed.astype(jnp.bfloat16)
    query = jnp.dot(normed_low, query_mat, preferred_element_type=jnp.float32)
    keyed = jnp.dot(normed_low, key_mat, preferred_element_type=jnp.float32)
    own_value = jnp.dot(normed_low, value_mat, preferred_element_type=jnp.float32)
    heads_shape = query.shape[:2] + (head_count, head_dim)
    query_rotated_rows = rotate(query.reshape(heads_shape), cos_rows, sin_rows).astype(jnp.bfloat16)
    key_rot = (
        rotate(keyed.reshape(heads_shape), cos_rows, sin_rows)
        .astype(jnp.bfloat16)
        .reshape(query.shape)
    )
    value_mix = (0.5 * own_value + 0.5 * first_wide).astype(jnp.bfloat16)

    kv_own = jnp.concatenate([key_rot, value_mix], axis=-1).reshape(rows, 2 * width)
    kv_all = lax.all_to_all(
        jnp.broadcast_to(kv_own[None], (n_ctx, rows, 2 * width)), "ctx", 0, 0, tiled=False
    ).reshape(total_len, 2 * width)
    meta = jnp.stack([lax.axis_index("ctx") * rows, slot_lengths[0]]).astype(jnp.int32)
    query_flat = query_rotated_rows.reshape(rows, width)
    mixed_low = attention_forward(
        meta, query_flat, kv_all, head_dim, score_scale
    ).reshape(slots, rows, width)

    middle = tokens_wide + jnp.dot(mixed_low, out_mat, preferred_element_type=jnp.float32)
    normed_two, inverse_two = norm_apply(middle, midnorm_full.astype(jnp.float32))
    normed_two = normed_two.astype(jnp.bfloat16)
    gate = jnp.dot(normed_two, gate_mat, preferred_element_type=jnp.float32)
    upper = jnp.dot(normed_two, upper_mat, preferred_element_type=jnp.float32)
    hidden = (jax.nn.silu(gate) * upper).astype(jnp.bfloat16)
    branch = jnp.dot(hidden, down_mat, preferred_element_type=jnp.float32)
    layer_out = jnp.where(valid_wide, middle + branch, 0.0).astype(jnp.bfloat16)

    cot_wide = jnp.where(valid_wide, cotangent.astype(jnp.float32), 0.0)
    cot_low = cot_wide.astype(jnp.bfloat16)
    down_total = jnp.einsum("srf,sre->fe", hidden, cot_low, preferred_element_type=jnp.float32)
    hidden_back = jnp.einsum("sre,fe->srf", cot_low, down_mat, preferred_element_type=jnp.float32)
    sigma = jax.nn.sigmoid(gate)
    gate_back = (hidden_back * upper * sigma * (1.0 + gate * (1.0 - sigma))).astype(jnp.bfloat16)
    upper_back = (hidden_back * gate * sigma).astype(jnp.bfloat16)
    gate_total = jnp.einsum(
        "srd,srf->df", normed_two, gate_back, preferred_element_type=jnp.float32
    )
    upper_total = jnp.einsum(
        "srd,srf->df", normed_two, upper_back, preferred_element_type=jnp.float32
    )
    normed_two_back = jnp.einsum(
        "srf,df->srd", gate_back, gate_mat, preferred_element_type=jnp.float32
    )
    normed_two_back = normed_two_back + jnp.einsum(
        "srf,df->srd", upper_back, upper_mat, preferred_element_type=jnp.float32
    )
    middle_norm_back, midnorm_total = norm_back(
        middle, inverse_two, midnorm_full.astype(jnp.float32), normed_two_back
    )
    middle_back = cot_wide + middle_norm_back
    middle_low = middle_back.astype(jnp.bfloat16)
    out_total = jnp.einsum("srd,sre->de", mixed_low, middle_low, preferred_element_type=jnp.float32)

    down_share = lax.psum_scatter(
        down_total.astype(jnp.bfloat16).reshape(n_fsdp, d_rows, width),
        "fsdp",
        scatter_dimension=0,
        tiled=False,
    )
    mlp_grads = jnp.concatenate(
        [
            gate_total.reshape(n_fsdp, w_rows, ff),
            upper_total.reshape(n_fsdp, w_rows, ff),
            out_total.reshape(n_fsdp, w_rows, width),
        ],
        axis=2,
    ).astype(jnp.bfloat16)
    mlp_grads, down_share = lax.optimization_barrier((mlp_grads, down_share))
    down_share = ctx_allreduce(down_share, n_ctx)
    mlp_share = lax.psum_scatter(mlp_grads, "fsdp", scatter_dimension=0, tiled=False)

    blended_value_gradient = jnp.einsum(
        "sre,de->srd", middle_low, out_mat, preferred_element_type=jnp.float32
    ).astype(jnp.bfloat16)
    query_rot_back, kv_back = attention_backward(
        meta, query_flat, kv_all, blended_value_gradient.reshape(rows, width), head_dim, score_scale
    )
    query_rot_back = query_rot_back.reshape(slots, rows, head_count, head_dim)
    key_value = jnp.sum(
        lax.all_to_all(kv_back.reshape(n_ctx, rows, 2 * width), "ctx", 0, 0, tiled=False).astype(
            jnp.float32
        ),
        axis=0,
    )
    key_value = key_value.reshape(rows, width // HEAD_BLOCK, 2, HEAD_BLOCK)
    key_rot_back = key_value[:, :, 0, :].reshape(slots, rows, head_count, head_dim)
    value_mix_back = key_value[:, :, 1, :].reshape(slots, rows, width)
    first_grad = 0.5 * value_mix_back
    query_back = (
        rotate(query_rot_back, cos_rows, -sin_rows).reshape(slots, rows, width).astype(jnp.bfloat16)
    )
    key_back = (
        rotate(key_rot_back, cos_rows, -sin_rows).reshape(slots, rows, width).astype(jnp.bfloat16)
    )
    value_back = (0.5 * value_mix_back).astype(jnp.bfloat16)
    query_total = jnp.einsum(
        "srd,sre->de", normed_low, query_back, preferred_element_type=jnp.float32
    )
    key_total = jnp.einsum("srd,sre->de", normed_low, key_back, preferred_element_type=jnp.float32)
    value_total = jnp.einsum(
        "srd,sre->de", normed_low, value_back, preferred_element_type=jnp.float32
    )
    normed_back = jnp.einsum(
        "sre,de->srd", query_back, query_mat, preferred_element_type=jnp.float32
    )
    normed_back = normed_back + jnp.einsum(
        "sre,de->srd", key_back, key_mat, preferred_element_type=jnp.float32
    )
    normed_back = normed_back + jnp.einsum(
        "sre,de->srd", value_back, value_mat, preferred_element_type=jnp.float32
    )
    tokens_norm_back, prenorm_total = norm_back(
        tokens_wide, inverse, prenorm_full.astype(jnp.float32), normed_back
    )
    tokens_grad = middle_back + tokens_norm_back

    attn_grads = jnp.concatenate(
        [
            query_total.reshape(n_fsdp, w_rows, width),
            key_total.reshape(n_fsdp, w_rows, width),
            value_total.reshape(n_fsdp, w_rows, width),
            gain_block(
                prenorm_total.reshape(n_fsdp, g_len),
                midnorm_total.reshape(n_fsdp, g_len),
                width,
                leading=(n_fsdp,),
            ),
        ],
        axis=1,
    ).astype(jnp.bfloat16)
    attn_grads, mlp_share = lax.optimization_barrier((attn_grads, mlp_share))
    mlp_share = ctx_allreduce(mlp_share, n_ctx)
    attn_share = lax.psum_scatter(attn_grads, "fsdp", scatter_dimension=0, tiled=False)
    attn_share = ctx_allreduce(attn_share, n_ctx)

    def attn_grad(i):
        return attn_share[i * w_rows:(i + 1) * w_rows]

    query_grad, key_grad, value_grad = (attn_grad(i) for i in range(3))
    prenorm_grad = attn_share[3 * w_rows, 0:g_len]
    midnorm_grad = attn_share[3 * w_rows, g_len:2 * g_len]
    gate_grad = mlp_share[:, 0:ff]
    up_grad = mlp_share[:, ff:2 * ff]
    down_grad = down_share
    out_grad = mlp_share[:, 2 * ff:]
    return (
        layer_out,
        tokens_grad,
        first_grad,
        query_grad,
        key_grad,
        value_grad,
        out_grad,
        gate_grad,
        up_grad,
        down_grad,
        prenorm_grad,
        midnorm_grad,
    )


def solution(mesh):
    placed = (
        P("fsdp", "ctx", None),
        P("fsdp", "ctx", None),
        P("fsdp", None),
        P("fsdp", None),
        P("fsdp", None),
        P("fsdp", None),
        P("fsdp", None),
        P("fsdp", None),
        P("fsdp", None),
        P("fsdp"),
        P("fsdp"),
        P("fsdp", "ctx", None),
        P(),
        P(),
    )
    return jax.shard_map(
        body,
        mesh=mesh,
        in_specs=placed,
        out_specs=(
            P("fsdp", "ctx", None),
            P("fsdp", "ctx", None),
            P("fsdp", "ctx", None),
            P("fsdp", None),
            P("fsdp", None),
            P("fsdp", None),
            P("fsdp", None),
            P("fsdp", None),
            P("fsdp", None),
            P("fsdp", None),
            P("fsdp"),
            P("fsdp"),
        ),
        check_vma=False,
    )
```

```python
import functools
import math

import jax
import jax.numpy as jnp
from jax import lax
from jax.experimental import pallas as pl
from jax.experimental.pallas import tpu as pltpu
from jax.sharding import PartitionSpec as P

H = 16


EPS = 1e-06
MASKED = -1e30
GAIN_ROWS = 16
FSDP = ("zh", "y", "core")
CTX = ("zl", "x")
Z_CROSS = [(0, 3), (3, 0), (1, 2), (2, 1)]


HEAD_BLOCK = 128
NT_DIMS = (((1,), (1,)), ((), ()))
TN_DIMS = (((0,), (0,)), ((), ()))


def attention_shares(query, keys, first_row, slot_len, scale):
    scores = lax.dot_general(query, keys, NT_DIMS, preferred_element_type=jnp.float32) * scale
    shape = scores.shape
    query_pos = first_row + lax.broadcasted_iota(jnp.int32, shape, 0)
    key_pos = lax.broadcasted_iota(jnp.int32, shape, 1)
    allowed = (key_pos <= query_pos) & (key_pos < slot_len)
    scores = jnp.where(allowed, scores, MASKED)
    peak = jnp.max(scores, axis=-1, keepdims=True)
    raised = jnp.exp(scores - peak)
    denominator = jnp.sum(raised, axis=-1, keepdims=True)
    return raised / denominator


def attn_fwd_kernel(head_dim, scale, meta_ref, q_ref, k_ref, v_ref, o_ref):
    first_row = meta_ref[0]
    slot_len = meta_ref[1]
    for j in range(q_ref.shape[1] // head_dim):
        cols = slice(j * head_dim, (j + 1) * head_dim)
        shares = attention_shares(q_ref[:, cols], k_ref[:, cols], first_row, slot_len, scale)
        mixed = jnp.dot(
            shares.astype(jnp.bfloat16), v_ref[:, cols], preferred_element_type=jnp.float32
        )
        o_ref[:, cols] = mixed.astype(o_ref.dtype)


def attn_bwd_kernel(head_dim, scale, meta_ref, q_ref, k_ref, v_ref, do_ref, dq_ref, dkv_ref):
    first_row = meta_ref[0]
    slot_len = meta_ref[1]
    for j in range(q_ref.shape[1] // head_dim):
        cols = slice(j * head_dim, (j + 1) * head_dim)
        query = q_ref[:, cols]
        keys = k_ref[:, cols]
        back = do_ref[:, cols]
        shares = attention_shares(query, keys, first_row, slot_len, scale)
        prob_back = lax.dot_general(back, v_ref[:, cols], NT_DIMS, preferred_element_type=jnp.float32)
        inner = jnp.sum(shares * prob_back, axis=-1, keepdims=True)
        score_back = (shares * (prob_back - inner)).astype(jnp.bfloat16)
        dq_ref[:, cols] = (
            jnp.dot(score_back, keys, preferred_element_type=jnp.float32) * scale
        )
        dkv_ref[:, cols] = (
            lax.dot_general(score_back, query, TN_DIMS, preferred_element_type=jnp.float32) * scale
        ).astype(dkv_ref.dtype)
        half = q_ref.shape[1]
        dkv_ref[:, half + j * head_dim:half + (j + 1) * head_dim] = lax.dot_general(
            shares.astype(jnp.bfloat16), back, TN_DIMS, preferred_element_type=jnp.float32
        ).astype(dkv_ref.dtype)


def attention_forward(meta, query_rows, kv_rows, head_dim, scale):
    rows, width = query_rows.shape
    keys = kv_rows.shape[0]
    blocks = width // HEAD_BLOCK
    return pl.pallas_call(
        functools.partial(attn_fwd_kernel, head_dim, scale),
        out_shape=jax.ShapeDtypeStruct((rows, width), jnp.bfloat16),
        grid_spec=pltpu.PrefetchScalarGridSpec(
            num_scalar_prefetch=1,
            grid=(blocks,),
            in_specs=[
                pl.BlockSpec((rows, HEAD_BLOCK), lambda h, m: (0, h)),
                pl.BlockSpec((keys, HEAD_BLOCK), lambda h, m: (0, h)),
                pl.BlockSpec((keys, HEAD_BLOCK), lambda h, m: (0, h + blocks)),
            ],
            out_specs=pl.BlockSpec((rows, HEAD_BLOCK), lambda h, m: (0, h)),
        ),
        compiler_params=pltpu.CompilerParams(
            dimension_semantics=("arbitrary",), vmem_limit_bytes=48 * 1024 * 1024
        ),
        cost_estimate=pl.CostEstimate(
            flops=4 * rows * keys * width,
            transcendentals=rows * keys * (width // head_dim),
            bytes_accessed=2 * (2 * rows * width + 2 * keys * width),
        ),
    )(meta, query_rows, kv_rows, kv_rows)


def attention_backward(meta, query_rows, kv_rows, back_rows, head_dim, scale):
    rows, width = query_rows.shape
    keys = kv_rows.shape[0]
    blocks = width // HEAD_BLOCK
    return pl.pallas_call(
        functools.partial(attn_bwd_kernel, head_dim, scale),
        out_shape=(
            jax.ShapeDtypeStruct((rows, width), jnp.float32),
            jax.ShapeDtypeStruct((keys, 2 * width), jnp.bfloat16),
        ),
        grid_spec=pltpu.PrefetchScalarGridSpec(
            num_scalar_prefetch=1,
            grid=(blocks,),
            in_specs=[
                pl.BlockSpec((rows, HEAD_BLOCK), lambda h, m: (0, h)),
                pl.BlockSpec((keys, HEAD_BLOCK), lambda h, m: (0, h)),
                pl.BlockSpec((keys, HEAD_BLOCK), lambda h, m: (0, h + blocks)),
                pl.BlockSpec((rows, HEAD_BLOCK), lambda h, m: (0, h)),
            ],
            out_specs=[
                pl.BlockSpec((rows, HEAD_BLOCK), lambda h, m: (0, h)),
                pl.BlockSpec((keys, 2 * HEAD_BLOCK), lambda h, m: (0, h)),
            ],
        ),
        compiler_params=pltpu.CompilerParams(
            dimension_semantics=("arbitrary",), vmem_limit_bytes=48 * 1024 * 1024
        ),
        cost_estimate=pl.CostEstimate(
            flops=10 * rows * keys * width,
            transcendentals=rows * keys * (width // head_dim),
            bytes_accessed=2 * (3 * rows * width + 4 * keys * width) + 4 * rows * width,
        ),
    )(meta, query_rows, kv_rows, kv_rows, back_rows)


def rope_tables(positions, half):
    freq = jnp.exp(
        jnp.arange(half, dtype=jnp.int32).astype(jnp.float32) * (-math.log(10000.0) / half)
    )
    angle = positions.astype(jnp.float32)[:, None] * freq[None, :]
    return (jnp.cos(angle), jnp.sin(angle))


def rotate(value_rows, cosine, sine):
    half = value_rows.shape[-1] // 2
    first = value_rows[..., :half]
    second = value_rows[..., half:]
    return jnp.concatenate(
        [first * cosine - second * sine, second * cosine + first * sine], axis=-1
    )


def norm_apply(value_rows, gain):
    inverse = lax.rsqrt(jnp.mean(value_rows * value_rows, axis=-1, keepdims=True) + EPS)
    return (value_rows * inverse * gain, inverse)


def norm_back(value_rows, inverse, gain, upstream):
    scaled = upstream * gain
    gain_part = jnp.sum(upstream * value_rows * inverse, axis=(0, 1))
    inner = jnp.mean(scaled * value_rows, axis=-1, keepdims=True)
    return (inverse * scaled - value_rows * inverse * inverse * inverse * inner, gain_part)


def gain_block(first, second, width, leading=()):
    pad_cols = width - first.shape[-1] - second.shape[-1]
    row = jnp.concatenate(
        [first, second, jnp.zeros(leading + (pad_cols,), first.dtype)], axis=-1
    )
    row = row[..., None, :]
    pads = [(0, 0)] * len(leading) + [(0, GAIN_ROWS - 1), (0, 0)]
    return jnp.pad(row, pads)


def zh_pair(mine, other):
    first = lax.axis_index("zh") == 0
    return jnp.stack([jnp.where(first, mine, other), jnp.where(first, other, mine)])


def fsdp_gather(pack):
    other = lax.ppermute(pack, ("zh", "zl"), Z_CROSS)
    both = lax.all_gather(zh_pair(pack, other), ("y", "core"), axis=0, tiled=False)
    return jnp.swapaxes(both, 0, 1).reshape((-1,) + pack.shape)


def fsdp_reduce_scatter(grads):
    n_yc = grads.shape[0] // 2
    by_yc = jnp.swapaxes(grads.reshape((2, n_yc) + grads.shape[1:]), 0, 1)
    block = grads.shape[1:]
    halves = lax.psum_scatter(
        by_yc.reshape((n_yc, 2 * block[0]) + block[1:]), ("y", "core"), scatter_dimension=0, tiled=False
    ).reshape((2,) + block)
    zh = lax.axis_index("zh")
    mine = lax.dynamic_index_in_dim(halves, zh, axis=0, keepdims=False)
    theirs = lax.dynamic_index_in_dim(halves, 1 - zh, axis=0, keepdims=False)
    got = lax.ppermute(theirs, ("zh", "zl"), Z_CROSS)
    return (mine.astype(jnp.float32) + got.astype(jnp.float32)).astype(jnp.bfloat16)


def ctx_allreduce(part, n_ctx):
    total = part
    step = 1
    while step < n_ctx:
        other = lax.ppermute(total, CTX, [(j, j ^ step) for j in range(n_ctx)])
        total = (total.astype(jnp.float32) + other.astype(jnp.float32)).astype(jnp.bfloat16)
        step *= 2
    return total.astype(jnp.float32)


def body(
    tokens,
    first_value,
    query_weight,
    key_weight,
    value_weight,
    out_weight,
    gate_weight,
    up_weight,
    down_weight,
    prenorm_gain,
    midnorm_gain,
    cotangent,
    lengths,
    assignment,
):
    slots, rows, width = tokens.shape
    assert slots == 1
    head_count = H
    head_dim = width // head_count
    score_scale = head_dim ** (-0.5)
    n_fsdp = lax.axis_size(FSDP)
    n_ctx = lax.axis_size(CTX)
    total_len = rows * n_ctx
    w_rows = query_weight.shape[0]
    g_len = prenorm_gain.shape[0]
    ff = gate_weight.shape[1]
    d_rows = down_weight.shape[0]

    slot_count = assignment.shape[0]
    chosen = assignment[:, None] == jnp.arange(slot_count, dtype=jnp.int32)[None, :]
    lengths_all = jnp.sum(jnp.where(chosen, lengths[None, :], 0), axis=1)
    slot_lengths = lax.dynamic_slice_in_dim(lengths_all, lax.axis_index(FSDP) * slots, slots)
    query_places = lax.axis_index(CTX) * rows + jnp.arange(rows, dtype=jnp.int32)
    valid = query_places[None, :] < slot_lengths[:, None]
    cosine, sine = rope_tables(query_places, head_dim // 2)
    cos_rows = cosine[None, :, None, :]
    sin_rows = sine[None, :, None, :]
    valid_wide = valid[:, :, None]

    attn_pack = jnp.concatenate(
        [query_weight, key_weight, value_weight, out_weight,
         gain_block(prenorm_gain, midnorm_gain, width)],
        axis=0,
    )
    attn_all = fsdp_gather(attn_pack)

    def attn_part(i):
        return attn_all[:, i * w_rows:(i + 1) * w_rows, :].reshape(n_fsdp * w_rows, width)

    query_mat, key_mat, value_mat, out_mat = (attn_part(i) for i in range(4))
    prenorm_full = attn_all[:, 4 * w_rows, 0:g_len].reshape(n_fsdp * g_len)
    midnorm_full = attn_all[:, 4 * w_rows, g_len:2 * g_len].reshape(n_fsdp * g_len)

    mlp_pack = jnp.concatenate(
        [gate_weight, up_weight, down_weight.reshape(w_rows, ff)], axis=1
    )
    mlp_all = fsdp_gather(mlp_pack)
    gate_mat = mlp_all[:, :, 0:ff].reshape(n_fsdp * w_rows, ff)
    upper_mat = mlp_all[:, :, ff:2 * ff].reshape(n_fsdp * w_rows, ff)
    down_mat = mlp_all[:, :, 2 * ff:].reshape(n_fsdp, d_rows, width).reshape(n_fsdp * d_rows, width)

    tokens_wide = tokens.astype(jnp.float32)
    first_wide = first_value.astype(jnp.float32)
    normed, inverse = norm_apply(tokens_wide, prenorm_full.astype(jnp.float32))
    normed_low = normed.astype(jnp.bfloat16)
    query = jnp.dot(normed_low, query_mat, preferred_element_type=jnp.float32)
    keyed = jnp.dot(normed_low, key_mat, preferred_element_type=jnp.float32)
    own_value = jnp.dot(normed_low, value_mat, preferred_element_type=jnp.float32)
    heads_shape = query.shape[:2] + (head_count, head_dim)
    query_rotated_rows = rotate(query.reshape(heads_shape), cos_rows, sin_rows).astype(jnp.bfloat16)
    key_rot = (
        rotate(keyed.reshape(heads_shape), cos_rows, sin_rows)
        .astype(jnp.bfloat16)
        .reshape(query.shape)
    )
    value_mix = (0.5 * own_value + 0.5 * first_wide).astype(jnp.bfloat16)

    kv_own = jnp.concatenate([key_rot, value_mix], axis=-1).reshape(rows, 2 * width)
    kv_all = lax.all_to_all(
        jnp.broadcast_to(kv_own[None], (n_ctx, rows, 2 * width)), CTX, 0, 0, tiled=False
    ).reshape(total_len, 2 * width)
    meta = jnp.stack([lax.axis_index(CTX) * rows, slot_lengths[0]]).astype(jnp.int32)
    query_flat = query_rotated_rows.reshape(rows, width)
    mixed_low = attention_forward(
        meta, query_flat, kv_all, head_dim, score_scale
    ).reshape(slots, rows, width)

    middle = tokens_wide + jnp.dot(mixed_low, out_mat, preferred_element_type=jnp.float32)
    normed_two, inverse_two = norm_apply(middle, midnorm_full.astype(jnp.float32))
    normed_two = normed_two.astype(jnp.bfloat16)
    gate = jnp.dot(normed_two, gate_mat, preferred_element_type=jnp.float32)
    upper = jnp.dot(normed_two, upper_mat, preferred_element_type=jnp.float32)
    hidden = (jax.nn.silu(gate) * upper).astype(jnp.bfloat16)
    branch = jnp.dot(hidden, down_mat, preferred_element_type=jnp.float32)
    layer_out = jnp.where(valid_wide, middle + branch, 0.0).astype(jnp.bfloat16)

    cot_wide = jnp.where(valid_wide, cotangent.astype(jnp.float32), 0.0)
    cot_low = cot_wide.astype(jnp.bfloat16)
    down_total = jnp.einsum("srf,sre->fe", hidden, cot_low, preferred_element_type=jnp.float32)
    hidden_back = jnp.einsum("sre,fe->srf", cot_low, down_mat, preferred_element_type=jnp.float32)
    sigma = jax.nn.sigmoid(gate)
    gate_back = (hidden_back * upper * sigma * (1.0 + gate * (1.0 - sigma))).astype(jnp.bfloat16)
    upper_back = (hidden_back * gate * sigma).astype(jnp.bfloat16)
    gate_total = jnp.einsum(
        "srd,srf->df", normed_two, gate_back, preferred_element_type=jnp.float32
    )
    upper_total = jnp.einsum(
        "srd,srf->df", normed_two, upper_back, preferred_element_type=jnp.float32
    )
    normed_two_back = jnp.einsum(
        "srf,df->srd", gate_back, gate_mat, preferred_element_type=jnp.float32
    )
    normed_two_back = normed_two_back + jnp.einsum(
        "srf,df->srd", upper_back, upper_mat, preferred_element_type=jnp.float32
    )
    middle_norm_back, midnorm_total = norm_back(
        middle, inverse_two, midnorm_full.astype(jnp.float32), normed_two_back
    )
    middle_back = cot_wide + middle_norm_back
    middle_low = middle_back.astype(jnp.bfloat16)
    out_total = jnp.einsum("srd,sre->de", mixed_low, middle_low, preferred_element_type=jnp.float32)

    mlp_grads = jnp.concatenate(
        [
            gate_total.reshape(n_fsdp, w_rows, ff),
            upper_total.reshape(n_fsdp, w_rows, ff),
            down_total.reshape(n_fsdp, d_rows, width).reshape(n_fsdp, w_rows, ff),
            out_total.reshape(n_fsdp, w_rows, width),
        ],
        axis=2,
    ).astype(jnp.bfloat16)
    mlp_share = fsdp_reduce_scatter(mlp_grads)

    blended_value_gradient = jnp.einsum(
        "sre,de->srd", middle_low, out_mat, preferred_element_type=jnp.float32
    ).astype(jnp.bfloat16)
    query_rot_back, kv_back = attention_backward(
        meta, query_flat, kv_all, blended_value_gradient.reshape(rows, width), head_dim, score_scale
    )
    query_rot_back = query_rot_back.reshape(slots, rows, head_count, head_dim)
    key_value = jnp.sum(
        lax.all_to_all(kv_back.reshape(n_ctx, rows, 2 * width), CTX, 0, 0, tiled=False).astype(
            jnp.float32
        ),
        axis=0,
    )
    key_value = key_value.reshape(rows, width // HEAD_BLOCK, 2, HEAD_BLOCK)
    key_rot_back = key_value[:, :, 0, :].reshape(slots, rows, head_count, head_dim)
    value_mix_back = key_value[:, :, 1, :].reshape(slots, rows, width)
    first_grad = 0.5 * value_mix_back
    query_back = (
        rotate(query_rot_back, cos_rows, -sin_rows).reshape(slots, rows, width).astype(jnp.bfloat16)
    )
    key_back = (
        rotate(key_rot_back, cos_rows, -sin_rows).reshape(slots, rows, width).astype(jnp.bfloat16)
    )
    value_back = (0.5 * value_mix_back).astype(jnp.bfloat16)
    query_total = jnp.einsum(
        "srd,sre->de", normed_low, query_back, preferred_element_type=jnp.float32
    )
    key_total = jnp.einsum("srd,sre->de", normed_low, key_back, preferred_element_type=jnp.float32)
    value_total = jnp.einsum(
        "srd,sre->de", normed_low, value_back, preferred_element_type=jnp.float32
    )
    normed_back = jnp.einsum(
        "sre,de->srd", query_back, query_mat, preferred_element_type=jnp.float32
    )
    normed_back = normed_back + jnp.einsum(
        "sre,de->srd", key_back, key_mat, preferred_element_type=jnp.float32
    )
    normed_back = normed_back + jnp.einsum(
        "sre,de->srd", value_back, value_mat, preferred_element_type=jnp.float32
    )
    tokens_norm_back, prenorm_total = norm_back(
        tokens_wide, inverse, prenorm_full.astype(jnp.float32), normed_back
    )
    tokens_grad = middle_back + tokens_norm_back

    attn_grads = jnp.concatenate(
        [
            query_total.reshape(n_fsdp, w_rows, width),
            key_total.reshape(n_fsdp, w_rows, width),
            value_total.reshape(n_fsdp, w_rows, width),
            gain_block(
                prenorm_total.reshape(n_fsdp, g_len),
                midnorm_total.reshape(n_fsdp, g_len),
                width,
                leading=(n_fsdp,),
            ),
        ],
        axis=1,
    ).astype(jnp.bfloat16)
    attn_grads, mlp_share = lax.optimization_barrier((attn_grads, mlp_share))
    mlp_share = ctx_allreduce(mlp_share, n_ctx)
    attn_share = fsdp_reduce_scatter(attn_grads)
    attn_share = ctx_allreduce(attn_share, n_ctx)

    def attn_grad(i):
        return attn_share[i * w_rows:(i + 1) * w_rows]

    query_grad, key_grad, value_grad = (attn_grad(i) for i in range(3))
    prenorm_grad = attn_share[3 * w_rows, 0:g_len]
    midnorm_grad = attn_share[3 * w_rows, g_len:2 * g_len]
    gate_grad = mlp_share[:, 0:ff]
    up_grad = mlp_share[:, ff:2 * ff]
    down_grad = mlp_share[:, 2 * ff:3 * ff].reshape(d_rows, width)
    out_grad = mlp_share[:, 3 * ff:]
    return (
        layer_out,
        tokens_grad,
        first_grad,
        query_grad,
        key_grad,
        value_grad,
        out_grad,
        gate_grad,
        up_grad,
        down_grad,
        prenorm_grad,
        midnorm_grad,
    )


def solution(mesh):
    zh = 2
    zl = 2
    n_f, n_c = mesh.devices.shape
    fine = jax.sharding.Mesh(
        mesh.devices.reshape(zh, n_f // (2 * zh), 2, zl, n_c // zl), FSDP + CTX
    )
    placed = (
        P(FSDP, CTX, None),
        P(FSDP, CTX, None),
        P(FSDP, None),
        P(FSDP, None),
        P(FSDP, None),
        P(FSDP, None),
        P(FSDP, None),
        P(FSDP, None),
        P(FSDP, None),
        P(FSDP),
        P(FSDP),
        P(FSDP, CTX, None),
        P(),
        P(),
    )
    return jax.shard_map(
        body,
        mesh=fine,
        in_specs=placed,
        out_specs=(
            P(FSDP, CTX, None),
            P(FSDP, CTX, None),
            P(FSDP, CTX, None),
            P(FSDP, None),
            P(FSDP, None),
            P(FSDP, None),
            P(FSDP, None),
            P(FSDP, None),
            P(FSDP, None),
            P(FSDP, None),
            P(FSDP),
            P(FSDP),
        ),
        check_vma=False,
    )
```

```python
import functools
import math

import jax
import jax.numpy as jnp
from jax import lax
from jax.experimental import pallas as pl
from jax.experimental.pallas import tpu as pltpu
from jax.sharding import PartitionSpec as P

H = 16


EPS = 1e-06
MASKED = -1e30
GAIN_ROWS = 16
FSDP = ("zh", "y", "core")
CTX = ("zl", "x")
Z_CROSS = [(0, 3), (3, 0), (1, 2), (2, 1)]


HEAD_BLOCK = 128
NT_DIMS = (((1,), (1,)), ((), ()))
TN_DIMS = (((0,), (0,)), ((), ()))


def attention_shares(query, keys, first_row, slot_len, scale):
    scores = lax.dot_general(query, keys, NT_DIMS, preferred_element_type=jnp.float32) * scale
    shape = scores.shape
    query_pos = first_row + lax.broadcasted_iota(jnp.int32, shape, 0)
    key_pos = lax.broadcasted_iota(jnp.int32, shape, 1)
    allowed = (key_pos <= query_pos) & (key_pos < slot_len)
    scores = jnp.where(allowed, scores, MASKED)
    peak = jnp.max(scores, axis=-1, keepdims=True)
    raised = jnp.exp(scores - peak)
    denominator = jnp.sum(raised, axis=-1, keepdims=True)
    return raised / denominator


def attn_fwd_kernel(head_dim, scale, meta_ref, q_ref, k_ref, v_ref, o_ref):
    first_row = meta_ref[0]
    slot_len = meta_ref[1]
    for j in range(q_ref.shape[1] // head_dim):
        cols = slice(j * head_dim, (j + 1) * head_dim)
        shares = attention_shares(q_ref[:, cols], k_ref[:, cols], first_row, slot_len, scale)
        mixed = jnp.dot(
            shares.astype(jnp.bfloat16), v_ref[:, cols], preferred_element_type=jnp.float32
        )
        o_ref[:, cols] = mixed.astype(o_ref.dtype)


def attn_bwd_kernel(head_dim, scale, meta_ref, q_ref, k_ref, v_ref, do_ref, dq_ref, dkv_ref):
    first_row = meta_ref[0]
    slot_len = meta_ref[1]
    for j in range(q_ref.shape[1] // head_dim):
        cols = slice(j * head_dim, (j + 1) * head_dim)
        query = q_ref[:, cols]
        keys = k_ref[:, cols]
        back = do_ref[:, cols]
        shares = attention_shares(query, keys, first_row, slot_len, scale)
        prob_back = lax.dot_general(back, v_ref[:, cols], NT_DIMS, preferred_element_type=jnp.float32)
        inner = jnp.sum(shares * prob_back, axis=-1, keepdims=True)
        score_back = (shares * (prob_back - inner)).astype(jnp.bfloat16)
        dq_ref[:, cols] = (
            jnp.dot(score_back, keys, preferred_element_type=jnp.float32) * scale
        )
        dkv_ref[:, cols] = (
            lax.dot_general(score_back, query, TN_DIMS, preferred_element_type=jnp.float32) * scale
        ).astype(dkv_ref.dtype)
        half = q_ref.shape[1]
        dkv_ref[:, half + j * head_dim:half + (j + 1) * head_dim] = lax.dot_general(
            shares.astype(jnp.bfloat16), back, TN_DIMS, preferred_element_type=jnp.float32
        ).astype(dkv_ref.dtype)


def attention_forward(meta, query_rows, kv_rows, head_dim, scale):
    rows, width = query_rows.shape
    keys = kv_rows.shape[0]
    blocks = width // HEAD_BLOCK
    return pl.pallas_call(
        functools.partial(attn_fwd_kernel, head_dim, scale),
        out_shape=jax.ShapeDtypeStruct((rows, width), jnp.bfloat16),
        grid_spec=pltpu.PrefetchScalarGridSpec(
            num_scalar_prefetch=1,
            grid=(blocks,),
            in_specs=[
                pl.BlockSpec((rows, HEAD_BLOCK), lambda h, m: (0, h)),
                pl.BlockSpec((keys, HEAD_BLOCK), lambda h, m: (0, h)),
                pl.BlockSpec((keys, HEAD_BLOCK), lambda h, m: (0, h + blocks)),
            ],
            out_specs=pl.BlockSpec((rows, HEAD_BLOCK), lambda h, m: (0, h)),
        ),
        compiler_params=pltpu.CompilerParams(
            dimension_semantics=("arbitrary",), vmem_limit_bytes=48 * 1024 * 1024
        ),
        cost_estimate=pl.CostEstimate(
            flops=4 * rows * keys * width,
            transcendentals=rows * keys * (width // head_dim),
            bytes_accessed=2 * (2 * rows * width + 2 * keys * width),
        ),
    )(meta, query_rows, kv_rows, kv_rows)


def attention_backward(meta, query_rows, kv_rows, back_rows, head_dim, scale):
    rows, width = query_rows.shape
    keys = kv_rows.shape[0]
    blocks = width // HEAD_BLOCK
    return pl.pallas_call(
        functools.partial(attn_bwd_kernel, head_dim, scale),
        out_shape=(
            jax.ShapeDtypeStruct((rows, width), jnp.float32),
            jax.ShapeDtypeStruct((keys, 2 * width), jnp.bfloat16),
        ),
        grid_spec=pltpu.PrefetchScalarGridSpec(
            num_scalar_prefetch=1,
            grid=(blocks,),
            in_specs=[
                pl.BlockSpec((rows, HEAD_BLOCK), lambda h, m: (0, h)),
                pl.BlockSpec((keys, HEAD_BLOCK), lambda h, m: (0, h)),
                pl.BlockSpec((keys, HEAD_BLOCK), lambda h, m: (0, h + blocks)),
                pl.BlockSpec((rows, HEAD_BLOCK), lambda h, m: (0, h)),
            ],
            out_specs=[
                pl.BlockSpec((rows, HEAD_BLOCK), lambda h, m: (0, h)),
                pl.BlockSpec((keys, 2 * HEAD_BLOCK), lambda h, m: (0, h)),
            ],
        ),
        compiler_params=pltpu.CompilerParams(
            dimension_semantics=("arbitrary",), vmem_limit_bytes=48 * 1024 * 1024
        ),
        cost_estimate=pl.CostEstimate(
            flops=10 * rows * keys * width,
            transcendentals=rows * keys * (width // head_dim),
            bytes_accessed=2 * (3 * rows * width + 4 * keys * width) + 4 * rows * width,
        ),
    )(meta, query_rows, kv_rows, kv_rows, back_rows)


def rope_tables(positions, half):
    freq = jnp.exp(
        jnp.arange(half, dtype=jnp.int32).astype(jnp.float32) * (-math.log(10000.0) / half)
    )
    angle = positions.astype(jnp.float32)[:, None] * freq[None, :]
    return (jnp.cos(angle), jnp.sin(angle))


def rotate(value_rows, cosine, sine):
    half = value_rows.shape[-1] // 2
    first = value_rows[..., :half]
    second = value_rows[..., half:]
    return jnp.concatenate(
        [first * cosine - second * sine, second * cosine + first * sine], axis=-1
    )


def norm_apply(value_rows, gain):
    inverse = lax.rsqrt(jnp.mean(value_rows * value_rows, axis=-1, keepdims=True) + EPS)
    return (value_rows * inverse * gain, inverse)


def norm_back(value_rows, inverse, gain, upstream):
    scaled = upstream * gain
    gain_part = jnp.sum(upstream * value_rows * inverse, axis=(0, 1))
    inner = jnp.mean(scaled * value_rows, axis=-1, keepdims=True)
    return (inverse * scaled - value_rows * inverse * inverse * inverse * inner, gain_part)


def gain_block(first, second, width, leading=()):
    pad_cols = width - first.shape[-1] - second.shape[-1]
    row = jnp.concatenate(
        [first, second, jnp.zeros(leading + (pad_cols,), first.dtype)], axis=-1
    )
    row = row[..., None, :]
    pads = [(0, 0)] * len(leading) + [(0, GAIN_ROWS - 1), (0, 0)]
    return jnp.pad(row, pads)


def to_gathered(rows, block):
    lead = rows.shape[:-1]
    return jnp.swapaxes(rows.reshape(lead + (2, -1, block)), -3, -2).reshape(rows.shape)


def from_gathered(rows, block):
    lead = rows.shape[:-1]
    return jnp.swapaxes(rows.reshape(lead + (-1, 2, block)), -3, -2).reshape(rows.shape)


def zh_pair(mine, other):
    first = lax.axis_index("zh") == 0
    return jnp.stack([jnp.where(first, mine, other), jnp.where(first, other, mine)])


def fsdp_gather(pack):
    other = lax.ppermute(pack, ("zh", "zl"), Z_CROSS)
    both = lax.all_gather(zh_pair(pack, other), ("y", "core"), axis=0, tiled=False)
    return both.reshape((-1,) + pack.shape)


def fsdp_reduce_scatter(grads):
    n_yc = grads.shape[0] // 2
    by_yc = grads
    block = grads.shape[1:]
    halves = lax.psum_scatter(
        by_yc.reshape((n_yc, 2 * block[0]) + block[1:]), ("y", "core"), scatter_dimension=0, tiled=False
    ).reshape((2,) + block)
    zh = lax.axis_index("zh")
    mine = lax.dynamic_index_in_dim(halves, zh, axis=0, keepdims=False)
    theirs = lax.dynamic_index_in_dim(halves, 1 - zh, axis=0, keepdims=False)
    got = lax.ppermute(theirs, ("zh", "zl"), Z_CROSS)
    return (mine.astype(jnp.float32) + got.astype(jnp.float32)).astype(jnp.bfloat16)


def ctx_allreduce(part, n_ctx):
    total = part
    step = 1
    while step < n_ctx:
        other = lax.ppermute(total, CTX, [(j, j ^ step) for j in range(n_ctx)])
        total = (total.astype(jnp.float32) + other.astype(jnp.float32)).astype(jnp.bfloat16)
        step *= 2
    return total.astype(jnp.float32)


def body(
    tokens,
    first_value,
    query_weight,
    key_weight,
    value_weight,
    out_weight,
    gate_weight,
    up_weight,
    down_weight,
    prenorm_gain,
    midnorm_gain,
    cotangent,
    lengths,
    assignment,
):
    slots, rows, width = tokens.shape
    assert slots == 1
    head_count = H
    head_dim = width // head_count
    score_scale = head_dim ** (-0.5)
    n_fsdp = lax.axis_size(FSDP)
    n_ctx = lax.axis_size(CTX)
    total_len = rows * n_ctx
    w_rows = query_weight.shape[0]
    g_len = prenorm_gain.shape[0]
    ff = gate_weight.shape[1]
    d_rows = down_weight.shape[0]

    slot_count = assignment.shape[0]
    chosen = assignment[:, None] == jnp.arange(slot_count, dtype=jnp.int32)[None, :]
    lengths_all = jnp.sum(jnp.where(chosen, lengths[None, :], 0), axis=1)
    slot_lengths = lax.dynamic_slice_in_dim(lengths_all, lax.axis_index(FSDP) * slots, slots)
    query_places = lax.axis_index(CTX) * rows + jnp.arange(rows, dtype=jnp.int32)
    valid = query_places[None, :] < slot_lengths[:, None]
    cosine, sine = rope_tables(query_places, head_dim // 2)
    cos_rows = cosine[None, :, None, :]
    sin_rows = sine[None, :, None, :]
    valid_wide = valid[:, :, None]

    attn_pack = jnp.concatenate(
        [query_weight, key_weight, value_weight, out_weight,
         gain_block(prenorm_gain, midnorm_gain, width)],
        axis=0,
    )
    attn_all = fsdp_gather(attn_pack)

    def attn_part(i):
        return attn_all[:, i * w_rows:(i + 1) * w_rows, :].reshape(n_fsdp * w_rows, width)

    query_mat, key_mat, value_mat, out_mat = (attn_part(i) for i in range(4))
    prenorm_full = from_gathered(attn_all[:, 4 * w_rows, 0:g_len].reshape(n_fsdp * g_len), g_len)
    midnorm_full = from_gathered(
        attn_all[:, 4 * w_rows, g_len:2 * g_len].reshape(n_fsdp * g_len), g_len
    )

    mlp_pack = jnp.concatenate(
        [gate_weight, up_weight, down_weight.reshape(w_rows, ff)], axis=1
    )
    mlp_all = fsdp_gather(mlp_pack)
    gate_mat = mlp_all[:, :, 0:ff].reshape(n_fsdp * w_rows, ff)
    upper_mat = mlp_all[:, :, ff:2 * ff].reshape(n_fsdp * w_rows, ff)
    down_mat = mlp_all[:, :, 2 * ff:].reshape(n_fsdp, d_rows, width).reshape(n_fsdp * d_rows, width)

    tokens_wide = tokens.astype(jnp.float32)
    first_wide = first_value.astype(jnp.float32)
    normed, inverse = norm_apply(tokens_wide, prenorm_full.astype(jnp.float32))
    normed_low = normed.astype(jnp.bfloat16)
    normed_low_g = to_gathered(normed_low, w_rows)
    query = jnp.dot(normed_low_g, query_mat, preferred_element_type=jnp.float32)
    keyed = jnp.dot(normed_low_g, key_mat, preferred_element_type=jnp.float32)
    own_value = jnp.dot(normed_low_g, value_mat, preferred_element_type=jnp.float32)
    heads_shape = query.shape[:2] + (head_count, head_dim)
    query_rotated_rows = rotate(query.reshape(heads_shape), cos_rows, sin_rows).astype(jnp.bfloat16)
    key_rot = (
        rotate(keyed.reshape(heads_shape), cos_rows, sin_rows)
        .astype(jnp.bfloat16)
        .reshape(query.shape)
    )
    value_mix = (0.5 * own_value + 0.5 * first_wide).astype(jnp.bfloat16)

    kv_own = jnp.concatenate([key_rot, value_mix], axis=-1).reshape(rows, 2 * width)
    kv_all = lax.all_to_all(
        jnp.broadcast_to(kv_own[None], (n_ctx, rows, 2 * width)), CTX, 0, 0, tiled=False
    ).reshape(total_len, 2 * width)
    meta = jnp.stack([lax.axis_index(CTX) * rows, slot_lengths[0]]).astype(jnp.int32)
    query_flat = query_rotated_rows.reshape(rows, width)
    mixed_low = attention_forward(
        meta, query_flat, kv_all, head_dim, score_scale
    ).reshape(slots, rows, width)

    mixed_low_g = to_gathered(mixed_low, w_rows)
    middle = tokens_wide + jnp.dot(mixed_low_g, out_mat, preferred_element_type=jnp.float32)
    normed_two, inverse_two = norm_apply(middle, midnorm_full.astype(jnp.float32))
    normed_two = normed_two.astype(jnp.bfloat16)
    normed_two_g = to_gathered(normed_two, w_rows)
    gate = jnp.dot(normed_two_g, gate_mat, preferred_element_type=jnp.float32)
    upper = jnp.dot(normed_two_g, upper_mat, preferred_element_type=jnp.float32)
    hidden = (jax.nn.silu(gate) * upper).astype(jnp.bfloat16)
    hidden_g = to_gathered(hidden, d_rows)
    branch = jnp.dot(hidden_g, down_mat, preferred_element_type=jnp.float32)
    layer_out = jnp.where(valid_wide, middle + branch, 0.0).astype(jnp.bfloat16)

    cot_wide = jnp.where(valid_wide, cotangent.astype(jnp.float32), 0.0)
    cot_low = cot_wide.astype(jnp.bfloat16)
    down_total = jnp.einsum("srf,sre->fe", hidden_g, cot_low, preferred_element_type=jnp.float32)
    hidden_back = from_gathered(
        jnp.einsum("sre,fe->srf", cot_low, down_mat, preferred_element_type=jnp.float32), d_rows
    )
    sigma = jax.nn.sigmoid(gate)
    gate_back = (hidden_back * upper * sigma * (1.0 + gate * (1.0 - sigma))).astype(jnp.bfloat16)
    upper_back = (hidden_back * gate * sigma).astype(jnp.bfloat16)
    gate_total = jnp.einsum(
        "srd,srf->df", normed_two_g, gate_back, preferred_element_type=jnp.float32
    )
    upper_total = jnp.einsum(
        "srd,srf->df", normed_two_g, upper_back, preferred_element_type=jnp.float32
    )
    normed_two_back = jnp.einsum(
        "srf,df->srd", gate_back, gate_mat, preferred_element_type=jnp.float32
    )
    normed_two_back = normed_two_back + jnp.einsum(
        "srf,df->srd", upper_back, upper_mat, preferred_element_type=jnp.float32
    )
    normed_two_back = from_gathered(normed_two_back, w_rows)
    middle_norm_back, midnorm_total = norm_back(
        middle, inverse_two, midnorm_full.astype(jnp.float32), normed_two_back
    )
    middle_back = cot_wide + middle_norm_back
    middle_low = middle_back.astype(jnp.bfloat16)
    out_total = jnp.einsum("srd,sre->de", mixed_low_g, middle_low, preferred_element_type=jnp.float32)

    mlp_grads = jnp.concatenate(
        [
            gate_total.reshape(n_fsdp, w_rows, ff),
            upper_total.reshape(n_fsdp, w_rows, ff),
            down_total.reshape(n_fsdp, d_rows, width).reshape(n_fsdp, w_rows, ff),
            out_total.reshape(n_fsdp, w_rows, width),
        ],
        axis=2,
    ).astype(jnp.bfloat16)
    mlp_share = fsdp_reduce_scatter(mlp_grads)

    blended_value_gradient = from_gathered(
        jnp.einsum("sre,de->srd", middle_low, out_mat, preferred_element_type=jnp.float32).astype(
            jnp.bfloat16
        ),
        w_rows,
    )
    query_rot_back, kv_back = attention_backward(
        meta, query_flat, kv_all, blended_value_gradient.reshape(rows, width), head_dim, score_scale
    )
    query_rot_back = query_rot_back.reshape(slots, rows, head_count, head_dim)
    key_value = jnp.sum(
        lax.all_to_all(kv_back.reshape(n_ctx, rows, 2 * width), CTX, 0, 0, tiled=False).astype(
            jnp.float32
        ),
        axis=0,
    )
    key_value = key_value.reshape(rows, width // HEAD_BLOCK, 2, HEAD_BLOCK)
    key_rot_back = key_value[:, :, 0, :].reshape(slots, rows, head_count, head_dim)
    value_mix_back = key_value[:, :, 1, :].reshape(slots, rows, width)
    first_grad = 0.5 * value_mix_back
    query_back = (
        rotate(query_rot_back, cos_rows, -sin_rows).reshape(slots, rows, width).astype(jnp.bfloat16)
    )
    key_back = (
        rotate(key_rot_back, cos_rows, -sin_rows).reshape(slots, rows, width).astype(jnp.bfloat16)
    )
    value_back = (0.5 * value_mix_back).astype(jnp.bfloat16)
    query_total = jnp.einsum(
        "srd,sre->de", normed_low_g, query_back, preferred_element_type=jnp.float32
    )
    key_total = jnp.einsum("srd,sre->de", normed_low_g, key_back, preferred_element_type=jnp.float32)
    value_total = jnp.einsum(
        "srd,sre->de", normed_low_g, value_back, preferred_element_type=jnp.float32
    )
    normed_back = jnp.einsum(
        "sre,de->srd", query_back, query_mat, preferred_element_type=jnp.float32
    )
    normed_back = normed_back + jnp.einsum(
        "sre,de->srd", key_back, key_mat, preferred_element_type=jnp.float32
    )
    normed_back = normed_back + jnp.einsum(
        "sre,de->srd", value_back, value_mat, preferred_element_type=jnp.float32
    )
    normed_back = from_gathered(normed_back, w_rows)
    tokens_norm_back, prenorm_total = norm_back(
        tokens_wide, inverse, prenorm_full.astype(jnp.float32), normed_back
    )
    tokens_grad = middle_back + tokens_norm_back

    attn_grads = jnp.concatenate(
        [
            query_total.reshape(n_fsdp, w_rows, width),
            key_total.reshape(n_fsdp, w_rows, width),
            value_total.reshape(n_fsdp, w_rows, width),
            gain_block(
                to_gathered(prenorm_total, g_len).reshape(n_fsdp, g_len),
                to_gathered(midnorm_total, g_len).reshape(n_fsdp, g_len),
                width,
                leading=(n_fsdp,),
            ),
        ],
        axis=1,
    ).astype(jnp.bfloat16)
    attn_grads, mlp_share = lax.optimization_barrier((attn_grads, mlp_share))
    mlp_share = ctx_allreduce(mlp_share, n_ctx)
    attn_share = fsdp_reduce_scatter(attn_grads)
    attn_share = ctx_allreduce(attn_share, n_ctx)

    def attn_grad(i):
        return attn_share[i * w_rows:(i + 1) * w_rows]

    query_grad, key_grad, value_grad = (attn_grad(i) for i in range(3))
    prenorm_grad = attn_share[3 * w_rows, 0:g_len]
    midnorm_grad = attn_share[3 * w_rows, g_len:2 * g_len]
    gate_grad = mlp_share[:, 0:ff]
    up_grad = mlp_share[:, ff:2 * ff]
    down_grad = mlp_share[:, 2 * ff:3 * ff].reshape(d_rows, width)
    out_grad = mlp_share[:, 3 * ff:]
    return (
        layer_out,
        tokens_grad,
        first_grad,
        query_grad,
        key_grad,
        value_grad,
        out_grad,
        gate_grad,
        up_grad,
        down_grad,
        prenorm_grad,
        midnorm_grad,
    )


def solution(mesh):
    zh = 2
    zl = 2
    n_f, n_c = mesh.devices.shape
    fine = jax.sharding.Mesh(
        mesh.devices.reshape(zh, n_f // (2 * zh), 2, zl, n_c // zl), FSDP + CTX
    )
    placed = (
        P(FSDP, CTX, None),
        P(FSDP, CTX, None),
        P(FSDP, None),
        P(FSDP, None),
        P(FSDP, None),
        P(FSDP, None),
        P(FSDP, None),
        P(FSDP, None),
        P(FSDP, None),
        P(FSDP),
        P(FSDP),
        P(FSDP, CTX, None),
        P(),
        P(),
    )
    return jax.shard_map(
        body,
        mesh=fine,
        in_specs=placed,
        out_specs=(
            P(FSDP, CTX, None),
            P(FSDP, CTX, None),
            P(FSDP, CTX, None),
            P(FSDP, None),
            P(FSDP, None),
            P(FSDP, None),
            P(FSDP, None),
            P(FSDP, None),
            P(FSDP, None),
            P(FSDP, None),
            P(FSDP),
            P(FSDP),
        ),
        check_vma=False,
    )
```

```python
import functools
import math

import jax
import jax.numpy as jnp
from jax import lax
from jax.experimental import pallas as pl
from jax.experimental.pallas import tpu as pltpu
from jax.sharding import PartitionSpec as P

H = 16


EPS = 1e-06
MASKED = -1e30
GAIN_ROWS = 16
FSDP = ("zh", "y", "core")
CTX = ("zl", "x")
Z_CROSS = [(0, 3), (3, 0), (1, 2), (2, 1)]


HEAD_BLOCK = 128
NT_DIMS = (((1,), (1,)), ((), ()))
TN_DIMS = (((0,), (0,)), ((), ()))


def attention_shares(query, keys, first_row, slot_len, scale):
    scores = lax.dot_general(query, keys, NT_DIMS, preferred_element_type=jnp.float32) * scale
    shape = scores.shape
    query_pos = first_row + lax.broadcasted_iota(jnp.int32, shape, 0)
    key_pos = lax.broadcasted_iota(jnp.int32, shape, 1)
    allowed = (key_pos <= query_pos) & (key_pos < slot_len)
    scores = jnp.where(allowed, scores, MASKED)
    peak = jnp.max(scores, axis=-1, keepdims=True)
    raised = jnp.exp(scores - peak)
    denominator = jnp.sum(raised, axis=-1, keepdims=True)
    return raised / denominator


def attn_fwd_kernel(head_dim, scale, meta_ref, q_ref, k_ref, v_ref, o_ref):
    first_row = meta_ref[0]
    slot_len = meta_ref[1]
    for j in range(q_ref.shape[1] // head_dim):
        cols = slice(j * head_dim, (j + 1) * head_dim)
        shares = attention_shares(q_ref[:, cols], k_ref[:, cols], first_row, slot_len, scale)
        mixed = jnp.dot(
            shares.astype(jnp.bfloat16), v_ref[:, cols], preferred_element_type=jnp.float32
        )
        o_ref[:, cols] = mixed.astype(o_ref.dtype)


def attn_bwd_kernel(head_dim, scale, meta_ref, q_ref, k_ref, v_ref, do_ref, dq_ref, dkv_ref):
    first_row = meta_ref[0]
    slot_len = meta_ref[1]
    for j in range(q_ref.shape[1] // head_dim):
        cols = slice(j * head_dim, (j + 1) * head_dim)
        query = q_ref[:, cols]
        keys = k_ref[:, cols]
        back = do_ref[:, cols]
        shares = attention_shares(query, keys, first_row, slot_len, scale)
        prob_back = lax.dot_general(back, v_ref[:, cols], NT_DIMS, preferred_element_type=jnp.float32)
        inner = jnp.sum(shares * prob_back, axis=-1, keepdims=True)
        score_back = (shares * (prob_back - inner)).astype(jnp.bfloat16)
        dq_ref[:, cols] = (
            jnp.dot(score_back, keys, preferred_element_type=jnp.float32) * scale
        )
        dkv_ref[:, cols] = (
            lax.dot_general(score_back, query, TN_DIMS, preferred_element_type=jnp.float32) * scale
        ).astype(dkv_ref.dtype)
        half = q_ref.shape[1]
        dkv_ref[:, half + j * head_dim:half + (j + 1) * head_dim] = lax.dot_general(
            shares.astype(jnp.bfloat16), back, TN_DIMS, preferred_element_type=jnp.float32
        ).astype(dkv_ref.dtype)


def attention_forward(meta, query_rows, kv_rows, head_dim, scale):
    rows, width = query_rows.shape
    keys = kv_rows.shape[0]
    blocks = width // HEAD_BLOCK
    return pl.pallas_call(
        functools.partial(attn_fwd_kernel, head_dim, scale),
        out_shape=jax.ShapeDtypeStruct((rows, width), jnp.bfloat16),
        grid_spec=pltpu.PrefetchScalarGridSpec(
            num_scalar_prefetch=1,
            grid=(blocks,),
            in_specs=[
                pl.BlockSpec((rows, HEAD_BLOCK), lambda h, m: (0, h)),
                pl.BlockSpec((keys, HEAD_BLOCK), lambda h, m: (0, h)),
                pl.BlockSpec((keys, HEAD_BLOCK), lambda h, m: (0, h + blocks)),
            ],
            out_specs=pl.BlockSpec((rows, HEAD_BLOCK), lambda h, m: (0, h)),
        ),
        compiler_params=pltpu.CompilerParams(
            dimension_semantics=("arbitrary",), vmem_limit_bytes=48 * 1024 * 1024
        ),
        cost_estimate=pl.CostEstimate(
            flops=4 * rows * keys * width,
            transcendentals=rows * keys * (width // head_dim),
            bytes_accessed=2 * (2 * rows * width + 2 * keys * width),
        ),
    )(meta, query_rows, kv_rows, kv_rows)


def attention_backward(meta, query_rows, kv_rows, back_rows, head_dim, scale):
    rows, width = query_rows.shape
    keys = kv_rows.shape[0]
    blocks = width // HEAD_BLOCK
    return pl.pallas_call(
        functools.partial(attn_bwd_kernel, head_dim, scale),
        out_shape=(
            jax.ShapeDtypeStruct((rows, width), jnp.float32),
            jax.ShapeDtypeStruct((keys, 2 * width), jnp.bfloat16),
        ),
        grid_spec=pltpu.PrefetchScalarGridSpec(
            num_scalar_prefetch=1,
            grid=(blocks,),
            in_specs=[
                pl.BlockSpec((rows, HEAD_BLOCK), lambda h, m: (0, h)),
                pl.BlockSpec((keys, HEAD_BLOCK), lambda h, m: (0, h)),
                pl.BlockSpec((keys, HEAD_BLOCK), lambda h, m: (0, h + blocks)),
                pl.BlockSpec((rows, HEAD_BLOCK), lambda h, m: (0, h)),
            ],
            out_specs=[
                pl.BlockSpec((rows, HEAD_BLOCK), lambda h, m: (0, h)),
                pl.BlockSpec((keys, 2 * HEAD_BLOCK), lambda h, m: (0, h)),
            ],
        ),
        compiler_params=pltpu.CompilerParams(
            dimension_semantics=("arbitrary",), vmem_limit_bytes=48 * 1024 * 1024
        ),
        cost_estimate=pl.CostEstimate(
            flops=10 * rows * keys * width,
            transcendentals=rows * keys * (width // head_dim),
            bytes_accessed=2 * (3 * rows * width + 4 * keys * width) + 4 * rows * width,
        ),
    )(meta, query_rows, kv_rows, kv_rows, back_rows)


def rope_tables(positions, half):
    freq = jnp.exp(
        jnp.arange(half, dtype=jnp.int32).astype(jnp.float32) * (-math.log(10000.0) / half)
    )
    angle = positions.astype(jnp.float32)[:, None] * freq[None, :]
    return (jnp.cos(angle), jnp.sin(angle))


def rotate(value_rows, cosine, sine):
    half = value_rows.shape[-1] // 2
    first = value_rows[..., :half]
    second = value_rows[..., half:]
    return jnp.concatenate(
        [first * cosine - second * sine, second * cosine + first * sine], axis=-1
    )


def norm_apply(value_rows, gain):
    inverse = lax.rsqrt(jnp.mean(value_rows * value_rows, axis=-1, keepdims=True) + EPS)
    return (value_rows * inverse * gain, inverse)


def norm_back(value_rows, inverse, gain, upstream):
    scaled = upstream * gain
    gain_part = jnp.sum(upstream * value_rows * inverse, axis=(0, 1))
    inner = jnp.mean(scaled * value_rows, axis=-1, keepdims=True)
    return (inverse * scaled - value_rows * inverse * inverse * inverse * inner, gain_part)


def gain_block(first, second, width, leading=()):
    pad_cols = width - first.shape[-1] - second.shape[-1]
    row = jnp.concatenate(
        [first, second, jnp.zeros(leading + (pad_cols,), first.dtype)], axis=-1
    )
    row = row[..., None, :]
    pads = [(0, 0)] * len(leading) + [(0, GAIN_ROWS - 1), (0, 0)]
    return jnp.pad(row, pads)


def to_gathered(rows, block):
    lead = rows.shape[:-1]
    return jnp.swapaxes(rows.reshape(lead + (2, -1, block)), -3, -2).reshape(rows.shape)


def from_gathered(rows, block):
    lead = rows.shape[:-1]
    return jnp.swapaxes(rows.reshape(lead + (-1, 2, block)), -3, -2).reshape(rows.shape)


def zh_pair(mine, other):
    first = lax.axis_index("zh") == 0
    return jnp.stack([jnp.where(first, mine, other), jnp.where(first, other, mine)])


def fsdp_gather(pack):
    other = lax.ppermute(pack, ("zh", "zl"), Z_CROSS)
    both = lax.all_gather(zh_pair(pack, other), ("y", "core"), axis=0, tiled=False)
    return both.reshape((-1,) + pack.shape)


def fsdp_reduce_scatter(grads):
    return z_combine(yc_reduce_scatter(grads))


def yc_reduce_scatter(grads):
    n_yc = grads.shape[0] // 2
    by_yc = grads
    block = grads.shape[1:]
    halves = lax.psum_scatter(
        by_yc.reshape((n_yc, 2 * block[0]) + block[1:]), ("y", "core"), scatter_dimension=0, tiled=False
    ).reshape((2,) + block)
    return halves


def z_combine(halves):
    zh = lax.axis_index("zh")
    mine = lax.dynamic_index_in_dim(halves, zh, axis=0, keepdims=False)
    theirs = lax.dynamic_index_in_dim(halves, 1 - zh, axis=0, keepdims=False)
    got = lax.ppermute(theirs, ("zh", "zl"), Z_CROSS)
    return (mine.astype(jnp.float32) + got.astype(jnp.float32)).astype(jnp.bfloat16)


def ctx_allreduce(part, n_ctx):
    total = part
    step = 1
    while step < n_ctx:
        other = lax.ppermute(total, CTX, [(j, j ^ step) for j in range(n_ctx)])
        total = (total.astype(jnp.float32) + other.astype(jnp.float32)).astype(jnp.bfloat16)
        step *= 2
    return total.astype(jnp.float32)


def body(
    tokens,
    first_value,
    query_weight,
    key_weight,
    value_weight,
    out_weight,
    gate_weight,
    up_weight,
    down_weight,
    prenorm_gain,
    midnorm_gain,
    cotangent,
    lengths,
    assignment,
):
    slots, rows, width = tokens.shape
    assert slots == 1
    head_count = H
    head_dim = width // head_count
    score_scale = head_dim ** (-0.5)
    n_fsdp = lax.axis_size(FSDP)
    n_ctx = lax.axis_size(CTX)
    total_len = rows * n_ctx
    w_rows = query_weight.shape[0]
    g_len = prenorm_gain.shape[0]
    ff = gate_weight.shape[1]
    d_rows = down_weight.shape[0]

    slot_count = assignment.shape[0]
    chosen = assignment[:, None] == jnp.arange(slot_count, dtype=jnp.int32)[None, :]
    lengths_all = jnp.sum(jnp.where(chosen, lengths[None, :], 0), axis=1)
    slot_lengths = lax.dynamic_slice_in_dim(lengths_all, lax.axis_index(FSDP) * slots, slots)
    query_places = lax.axis_index(CTX) * rows + jnp.arange(rows, dtype=jnp.int32)
    valid = query_places[None, :] < slot_lengths[:, None]
    cosine, sine = rope_tables(query_places, head_dim // 2)
    cos_rows = cosine[None, :, None, :]
    sin_rows = sine[None, :, None, :]
    valid_wide = valid[:, :, None]

    attn_pack = jnp.concatenate(
        [query_weight, key_weight, value_weight, out_weight,
         gain_block(prenorm_gain, midnorm_gain, width)],
        axis=0,
    )
    attn_all = fsdp_gather(attn_pack)

    def attn_part(i):
        return attn_all[:, i * w_rows:(i + 1) * w_rows, :].reshape(n_fsdp * w_rows, width)

    query_mat, key_mat, value_mat, out_mat = (attn_part(i) for i in range(4))
    prenorm_full = from_gathered(attn_all[:, 4 * w_rows, 0:g_len].reshape(n_fsdp * g_len), g_len)
    midnorm_full = from_gathered(
        attn_all[:, 4 * w_rows, g_len:2 * g_len].reshape(n_fsdp * g_len), g_len
    )

    mlp_pack = jnp.concatenate(
        [gate_weight, up_weight, down_weight.reshape(w_rows, ff)], axis=1
    )
    mlp_all = fsdp_gather(mlp_pack)
    gate_mat = mlp_all[:, :, 0:ff].reshape(n_fsdp * w_rows, ff)
    upper_mat = mlp_all[:, :, ff:2 * ff].reshape(n_fsdp * w_rows, ff)
    down_mat = mlp_all[:, :, 2 * ff:].reshape(n_fsdp, d_rows, width).reshape(n_fsdp * d_rows, width)

    tokens_wide = tokens.astype(jnp.float32)
    first_wide = first_value.astype(jnp.float32)
    normed, inverse = norm_apply(tokens_wide, prenorm_full.astype(jnp.float32))
    normed_low = normed.astype(jnp.bfloat16)
    normed_low_g = to_gathered(normed_low, w_rows)
    query = jnp.dot(normed_low_g, query_mat, preferred_element_type=jnp.float32)
    keyed = jnp.dot(normed_low_g, key_mat, preferred_element_type=jnp.float32)
    own_value = jnp.dot(normed_low_g, value_mat, preferred_element_type=jnp.float32)
    heads_shape = query.shape[:2] + (head_count, head_dim)
    query_rotated_rows = rotate(query.reshape(heads_shape), cos_rows, sin_rows).astype(jnp.bfloat16)
    key_rot = (
        rotate(keyed.reshape(heads_shape), cos_rows, sin_rows)
        .astype(jnp.bfloat16)
        .reshape(query.shape)
    )
    value_mix = (0.5 * own_value + 0.5 * first_wide).astype(jnp.bfloat16)

    kv_own = jnp.concatenate([key_rot, value_mix], axis=-1).reshape(rows, 2 * width)
    kv_all = lax.all_to_all(
        jnp.broadcast_to(kv_own[None], (n_ctx, rows, 2 * width)), CTX, 0, 0, tiled=False
    ).reshape(total_len, 2 * width)
    meta = jnp.stack([lax.axis_index(CTX) * rows, slot_lengths[0]]).astype(jnp.int32)
    query_flat = query_rotated_rows.reshape(rows, width)
    mixed_low = attention_forward(
        meta, query_flat, kv_all, head_dim, score_scale
    ).reshape(slots, rows, width)

    mixed_low_g = to_gathered(mixed_low, w_rows)
    middle = tokens_wide + jnp.dot(mixed_low_g, out_mat, preferred_element_type=jnp.float32)
    normed_two, inverse_two = norm_apply(middle, midnorm_full.astype(jnp.float32))
    normed_two = normed_two.astype(jnp.bfloat16)
    normed_two_g = to_gathered(normed_two, w_rows)
    gate = jnp.dot(normed_two_g, gate_mat, preferred_element_type=jnp.float32)
    upper = jnp.dot(normed_two_g, upper_mat, preferred_element_type=jnp.float32)
    hidden = (jax.nn.silu(gate) * upper).astype(jnp.bfloat16)
    hidden_g = to_gathered(hidden, d_rows)
    branch = jnp.dot(hidden_g, down_mat, preferred_element_type=jnp.float32)
    layer_out = jnp.where(valid_wide, middle + branch, 0.0).astype(jnp.bfloat16)

    cot_wide = jnp.where(valid_wide, cotangent.astype(jnp.float32), 0.0)
    cot_low = cot_wide.astype(jnp.bfloat16)
    down_total = jnp.einsum("srf,sre->fe", hidden_g, cot_low, preferred_element_type=jnp.float32)
    hidden_back = from_gathered(
        jnp.einsum("sre,fe->srf", cot_low, down_mat, preferred_element_type=jnp.float32), d_rows
    )
    sigma = jax.nn.sigmoid(gate)
    gate_back = (hidden_back * upper * sigma * (1.0 + gate * (1.0 - sigma))).astype(jnp.bfloat16)
    upper_back = (hidden_back * gate * sigma).astype(jnp.bfloat16)
    gate_total = jnp.einsum(
        "srd,srf->df", normed_two_g, gate_back, preferred_element_type=jnp.float32
    )
    upper_total = jnp.einsum(
        "srd,srf->df", normed_two_g, upper_back, preferred_element_type=jnp.float32
    )
    normed_two_back = jnp.einsum(
        "srf,df->srd", gate_back, gate_mat, preferred_element_type=jnp.float32
    )
    normed_two_back = normed_two_back + jnp.einsum(
        "srf,df->srd", upper_back, upper_mat, preferred_element_type=jnp.float32
    )
    normed_two_back = from_gathered(normed_two_back, w_rows)
    middle_norm_back, midnorm_total = norm_back(
        middle, inverse_two, midnorm_full.astype(jnp.float32), normed_two_back
    )
    middle_back = cot_wide + middle_norm_back
    middle_low = middle_back.astype(jnp.bfloat16)
    out_total = jnp.einsum("srd,sre->de", mixed_low_g, middle_low, preferred_element_type=jnp.float32)

    blended_value_gradient = from_gathered(
        jnp.einsum("sre,de->srd", middle_low, out_mat, preferred_element_type=jnp.float32).astype(
            jnp.bfloat16
        ),
        w_rows,
    )
    query_rot_back, kv_back = attention_backward(
        meta, query_flat, kv_all, blended_value_gradient.reshape(rows, width), head_dim, score_scale
    )
    query_rot_back = query_rot_back.reshape(slots, rows, head_count, head_dim)
    query_back = (
        rotate(query_rot_back, cos_rows, -sin_rows).reshape(slots, rows, width).astype(jnp.bfloat16)
    )
    query_total = jnp.einsum(
        "srd,sre->de", normed_low_g, query_back, preferred_element_type=jnp.float32
    )
    mlp_grads = jnp.concatenate(
        [
            gate_total.reshape(n_fsdp, w_rows, ff),
            upper_total.reshape(n_fsdp, w_rows, ff),
            down_total.reshape(n_fsdp, d_rows, width).reshape(n_fsdp, w_rows, ff),
            out_total.reshape(n_fsdp, w_rows, width),
            query_total.reshape(n_fsdp, w_rows, width),
        ],
        axis=2,
    ).astype(jnp.bfloat16)
    mlp_halves = yc_reduce_scatter(mlp_grads)

    key_value = jnp.sum(
        lax.all_to_all(kv_back.reshape(n_ctx, rows, 2 * width), CTX, 0, 0, tiled=False).astype(
            jnp.float32
        ),
        axis=0,
    )
    key_value = key_value.reshape(rows, width // HEAD_BLOCK, 2, HEAD_BLOCK)
    key_rot_back = key_value[:, :, 0, :].reshape(slots, rows, head_count, head_dim)
    value_mix_back = key_value[:, :, 1, :].reshape(slots, rows, width)
    first_grad = 0.5 * value_mix_back
    key_back = (
        rotate(key_rot_back, cos_rows, -sin_rows).reshape(slots, rows, width).astype(jnp.bfloat16)
    )
    value_back = (0.5 * value_mix_back).astype(jnp.bfloat16)
    key_total = jnp.einsum("srd,sre->de", normed_low_g, key_back, preferred_element_type=jnp.float32)
    value_total = jnp.einsum(
        "srd,sre->de", normed_low_g, value_back, preferred_element_type=jnp.float32
    )
    normed_back = jnp.einsum(
        "sre,de->srd", query_back, query_mat, preferred_element_type=jnp.float32
    )
    normed_back = normed_back + jnp.einsum(
        "sre,de->srd", key_back, key_mat, preferred_element_type=jnp.float32
    )
    normed_back = normed_back + jnp.einsum(
        "sre,de->srd", value_back, value_mat, preferred_element_type=jnp.float32
    )
    normed_back = from_gathered(normed_back, w_rows)
    tokens_norm_back, prenorm_total = norm_back(
        tokens_wide, inverse, prenorm_full.astype(jnp.float32), normed_back
    )
    tokens_grad = middle_back + tokens_norm_back

    attn_grads = jnp.concatenate(
        [
            key_total.reshape(n_fsdp, w_rows, width),
            value_total.reshape(n_fsdp, w_rows, width),
            gain_block(
                to_gathered(prenorm_total, g_len).reshape(n_fsdp, g_len),
                to_gathered(midnorm_total, g_len).reshape(n_fsdp, g_len),
                width,
                leading=(n_fsdp,),
            ),
        ],
        axis=1,
    ).astype(jnp.bfloat16)
    attn_grads, mlp_halves = lax.optimization_barrier((attn_grads, mlp_halves))
    mlp_share = ctx_allreduce(z_combine(mlp_halves), n_ctx)
    attn_share = fsdp_reduce_scatter(attn_grads)
    attn_share = ctx_allreduce(attn_share, n_ctx)

    def attn_grad(i):
        return attn_share[i * w_rows:(i + 1) * w_rows]

    key_grad, value_grad = (attn_grad(i) for i in range(2))
    prenorm_grad = attn_share[2 * w_rows, 0:g_len]
    midnorm_grad = attn_share[2 * w_rows, g_len:2 * g_len]
    gate_grad = mlp_share[:, 0:ff]
    up_grad = mlp_share[:, ff:2 * ff]
    down_grad = mlp_share[:, 2 * ff:3 * ff].reshape(d_rows, width)
    out_grad = mlp_share[:, 3 * ff:3 * ff + width]
    query_grad = mlp_share[:, 3 * ff + width:]
    return (
        layer_out,
        tokens_grad,
        first_grad,
        query_grad,
        key_grad,
        value_grad,
        out_grad,
        gate_grad,
        up_grad,
        down_grad,
        prenorm_grad,
        midnorm_grad,
    )


def solution(mesh):
    zh = 2
    zl = 2
    n_f, n_c = mesh.devices.shape
    fine = jax.sharding.Mesh(
        mesh.devices.reshape(zh, n_f // (2 * zh), 2, zl, n_c // zl), FSDP + CTX
    )
    placed = (
        P(FSDP, CTX, None),
        P(FSDP, CTX, None),
        P(FSDP, None),
        P(FSDP, None),
        P(FSDP, None),
        P(FSDP, None),
        P(FSDP, None),
        P(FSDP, None),
        P(FSDP, None),
        P(FSDP),
        P(FSDP),
        P(FSDP, CTX, None),
        P(),
        P(),
    )
    return jax.shard_map(
        body,
        mesh=fine,
        in_specs=placed,
        out_specs=(
            P(FSDP, CTX, None),
            P(FSDP, CTX, None),
            P(FSDP, CTX, None),
            P(FSDP, None),
            P(FSDP, None),
            P(FSDP, None),
            P(FSDP, None),
            P(FSDP, None),
            P(FSDP, None),
            P(FSDP, None),
            P(FSDP),
            P(FSDP),
        ),
        check_vma=False,
    )
```

```python
import functools
import math

import jax
import jax.numpy as jnp
from jax import lax
from jax.experimental import pallas as pl
from jax.experimental.pallas import tpu as pltpu
from jax.sharding import PartitionSpec as P

H = 16


EPS = 1e-06
MASKED = -1e30
GAIN_ROWS = 16
FSDP = ("zh", "y", "core")
CTX = ("zl", "x")
Z_CROSS = [(0, 3), (3, 0), (1, 2), (2, 1)]


HEAD_BLOCK = 128
NT_DIMS = (((1,), (1,)), ((), ()))
TN_DIMS = (((0,), (0,)), ((), ()))


def attention_shares(query, keys, first_row, slot_len, scale):
    scores = lax.dot_general(query, keys, NT_DIMS, preferred_element_type=jnp.float32) * scale
    shape = scores.shape
    query_pos = first_row + lax.broadcasted_iota(jnp.int32, shape, 0)
    key_pos = lax.broadcasted_iota(jnp.int32, shape, 1)
    allowed = (key_pos <= query_pos) & (key_pos < slot_len)
    scores = jnp.where(allowed, scores, MASKED)
    peak = jnp.max(scores, axis=-1, keepdims=True)
    raised = jnp.exp(scores - peak)
    denominator = jnp.sum(raised, axis=-1, keepdims=True)
    return raised / denominator


def attn_fwd_kernel(head_dim, scale, meta_ref, q_ref, k_ref, v_ref, o_ref):
    first_row = meta_ref[0]
    slot_len = meta_ref[1]
    for j in range(q_ref.shape[1] // head_dim):
        cols = slice(j * head_dim, (j + 1) * head_dim)
        shares = attention_shares(q_ref[:, cols], k_ref[:, cols], first_row, slot_len, scale)
        mixed = jnp.dot(
            shares.astype(jnp.bfloat16), v_ref[:, cols], preferred_element_type=jnp.float32
        )
        o_ref[:, cols] = mixed.astype(o_ref.dtype)


def attn_bwd_kernel(head_dim, scale, meta_ref, q_ref, k_ref, v_ref, do_ref, dq_ref, dkv_ref):
    first_row = meta_ref[0]
    slot_len = meta_ref[1]
    for j in range(q_ref.shape[1] // head_dim):
        cols = slice(j * head_dim, (j + 1) * head_dim)
        query = q_ref[:, cols]
        keys = k_ref[:, cols]
        back = do_ref[:, cols]
        shares = attention_shares(query, keys, first_row, slot_len, scale)
        prob_back = lax.dot_general(back, v_ref[:, cols], NT_DIMS, preferred_element_type=jnp.float32)
        inner = jnp.sum(shares * prob_back, axis=-1, keepdims=True)
        score_back = (shares * (prob_back - inner)).astype(jnp.bfloat16)
        dq_ref[:, cols] = (
            jnp.dot(score_back, keys, preferred_element_type=jnp.float32) * scale
        )
        dkv_ref[:, cols] = (
            lax.dot_general(score_back, query, TN_DIMS, preferred_element_type=jnp.float32) * scale
        ).astype(dkv_ref.dtype)
        half = q_ref.shape[1]
        dkv_ref[:, half + j * head_dim:half + (j + 1) * head_dim] = lax.dot_general(
            shares.astype(jnp.bfloat16), back, TN_DIMS, preferred_element_type=jnp.float32
        ).astype(dkv_ref.dtype)


def attention_forward(meta, query_rows, kv_rows, head_dim, scale):
    rows, width = query_rows.shape
    keys = kv_rows.shape[0]
    blocks = width // HEAD_BLOCK
    return pl.pallas_call(
        functools.partial(attn_fwd_kernel, head_dim, scale),
        out_shape=jax.ShapeDtypeStruct((rows, width), jnp.bfloat16),
        grid_spec=pltpu.PrefetchScalarGridSpec(
            num_scalar_prefetch=1,
            grid=(blocks,),
            in_specs=[
                pl.BlockSpec((rows, HEAD_BLOCK), lambda h, m: (0, h)),
                pl.BlockSpec((keys, HEAD_BLOCK), lambda h, m: (0, h)),
                pl.BlockSpec((keys, HEAD_BLOCK), lambda h, m: (0, h + blocks)),
            ],
            out_specs=pl.BlockSpec((rows, HEAD_BLOCK), lambda h, m: (0, h)),
        ),
        compiler_params=pltpu.CompilerParams(
            dimension_semantics=("arbitrary",), vmem_limit_bytes=48 * 1024 * 1024
        ),
        cost_estimate=pl.CostEstimate(
            flops=4 * rows * keys * width,
            transcendentals=rows * keys * (width // head_dim),
            bytes_accessed=2 * (2 * rows * width + 2 * keys * width),
        ),
    )(meta, query_rows, kv_rows, kv_rows)


def attention_backward(meta, query_rows, kv_rows, back_rows, head_dim, scale):
    rows, width = query_rows.shape
    keys = kv_rows.shape[0]
    blocks = width // HEAD_BLOCK
    return pl.pallas_call(
        functools.partial(attn_bwd_kernel, head_dim, scale),
        out_shape=(
            jax.ShapeDtypeStruct((rows, width), jnp.float32),
            jax.ShapeDtypeStruct((keys, 2 * width), jnp.bfloat16),
        ),
        grid_spec=pltpu.PrefetchScalarGridSpec(
            num_scalar_prefetch=1,
            grid=(blocks,),
            in_specs=[
                pl.BlockSpec((rows, HEAD_BLOCK), lambda h, m: (0, h)),
                pl.BlockSpec((keys, HEAD_BLOCK), lambda h, m: (0, h)),
                pl.BlockSpec((keys, HEAD_BLOCK), lambda h, m: (0, h + blocks)),
                pl.BlockSpec((rows, HEAD_BLOCK), lambda h, m: (0, h)),
            ],
            out_specs=[
                pl.BlockSpec((rows, HEAD_BLOCK), lambda h, m: (0, h)),
                pl.BlockSpec((keys, 2 * HEAD_BLOCK), lambda h, m: (0, h)),
            ],
        ),
        compiler_params=pltpu.CompilerParams(
            dimension_semantics=("arbitrary",), vmem_limit_bytes=48 * 1024 * 1024
        ),
        cost_estimate=pl.CostEstimate(
            flops=10 * rows * keys * width,
            transcendentals=rows * keys * (width // head_dim),
            bytes_accessed=2 * (3 * rows * width + 4 * keys * width) + 4 * rows * width,
        ),
    )(meta, query_rows, kv_rows, kv_rows, back_rows)


def rope_tables(positions, half):
    freq = jnp.exp(
        jnp.arange(half, dtype=jnp.int32).astype(jnp.float32) * (-math.log(10000.0) / half)
    )
    angle = positions.astype(jnp.float32)[:, None] * freq[None, :]
    return (jnp.cos(angle), jnp.sin(angle))


def rotate(value_rows, cosine, sine):
    half = value_rows.shape[-1] // 2
    first = value_rows[..., :half]
    second = value_rows[..., half:]
    return jnp.concatenate(
        [first * cosine - second * sine, second * cosine + first * sine], axis=-1
    )


def norm_apply(value_rows, gain):
    inverse = lax.rsqrt(jnp.mean(value_rows * value_rows, axis=-1, keepdims=True) + EPS)
    return (value_rows * inverse * gain, inverse)


def norm_back(value_rows, inverse, gain, upstream):
    scaled = upstream * gain
    gain_part = jnp.sum(upstream * value_rows * inverse, axis=(0, 1))
    inner = jnp.mean(scaled * value_rows, axis=-1, keepdims=True)
    return (inverse * scaled - value_rows * inverse * inverse * inverse * inner, gain_part)


def gain_block(first, second, width, leading=()):
    pad_cols = width - first.shape[-1] - second.shape[-1]
    row = jnp.concatenate(
        [first, second, jnp.zeros(leading + (pad_cols,), first.dtype)], axis=-1
    )
    row = row[..., None, :]
    pads = [(0, 0)] * len(leading) + [(0, GAIN_ROWS - 1), (0, 0)]
    return jnp.pad(row, pads)


def to_gathered(rows, block):
    lead = rows.shape[:-1]
    return jnp.swapaxes(rows.reshape(lead + (2, -1, block)), -3, -2).reshape(rows.shape)


def from_gathered(rows, block):
    lead = rows.shape[:-1]
    return jnp.swapaxes(rows.reshape(lead + (-1, 2, block)), -3, -2).reshape(rows.shape)


def zh_pair(mine, other):
    first = lax.axis_index("zh") == 0
    return jnp.stack([jnp.where(first, mine, other), jnp.where(first, other, mine)])


def fsdp_gather(pack):
    other = lax.ppermute(pack, ("zh", "zl"), Z_CROSS)
    both = lax.all_gather(zh_pair(pack, other), ("y", "core"), axis=0, tiled=False)
    return both.reshape((-1,) + pack.shape)


def fsdp_reduce_scatter(grads):
    return z_combine(yc_reduce_scatter(grads))


def yc_reduce_scatter(grads):
    n_yc = grads.shape[0] // 2
    by_yc = grads
    block = grads.shape[1:]
    halves = lax.psum_scatter(
        by_yc.reshape((n_yc, 2 * block[0]) + block[1:]), ("y", "core"), scatter_dimension=0, tiled=False
    ).reshape((2,) + block)
    return halves


def z_combine(halves):
    zh = lax.axis_index("zh")
    mine = lax.dynamic_index_in_dim(halves, zh, axis=0, keepdims=False)
    theirs = lax.dynamic_index_in_dim(halves, 1 - zh, axis=0, keepdims=False)
    got = lax.ppermute(theirs, ("zh", "zl"), Z_CROSS)
    return (mine.astype(jnp.float32) + got.astype(jnp.float32)).astype(jnp.bfloat16)


def ctx_allreduce(part, n_ctx):
    total = part
    step = 1
    while step < n_ctx:
        other = lax.ppermute(total, CTX, [(j, j ^ step) for j in range(n_ctx)])
        total = (total.astype(jnp.float32) + other.astype(jnp.float32)).astype(jnp.bfloat16)
        step *= 2
    return total.astype(jnp.float32)


def body(
    tokens,
    first_value,
    query_weight,
    key_weight,
    value_weight,
    out_weight,
    gate_weight,
    up_weight,
    down_weight,
    prenorm_gain,
    midnorm_gain,
    cotangent,
    lengths,
    assignment,
):
    slots, rows, width = tokens.shape
    assert slots == 1
    head_count = H
    head_dim = width // head_count
    score_scale = head_dim ** (-0.5)
    n_fsdp = lax.axis_size(FSDP)
    n_ctx = lax.axis_size(CTX)
    total_len = rows * n_ctx
    w_rows = query_weight.shape[0]
    g_len = prenorm_gain.shape[0]
    ff = gate_weight.shape[1]
    d_rows = down_weight.shape[0]

    slot_count = assignment.shape[0]
    chosen = assignment[:, None] == jnp.arange(slot_count, dtype=jnp.int32)[None, :]
    lengths_all = jnp.sum(jnp.where(chosen, lengths[None, :], 0), axis=1)
    slot_lengths = lax.dynamic_slice_in_dim(lengths_all, lax.axis_index(FSDP) * slots, slots)
    query_places = lax.axis_index(CTX) * rows + jnp.arange(rows, dtype=jnp.int32)
    valid = query_places[None, :] < slot_lengths[:, None]
    cosine, sine = rope_tables(query_places, head_dim // 2)
    cos_rows = cosine[None, :, None, :]
    sin_rows = sine[None, :, None, :]
    valid_wide = valid[:, :, None]

    attn_pack = jnp.concatenate(
        [query_weight, key_weight, value_weight, out_weight,
         gain_block(prenorm_gain, midnorm_gain, width)],
        axis=0,
    )
    attn_all = fsdp_gather(attn_pack)

    def attn_part(i):
        return attn_all[:, i * w_rows:(i + 1) * w_rows, :].reshape(n_fsdp * w_rows, width)

    query_mat, key_mat, value_mat, out_mat = (attn_part(i) for i in range(4))
    prenorm_full = from_gathered(attn_all[:, 4 * w_rows, 0:g_len].reshape(n_fsdp * g_len), g_len)
    midnorm_full = from_gathered(
        attn_all[:, 4 * w_rows, g_len:2 * g_len].reshape(n_fsdp * g_len), g_len
    )

    mlp_pack = jnp.concatenate(
        [gate_weight, up_weight, down_weight.reshape(w_rows, ff)], axis=1
    )
    mlp_all = fsdp_gather(mlp_pack)
    gate_mat = mlp_all[:, :, 0:ff].reshape(n_fsdp * w_rows, ff)
    upper_mat = mlp_all[:, :, ff:2 * ff].reshape(n_fsdp * w_rows, ff)
    down_mat = mlp_all[:, :, 2 * ff:].reshape(n_fsdp, d_rows, width).reshape(n_fsdp * d_rows, width)

    tokens_wide = tokens.astype(jnp.float32)
    first_wide = first_value.astype(jnp.float32)
    normed, inverse = norm_apply(tokens_wide, prenorm_full.astype(jnp.float32))
    normed_low = normed.astype(jnp.bfloat16)
    normed_low_g = to_gathered(normed_low, w_rows)
    query = jnp.dot(normed_low_g, query_mat, preferred_element_type=jnp.float32)
    keyed = jnp.dot(normed_low_g, key_mat, preferred_element_type=jnp.float32)
    own_value = jnp.dot(normed_low_g, value_mat, preferred_element_type=jnp.float32)
    heads_shape = query.shape[:2] + (head_count, head_dim)
    query_rotated_rows = rotate(query.reshape(heads_shape), cos_rows, sin_rows).astype(jnp.bfloat16)
    key_rot = (
        rotate(keyed.reshape(heads_shape), cos_rows, sin_rows)
        .astype(jnp.bfloat16)
        .reshape(query.shape)
    )
    value_mix = (0.5 * own_value + 0.5 * first_wide).astype(jnp.bfloat16)

    kv_own = jnp.concatenate([key_rot, value_mix], axis=-1).reshape(rows, 2 * width)
    kv_all = lax.all_to_all(
        jnp.broadcast_to(kv_own[None], (n_ctx, rows, 2 * width)), CTX, 0, 0, tiled=False
    ).reshape(total_len, 2 * width)
    meta = jnp.stack([lax.axis_index(CTX) * rows, slot_lengths[0]]).astype(jnp.int32)
    query_flat = query_rotated_rows.reshape(rows, width)
    mixed_low = attention_forward(
        meta, query_flat, kv_all, head_dim, score_scale
    ).reshape(slots, rows, width)

    mixed_low_g = to_gathered(mixed_low, w_rows)
    middle = tokens_wide + jnp.dot(mixed_low_g, out_mat, preferred_element_type=jnp.float32)
    normed_two, inverse_two = norm_apply(middle, midnorm_full.astype(jnp.float32))
    normed_two = normed_two.astype(jnp.bfloat16)
    normed_two_g = to_gathered(normed_two, w_rows)
    gate = jnp.dot(normed_two_g, gate_mat, preferred_element_type=jnp.float32)
    upper = jnp.dot(normed_two_g, upper_mat, preferred_element_type=jnp.float32)
    hidden = (jax.nn.silu(gate) * upper).astype(jnp.bfloat16)
    hidden_g = to_gathered(hidden, d_rows)
    branch = jnp.dot(hidden_g, down_mat, preferred_element_type=jnp.float32)
    layer_out = jnp.where(valid_wide, middle + branch, 0.0).astype(jnp.bfloat16)

    cot_wide = jnp.where(valid_wide, cotangent.astype(jnp.float32), 0.0)
    cot_low = cot_wide.astype(jnp.bfloat16)
    down_total = jnp.einsum("srf,sre->fe", hidden_g, cot_low, preferred_element_type=jnp.float32)
    hidden_back = from_gathered(
        jnp.einsum("sre,fe->srf", cot_low, down_mat, preferred_element_type=jnp.float32), d_rows
    )
    sigma = jax.nn.sigmoid(gate)
    gate_back = (hidden_back * upper * sigma * (1.0 + gate * (1.0 - sigma))).astype(jnp.bfloat16)
    upper_back = (hidden_back * gate * sigma).astype(jnp.bfloat16)
    gate_total = jnp.einsum(
        "srd,srf->df", normed_two_g, gate_back, preferred_element_type=jnp.float32
    )
    upper_total = jnp.einsum(
        "srd,srf->df", normed_two_g, upper_back, preferred_element_type=jnp.float32
    )
    normed_two_back = jnp.einsum(
        "srf,df->srd", gate_back, gate_mat, preferred_element_type=jnp.float32
    )
    normed_two_back = normed_two_back + jnp.einsum(
        "srf,df->srd", upper_back, upper_mat, preferred_element_type=jnp.float32
    )
    normed_two_back = from_gathered(normed_two_back, w_rows)
    middle_norm_back, midnorm_total = norm_back(
        middle, inverse_two, midnorm_full.astype(jnp.float32), normed_two_back
    )
    middle_back = cot_wide + middle_norm_back
    middle_low = middle_back.astype(jnp.bfloat16)
    out_total = jnp.einsum("srd,sre->de", mixed_low_g, middle_low, preferred_element_type=jnp.float32)

    mlp_grads = jnp.concatenate(
        [
            gate_total.reshape(n_fsdp, w_rows, ff),
            upper_total.reshape(n_fsdp, w_rows, ff),
            down_total.reshape(n_fsdp, d_rows, width).reshape(n_fsdp, w_rows, ff),
            out_total.reshape(n_fsdp, w_rows, width),
        ],
        axis=2,
    ).astype(jnp.bfloat16)
    mlp_halves = yc_reduce_scatter(mlp_grads)

    blended_value_gradient = from_gathered(
        jnp.einsum("sre,de->srd", middle_low, out_mat, preferred_element_type=jnp.float32).astype(
            jnp.bfloat16
        ),
        w_rows,
    )
    query_rot_back, kv_back = attention_backward(
        meta, query_flat, kv_all, blended_value_gradient.reshape(rows, width), head_dim, score_scale
    )
    query_rot_back = query_rot_back.reshape(slots, rows, head_count, head_dim)
    key_value = jnp.sum(
        lax.all_to_all(kv_back.reshape(n_ctx, rows, 2 * width), CTX, 0, 0, tiled=False).astype(
            jnp.float32
        ),
        axis=0,
    )
    key_value = key_value.reshape(rows, width // HEAD_BLOCK, 2, HEAD_BLOCK)
    key_rot_back = key_value[:, :, 0, :].reshape(slots, rows, head_count, head_dim)
    value_mix_back = key_value[:, :, 1, :].reshape(slots, rows, width)
    first_grad = 0.5 * value_mix_back
    query_back = (
        rotate(query_rot_back, cos_rows, -sin_rows).reshape(slots, rows, width).astype(jnp.bfloat16)
    )
    key_back = (
        rotate(key_rot_back, cos_rows, -sin_rows).reshape(slots, rows, width).astype(jnp.bfloat16)
    )
    value_back = (0.5 * value_mix_back).astype(jnp.bfloat16)
    query_total = jnp.einsum(
        "srd,sre->de", normed_low_g, query_back, preferred_element_type=jnp.float32
    )
    key_total = jnp.einsum("srd,sre->de", normed_low_g, key_back, preferred_element_type=jnp.float32)
    value_total = jnp.einsum(
        "srd,sre->de", normed_low_g, value_back, preferred_element_type=jnp.float32
    )
    normed_back = jnp.einsum(
        "sre,de->srd", query_back, query_mat, preferred_element_type=jnp.float32
    )
    normed_back = normed_back + jnp.einsum(
        "sre,de->srd", key_back, key_mat, preferred_element_type=jnp.float32
    )
    normed_back = normed_back + jnp.einsum(
        "sre,de->srd", value_back, value_mat, preferred_element_type=jnp.float32
    )
    normed_back = from_gathered(normed_back, w_rows)
    tokens_norm_back, prenorm_total = norm_back(
        tokens_wide, inverse, prenorm_full.astype(jnp.float32), normed_back
    )
    tokens_grad = middle_back + tokens_norm_back

    attn_grads = jnp.concatenate(
        [
            query_total.reshape(n_fsdp, w_rows, width),
            key_total.reshape(n_fsdp, w_rows, width),
            value_total.reshape(n_fsdp, w_rows, width),
            gain_block(
                to_gathered(prenorm_total, g_len).reshape(n_fsdp, g_len),
                to_gathered(midnorm_total, g_len).reshape(n_fsdp, g_len),
                width,
                leading=(n_fsdp,),
            ),
        ],
        axis=1,
    ).astype(jnp.bfloat16)
    attn_grads, mlp_halves = lax.optimization_barrier((attn_grads, mlp_halves))
    mlp_share = ctx_allreduce(z_combine(mlp_halves), n_ctx)
    attn_share = fsdp_reduce_scatter(attn_grads)
    attn_share = ctx_allreduce(attn_share, n_ctx)

    def attn_grad(i):
        return attn_share[i * w_rows:(i + 1) * w_rows]

    query_grad, key_grad, value_grad = (attn_grad(i) for i in range(3))
    prenorm_grad = attn_share[3 * w_rows, 0:g_len]
    midnorm_grad = attn_share[3 * w_rows, g_len:2 * g_len]
    gate_grad = mlp_share[:, 0:ff]
    up_grad = mlp_share[:, ff:2 * ff]
    down_grad = mlp_share[:, 2 * ff:3 * ff].reshape(d_rows, width)
    out_grad = mlp_share[:, 3 * ff:]
    return (
        layer_out,
        tokens_grad,
        first_grad,
        query_grad,
        key_grad,
        value_grad,
        out_grad,
        gate_grad,
        up_grad,
        down_grad,
        prenorm_grad,
        midnorm_grad,
    )


def solution(mesh):
    zh = 2
    zl = 2
    n_f, n_c = mesh.devices.shape
    fine = jax.sharding.Mesh(
        mesh.devices.reshape(zh, n_f // (2 * zh), 2, zl, n_c // zl), FSDP + CTX
    )
    placed = (
        P(FSDP, CTX, None),
        P(FSDP, CTX, None),
        P(FSDP, None),
        P(FSDP, None),
        P(FSDP, None),
        P(FSDP, None),
        P(FSDP, None),
        P(FSDP, None),
        P(FSDP, None),
        P(FSDP),
        P(FSDP),
        P(FSDP, CTX, None),
        P(),
        P(),
    )
    return jax.shard_map(
        body,
        mesh=fine,
        in_specs=placed,
        out_specs=(
            P(FSDP, CTX, None),
            P(FSDP, CTX, None),
            P(FSDP, CTX, None),
            P(FSDP, None),
            P(FSDP, None),
            P(FSDP, None),
            P(FSDP, None),
            P(FSDP, None),
            P(FSDP, None),
            P(FSDP, None),
            P(FSDP),
            P(FSDP),
        ),
        check_vma=False,
    )
```

```python
import functools
import math

import jax
import jax.numpy as jnp
from jax import lax
from jax.experimental import pallas as pl
from jax.experimental.pallas import tpu as pltpu
from jax.sharding import PartitionSpec as P

H = 16


EPS = 1e-06
MASKED = -1e30
GAIN_ROWS = 16
FSDP = ("zh", "y", "core")
CTX = ("zl", "x")
Z_CROSS = [(0, 3), (3, 0), (1, 2), (2, 1)]


HEAD_BLOCK = 128
NT_DIMS = (((1,), (1,)), ((), ()))
TN_DIMS = (((0,), (0,)), ((), ()))


def attention_shares(query, keys, first_row, slot_len, scale):
    scores = lax.dot_general(query, keys, NT_DIMS, preferred_element_type=jnp.float32) * scale
    shape = scores.shape
    query_pos = first_row + lax.broadcasted_iota(jnp.int32, shape, 0)
    key_pos = lax.broadcasted_iota(jnp.int32, shape, 1)
    allowed = (key_pos <= query_pos) & (key_pos < slot_len)
    scores = jnp.where(allowed, scores, MASKED)
    peak = jnp.max(scores, axis=-1, keepdims=True)
    raised = jnp.exp(scores - peak)
    denominator = jnp.sum(raised, axis=-1, keepdims=True)
    return raised / denominator


def attn_fwd_kernel(head_dim, scale, meta_ref, q_ref, k_ref, v_ref, o_ref):
    first_row = meta_ref[0]
    slot_len = meta_ref[1]
    for j in range(q_ref.shape[1] // head_dim):
        cols = slice(j * head_dim, (j + 1) * head_dim)
        shares = attention_shares(q_ref[:, cols], k_ref[:, cols], first_row, slot_len, scale)
        mixed = jnp.dot(
            shares.astype(jnp.bfloat16), v_ref[:, cols], preferred_element_type=jnp.float32
        )
        o_ref[:, cols] = mixed.astype(o_ref.dtype)


def attn_bwd_kernel(head_dim, scale, meta_ref, q_ref, k_ref, v_ref, do_ref, dq_ref, dkv_ref):
    first_row = meta_ref[0]
    slot_len = meta_ref[1]
    for j in range(q_ref.shape[1] // head_dim):
        cols = slice(j * head_dim, (j + 1) * head_dim)
        query = q_ref[:, cols]
        keys = k_ref[:, cols]
        back = do_ref[:, cols]
        shares = attention_shares(query, keys, first_row, slot_len, scale)
        prob_back = lax.dot_general(back, v_ref[:, cols], NT_DIMS, preferred_element_type=jnp.float32)
        inner = jnp.sum(shares * prob_back, axis=-1, keepdims=True)
        score_back = (shares * (prob_back - inner)).astype(jnp.bfloat16)
        dq_ref[:, cols] = (
            jnp.dot(score_back, keys, preferred_element_type=jnp.float32) * scale
        )
        dkv_ref[:, cols] = (
            lax.dot_general(score_back, query, TN_DIMS, preferred_element_type=jnp.float32) * scale
        ).astype(dkv_ref.dtype)
        half = q_ref.shape[1]
        dkv_ref[:, half + j * head_dim:half + (j + 1) * head_dim] = lax.dot_general(
            shares.astype(jnp.bfloat16), back, TN_DIMS, preferred_element_type=jnp.float32
        ).astype(dkv_ref.dtype)


def attention_forward(meta, query_rows, kv_rows, head_dim, scale):
    rows, width = query_rows.shape
    keys = kv_rows.shape[0]
    blocks = width // HEAD_BLOCK
    return pl.pallas_call(
        functools.partial(attn_fwd_kernel, head_dim, scale),
        out_shape=jax.ShapeDtypeStruct((rows, width), jnp.bfloat16),
        grid_spec=pltpu.PrefetchScalarGridSpec(
            num_scalar_prefetch=1,
            grid=(blocks,),
            in_specs=[
                pl.BlockSpec((rows, HEAD_BLOCK), lambda h, m: (0, h)),
                pl.BlockSpec((keys, HEAD_BLOCK), lambda h, m: (0, h)),
                pl.BlockSpec((keys, HEAD_BLOCK), lambda h, m: (0, h + blocks)),
            ],
            out_specs=pl.BlockSpec((rows, HEAD_BLOCK), lambda h, m: (0, h)),
        ),
        compiler_params=pltpu.CompilerParams(
            dimension_semantics=("arbitrary",), vmem_limit_bytes=48 * 1024 * 1024
        ),
        cost_estimate=pl.CostEstimate(
            flops=4 * rows * keys * width,
            transcendentals=rows * keys * (width // head_dim),
            bytes_accessed=2 * (2 * rows * width + 2 * keys * width),
        ),
    )(meta, query_rows, kv_rows, kv_rows)


def attention_backward(meta, query_rows, kv_rows, back_rows, head_dim, scale):
    rows, width = query_rows.shape
    keys = kv_rows.shape[0]
    blocks = width // HEAD_BLOCK
    return pl.pallas_call(
        functools.partial(attn_bwd_kernel, head_dim, scale),
        out_shape=(
            jax.ShapeDtypeStruct((rows, width), jnp.float32),
            jax.ShapeDtypeStruct((keys, 2 * width), jnp.bfloat16),
        ),
        grid_spec=pltpu.PrefetchScalarGridSpec(
            num_scalar_prefetch=1,
            grid=(blocks,),
            in_specs=[
                pl.BlockSpec((rows, HEAD_BLOCK), lambda h, m: (0, h)),
                pl.BlockSpec((keys, HEAD_BLOCK), lambda h, m: (0, h)),
                pl.BlockSpec((keys, HEAD_BLOCK), lambda h, m: (0, h + blocks)),
                pl.BlockSpec((rows, HEAD_BLOCK), lambda h, m: (0, h)),
            ],
            out_specs=[
                pl.BlockSpec((rows, HEAD_BLOCK), lambda h, m: (0, h)),
                pl.BlockSpec((keys, 2 * HEAD_BLOCK), lambda h, m: (0, h)),
            ],
        ),
        compiler_params=pltpu.CompilerParams(
            dimension_semantics=("arbitrary",), vmem_limit_bytes=48 * 1024 * 1024
        ),
        cost_estimate=pl.CostEstimate(
            flops=10 * rows * keys * width,
            transcendentals=rows * keys * (width // head_dim),
            bytes_accessed=2 * (3 * rows * width + 4 * keys * width) + 4 * rows * width,
        ),
    )(meta, query_rows, kv_rows, kv_rows, back_rows)


def rope_tables(positions, half):
    freq = jnp.exp(
        jnp.arange(half, dtype=jnp.int32).astype(jnp.float32) * (-math.log(10000.0) / half)
    )
    angle = positions.astype(jnp.float32)[:, None] * freq[None, :]
    return (jnp.cos(angle), jnp.sin(angle))


def rotate(value_rows, cosine, sine):
    half = value_rows.shape[-1] // 2
    first = value_rows[..., :half]
    second = value_rows[..., half:]
    return jnp.concatenate(
        [first * cosine - second * sine, second * cosine + first * sine], axis=-1
    )


def norm_apply(value_rows, gain):
    inverse = lax.rsqrt(jnp.mean(value_rows * value_rows, axis=-1, keepdims=True) + EPS)
    return (value_rows * inverse * gain, inverse)


def norm_back(value_rows, inverse, gain, upstream):
    scaled = upstream * gain
    gain_part = jnp.sum(upstream * value_rows * inverse, axis=(0, 1))
    inner = jnp.mean(scaled * value_rows, axis=-1, keepdims=True)
    return (inverse * scaled - value_rows * inverse * inverse * inverse * inner, gain_part)


def gain_block(first, second, width, leading=()):
    pad_cols = width - first.shape[-1] - second.shape[-1]
    row = jnp.concatenate(
        [first, second, jnp.zeros(leading + (pad_cols,), first.dtype)], axis=-1
    )
    row = row[..., None, :]
    pads = [(0, 0)] * len(leading) + [(0, GAIN_ROWS - 1), (0, 0)]
    return jnp.pad(row, pads)


def to_gathered(rows, block):
    lead = rows.shape[:-1]
    return jnp.swapaxes(rows.reshape(lead + (2, -1, block)), -3, -2).reshape(rows.shape)


def from_gathered(rows, block):
    lead = rows.shape[:-1]
    return jnp.swapaxes(rows.reshape(lead + (-1, 2, block)), -3, -2).reshape(rows.shape)


def zh_pair(mine, other):
    first = lax.axis_index("zh") == 0
    return jnp.stack([jnp.where(first, mine, other), jnp.where(first, other, mine)])


def fsdp_gather(pack):
    other = lax.ppermute(pack, ("zh", "zl"), Z_CROSS)
    both = lax.all_gather(zh_pair(pack, other), ("y", "core"), axis=0, tiled=False)
    return both.reshape((-1,) + pack.shape)


def fsdp_reduce_scatter(grads):
    return z_combine(yc_reduce_scatter(grads))


def yc_reduce_scatter(grads):
    n_yc = grads.shape[0] // 2
    by_yc = grads
    block = grads.shape[1:]
    halves = lax.psum_scatter(
        by_yc.reshape((n_yc, 2 * block[0]) + block[1:]), ("y", "core"), scatter_dimension=0, tiled=False
    ).reshape((2,) + block)
    return halves


def z_combine(halves):
    zh = lax.axis_index("zh")
    mine = lax.dynamic_index_in_dim(halves, zh, axis=0, keepdims=False)
    theirs = lax.dynamic_index_in_dim(halves, 1 - zh, axis=0, keepdims=False)
    got = lax.ppermute(theirs, ("zh", "zl"), Z_CROSS)
    return (mine.astype(jnp.float32) + got.astype(jnp.float32)).astype(jnp.bfloat16)


def ctx_allreduce(part, n_ctx):
    total = part
    step = 1
    while step < n_ctx:
        other = lax.ppermute(total, CTX, [(j, j ^ step) for j in range(n_ctx)])
        total = (total.astype(jnp.float32) + other.astype(jnp.float32)).astype(jnp.bfloat16)
        step *= 2
    return total.astype(jnp.float32)


def body(
    tokens,
    first_value,
    query_weight,
    key_weight,
    value_weight,
    out_weight,
    gate_weight,
    up_weight,
    down_weight,
    prenorm_gain,
    midnorm_gain,
    cotangent,
    lengths,
    assignment,
):
    slots, rows, width = tokens.shape
    assert slots == 1
    head_count = H
    head_dim = width // head_count
    score_scale = head_dim ** (-0.5)
    n_fsdp = lax.axis_size(FSDP)
    n_ctx = lax.axis_size(CTX)
    total_len = rows * n_ctx
    w_rows = query_weight.shape[0]
    g_len = prenorm_gain.shape[0]
    ff = gate_weight.shape[1]
    d_rows = down_weight.shape[0]

    slot_count = assignment.shape[0]
    chosen = assignment[:, None] == jnp.arange(slot_count, dtype=jnp.int32)[None, :]
    lengths_all = jnp.sum(jnp.where(chosen, lengths[None, :], 0), axis=1)
    slot_lengths = lax.dynamic_slice_in_dim(lengths_all, lax.axis_index(FSDP) * slots, slots)
    query_places = lax.axis_index(CTX) * rows + jnp.arange(rows, dtype=jnp.int32)
    valid = query_places[None, :] < slot_lengths[:, None]
    cosine, sine = rope_tables(query_places, head_dim // 2)
    cos_rows = cosine[None, :, None, :]
    sin_rows = sine[None, :, None, :]
    valid_wide = valid[:, :, None]

    attn_pack = jnp.concatenate(
        [query_weight, key_weight, value_weight, out_weight,
         gain_block(prenorm_gain, midnorm_gain, width)],
        axis=0,
    )
    attn_all = fsdp_gather(attn_pack)

    def attn_part(i):
        return attn_all[:, i * w_rows:(i + 1) * w_rows, :].reshape(n_fsdp * w_rows, width)

    query_mat, key_mat, value_mat, out_mat = (attn_part(i) for i in range(4))
    prenorm_full = from_gathered(attn_all[:, 4 * w_rows, 0:g_len].reshape(n_fsdp * g_len), g_len)
    midnorm_full = from_gathered(
        attn_all[:, 4 * w_rows, g_len:2 * g_len].reshape(n_fsdp * g_len), g_len
    )

    mlp_pack = jnp.concatenate(
        [gate_weight, up_weight, down_weight.reshape(w_rows, ff)], axis=1
    )
    mlp_all = fsdp_gather(mlp_pack)
    gate_mat = mlp_all[:, :, 0:ff].reshape(n_fsdp * w_rows, ff)
    upper_mat = mlp_all[:, :, ff:2 * ff].reshape(n_fsdp * w_rows, ff)
    down_mat = mlp_all[:, :, 2 * ff:].reshape(n_fsdp, d_rows, width).reshape(n_fsdp * d_rows, width)

    tokens_wide = tokens.astype(jnp.float32)
    first_wide = first_value.astype(jnp.float32)
    normed, inverse = norm_apply(tokens_wide, prenorm_full.astype(jnp.float32))
    normed_low = normed.astype(jnp.bfloat16)
    normed_low_g = to_gathered(normed_low, w_rows)
    query = jnp.dot(normed_low_g, query_mat, preferred_element_type=jnp.float32)
    keyed = jnp.dot(normed_low_g, key_mat, preferred_element_type=jnp.float32)
    own_value = jnp.dot(normed_low_g, value_mat, preferred_element_type=jnp.float32)
    heads_shape = query.shape[:2] + (head_count, head_dim)
    query_rotated_rows = rotate(query.reshape(heads_shape), cos_rows, sin_rows).astype(jnp.bfloat16)
    key_rot = (
        rotate(keyed.reshape(heads_shape), cos_rows, sin_rows)
        .astype(jnp.bfloat16)
        .reshape(query.shape)
    )
    value_mix = (0.5 * own_value + 0.5 * first_wide).astype(jnp.bfloat16)

    kv_own = jnp.concatenate([key_rot, value_mix], axis=-1).reshape(rows, 2 * width)
    kv_all = lax.all_to_all(
        jnp.broadcast_to(kv_own[None], (n_ctx, rows, 2 * width)), CTX, 0, 0, tiled=False
    ).reshape(total_len, 2 * width)
    meta = jnp.stack([lax.axis_index(CTX) * rows, slot_lengths[0]]).astype(jnp.int32)
    query_flat = query_rotated_rows.reshape(rows, width)
    mixed_low = attention_forward(
        meta, query_flat, kv_all, head_dim, score_scale
    ).reshape(slots, rows, width)

    mixed_low_g = to_gathered(mixed_low, w_rows)
    middle = tokens_wide + jnp.dot(mixed_low_g, out_mat, preferred_element_type=jnp.float32)
    normed_two, inverse_two = norm_apply(middle, midnorm_full.astype(jnp.float32))
    normed_two = normed_two.astype(jnp.bfloat16)
    normed_two_g = to_gathered(normed_two, w_rows)
    gate = jnp.dot(normed_two_g, gate_mat, preferred_element_type=jnp.float32)
    upper = jnp.dot(normed_two_g, upper_mat, preferred_element_type=jnp.float32)
    hidden = (jax.nn.silu(gate) * upper).astype(jnp.bfloat16)
    hidden_g = to_gathered(hidden, d_rows)
    branch = jnp.dot(hidden_g, down_mat, preferred_element_type=jnp.float32)
    layer_out = jnp.where(valid_wide, middle + branch, 0.0).astype(jnp.bfloat16)

    cot_wide = jnp.where(valid_wide, cotangent.astype(jnp.float32), 0.0)
    cot_low = cot_wide.astype(jnp.bfloat16)
    down_total = jnp.einsum("srf,sre->fe", hidden_g, cot_low, preferred_element_type=jnp.float32)
    hidden_back = from_gathered(
        jnp.einsum("sre,fe->srf", cot_low, down_mat, preferred_element_type=jnp.float32), d_rows
    )
    sigma = jax.nn.sigmoid(gate)
    gate_back = (hidden_back * upper * sigma * (1.0 + gate * (1.0 - sigma))).astype(jnp.bfloat16)
    upper_back = (hidden_back * gate * sigma).astype(jnp.bfloat16)
    gate_total = jnp.einsum(
        "srd,srf->df", normed_two_g, gate_back, preferred_element_type=jnp.float32
    )
    upper_total = jnp.einsum(
        "srd,srf->df", normed_two_g, upper_back, preferred_element_type=jnp.float32
    )
    normed_two_back = jnp.einsum(
        "srf,df->srd", gate_back, gate_mat, preferred_element_type=jnp.float32
    )
    normed_two_back = normed_two_back + jnp.einsum(
        "srf,df->srd", upper_back, upper_mat, preferred_element_type=jnp.float32
    )
    normed_two_back = from_gathered(normed_two_back, w_rows)
    middle_norm_back, midnorm_total = norm_back(
        middle, inverse_two, midnorm_full.astype(jnp.float32), normed_two_back
    )
    middle_back = cot_wide + middle_norm_back
    middle_low = middle_back.astype(jnp.bfloat16)
    out_total = jnp.einsum("srd,sre->de", mixed_low_g, middle_low, preferred_element_type=jnp.float32)

    mlp_grads = jnp.concatenate(
        [
            gate_total.reshape(n_fsdp, w_rows, ff),
            upper_total.reshape(n_fsdp, w_rows, ff),
            down_total.reshape(n_fsdp, d_rows, width).reshape(n_fsdp, w_rows, ff),
            out_total.reshape(n_fsdp, w_rows, width),
        ],
        axis=2,
    ).astype(jnp.bfloat16)
    mlp_halves = yc_reduce_scatter(mlp_grads)

    blended_value_gradient = from_gathered(
        jnp.einsum("sre,de->srd", middle_low, out_mat, preferred_element_type=jnp.float32).astype(
            jnp.bfloat16
        ),
        w_rows,
    )
    query_rot_back, kv_back = attention_backward(
        meta, query_flat, kv_all, blended_value_gradient.reshape(rows, width), head_dim, score_scale
    )
    query_rot_back = query_rot_back.reshape(slots, rows, head_count, head_dim)
    key_value = jnp.sum(
        lax.all_to_all(kv_back.reshape(n_ctx, rows, 2 * width), CTX, 0, 0, tiled=False).astype(
            jnp.float32
        ),
        axis=0,
    )
    key_value = key_value.reshape(rows, width // HEAD_BLOCK, 2, HEAD_BLOCK)
    key_rot_back = key_value[:, :, 0, :].reshape(slots, rows, head_count, head_dim)
    value_mix_back = key_value[:, :, 1, :].reshape(slots, rows, width)
    first_grad = 0.5 * value_mix_back
    query_back = (
        rotate(query_rot_back, cos_rows, -sin_rows).reshape(slots, rows, width).astype(jnp.bfloat16)
    )
    key_back = (
        rotate(key_rot_back, cos_rows, -sin_rows).reshape(slots, rows, width).astype(jnp.bfloat16)
    )
    value_back = (0.5 * value_mix_back).astype(jnp.bfloat16)
    query_total = jnp.einsum(
        "srd,sre->de", normed_low_g, query_back, preferred_element_type=jnp.float32
    )
    key_total = jnp.einsum("srd,sre->de", normed_low_g, key_back, preferred_element_type=jnp.float32)
    value_total = jnp.einsum(
        "srd,sre->de", normed_low_g, value_back, preferred_element_type=jnp.float32
    )
    normed_back = jnp.einsum(
        "sre,de->srd", query_back, query_mat, preferred_element_type=jnp.float32
    )
    normed_back = normed_back + jnp.einsum(
        "sre,de->srd", key_back, key_mat, preferred_element_type=jnp.float32
    )
    normed_back = normed_back + jnp.einsum(
        "sre,de->srd", value_back, value_mat, preferred_element_type=jnp.float32
    )
    normed_back = from_gathered(normed_back, w_rows)
    tokens_norm_back, prenorm_total = norm_back(
        tokens_wide, inverse, prenorm_full.astype(jnp.float32), normed_back
    )
    tokens_grad = middle_back + tokens_norm_back

    attn_grads = jnp.concatenate(
        [
            query_total.reshape(n_fsdp, w_rows, width),
            key_total.reshape(n_fsdp, w_rows, width),
            value_total.reshape(n_fsdp, w_rows, width),
            gain_block(
                to_gathered(prenorm_total, g_len).reshape(n_fsdp, g_len),
                to_gathered(midnorm_total, g_len).reshape(n_fsdp, g_len),
                width,
                leading=(n_fsdp,),
            ),
        ],
        axis=1,
    ).astype(jnp.bfloat16)
    mlp_sum = lax.psum(mlp_halves, ("zh",) + CTX)
    attn_grads, mlp_sum = lax.optimization_barrier((attn_grads, mlp_sum))
    mlp_share = lax.dynamic_index_in_dim(
        mlp_sum, lax.axis_index("zh"), axis=0, keepdims=False
    ).astype(jnp.float32)
    attn_share = fsdp_reduce_scatter(attn_grads)
    attn_share = ctx_allreduce(attn_share, n_ctx)

    def attn_grad(i):
        return attn_share[i * w_rows:(i + 1) * w_rows]

    query_grad, key_grad, value_grad = (attn_grad(i) for i in range(3))
    prenorm_grad = attn_share[3 * w_rows, 0:g_len]
    midnorm_grad = attn_share[3 * w_rows, g_len:2 * g_len]
    gate_grad = mlp_share[:, 0:ff]
    up_grad = mlp_share[:, ff:2 * ff]
    down_grad = mlp_share[:, 2 * ff:3 * ff].reshape(d_rows, width)
    out_grad = mlp_share[:, 3 * ff:]
    return (
        layer_out,
        tokens_grad,
        first_grad,
        query_grad,
        key_grad,
        value_grad,
        out_grad,
        gate_grad,
        up_grad,
        down_grad,
        prenorm_grad,
        midnorm_grad,
    )


def solution(mesh):
    zh = 2
    zl = 2
    n_f, n_c = mesh.devices.shape
    fine = jax.sharding.Mesh(
        mesh.devices.reshape(zh, n_f // (2 * zh), 2, zl, n_c // zl), FSDP + CTX
    )
    placed = (
        P(FSDP, CTX, None),
        P(FSDP, CTX, None),
        P(FSDP, None),
        P(FSDP, None),
        P(FSDP, None),
        P(FSDP, None),
        P(FSDP, None),
        P(FSDP, None),
        P(FSDP, None),
        P(FSDP),
        P(FSDP),
        P(FSDP, CTX, None),
        P(),
        P(),
    )
    return jax.shard_map(
        body,
        mesh=fine,
        in_specs=placed,
        out_specs=(
            P(FSDP, CTX, None),
            P(FSDP, CTX, None),
            P(FSDP, CTX, None),
            P(FSDP, None),
            P(FSDP, None),
            P(FSDP, None),
            P(FSDP, None),
            P(FSDP, None),
            P(FSDP, None),
            P(FSDP, None),
            P(FSDP),
            P(FSDP),
        ),
        check_vma=False,
    )
```

```python
import functools
import math

import jax
import jax.numpy as jnp
from jax import lax
from jax.experimental import pallas as pl
from jax.experimental.pallas import tpu as pltpu
from jax.sharding import PartitionSpec as P

H = 16


EPS = 1e-06
MASKED = -1e30
GAIN_ROWS = 16
FSDP = ("zh", "y", "core")
CTX = ("zl", "x")
Z_CROSS = [(0, 3), (3, 0), (1, 2), (2, 1)]


HEAD_BLOCK = 128
NT_DIMS = (((1,), (1,)), ((), ()))
TN_DIMS = (((0,), (0,)), ((), ()))


def attention_shares(query, keys, first_row, slot_len, scale):
    scores = lax.dot_general(query, keys, NT_DIMS, preferred_element_type=jnp.float32) * scale
    shape = scores.shape
    query_pos = first_row + lax.broadcasted_iota(jnp.int32, shape, 0)
    key_pos = lax.broadcasted_iota(jnp.int32, shape, 1)
    allowed = (key_pos <= query_pos) & (key_pos < slot_len)
    scores = jnp.where(allowed, scores, MASKED)
    peak = jnp.max(scores, axis=-1, keepdims=True)
    raised = jnp.exp(scores - peak)
    denominator = jnp.sum(raised, axis=-1, keepdims=True)
    return raised / denominator


def attn_fwd_kernel(head_dim, scale, meta_ref, q_ref, k_ref, v_ref, o_ref):
    first_row = meta_ref[0]
    slot_len = meta_ref[1]
    for j in range(q_ref.shape[1] // head_dim):
        cols = slice(j * head_dim, (j + 1) * head_dim)
        shares = attention_shares(q_ref[:, cols], k_ref[:, cols], first_row, slot_len, scale)
        mixed = jnp.dot(
            shares.astype(jnp.bfloat16), v_ref[:, cols], preferred_element_type=jnp.float32
        )
        o_ref[:, cols] = mixed.astype(o_ref.dtype)


def attn_bwd_kernel(head_dim, scale, meta_ref, q_ref, k_ref, v_ref, do_ref, dq_ref, dkv_ref):
    first_row = meta_ref[0]
    slot_len = meta_ref[1]
    for j in range(q_ref.shape[1] // head_dim):
        cols = slice(j * head_dim, (j + 1) * head_dim)
        query = q_ref[:, cols]
        keys = k_ref[:, cols]
        back = do_ref[:, cols]
        shares = attention_shares(query, keys, first_row, slot_len, scale)
        prob_back = lax.dot_general(back, v_ref[:, cols], NT_DIMS, preferred_element_type=jnp.float32)
        inner = jnp.sum(shares * prob_back, axis=-1, keepdims=True)
        score_back = (shares * (prob_back - inner)).astype(jnp.bfloat16)
        dq_ref[:, cols] = (
            jnp.dot(score_back, keys, preferred_element_type=jnp.float32) * scale
        )
        dkv_ref[:, cols] = (
            lax.dot_general(score_back, query, TN_DIMS, preferred_element_type=jnp.float32) * scale
        ).astype(dkv_ref.dtype)
        half = q_ref.shape[1]
        dkv_ref[:, half + j * head_dim:half + (j + 1) * head_dim] = lax.dot_general(
            shares.astype(jnp.bfloat16), back, TN_DIMS, preferred_element_type=jnp.float32
        ).astype(dkv_ref.dtype)


def attention_forward(meta, query_rows, kv_rows, head_dim, scale):
    rows, width = query_rows.shape
    keys = kv_rows.shape[0]
    blocks = width // HEAD_BLOCK
    return pl.pallas_call(
        functools.partial(attn_fwd_kernel, head_dim, scale),
        out_shape=jax.ShapeDtypeStruct((rows, width), jnp.bfloat16),
        grid_spec=pltpu.PrefetchScalarGridSpec(
            num_scalar_prefetch=1,
            grid=(blocks,),
            in_specs=[
                pl.BlockSpec((rows, HEAD_BLOCK), lambda h, m: (0, h)),
                pl.BlockSpec((keys, HEAD_BLOCK), lambda h, m: (0, h)),
                pl.BlockSpec((keys, HEAD_BLOCK), lambda h, m: (0, h + blocks)),
            ],
            out_specs=pl.BlockSpec((rows, HEAD_BLOCK), lambda h, m: (0, h)),
        ),
        compiler_params=pltpu.CompilerParams(
            dimension_semantics=("arbitrary",), vmem_limit_bytes=48 * 1024 * 1024
        ),
        cost_estimate=pl.CostEstimate(
            flops=4 * rows * keys * width,
            transcendentals=rows * keys * (width // head_dim),
            bytes_accessed=2 * (2 * rows * width + 2 * keys * width),
        ),
    )(meta, query_rows, kv_rows, kv_rows)


def attention_backward(meta, query_rows, kv_rows, back_rows, head_dim, scale):
    rows, width = query_rows.shape
    keys = kv_rows.shape[0]
    blocks = width // HEAD_BLOCK
    return pl.pallas_call(
        functools.partial(attn_bwd_kernel, head_dim, scale),
        out_shape=(
            jax.ShapeDtypeStruct((rows, width), jnp.float32),
            jax.ShapeDtypeStruct((keys, 2 * width), jnp.bfloat16),
        ),
        grid_spec=pltpu.PrefetchScalarGridSpec(
            num_scalar_prefetch=1,
            grid=(blocks,),
            in_specs=[
                pl.BlockSpec((rows, HEAD_BLOCK), lambda h, m: (0, h)),
                pl.BlockSpec((keys, HEAD_BLOCK), lambda h, m: (0, h)),
                pl.BlockSpec((keys, HEAD_BLOCK), lambda h, m: (0, h + blocks)),
                pl.BlockSpec((rows, HEAD_BLOCK), lambda h, m: (0, h)),
            ],
            out_specs=[
                pl.BlockSpec((rows, HEAD_BLOCK), lambda h, m: (0, h)),
                pl.BlockSpec((keys, 2 * HEAD_BLOCK), lambda h, m: (0, h)),
            ],
        ),
        compiler_params=pltpu.CompilerParams(
            dimension_semantics=("arbitrary",), vmem_limit_bytes=48 * 1024 * 1024
        ),
        cost_estimate=pl.CostEstimate(
            flops=10 * rows * keys * width,
            transcendentals=rows * keys * (width // head_dim),
            bytes_accessed=2 * (3 * rows * width + 4 * keys * width) + 4 * rows * width,
        ),
    )(meta, query_rows, kv_rows, kv_rows, back_rows)


def rope_tables(positions, half):
    freq = jnp.exp(
        jnp.arange(half, dtype=jnp.int32).astype(jnp.float32) * (-math.log(10000.0) / half)
    )
    angle = positions.astype(jnp.float32)[:, None] * freq[None, :]
    return (jnp.cos(angle), jnp.sin(angle))


def rotate(value_rows, cosine, sine):
    half = value_rows.shape[-1] // 2
    first = value_rows[..., :half]
    second = value_rows[..., half:]
    return jnp.concatenate(
        [first * cosine - second * sine, second * cosine + first * sine], axis=-1
    )


def norm_apply(value_rows, gain):
    inverse = lax.rsqrt(jnp.mean(value_rows * value_rows, axis=-1, keepdims=True) + EPS)
    return (value_rows * inverse * gain, inverse)


def norm_back(value_rows, inverse, gain, upstream):
    scaled = upstream * gain
    gain_part = jnp.sum(upstream * value_rows * inverse, axis=(0, 1))
    inner = jnp.mean(scaled * value_rows, axis=-1, keepdims=True)
    return (inverse * scaled - value_rows * inverse * inverse * inverse * inner, gain_part)


def gain_block(first, second, width, leading=()):
    pad_cols = width - first.shape[-1] - second.shape[-1]
    row = jnp.concatenate(
        [first, second, jnp.zeros(leading + (pad_cols,), first.dtype)], axis=-1
    )
    row = row[..., None, :]
    pads = [(0, 0)] * len(leading) + [(0, GAIN_ROWS - 1), (0, 0)]
    return jnp.pad(row, pads)


def to_gathered(rows, block):
    lead = rows.shape[:-1]
    return jnp.swapaxes(rows.reshape(lead + (2, -1, block)), -3, -2).reshape(rows.shape)


def from_gathered(rows, block):
    lead = rows.shape[:-1]
    return jnp.swapaxes(rows.reshape(lead + (-1, 2, block)), -3, -2).reshape(rows.shape)


def zh_pair(mine, other):
    first = lax.axis_index("zh") == 0
    return jnp.stack([jnp.where(first, mine, other), jnp.where(first, other, mine)])


def fsdp_gather(pack):
    other = lax.ppermute(pack, ("zh", "zl"), Z_CROSS)
    both = lax.all_gather(zh_pair(pack, other), ("y", "core"), axis=0, tiled=False)
    return both.reshape((-1,) + pack.shape)


def fsdp_reduce_scatter(grads):
    return z_combine(yc_reduce_scatter(grads))


def yc_reduce_scatter(grads):
    n_yc = grads.shape[0] // 2
    by_yc = grads
    block = grads.shape[1:]
    halves = lax.psum_scatter(
        by_yc.reshape((n_yc, 2 * block[0]) + block[1:]), ("y", "core"), scatter_dimension=0, tiled=False
    ).reshape((2,) + block)
    return halves


def z_combine(halves):
    zh = lax.axis_index("zh")
    mine = lax.dynamic_index_in_dim(halves, zh, axis=0, keepdims=False)
    theirs = lax.dynamic_index_in_dim(halves, 1 - zh, axis=0, keepdims=False)
    got = lax.ppermute(theirs, ("zh", "zl"), Z_CROSS)
    return (mine.astype(jnp.float32) + got.astype(jnp.float32)).astype(jnp.bfloat16)


def ctx_allreduce(part, n_ctx):
    total = part
    step = 1
    while step < n_ctx:
        other = lax.ppermute(total, CTX, [(j, j ^ step) for j in range(n_ctx)])
        total = (total.astype(jnp.float32) + other.astype(jnp.float32)).astype(jnp.bfloat16)
        step *= 2
    return total.astype(jnp.float32)


def body(
    tokens,
    first_value,
    query_weight,
    key_weight,
    value_weight,
    out_weight,
    gate_weight,
    up_weight,
    down_weight,
    prenorm_gain,
    midnorm_gain,
    cotangent,
    lengths,
    assignment,
):
    slots, rows, width = tokens.shape
    assert slots == 1
    head_count = H
    head_dim = width // head_count
    score_scale = head_dim ** (-0.5)
    n_fsdp = lax.axis_size(FSDP)
    n_ctx = lax.axis_size(CTX)
    total_len = rows * n_ctx
    w_rows = query_weight.shape[0]
    g_len = prenorm_gain.shape[0]
    ff = gate_weight.shape[1]
    d_rows = down_weight.shape[0]

    slot_count = assignment.shape[0]
    chosen = assignment[:, None] == jnp.arange(slot_count, dtype=jnp.int32)[None, :]
    lengths_all = jnp.sum(jnp.where(chosen, lengths[None, :], 0), axis=1)
    slot_lengths = lax.dynamic_slice_in_dim(lengths_all, lax.axis_index(FSDP) * slots, slots)
    query_places = lax.axis_index(CTX) * rows + jnp.arange(rows, dtype=jnp.int32)
    valid = query_places[None, :] < slot_lengths[:, None]
    cosine, sine = rope_tables(query_places, head_dim // 2)
    cos_rows = cosine[None, :, None, :]
    sin_rows = sine[None, :, None, :]
    valid_wide = valid[:, :, None]

    attn_pack = jnp.concatenate(
        [query_weight, key_weight, value_weight, out_weight,
         gain_block(prenorm_gain, midnorm_gain, width)],
        axis=0,
    )
    attn_all = fsdp_gather(attn_pack)

    def attn_part(i):
        return attn_all[:, i * w_rows:(i + 1) * w_rows, :].reshape(n_fsdp * w_rows, width)

    query_mat, key_mat, value_mat, out_mat = (attn_part(i) for i in range(4))
    prenorm_full = from_gathered(attn_all[:, 4 * w_rows, 0:g_len].reshape(n_fsdp * g_len), g_len)
    midnorm_full = from_gathered(
        attn_all[:, 4 * w_rows, g_len:2 * g_len].reshape(n_fsdp * g_len), g_len
    )

    mlp_pack = jnp.concatenate(
        [gate_weight, up_weight, down_weight.reshape(w_rows, ff)], axis=1
    )
    mlp_all = fsdp_gather(mlp_pack)
    gate_mat = mlp_all[:, :, 0:ff].reshape(n_fsdp * w_rows, ff)
    upper_mat = mlp_all[:, :, ff:2 * ff].reshape(n_fsdp * w_rows, ff)
    down_mat = mlp_all[:, :, 2 * ff:].reshape(n_fsdp, d_rows, width).reshape(n_fsdp * d_rows, width)

    tokens_wide = tokens.astype(jnp.float32)
    first_wide = first_value.astype(jnp.float32)
    normed, inverse = norm_apply(tokens_wide, prenorm_full.astype(jnp.float32))
    normed_low = normed.astype(jnp.bfloat16)
    normed_low_g = to_gathered(normed_low, w_rows)
    query = jnp.dot(normed_low_g, query_mat, preferred_element_type=jnp.float32)
    keyed = jnp.dot(normed_low_g, key_mat, preferred_element_type=jnp.float32)
    own_value = jnp.dot(normed_low_g, value_mat, preferred_element_type=jnp.float32)
    heads_shape = query.shape[:2] + (head_count, head_dim)
    query_rotated_rows = rotate(query.reshape(heads_shape), cos_rows, sin_rows).astype(jnp.bfloat16)
    key_rot = (
        rotate(keyed.reshape(heads_shape), cos_rows, sin_rows)
        .astype(jnp.bfloat16)
        .reshape(query.shape)
    )
    value_mix = (0.5 * own_value + 0.5 * first_wide).astype(jnp.bfloat16)

    kv_own = jnp.concatenate([key_rot, value_mix], axis=-1).reshape(rows, 2 * width)
    kv_all = lax.all_to_all(
        jnp.broadcast_to(kv_own[None], (n_ctx, rows, 2 * width)), CTX, 0, 0, tiled=False
    ).reshape(total_len, 2 * width)
    meta = jnp.stack([lax.axis_index(CTX) * rows, slot_lengths[0]]).astype(jnp.int32)
    query_flat = query_rotated_rows.reshape(rows, width)
    mixed_low = attention_forward(
        meta, query_flat, kv_all, head_dim, score_scale
    ).reshape(slots, rows, width)

    mixed_low_g = to_gathered(mixed_low, w_rows)
    middle = tokens_wide + jnp.dot(mixed_low_g, out_mat, preferred_element_type=jnp.float32)
    normed_two, inverse_two = norm_apply(middle, midnorm_full.astype(jnp.float32))
    normed_two = normed_two.astype(jnp.bfloat16)
    normed_two_g = to_gathered(normed_two, w_rows)
    gate = jnp.dot(normed_two_g, gate_mat, preferred_element_type=jnp.float32)
    upper = jnp.dot(normed_two_g, upper_mat, preferred_element_type=jnp.float32)
    hidden = (jax.nn.silu(gate) * upper).astype(jnp.bfloat16)
    hidden_g = to_gathered(hidden, d_rows)
    branch = jnp.dot(hidden_g, down_mat, preferred_element_type=jnp.float32)
    layer_out = jnp.where(valid_wide, middle + branch, 0.0).astype(jnp.bfloat16)

    cot_wide = jnp.where(valid_wide, cotangent.astype(jnp.float32), 0.0)
    cot_low = cot_wide.astype(jnp.bfloat16)
    down_total = jnp.einsum("srf,sre->fe", hidden_g, cot_low, preferred_element_type=jnp.float32)
    hidden_back = from_gathered(
        jnp.einsum("sre,fe->srf", cot_low, down_mat, preferred_element_type=jnp.float32), d_rows
    )
    sigma = jax.nn.sigmoid(gate)
    gate_back = (hidden_back * upper * sigma * (1.0 + gate * (1.0 - sigma))).astype(jnp.bfloat16)
    upper_back = (hidden_back * gate * sigma).astype(jnp.bfloat16)
    gate_total = jnp.einsum(
        "srd,srf->df", normed_two_g, gate_back, preferred_element_type=jnp.float32
    )
    upper_total = jnp.einsum(
        "srd,srf->df", normed_two_g, upper_back, preferred_element_type=jnp.float32
    )
    normed_two_back = jnp.einsum(
        "srf,df->srd", gate_back, gate_mat, preferred_element_type=jnp.float32
    )
    normed_two_back = normed_two_back + jnp.einsum(
        "srf,df->srd", upper_back, upper_mat, preferred_element_type=jnp.float32
    )
    normed_two_back = from_gathered(normed_two_back, w_rows)
    middle_norm_back, midnorm_total = norm_back(
        middle, inverse_two, midnorm_full.astype(jnp.float32), normed_two_back
    )
    middle_back = cot_wide + middle_norm_back
    middle_low = middle_back.astype(jnp.bfloat16)
    out_total = jnp.einsum("srd,sre->de", mixed_low_g, middle_low, preferred_element_type=jnp.float32)

    down_share = ctx_allreduce(
        z_combine(yc_reduce_scatter(down_total.astype(jnp.bfloat16).reshape(n_fsdp, d_rows, width))),
        n_ctx,
    )
    mlp_grads = jnp.concatenate(
        [
            gate_total.reshape(n_fsdp, w_rows, ff),
            upper_total.reshape(n_fsdp, w_rows, ff),
            out_total.reshape(n_fsdp, w_rows, width),
        ],
        axis=2,
    ).astype(jnp.bfloat16)
    mlp_halves = yc_reduce_scatter(mlp_grads)

    blended_value_gradient = from_gathered(
        jnp.einsum("sre,de->srd", middle_low, out_mat, preferred_element_type=jnp.float32).astype(
            jnp.bfloat16
        ),
        w_rows,
    )
    query_rot_back, kv_back = attention_backward(
        meta, query_flat, kv_all, blended_value_gradient.reshape(rows, width), head_dim, score_scale
    )
    query_rot_back = query_rot_back.reshape(slots, rows, head_count, head_dim)
    key_value = jnp.sum(
        lax.all_to_all(kv_back.reshape(n_ctx, rows, 2 * width), CTX, 0, 0, tiled=False).astype(
            jnp.float32
        ),
        axis=0,
    )
    key_value = key_value.reshape(rows, width // HEAD_BLOCK, 2, HEAD_BLOCK)
    key_rot_back = key_value[:, :, 0, :].reshape(slots, rows, head_count, head_dim)
    value_mix_back = key_value[:, :, 1, :].reshape(slots, rows, width)
    first_grad = 0.5 * value_mix_back
    query_back = (
        rotate(query_rot_back, cos_rows, -sin_rows).reshape(slots, rows, width).astype(jnp.bfloat16)
    )
    key_back = (
        rotate(key_rot_back, cos_rows, -sin_rows).reshape(slots, rows, width).astype(jnp.bfloat16)
    )
    value_back = (0.5 * value_mix_back).astype(jnp.bfloat16)
    query_total = jnp.einsum(
        "srd,sre->de", normed_low_g, query_back, preferred_element_type=jnp.float32
    )
    key_total = jnp.einsum("srd,sre->de", normed_low_g, key_back, preferred_element_type=jnp.float32)
    value_total = jnp.einsum(
        "srd,sre->de", normed_low_g, value_back, preferred_element_type=jnp.float32
    )
    normed_back = jnp.einsum(
        "sre,de->srd", query_back, query_mat, preferred_element_type=jnp.float32
    )
    normed_back = normed_back + jnp.einsum(
        "sre,de->srd", key_back, key_mat, preferred_element_type=jnp.float32
    )
    normed_back = normed_back + jnp.einsum(
        "sre,de->srd", value_back, value_mat, preferred_element_type=jnp.float32
    )
    normed_back = from_gathered(normed_back, w_rows)
    tokens_norm_back, prenorm_total = norm_back(
        tokens_wide, inverse, prenorm_full.astype(jnp.float32), normed_back
    )
    tokens_grad = middle_back + tokens_norm_back

    attn_grads = jnp.concatenate(
        [
            query_total.reshape(n_fsdp, w_rows, width),
            key_total.reshape(n_fsdp, w_rows, width),
            value_total.reshape(n_fsdp, w_rows, width),
            gain_block(
                to_gathered(prenorm_total, g_len).reshape(n_fsdp, g_len),
                to_gathered(midnorm_total, g_len).reshape(n_fsdp, g_len),
                width,
                leading=(n_fsdp,),
            ),
        ],
        axis=1,
    ).astype(jnp.bfloat16)
    attn_grads, mlp_halves = lax.optimization_barrier((attn_grads, mlp_halves))
    mlp_share = ctx_allreduce(z_combine(mlp_halves), n_ctx)
    attn_share = fsdp_reduce_scatter(attn_grads)
    attn_share = ctx_allreduce(attn_share, n_ctx)

    def attn_grad(i):
        return attn_share[i * w_rows:(i + 1) * w_rows]

    query_grad, key_grad, value_grad = (attn_grad(i) for i in range(3))
    prenorm_grad = attn_share[3 * w_rows, 0:g_len]
    midnorm_grad = attn_share[3 * w_rows, g_len:2 * g_len]
    gate_grad = mlp_share[:, 0:ff]
    up_grad = mlp_share[:, ff:2 * ff]
    down_grad = down_share
    out_grad = mlp_share[:, 2 * ff:]
    return (
        layer_out,
        tokens_grad,
        first_grad,
        query_grad,
        key_grad,
        value_grad,
        out_grad,
        gate_grad,
        up_grad,
        down_grad,
        prenorm_grad,
        midnorm_grad,
    )


def solution(mesh):
    zh = 2
    zl = 2
    n_f, n_c = mesh.devices.shape
    fine = jax.sharding.Mesh(
        mesh.devices.reshape(zh, n_f // (2 * zh), 2, zl, n_c // zl), FSDP + CTX
    )
    placed = (
        P(FSDP, CTX, None),
        P(FSDP, CTX, None),
        P(FSDP, None),
        P(FSDP, None),
        P(FSDP, None),
        P(FSDP, None),
        P(FSDP, None),
        P(FSDP, None),
        P(FSDP, None),
        P(FSDP),
        P(FSDP),
        P(FSDP, CTX, None),
        P(),
        P(),
    )
    return jax.shard_map(
        body,
        mesh=fine,
        in_specs=placed,
        out_specs=(
            P(FSDP, CTX, None),
            P(FSDP, CTX, None),
            P(FSDP, CTX, None),
            P(FSDP, None),
            P(FSDP, None),
            P(FSDP, None),
            P(FSDP, None),
            P(FSDP, None),
            P(FSDP, None),
            P(FSDP, None),
            P(FSDP),
            P(FSDP),
        ),
        check_vma=False,
    )
```

```python
import functools
import math

import jax
import jax.numpy as jnp
from jax import lax
from jax.experimental import pallas as pl
from jax.experimental.pallas import tpu as pltpu
from jax.sharding import PartitionSpec as P

H = 16


EPS = 1e-06
MASKED = -1e30
GAIN_ROWS = 16
FSDP = ("zh", "y", "core")
CTX = ("zl", "x")
Z_CROSS = [(0, 3), (3, 0), (1, 2), (2, 1)]


HEAD_BLOCK = 128
NT_DIMS = (((1,), (1,)), ((), ()))
TN_DIMS = (((0,), (0,)), ((), ()))


def attention_shares(query, keys, first_row, slot_len, scale):
    scores = lax.dot_general(query, keys, NT_DIMS, preferred_element_type=jnp.float32) * scale
    shape = scores.shape
    query_pos = first_row + lax.broadcasted_iota(jnp.int32, shape, 0)
    key_pos = lax.broadcasted_iota(jnp.int32, shape, 1)
    allowed = (key_pos <= query_pos) & (key_pos < slot_len)
    scores = jnp.where(allowed, scores, MASKED)
    peak = jnp.max(scores, axis=-1, keepdims=True)
    raised = jnp.exp(scores - peak)
    denominator = jnp.sum(raised, axis=-1, keepdims=True)
    return raised / denominator


def attn_fwd_kernel(head_dim, scale, meta_ref, q_ref, k_ref, v_ref, o_ref):
    first_row = meta_ref[0]
    slot_len = meta_ref[1]
    for j in range(q_ref.shape[1] // head_dim):
        cols = slice(j * head_dim, (j + 1) * head_dim)
        shares = attention_shares(q_ref[:, cols], k_ref[:, cols], first_row, slot_len, scale)
        mixed = jnp.dot(
            shares.astype(jnp.bfloat16), v_ref[:, cols], preferred_element_type=jnp.float32
        )
        o_ref[:, cols] = mixed.astype(o_ref.dtype)


def attn_bwd_kernel(head_dim, scale, meta_ref, q_ref, k_ref, v_ref, do_ref, dq_ref, dkv_ref):
    first_row = meta_ref[0]
    slot_len = meta_ref[1]
    for j in range(q_ref.shape[1] // head_dim):
        cols = slice(j * head_dim, (j + 1) * head_dim)
        query = q_ref[:, cols]
        keys = k_ref[:, cols]
        back = do_ref[:, cols]
        shares = attention_shares(query, keys, first_row, slot_len, scale)
        prob_back = lax.dot_general(back, v_ref[:, cols], NT_DIMS, preferred_element_type=jnp.float32)
        inner = jnp.sum(shares * prob_back, axis=-1, keepdims=True)
        score_back = (shares * (prob_back - inner)).astype(jnp.bfloat16)
        dq_ref[:, cols] = (
            jnp.dot(score_back, keys, preferred_element_type=jnp.float32) * scale
        )
        dkv_ref[:, cols] = (
            lax.dot_general(score_back, query, TN_DIMS, preferred_element_type=jnp.float32) * scale
        ).astype(dkv_ref.dtype)
        half = q_ref.shape[1]
        dkv_ref[:, half + j * head_dim:half + (j + 1) * head_dim] = lax.dot_general(
            shares.astype(jnp.bfloat16), back, TN_DIMS, preferred_element_type=jnp.float32
        ).astype(dkv_ref.dtype)


def attention_forward(meta, query_rows, kv_rows, head_dim, scale):
    rows, width = query_rows.shape
    keys = kv_rows.shape[0]
    blocks = width // HEAD_BLOCK
    return pl.pallas_call(
        functools.partial(attn_fwd_kernel, head_dim, scale),
        out_shape=jax.ShapeDtypeStruct((rows, width), jnp.bfloat16),
        grid_spec=pltpu.PrefetchScalarGridSpec(
            num_scalar_prefetch=1,
            grid=(blocks,),
            in_specs=[
                pl.BlockSpec((rows, HEAD_BLOCK), lambda h, m: (0, h)),
                pl.BlockSpec((keys, HEAD_BLOCK), lambda h, m: (0, h)),
                pl.BlockSpec((keys, HEAD_BLOCK), lambda h, m: (0, h + blocks)),
            ],
            out_specs=pl.BlockSpec((rows, HEAD_BLOCK), lambda h, m: (0, h)),
        ),
        compiler_params=pltpu.CompilerParams(
            dimension_semantics=("arbitrary",), vmem_limit_bytes=48 * 1024 * 1024
        ),
        cost_estimate=pl.CostEstimate(
            flops=4 * rows * keys * width,
            transcendentals=rows * keys * (width // head_dim),
            bytes_accessed=2 * (2 * rows * width + 2 * keys * width),
        ),
    )(meta, query_rows, kv_rows, kv_rows)


def attention_backward(meta, query_rows, kv_rows, back_rows, head_dim, scale):
    rows, width = query_rows.shape
    keys = kv_rows.shape[0]
    blocks = width // HEAD_BLOCK
    return pl.pallas_call(
        functools.partial(attn_bwd_kernel, head_dim, scale),
        out_shape=(
            jax.ShapeDtypeStruct((rows, width), jnp.float32),
            jax.ShapeDtypeStruct((keys, 2 * width), jnp.bfloat16),
        ),
        grid_spec=pltpu.PrefetchScalarGridSpec(
            num_scalar_prefetch=1,
            grid=(blocks,),
            in_specs=[
                pl.BlockSpec((rows, HEAD_BLOCK), lambda h, m: (0, h)),
                pl.BlockSpec((keys, HEAD_BLOCK), lambda h, m: (0, h)),
                pl.BlockSpec((keys, HEAD_BLOCK), lambda h, m: (0, h + blocks)),
                pl.BlockSpec((rows, HEAD_BLOCK), lambda h, m: (0, h)),
            ],
            out_specs=[
                pl.BlockSpec((rows, HEAD_BLOCK), lambda h, m: (0, h)),
                pl.BlockSpec((keys, 2 * HEAD_BLOCK), lambda h, m: (0, h)),
            ],
        ),
        compiler_params=pltpu.CompilerParams(
            dimension_semantics=("arbitrary",), vmem_limit_bytes=48 * 1024 * 1024
        ),
        cost_estimate=pl.CostEstimate(
            flops=10 * rows * keys * width,
            transcendentals=rows * keys * (width // head_dim),
            bytes_accessed=2 * (3 * rows * width + 4 * keys * width) + 4 * rows * width,
        ),
    )(meta, query_rows, kv_rows, kv_rows, back_rows)


def rope_tables(positions, half):
    freq = jnp.exp(
        jnp.arange(half, dtype=jnp.int32).astype(jnp.float32) * (-math.log(10000.0) / half)
    )
    angle = positions.astype(jnp.float32)[:, None] * freq[None, :]
    return (jnp.cos(angle), jnp.sin(angle))


def rotate(value_rows, cosine, sine):
    half = value_rows.shape[-1] // 2
    first = value_rows[..., :half]
    second = value_rows[..., half:]
    return jnp.concatenate(
        [first * cosine - second * sine, second * cosine + first * sine], axis=-1
    )


def norm_apply(value_rows, gain):
    inverse = lax.rsqrt(jnp.mean(value_rows * value_rows, axis=-1, keepdims=True) + EPS)
    return (value_rows * inverse * gain, inverse)


def norm_back(value_rows, inverse, gain, upstream):
    scaled = upstream * gain
    gain_part = jnp.sum(upstream * value_rows * inverse, axis=(0, 1))
    inner = jnp.mean(scaled * value_rows, axis=-1, keepdims=True)
    return (inverse * scaled - value_rows * inverse * inverse * inverse * inner, gain_part)


def gain_block(first, second, width, leading=()):
    pad_cols = width - first.shape[-1] - second.shape[-1]
    row = jnp.concatenate(
        [first, second, jnp.zeros(leading + (pad_cols,), first.dtype)], axis=-1
    )
    row = row[..., None, :]
    pads = [(0, 0)] * len(leading) + [(0, GAIN_ROWS - 1), (0, 0)]
    return jnp.pad(row, pads)


def to_gathered(rows, block):
    lead = rows.shape[:-1]
    return jnp.swapaxes(rows.reshape(lead + (2, -1, block)), -3, -2).reshape(rows.shape)


def from_gathered(rows, block):
    lead = rows.shape[:-1]
    return jnp.swapaxes(rows.reshape(lead + (-1, 2, block)), -3, -2).reshape(rows.shape)


def zh_pair(mine, other):
    first = lax.axis_index("zh") == 0
    return jnp.stack([jnp.where(first, mine, other), jnp.where(first, other, mine)])


def fsdp_gather(pack):
    other = lax.ppermute(pack, ("zh", "zl"), Z_CROSS)
    both = lax.all_gather(zh_pair(pack, other), ("y", "core"), axis=0, tiled=False)
    return both.reshape((-1,) + pack.shape)


def fsdp_reduce_scatter(grads):
    return z_combine(yc_reduce_scatter(grads))


def yc_reduce_scatter(grads):
    n_yc = grads.shape[0] // 2
    by_yc = grads
    block = grads.shape[1:]
    halves = lax.psum_scatter(
        by_yc.reshape((n_yc, 2 * block[0]) + block[1:]), ("y", "core"), scatter_dimension=0, tiled=False
    ).reshape((2,) + block)
    return halves


def z_combine(halves):
    zh = lax.axis_index("zh")
    mine = lax.dynamic_index_in_dim(halves, zh, axis=0, keepdims=False)
    theirs = lax.dynamic_index_in_dim(halves, 1 - zh, axis=0, keepdims=False)
    got = lax.ppermute(theirs, ("zh", "zl"), Z_CROSS)
    return (mine.astype(jnp.float32) + got.astype(jnp.float32)).astype(jnp.bfloat16)


def ctx_allreduce(part, n_ctx):
    total = part
    step = 1
    while step < n_ctx:
        other = lax.ppermute(total, CTX, [(j, j ^ step) for j in range(n_ctx)])
        total = (total.astype(jnp.float32) + other.astype(jnp.float32)).astype(jnp.bfloat16)
        step *= 2
    return total.astype(jnp.float32)


def body(
    tokens,
    first_value,
    query_weight,
    key_weight,
    value_weight,
    out_weight,
    gate_weight,
    up_weight,
    down_weight,
    prenorm_gain,
    midnorm_gain,
    cotangent,
    lengths,
    assignment,
):
    slots, rows, width = tokens.shape
    assert slots == 1
    head_count = H
    head_dim = width // head_count
    score_scale = head_dim ** (-0.5)
    n_fsdp = lax.axis_size(FSDP)
    n_ctx = lax.axis_size(CTX)
    total_len = rows * n_ctx
    w_rows = query_weight.shape[0]
    g_len = prenorm_gain.shape[0]
    ff = gate_weight.shape[1]
    d_rows = down_weight.shape[0]

    slot_count = assignment.shape[0]
    chosen = assignment[:, None] == jnp.arange(slot_count, dtype=jnp.int32)[None, :]
    lengths_all = jnp.sum(jnp.where(chosen, lengths[None, :], 0), axis=1)
    slot_lengths = lax.dynamic_slice_in_dim(lengths_all, lax.axis_index(FSDP) * slots, slots)
    query_places = lax.axis_index(CTX) * rows + jnp.arange(rows, dtype=jnp.int32)
    valid = query_places[None, :] < slot_lengths[:, None]
    cosine, sine = rope_tables(query_places, head_dim // 2)
    cos_rows = cosine[None, :, None, :]
    sin_rows = sine[None, :, None, :]
    valid_wide = valid[:, :, None]

    attn_pack = jnp.concatenate(
        [query_weight, key_weight, value_weight, out_weight,
         gain_block(prenorm_gain, midnorm_gain, width)],
        axis=0,
    )
    attn_all = fsdp_gather(attn_pack)

    def attn_part(i):
        return attn_all[:, i * w_rows:(i + 1) * w_rows, :].reshape(n_fsdp * w_rows, width)

    query_mat, key_mat, value_mat, out_mat = (attn_part(i) for i in range(4))
    prenorm_full = from_gathered(attn_all[:, 4 * w_rows, 0:g_len].reshape(n_fsdp * g_len), g_len)
    midnorm_full = from_gathered(
        attn_all[:, 4 * w_rows, g_len:2 * g_len].reshape(n_fsdp * g_len), g_len
    )

    mlp_pack = jnp.concatenate(
        [gate_weight, up_weight, down_weight.reshape(w_rows, ff)], axis=1
    )
    mlp_all = fsdp_gather(mlp_pack)
    gate_mat = mlp_all[:, :, 0:ff].reshape(n_fsdp * w_rows, ff)
    upper_mat = mlp_all[:, :, ff:2 * ff].reshape(n_fsdp * w_rows, ff)
    down_mat = mlp_all[:, :, 2 * ff:].reshape(n_fsdp, d_rows, width).reshape(n_fsdp * d_rows, width)

    tokens_wide = tokens.astype(jnp.float32)
    first_wide = first_value.astype(jnp.float32)
    normed, inverse = norm_apply(tokens_wide, prenorm_full.astype(jnp.float32))
    normed_low = normed.astype(jnp.bfloat16)
    normed_low_g = to_gathered(normed_low, w_rows)
    query = jnp.dot(normed_low_g, query_mat, preferred_element_type=jnp.float32)
    keyed = jnp.dot(normed_low_g, key_mat, preferred_element_type=jnp.float32)
    own_value = jnp.dot(normed_low_g, value_mat, preferred_element_type=jnp.float32)
    heads_shape = query.shape[:2] + (head_count, head_dim)
    query_rotated_rows = rotate(query.reshape(heads_shape), cos_rows, sin_rows).astype(jnp.bfloat16)
    key_rot = (
        rotate(keyed.reshape(heads_shape), cos_rows, sin_rows)
        .astype(jnp.bfloat16)
        .reshape(query.shape)
    )
    value_mix = (0.5 * own_value + 0.5 * first_wide).astype(jnp.bfloat16)

    kv_own = jnp.concatenate([key_rot, value_mix], axis=-1).reshape(rows, 2 * width)
    kv_all = lax.all_to_all(
        jnp.broadcast_to(kv_own[None], (n_ctx, rows, 2 * width)), CTX, 0, 0, tiled=False
    ).reshape(total_len, 2 * width)
    meta = jnp.stack([lax.axis_index(CTX) * rows, slot_lengths[0]]).astype(jnp.int32)
    query_flat = query_rotated_rows.reshape(rows, width)
    mixed_low = attention_forward(
        meta, query_flat, kv_all, head_dim, score_scale
    ).reshape(slots, rows, width)

    mixed_low_g = to_gathered(mixed_low, w_rows)
    middle = tokens_wide + jnp.dot(mixed_low_g, out_mat, preferred_element_type=jnp.float32)
    normed_two, inverse_two = norm_apply(middle, midnorm_full.astype(jnp.float32))
    normed_two = normed_two.astype(jnp.bfloat16)
    normed_two_g = to_gathered(normed_two, w_rows)
    gate = jnp.dot(normed_two_g, gate_mat, preferred_element_type=jnp.float32)
    upper = jnp.dot(normed_two_g, upper_mat, preferred_element_type=jnp.float32)
    hidden = (jax.nn.silu(gate) * upper).astype(jnp.bfloat16)
    hidden_g = to_gathered(hidden, d_rows)
    branch = jnp.dot(hidden_g, down_mat, preferred_element_type=jnp.float32)
    layer_out = jnp.where(valid_wide, middle + branch, 0.0).astype(jnp.bfloat16)

    cot_wide = jnp.where(valid_wide, cotangent.astype(jnp.float32), 0.0)
    cot_low = cot_wide.astype(jnp.bfloat16)
    down_total = jnp.einsum("srf,sre->fe", hidden_g, cot_low, preferred_element_type=jnp.float32)
    hidden_back = from_gathered(
        jnp.einsum("sre,fe->srf", cot_low, down_mat, preferred_element_type=jnp.float32), d_rows
    )
    sigma = jax.nn.sigmoid(gate)
    gate_back = (hidden_back * upper * sigma * (1.0 + gate * (1.0 - sigma))).astype(jnp.bfloat16)
    upper_back = (hidden_back * gate * sigma).astype(jnp.bfloat16)
    gate_total = jnp.einsum(
        "srd,srf->df", normed_two_g, gate_back, preferred_element_type=jnp.float32
    )
    upper_total = jnp.einsum(
        "srd,srf->df", normed_two_g, upper_back, preferred_element_type=jnp.float32
    )
    normed_two_back = jnp.einsum(
        "srf,df->srd", gate_back, gate_mat, preferred_element_type=jnp.float32
    )
    normed_two_back = normed_two_back + jnp.einsum(
        "srf,df->srd", upper_back, upper_mat, preferred_element_type=jnp.float32
    )
    normed_two_back = from_gathered(normed_two_back, w_rows)
    middle_norm_back, midnorm_total = norm_back(
        middle, inverse_two, midnorm_full.astype(jnp.float32), normed_two_back
    )
    middle_back = cot_wide + middle_norm_back
    middle_low = middle_back.astype(jnp.bfloat16)
    out_total = jnp.einsum("srd,sre->de", mixed_low_g, middle_low, preferred_element_type=jnp.float32)

    mlp_grads = jnp.concatenate(
        [
            gate_total.reshape(n_fsdp, w_rows, ff),
            upper_total.reshape(n_fsdp, w_rows, ff),
            out_total.reshape(n_fsdp, w_rows, width),
        ],
        axis=2,
    ).astype(jnp.bfloat16)
    down_grads = down_total.astype(jnp.bfloat16).reshape(n_fsdp, d_rows, width)
    mlp_grads, down_grads = lax.optimization_barrier((mlp_grads, down_grads))
    mlp_halves = yc_reduce_scatter(mlp_grads)
    down_share = ctx_allreduce(z_combine(yc_reduce_scatter(down_grads)), n_ctx)

    blended_value_gradient = from_gathered(
        jnp.einsum("sre,de->srd", middle_low, out_mat, preferred_element_type=jnp.float32).astype(
            jnp.bfloat16
        ),
        w_rows,
    )
    query_rot_back, kv_back = attention_backward(
        meta, query_flat, kv_all, blended_value_gradient.reshape(rows, width), head_dim, score_scale
    )
    query_rot_back = query_rot_back.reshape(slots, rows, head_count, head_dim)
    query_back = (
        rotate(query_rot_back, cos_rows, -sin_rows).reshape(slots, rows, width).astype(jnp.bfloat16)
    )
    query_total = jnp.einsum(
        "srd,sre->de", normed_low_g, query_back, preferred_element_type=jnp.float32
    )
    query_grads = query_total.astype(jnp.bfloat16).reshape(n_fsdp, w_rows, width)
    query_grads, kv_back = lax.optimization_barrier((query_grads, kv_back))
    query_share = ctx_allreduce(z_combine(yc_reduce_scatter(query_grads)), n_ctx)
    key_value = jnp.sum(
        lax.all_to_all(kv_back.reshape(n_ctx, rows, 2 * width), CTX, 0, 0, tiled=False).astype(
            jnp.float32
        ),
        axis=0,
    )
    key_value = key_value.reshape(rows, width // HEAD_BLOCK, 2, HEAD_BLOCK)
    key_rot_back = key_value[:, :, 0, :].reshape(slots, rows, head_count, head_dim)
    value_mix_back = key_value[:, :, 1, :].reshape(slots, rows, width)
    first_grad = 0.5 * value_mix_back
    key_back = (
        rotate(key_rot_back, cos_rows, -sin_rows).reshape(slots, rows, width).astype(jnp.bfloat16)
    )
    value_back = (0.5 * value_mix_back).astype(jnp.bfloat16)
    key_total = jnp.einsum("srd,sre->de", normed_low_g, key_back, preferred_element_type=jnp.float32)
    value_total = jnp.einsum(
        "srd,sre->de", normed_low_g, value_back, preferred_element_type=jnp.float32
    )
    normed_back = jnp.einsum(
        "sre,de->srd", query_back, query_mat, preferred_element_type=jnp.float32
    )
    normed_back = normed_back + jnp.einsum(
        "sre,de->srd", key_back, key_mat, preferred_element_type=jnp.float32
    )
    normed_back = normed_back + jnp.einsum(
        "sre,de->srd", value_back, value_mat, preferred_element_type=jnp.float32
    )
    normed_back = from_gathered(normed_back, w_rows)
    tokens_norm_back, prenorm_total = norm_back(
        tokens_wide, inverse, prenorm_full.astype(jnp.float32), normed_back
    )
    tokens_grad = middle_back + tokens_norm_back

    attn_grads = jnp.concatenate(
        [
            key_total.reshape(n_fsdp, w_rows, width),
            value_total.reshape(n_fsdp, w_rows, width),
            gain_block(
                to_gathered(prenorm_total, g_len).reshape(n_fsdp, g_len),
                to_gathered(midnorm_total, g_len).reshape(n_fsdp, g_len),
                width,
                leading=(n_fsdp,),
            ),
        ],
        axis=1,
    ).astype(jnp.bfloat16)
    attn_grads, mlp_halves = lax.optimization_barrier((attn_grads, mlp_halves))
    mlp_share = ctx_allreduce(z_combine(mlp_halves), n_ctx)
    attn_share = fsdp_reduce_scatter(attn_grads)
    attn_share = ctx_allreduce(attn_share, n_ctx)

    def attn_grad(i):
        return attn_share[i * w_rows:(i + 1) * w_rows]

    query_grad = query_share
    key_grad, value_grad = (attn_grad(i) for i in range(2))
    prenorm_grad = attn_share[2 * w_rows, 0:g_len]
    midnorm_grad = attn_share[2 * w_rows, g_len:2 * g_len]
    gate_grad = mlp_share[:, 0:ff]
    up_grad = mlp_share[:, ff:2 * ff]
    down_grad = down_share
    out_grad = mlp_share[:, 2 * ff:]
    return (
        layer_out,
        tokens_grad,
        first_grad,
        query_grad,
        key_grad,
        value_grad,
        out_grad,
        gate_grad,
        up_grad,
        down_grad,
        prenorm_grad,
        midnorm_grad,
    )


def solution(mesh):
    zh = 2
    zl = 2
    n_f, n_c = mesh.devices.shape
    fine = jax.sharding.Mesh(
        mesh.devices.reshape(zh, n_f // (2 * zh), 2, zl, n_c // zl), FSDP + CTX
    )
    placed = (
        P(FSDP, CTX, None),
        P(FSDP, CTX, None),
        P(FSDP, None),
        P(FSDP, None),
        P(FSDP, None),
        P(FSDP, None),
        P(FSDP, None),
        P(FSDP, None),
        P(FSDP, None),
        P(FSDP),
        P(FSDP),
        P(FSDP, CTX, None),
        P(),
        P(),
    )
    return jax.shard_map(
        body,
        mesh=fine,
        in_specs=placed,
        out_specs=(
            P(FSDP, CTX, None),
            P(FSDP, CTX, None),
            P(FSDP, CTX, None),
            P(FSDP, None),
            P(FSDP, None),
            P(FSDP, None),
            P(FSDP, None),
            P(FSDP, None),
            P(FSDP, None),
            P(FSDP, None),
            P(FSDP),
            P(FSDP),
        ),
        check_vma=False,
    )
```

```python
import functools
import math

import jax
import jax.numpy as jnp
from jax import lax
from jax.experimental import pallas as pl
from jax.experimental.pallas import tpu as pltpu
from jax.sharding import PartitionSpec as P

H = 16


EPS = 1e-06
MASKED = -1e30
GAIN_ROWS = 16
FSDP = ("zh", "y", "core")
CTX = ("zl", "x")
Z_CROSS = [(0, 3), (3, 0), (1, 2), (2, 1)]


HEAD_BLOCK = 128
NT_DIMS = (((1,), (1,)), ((), ()))
TN_DIMS = (((0,), (0,)), ((), ()))


def attention_shares(query, keys, first_row, slot_len, scale):
    scores = lax.dot_general(query, keys, NT_DIMS, preferred_element_type=jnp.float32) * scale
    shape = scores.shape
    query_pos = first_row + lax.broadcasted_iota(jnp.int32, shape, 0)
    key_pos = lax.broadcasted_iota(jnp.int32, shape, 1)
    allowed = (key_pos <= query_pos) & (key_pos < slot_len)
    scores = jnp.where(allowed, scores, MASKED)
    peak = jnp.max(scores, axis=-1, keepdims=True)
    raised = jnp.exp(scores - peak)
    denominator = jnp.sum(raised, axis=-1, keepdims=True)
    return raised / denominator


def attn_fwd_kernel(head_dim, scale, meta_ref, q_ref, k_ref, v_ref, o_ref):
    first_row = meta_ref[0]
    slot_len = meta_ref[1]
    for j in range(q_ref.shape[1] // head_dim):
        cols = slice(j * head_dim, (j + 1) * head_dim)
        shares = attention_shares(q_ref[:, cols], k_ref[:, cols], first_row, slot_len, scale)
        mixed = jnp.dot(
            shares.astype(jnp.bfloat16), v_ref[:, cols], preferred_element_type=jnp.float32
        )
        o_ref[:, cols] = mixed.astype(o_ref.dtype)


def attn_bwd_kernel(head_dim, scale, meta_ref, q_ref, k_ref, v_ref, do_ref, dq_ref, dkv_ref):
    first_row = meta_ref[0]
    slot_len = meta_ref[1]
    for j in range(q_ref.shape[1] // head_dim):
        cols = slice(j * head_dim, (j + 1) * head_dim)
        query = q_ref[:, cols]
        keys = k_ref[:, cols]
        back = do_ref[:, cols]
        shares = attention_shares(query, keys, first_row, slot_len, scale)
        prob_back = lax.dot_general(back, v_ref[:, cols], NT_DIMS, preferred_element_type=jnp.float32)
        inner = jnp.sum(shares * prob_back, axis=-1, keepdims=True)
        score_back = (shares * (prob_back - inner)).astype(jnp.bfloat16)
        dq_ref[:, cols] = (
            jnp.dot(score_back, keys, preferred_element_type=jnp.float32) * scale
        )
        dkv_ref[:, cols] = (
            lax.dot_general(score_back, query, TN_DIMS, preferred_element_type=jnp.float32) * scale
        ).astype(dkv_ref.dtype)
        half = q_ref.shape[1]
        dkv_ref[:, half + j * head_dim:half + (j + 1) * head_dim] = lax.dot_general(
            shares.astype(jnp.bfloat16), back, TN_DIMS, preferred_element_type=jnp.float32
        ).astype(dkv_ref.dtype)


def attention_forward(meta, query_rows, kv_rows, head_dim, scale):
    rows, width = query_rows.shape
    keys = kv_rows.shape[0]
    blocks = width // HEAD_BLOCK
    return pl.pallas_call(
        functools.partial(attn_fwd_kernel, head_dim, scale),
        out_shape=jax.ShapeDtypeStruct((rows, width), jnp.bfloat16),
        grid_spec=pltpu.PrefetchScalarGridSpec(
            num_scalar_prefetch=1,
            grid=(blocks,),
            in_specs=[
                pl.BlockSpec((rows, HEAD_BLOCK), lambda h, m: (0, h)),
                pl.BlockSpec((keys, HEAD_BLOCK), lambda h, m: (0, h)),
                pl.BlockSpec((keys, HEAD_BLOCK), lambda h, m: (0, h + blocks)),
            ],
            out_specs=pl.BlockSpec((rows, HEAD_BLOCK), lambda h, m: (0, h)),
        ),
        compiler_params=pltpu.CompilerParams(
            dimension_semantics=("arbitrary",), vmem_limit_bytes=48 * 1024 * 1024
        ),
        cost_estimate=pl.CostEstimate(
            flops=4 * rows * keys * width,
            transcendentals=rows * keys * (width // head_dim),
            bytes_accessed=2 * (2 * rows * width + 2 * keys * width),
        ),
    )(meta, query_rows, kv_rows, kv_rows)


def attention_backward(meta, query_rows, kv_rows, back_rows, head_dim, scale):
    rows, width = query_rows.shape
    keys = kv_rows.shape[0]
    blocks = width // HEAD_BLOCK
    return pl.pallas_call(
        functools.partial(attn_bwd_kernel, head_dim, scale),
        out_shape=(
            jax.ShapeDtypeStruct((rows, width), jnp.float32),
            jax.ShapeDtypeStruct((keys, 2 * width), jnp.bfloat16),
        ),
        grid_spec=pltpu.PrefetchScalarGridSpec(
            num_scalar_prefetch=1,
            grid=(blocks,),
            in_specs=[
                pl.BlockSpec((rows, HEAD_BLOCK), lambda h, m: (0, h)),
                pl.BlockSpec((keys, HEAD_BLOCK), lambda h, m: (0, h)),
                pl.BlockSpec((keys, HEAD_BLOCK), lambda h, m: (0, h + blocks)),
                pl.BlockSpec((rows, HEAD_BLOCK), lambda h, m: (0, h)),
            ],
            out_specs=[
                pl.BlockSpec((rows, HEAD_BLOCK), lambda h, m: (0, h)),
                pl.BlockSpec((keys, 2 * HEAD_BLOCK), lambda h, m: (0, h)),
            ],
        ),
        compiler_params=pltpu.CompilerParams(
            dimension_semantics=("arbitrary",), vmem_limit_bytes=48 * 1024 * 1024
        ),
        cost_estimate=pl.CostEstimate(
            flops=10 * rows * keys * width,
            transcendentals=rows * keys * (width // head_dim),
            bytes_accessed=2 * (3 * rows * width + 4 * keys * width) + 4 * rows * width,
        ),
    )(meta, query_rows, kv_rows, kv_rows, back_rows)


def rope_tables(positions, half):
    freq = jnp.exp(
        jnp.arange(half, dtype=jnp.int32).astype(jnp.float32) * (-math.log(10000.0) / half)
    )
    angle = positions.astype(jnp.float32)[:, None] * freq[None, :]
    return (jnp.cos(angle), jnp.sin(angle))


def rotate(value_rows, cosine, sine):
    half = value_rows.shape[-1] // 2
    first = value_rows[..., :half]
    second = value_rows[..., half:]
    return jnp.concatenate(
        [first * cosine - second * sine, second * cosine + first * sine], axis=-1
    )


def norm_apply(value_rows, gain):
    inverse = lax.rsqrt(jnp.mean(value_rows * value_rows, axis=-1, keepdims=True) + EPS)
    return (value_rows * inverse * gain, inverse)


def norm_back(value_rows, inverse, gain, upstream):
    scaled = upstream * gain
    gain_part = jnp.sum(upstream * value_rows * inverse, axis=(0, 1))
    inner = jnp.mean(scaled * value_rows, axis=-1, keepdims=True)
    return (inverse * scaled - value_rows * inverse * inverse * inverse * inner, gain_part)


def gain_block(first, second, width, leading=()):
    pad_cols = width - first.shape[-1] - second.shape[-1]
    row = jnp.concatenate(
        [first, second, jnp.zeros(leading + (pad_cols,), first.dtype)], axis=-1
    )
    row = row[..., None, :]
    pads = [(0, 0)] * len(leading) + [(0, GAIN_ROWS - 1), (0, 0)]
    return jnp.pad(row, pads)


def to_gathered(rows, block):
    lead = rows.shape[:-1]
    return jnp.swapaxes(rows.reshape(lead + (2, -1, block)), -3, -2).reshape(rows.shape)


def from_gathered(rows, block):
    lead = rows.shape[:-1]
    return jnp.swapaxes(rows.reshape(lead + (-1, 2, block)), -3, -2).reshape(rows.shape)


def zh_pair(mine, other):
    first = lax.axis_index("zh") == 0
    return jnp.stack([jnp.where(first, mine, other), jnp.where(first, other, mine)])


def fsdp_gather(pack):
    return yc_gather(z_exchange(pack))


def z_exchange(pack):
    return zh_pair(pack, lax.ppermute(pack, ("zh", "zl"), Z_CROSS))


def yc_gather(pair):
    both = lax.all_gather(pair, ("y", "core"), axis=0, tiled=False)
    return both.reshape((-1,) + pair.shape[1:])


def fsdp_reduce_scatter(grads):
    return z_combine(yc_reduce_scatter(grads))


def yc_reduce_scatter(grads):
    n_yc = grads.shape[0] // 2
    by_yc = grads
    block = grads.shape[1:]
    halves = lax.psum_scatter(
        by_yc.reshape((n_yc, 2 * block[0]) + block[1:]), ("y", "core"), scatter_dimension=0, tiled=False
    ).reshape((2,) + block)
    return halves


def z_combine(halves):
    zh = lax.axis_index("zh")
    mine = lax.dynamic_index_in_dim(halves, zh, axis=0, keepdims=False)
    theirs = lax.dynamic_index_in_dim(halves, 1 - zh, axis=0, keepdims=False)
    got = lax.ppermute(theirs, ("zh", "zl"), Z_CROSS)
    return (mine.astype(jnp.float32) + got.astype(jnp.float32)).astype(jnp.bfloat16)


def ctx_allreduce(part, n_ctx):
    total = part
    step = 1
    while step < n_ctx:
        other = lax.ppermute(total, CTX, [(j, j ^ step) for j in range(n_ctx)])
        total = (total.astype(jnp.float32) + other.astype(jnp.float32)).astype(jnp.bfloat16)
        step *= 2
    return total.astype(jnp.float32)


def body(
    tokens,
    first_value,
    query_weight,
    key_weight,
    value_weight,
    out_weight,
    gate_weight,
    up_weight,
    down_weight,
    prenorm_gain,
    midnorm_gain,
    cotangent,
    lengths,
    assignment,
):
    slots, rows, width = tokens.shape
    assert slots == 1
    head_count = H
    head_dim = width // head_count
    score_scale = head_dim ** (-0.5)
    n_fsdp = lax.axis_size(FSDP)
    n_ctx = lax.axis_size(CTX)
    total_len = rows * n_ctx
    w_rows = query_weight.shape[0]
    g_len = prenorm_gain.shape[0]
    ff = gate_weight.shape[1]
    d_rows = down_weight.shape[0]

    slot_count = assignment.shape[0]
    chosen = assignment[:, None] == jnp.arange(slot_count, dtype=jnp.int32)[None, :]
    lengths_all = jnp.sum(jnp.where(chosen, lengths[None, :], 0), axis=1)
    slot_lengths = lax.dynamic_slice_in_dim(lengths_all, lax.axis_index(FSDP) * slots, slots)
    query_places = lax.axis_index(CTX) * rows + jnp.arange(rows, dtype=jnp.int32)
    valid = query_places[None, :] < slot_lengths[:, None]
    cosine, sine = rope_tables(query_places, head_dim // 2)
    cos_rows = cosine[None, :, None, :]
    sin_rows = sine[None, :, None, :]
    valid_wide = valid[:, :, None]

    kv_pair = z_exchange(
        jnp.concatenate(
            [key_weight, value_weight, gain_block(prenorm_gain, midnorm_gain, width)], axis=0
        )
    )
    rest_pair = z_exchange(
        jnp.concatenate(
            [
                gate_weight,
                up_weight,
                down_weight.reshape(w_rows, ff),
                query_weight,
                out_weight,
            ],
            axis=1,
        )
    )
    kv_wall = yc_gather(kv_pair)
    rest_pair, kv_wall = lax.optimization_barrier((rest_pair, kv_wall))
    rest_wall = yc_gather(rest_pair)

    key_mat = kv_wall[:, 0:w_rows, :].reshape(n_fsdp * w_rows, width)
    value_mat = kv_wall[:, w_rows:2 * w_rows, :].reshape(n_fsdp * w_rows, width)
    prenorm_full = from_gathered(kv_wall[:, 2 * w_rows, 0:g_len].reshape(n_fsdp * g_len), g_len)
    midnorm_full = from_gathered(
        kv_wall[:, 2 * w_rows, g_len:2 * g_len].reshape(n_fsdp * g_len), g_len
    )
    gate_mat = rest_wall[:, :, 0:ff].reshape(n_fsdp * w_rows, ff)
    upper_mat = rest_wall[:, :, ff:2 * ff].reshape(n_fsdp * w_rows, ff)
    down_mat = (
        rest_wall[:, :, 2 * ff:3 * ff].reshape(n_fsdp, d_rows, width).reshape(n_fsdp * d_rows, width)
    )
    query_mat = rest_wall[:, :, 3 * ff:3 * ff + width].reshape(n_fsdp * w_rows, width)
    out_mat = rest_wall[:, :, 3 * ff + width:].reshape(n_fsdp * w_rows, width)

    tokens_wide = tokens.astype(jnp.float32)
    first_wide = first_value.astype(jnp.float32)
    normed, inverse = norm_apply(tokens_wide, prenorm_full.astype(jnp.float32))
    normed_low = normed.astype(jnp.bfloat16)
    normed_low_g = to_gathered(normed_low, w_rows)
    keyed = jnp.dot(normed_low_g, key_mat, preferred_element_type=jnp.float32)
    own_value = jnp.dot(normed_low_g, value_mat, preferred_element_type=jnp.float32)
    heads_shape = keyed.shape[:2] + (head_count, head_dim)
    key_rot = (
        rotate(keyed.reshape(heads_shape), cos_rows, sin_rows)
        .astype(jnp.bfloat16)
        .reshape(keyed.shape)
    )
    value_mix = (0.5 * own_value + 0.5 * first_wide).astype(jnp.bfloat16)

    kv_own = jnp.concatenate([key_rot, value_mix], axis=-1).reshape(rows, 2 * width)
    kv_all = lax.all_to_all(
        jnp.broadcast_to(kv_own[None], (n_ctx, rows, 2 * width)), CTX, 0, 0, tiled=False
    ).reshape(total_len, 2 * width)
    query_in, kv_all = lax.optimization_barrier((normed_low_g, kv_all))
    query = jnp.dot(query_in, query_mat, preferred_element_type=jnp.float32)
    query_rotated_rows = rotate(query.reshape(heads_shape), cos_rows, sin_rows).astype(jnp.bfloat16)
    meta = jnp.stack([lax.axis_index(CTX) * rows, slot_lengths[0]]).astype(jnp.int32)
    query_flat = query_rotated_rows.reshape(rows, width)
    mixed_low = attention_forward(
        meta, query_flat, kv_all, head_dim, score_scale
    ).reshape(slots, rows, width)

    mixed_low_g = to_gathered(mixed_low, w_rows)
    middle = tokens_wide + jnp.dot(mixed_low_g, out_mat, preferred_element_type=jnp.float32)
    normed_two, inverse_two = norm_apply(middle, midnorm_full.astype(jnp.float32))
    normed_two = normed_two.astype(jnp.bfloat16)
    normed_two_g = to_gathered(normed_two, w_rows)
    gate = jnp.dot(normed_two_g, gate_mat, preferred_element_type=jnp.float32)
    upper = jnp.dot(normed_two_g, upper_mat, preferred_element_type=jnp.float32)
    hidden = (jax.nn.silu(gate) * upper).astype(jnp.bfloat16)
    hidden_g = to_gathered(hidden, d_rows)
    branch = jnp.dot(hidden_g, down_mat, preferred_element_type=jnp.float32)
    layer_out = jnp.where(valid_wide, middle + branch, 0.0).astype(jnp.bfloat16)

    cot_wide = jnp.where(valid_wide, cotangent.astype(jnp.float32), 0.0)
    cot_low = cot_wide.astype(jnp.bfloat16)
    down_total = jnp.einsum("srf,sre->fe", hidden_g, cot_low, preferred_element_type=jnp.float32)
    hidden_back = from_gathered(
        jnp.einsum("sre,fe->srf", cot_low, down_mat, preferred_element_type=jnp.float32), d_rows
    )
    sigma = jax.nn.sigmoid(gate)
    gate_back = (hidden_back * upper * sigma * (1.0 + gate * (1.0 - sigma))).astype(jnp.bfloat16)
    upper_back = (hidden_back * gate * sigma).astype(jnp.bfloat16)
    gate_total = jnp.einsum(
        "srd,srf->df", normed_two_g, gate_back, preferred_element_type=jnp.float32
    )
    upper_total = jnp.einsum(
        "srd,srf->df", normed_two_g, upper_back, preferred_element_type=jnp.float32
    )
    normed_two_back = jnp.einsum(
        "srf,df->srd", gate_back, gate_mat, preferred_element_type=jnp.float32
    )
    normed_two_back = normed_two_back + jnp.einsum(
        "srf,df->srd", upper_back, upper_mat, preferred_element_type=jnp.float32
    )
    normed_two_back = from_gathered(normed_two_back, w_rows)
    middle_norm_back, midnorm_total = norm_back(
        middle, inverse_two, midnorm_full.astype(jnp.float32), normed_two_back
    )
    middle_back = cot_wide + middle_norm_back
    middle_low = middle_back.astype(jnp.bfloat16)
    out_total = jnp.einsum("srd,sre->de", mixed_low_g, middle_low, preferred_element_type=jnp.float32)

    down_share = ctx_allreduce(
        z_combine(yc_reduce_scatter(down_total.astype(jnp.bfloat16).reshape(n_fsdp, d_rows, width))),
        n_ctx,
    )
    mlp_grads = jnp.concatenate(
        [
            gate_total.reshape(n_fsdp, w_rows, ff),
            upper_total.reshape(n_fsdp, w_rows, ff),
            out_total.reshape(n_fsdp, w_rows, width),
        ],
        axis=2,
    ).astype(jnp.bfloat16)
    mlp_halves = yc_reduce_scatter(mlp_grads)

    blended_value_gradient = from_gathered(
        jnp.einsum("sre,de->srd", middle_low, out_mat, preferred_element_type=jnp.float32).astype(
            jnp.bfloat16
        ),
        w_rows,
    )
    query_rot_back, kv_back = attention_backward(
        meta, query_flat, kv_all, blended_value_gradient.reshape(rows, width), head_dim, score_scale
    )
    query_rot_back = query_rot_back.reshape(slots, rows, head_count, head_dim)
    key_value = jnp.sum(
        lax.all_to_all(kv_back.reshape(n_ctx, rows, 2 * width), CTX, 0, 0, tiled=False).astype(
            jnp.float32
        ),
        axis=0,
    )
    key_value = key_value.reshape(rows, width // HEAD_BLOCK, 2, HEAD_BLOCK)
    key_rot_back = key_value[:, :, 0, :].reshape(slots, rows, head_count, head_dim)
    value_mix_back = key_value[:, :, 1, :].reshape(slots, rows, width)
    first_grad = 0.5 * value_mix_back
    query_back = (
        rotate(query_rot_back, cos_rows, -sin_rows).reshape(slots, rows, width).astype(jnp.bfloat16)
    )
    key_back = (
        rotate(key_rot_back, cos_rows, -sin_rows).reshape(slots, rows, width).astype(jnp.bfloat16)
    )
    value_back = (0.5 * value_mix_back).astype(jnp.bfloat16)
    query_total = jnp.einsum(
        "srd,sre->de", normed_low_g, query_back, preferred_element_type=jnp.float32
    )
    key_total = jnp.einsum("srd,sre->de", normed_low_g, key_back, preferred_element_type=jnp.float32)
    value_total = jnp.einsum(
        "srd,sre->de", normed_low_g, value_back, preferred_element_type=jnp.float32
    )
    normed_back = jnp.einsum(
        "sre,de->srd", query_back, query_mat, preferred_element_type=jnp.float32
    )
    normed_back = normed_back + jnp.einsum(
        "sre,de->srd", key_back, key_mat, preferred_element_type=jnp.float32
    )
    normed_back = normed_back + jnp.einsum(
        "sre,de->srd", value_back, value_mat, preferred_element_type=jnp.float32
    )
    normed_back = from_gathered(normed_back, w_rows)
    tokens_norm_back, prenorm_total = norm_back(
        tokens_wide, inverse, prenorm_full.astype(jnp.float32), normed_back
    )
    tokens_grad = middle_back + tokens_norm_back

    attn_grads = jnp.concatenate(
        [
            query_total.reshape(n_fsdp, w_rows, width),
            key_total.reshape(n_fsdp, w_rows, width),
            value_total.reshape(n_fsdp, w_rows, width),
            gain_block(
                to_gathered(prenorm_total, g_len).reshape(n_fsdp, g_len),
                to_gathered(midnorm_total, g_len).reshape(n_fsdp, g_len),
                width,
                leading=(n_fsdp,),
            ),
        ],
        axis=1,
    ).astype(jnp.bfloat16)
    attn_grads, mlp_halves = lax.optimization_barrier((attn_grads, mlp_halves))
    mlp_share = ctx_allreduce(z_combine(mlp_halves), n_ctx)
    attn_share = fsdp_reduce_scatter(attn_grads)
    attn_share = ctx_allreduce(attn_share, n_ctx)

    def attn_grad(i):
        return attn_share[i * w_rows:(i + 1) * w_rows]

    query_grad, key_grad, value_grad = (attn_grad(i) for i in range(3))
    prenorm_grad = attn_share[3 * w_rows, 0:g_len]
    midnorm_grad = attn_share[3 * w_rows, g_len:2 * g_len]
    gate_grad = mlp_share[:, 0:ff]
    up_grad = mlp_share[:, ff:2 * ff]
    down_grad = down_share
    out_grad = mlp_share[:, 2 * ff:]
    return (
        layer_out,
        tokens_grad,
        first_grad,
        query_grad,
        key_grad,
        value_grad,
        out_grad,
        gate_grad,
        up_grad,
        down_grad,
        prenorm_grad,
        midnorm_grad,
    )


def solution(mesh):
    zh = 2
    zl = 2
    n_f, n_c = mesh.devices.shape
    fine = jax.sharding.Mesh(
        mesh.devices.reshape(zh, n_f // (2 * zh), 2, zl, n_c // zl), FSDP + CTX
    )
    placed = (
        P(FSDP, CTX, None),
        P(FSDP, CTX, None),
        P(FSDP, None),
        P(FSDP, None),
        P(FSDP, None),
        P(FSDP, None),
        P(FSDP, None),
        P(FSDP, None),
        P(FSDP, None),
        P(FSDP),
        P(FSDP),
        P(FSDP, CTX, None),
        P(),
        P(),
    )
    return jax.shard_map(
        body,
        mesh=fine,
        in_specs=placed,
        out_specs=(
            P(FSDP, CTX, None),
            P(FSDP, CTX, None),
            P(FSDP, CTX, None),
            P(FSDP, None),
            P(FSDP, None),
            P(FSDP, None),
            P(FSDP, None),
            P(FSDP, None),
            P(FSDP, None),
            P(FSDP, None),
            P(FSDP),
            P(FSDP),
        ),
        check_vma=False,
    )
```

```python
import functools
import math

import jax
import jax.numpy as jnp
from jax import lax
from jax.experimental import pallas as pl
from jax.experimental.pallas import tpu as pltpu
from jax.sharding import PartitionSpec as P

H = 16


EPS = 1e-06
MASKED = -1e30
GAIN_ROWS = 16
FSDP = ("zh", "y", "core")
CTX = ("zl", "x")
Z_CROSS = [(0, 3), (3, 0), (1, 2), (2, 1)]


HEAD_BLOCK = 128
NT_DIMS = (((1,), (1,)), ((), ()))
TN_DIMS = (((0,), (0,)), ((), ()))


def attention_shares(query, keys, first_row, slot_len, scale):
    scores = lax.dot_general(query, keys, NT_DIMS, preferred_element_type=jnp.float32) * scale
    shape = scores.shape
    query_pos = first_row + lax.broadcasted_iota(jnp.int32, shape, 0)
    key_pos = lax.broadcasted_iota(jnp.int32, shape, 1)
    allowed = (key_pos <= query_pos) & (key_pos < slot_len)
    scores = jnp.where(allowed, scores, MASKED)
    peak = jnp.max(scores, axis=-1, keepdims=True)
    raised = jnp.exp(scores - peak)
    denominator = jnp.sum(raised, axis=-1, keepdims=True)
    return raised / denominator


def attn_fwd_kernel(head_dim, scale, meta_ref, q_ref, k_ref, v_ref, o_ref):
    first_row = meta_ref[0]
    slot_len = meta_ref[1]
    for j in range(q_ref.shape[1] // head_dim):
        cols = slice(j * head_dim, (j + 1) * head_dim)
        shares = attention_shares(q_ref[:, cols], k_ref[:, cols], first_row, slot_len, scale)
        mixed = jnp.dot(
            shares.astype(jnp.bfloat16), v_ref[:, cols], preferred_element_type=jnp.float32
        )
        o_ref[:, cols] = mixed.astype(o_ref.dtype)


def attn_bwd_kernel(head_dim, scale, meta_ref, q_ref, k_ref, v_ref, do_ref, dq_ref, dkv_ref):
    first_row = meta_ref[0]
    slot_len = meta_ref[1]
    for j in range(q_ref.shape[1] // head_dim):
        cols = slice(j * head_dim, (j + 1) * head_dim)
        query = q_ref[:, cols]
        keys = k_ref[:, cols]
        back = do_ref[:, cols]
        shares = attention_shares(query, keys, first_row, slot_len, scale)
        prob_back = lax.dot_general(back, v_ref[:, cols], NT_DIMS, preferred_element_type=jnp.float32)
        inner = jnp.sum(shares * prob_back, axis=-1, keepdims=True)
        score_back = (shares * (prob_back - inner)).astype(jnp.bfloat16)
        dq_ref[:, cols] = (
            jnp.dot(score_back, keys, preferred_element_type=jnp.float32) * scale
        )
        dkv_ref[:, cols] = (
            lax.dot_general(score_back, query, TN_DIMS, preferred_element_type=jnp.float32) * scale
        ).astype(dkv_ref.dtype)
        half = q_ref.shape[1]
        dkv_ref[:, half + j * head_dim:half + (j + 1) * head_dim] = lax.dot_general(
            shares.astype(jnp.bfloat16), back, TN_DIMS, preferred_element_type=jnp.float32
        ).astype(dkv_ref.dtype)


def attention_forward(meta, query_rows, kv_rows, head_dim, scale):
    rows, width = query_rows.shape
    keys = kv_rows.shape[0]
    blocks = width // HEAD_BLOCK
    return pl.pallas_call(
        functools.partial(attn_fwd_kernel, head_dim, scale),
        out_shape=jax.ShapeDtypeStruct((rows, width), jnp.bfloat16),
        grid_spec=pltpu.PrefetchScalarGridSpec(
            num_scalar_prefetch=1,
            grid=(blocks,),
            in_specs=[
                pl.BlockSpec((rows, HEAD_BLOCK), lambda h, m: (0, h)),
                pl.BlockSpec((keys, HEAD_BLOCK), lambda h, m: (0, h)),
                pl.BlockSpec((keys, HEAD_BLOCK), lambda h, m: (0, h + blocks)),
            ],
            out_specs=pl.BlockSpec((rows, HEAD_BLOCK), lambda h, m: (0, h)),
        ),
        compiler_params=pltpu.CompilerParams(
            dimension_semantics=("arbitrary",), vmem_limit_bytes=48 * 1024 * 1024
        ),
        cost_estimate=pl.CostEstimate(
            flops=4 * rows * keys * width,
            transcendentals=rows * keys * (width // head_dim),
            bytes_accessed=2 * (2 * rows * width + 2 * keys * width),
        ),
    )(meta, query_rows, kv_rows, kv_rows)


def attention_backward(meta, query_rows, kv_rows, back_rows, head_dim, scale):
    rows, width = query_rows.shape
    keys = kv_rows.shape[0]
    blocks = width // HEAD_BLOCK
    return pl.pallas_call(
        functools.partial(attn_bwd_kernel, head_dim, scale),
        out_shape=(
            jax.ShapeDtypeStruct((rows, width), jnp.float32),
            jax.ShapeDtypeStruct((keys, 2 * width), jnp.bfloat16),
        ),
        grid_spec=pltpu.PrefetchScalarGridSpec(
            num_scalar_prefetch=1,
            grid=(blocks,),
            in_specs=[
                pl.BlockSpec((rows, HEAD_BLOCK), lambda h, m: (0, h)),
                pl.BlockSpec((keys, HEAD_BLOCK), lambda h, m: (0, h)),
                pl.BlockSpec((keys, HEAD_BLOCK), lambda h, m: (0, h + blocks)),
                pl.BlockSpec((rows, HEAD_BLOCK), lambda h, m: (0, h)),
            ],
            out_specs=[
                pl.BlockSpec((rows, HEAD_BLOCK), lambda h, m: (0, h)),
                pl.BlockSpec((keys, 2 * HEAD_BLOCK), lambda h, m: (0, h)),
            ],
        ),
        compiler_params=pltpu.CompilerParams(
            dimension_semantics=("arbitrary",), vmem_limit_bytes=48 * 1024 * 1024
        ),
        cost_estimate=pl.CostEstimate(
            flops=10 * rows * keys * width,
            transcendentals=rows * keys * (width // head_dim),
            bytes_accessed=2 * (3 * rows * width + 4 * keys * width) + 4 * rows * width,
        ),
    )(meta, query_rows, kv_rows, kv_rows, back_rows)


def rope_tables(positions, half):
    freq = jnp.exp(
        jnp.arange(half, dtype=jnp.int32).astype(jnp.float32) * (-math.log(10000.0) / half)
    )
    angle = positions.astype(jnp.float32)[:, None] * freq[None, :]
    return (jnp.cos(angle), jnp.sin(angle))


def rotate(value_rows, cosine, sine):
    half = value_rows.shape[-1] // 2
    first = value_rows[..., :half]
    second = value_rows[..., half:]
    return jnp.concatenate(
        [first * cosine - second * sine, second * cosine + first * sine], axis=-1
    )


def norm_apply(value_rows, gain):
    inverse = lax.rsqrt(jnp.mean(value_rows * value_rows, axis=-1, keepdims=True) + EPS)
    return (value_rows * inverse * gain, inverse)


def norm_back(value_rows, inverse, gain, upstream):
    scaled = upstream * gain
    gain_part = jnp.sum(upstream * value_rows * inverse, axis=(0, 1))
    inner = jnp.mean(scaled * value_rows, axis=-1, keepdims=True)
    return (inverse * scaled - value_rows * inverse * inverse * inverse * inner, gain_part)


def gain_block(first, second, width, leading=()):
    pad_cols = width - first.shape[-1] - second.shape[-1]
    row = jnp.concatenate(
        [first, second, jnp.zeros(leading + (pad_cols,), first.dtype)], axis=-1
    )
    row = row[..., None, :]
    pads = [(0, 0)] * len(leading) + [(0, GAIN_ROWS - 1), (0, 0)]
    return jnp.pad(row, pads)


def to_gathered(rows, block):
    lead = rows.shape[:-1]
    return jnp.swapaxes(rows.reshape(lead + (2, -1, block)), -3, -2).reshape(rows.shape)


def from_gathered(rows, block):
    lead = rows.shape[:-1]
    return jnp.swapaxes(rows.reshape(lead + (-1, 2, block)), -3, -2).reshape(rows.shape)


def zh_pair(mine, other):
    first = lax.axis_index("zh") == 0
    return jnp.stack([jnp.where(first, mine, other), jnp.where(first, other, mine)])


def fsdp_gather(pack):
    return yc_gather(z_exchange(pack))


def z_exchange(pack):
    return zh_pair(pack, lax.ppermute(pack, ("zh", "zl"), Z_CROSS))


def yc_gather(pair):
    both = lax.all_gather(pair, ("y", "core"), axis=0, tiled=False)
    return both.reshape((-1,) + pair.shape[1:])


def fsdp_reduce_scatter(grads):
    return z_combine(yc_reduce_scatter(grads))


def yc_reduce_scatter(grads):
    n_yc = grads.shape[0] // 2
    by_yc = grads
    block = grads.shape[1:]
    halves = lax.psum_scatter(
        by_yc.reshape((n_yc, 2 * block[0]) + block[1:]), ("y", "core"), scatter_dimension=0, tiled=False
    ).reshape((2,) + block)
    return halves


def z_combine(halves):
    zh = lax.axis_index("zh")
    mine = lax.dynamic_index_in_dim(halves, zh, axis=0, keepdims=False)
    theirs = lax.dynamic_index_in_dim(halves, 1 - zh, axis=0, keepdims=False)
    got = lax.ppermute(theirs, ("zh", "zl"), Z_CROSS)
    return (mine.astype(jnp.float32) + got.astype(jnp.float32)).astype(jnp.bfloat16)


def ctx_allreduce(part, n_ctx):
    total = part
    step = 1
    while step < n_ctx:
        other = lax.ppermute(total, CTX, [(j, j ^ step) for j in range(n_ctx)])
        total = (total.astype(jnp.float32) + other.astype(jnp.float32)).astype(jnp.bfloat16)
        step *= 2
    return total.astype(jnp.float32)


def body(
    tokens,
    first_value,
    query_weight,
    key_weight,
    value_weight,
    out_weight,
    gate_weight,
    up_weight,
    down_weight,
    prenorm_gain,
    midnorm_gain,
    cotangent,
    lengths,
    assignment,
):
    slots, rows, width = tokens.shape
    assert slots == 1
    head_count = H
    head_dim = width // head_count
    score_scale = head_dim ** (-0.5)
    n_fsdp = lax.axis_size(FSDP)
    n_ctx = lax.axis_size(CTX)
    total_len = rows * n_ctx
    w_rows = query_weight.shape[0]
    g_len = prenorm_gain.shape[0]
    ff = gate_weight.shape[1]
    d_rows = down_weight.shape[0]

    slot_count = assignment.shape[0]
    chosen = assignment[:, None] == jnp.arange(slot_count, dtype=jnp.int32)[None, :]
    lengths_all = jnp.sum(jnp.where(chosen, lengths[None, :], 0), axis=1)
    slot_lengths = lax.dynamic_slice_in_dim(lengths_all, lax.axis_index(FSDP) * slots, slots)
    query_places = lax.axis_index(CTX) * rows + jnp.arange(rows, dtype=jnp.int32)
    valid = query_places[None, :] < slot_lengths[:, None]
    cosine, sine = rope_tables(query_places, head_dim // 2)
    cos_rows = cosine[None, :, None, :]
    sin_rows = sine[None, :, None, :]
    valid_wide = valid[:, :, None]

    kv_pair = z_exchange(
        jnp.concatenate(
            [key_weight, value_weight, gain_block(prenorm_gain, midnorm_gain, width)], axis=0
        )
    )
    qod_pair = z_exchange(jnp.concatenate([query_weight, out_weight, down_weight], axis=0))
    gate_up_pair = z_exchange(jnp.concatenate([gate_weight, up_weight], axis=1))
    kv_wall = yc_gather(kv_pair)
    qod_pair, gate_up_pair, kv_wall = lax.optimization_barrier((qod_pair, gate_up_pair, kv_wall))
    qod_wall = yc_gather(qod_pair)
    gate_up_mat = yc_gather(gate_up_pair).reshape(n_fsdp * w_rows, 2 * ff)

    key_mat = kv_wall[:, 0:w_rows, :].reshape(n_fsdp * w_rows, width)
    value_mat = kv_wall[:, w_rows:2 * w_rows, :].reshape(n_fsdp * w_rows, width)
    prenorm_full = from_gathered(kv_wall[:, 2 * w_rows, 0:g_len].reshape(n_fsdp * g_len), g_len)
    midnorm_full = from_gathered(
        kv_wall[:, 2 * w_rows, g_len:2 * g_len].reshape(n_fsdp * g_len), g_len
    )
    query_mat = qod_wall[:, 0:w_rows, :].reshape(n_fsdp * w_rows, width)
    out_mat = qod_wall[:, w_rows:2 * w_rows, :].reshape(n_fsdp * w_rows, width)
    down_mat = qod_wall[:, 2 * w_rows:, :].reshape(n_fsdp * d_rows, width)

    tokens_wide = tokens.astype(jnp.float32)
    first_wide = first_value.astype(jnp.float32)
    normed, inverse = norm_apply(tokens_wide, prenorm_full.astype(jnp.float32))
    normed_low = normed.astype(jnp.bfloat16)
    normed_low_g = to_gathered(normed_low, w_rows)
    keyed = jnp.dot(normed_low_g, key_mat, preferred_element_type=jnp.float32)
    own_value = jnp.dot(normed_low_g, value_mat, preferred_element_type=jnp.float32)
    heads_shape = keyed.shape[:2] + (head_count, head_dim)
    key_rot = (
        rotate(keyed.reshape(heads_shape), cos_rows, sin_rows)
        .astype(jnp.bfloat16)
        .reshape(keyed.shape)
    )
    value_mix = (0.5 * own_value + 0.5 * first_wide).astype(jnp.bfloat16)

    kv_own = jnp.concatenate([key_rot, value_mix], axis=-1).reshape(rows, 2 * width)
    kv_all = lax.all_to_all(
        jnp.broadcast_to(kv_own[None], (n_ctx, rows, 2 * width)), CTX, 0, 0, tiled=False
    ).reshape(total_len, 2 * width)
    query_in, kv_all = lax.optimization_barrier((normed_low_g, kv_all))
    query = jnp.dot(query_in, query_mat, preferred_element_type=jnp.float32)
    query_rotated_rows = rotate(query.reshape(heads_shape), cos_rows, sin_rows).astype(jnp.bfloat16)
    meta = jnp.stack([lax.axis_index(CTX) * rows, slot_lengths[0]]).astype(jnp.int32)
    query_flat = query_rotated_rows.reshape(rows, width)
    mixed_low = attention_forward(
        meta, query_flat, kv_all, head_dim, score_scale
    ).reshape(slots, rows, width)

    mixed_low_g = to_gathered(mixed_low, w_rows)
    middle = tokens_wide + jnp.dot(mixed_low_g, out_mat, preferred_element_type=jnp.float32)
    normed_two, inverse_two = norm_apply(middle, midnorm_full.astype(jnp.float32))
    normed_two = normed_two.astype(jnp.bfloat16)
    normed_two_g = to_gathered(normed_two, w_rows)
    gate_up = jnp.dot(normed_two_g, gate_up_mat, preferred_element_type=jnp.float32)
    gate = gate_up[..., :ff]
    upper = gate_up[..., ff:]
    hidden = (jax.nn.silu(gate) * upper).astype(jnp.bfloat16)
    hidden_g = to_gathered(hidden, d_rows)
    branch = jnp.dot(hidden_g, down_mat, preferred_element_type=jnp.float32)
    layer_out = jnp.where(valid_wide, middle + branch, 0.0).astype(jnp.bfloat16)

    cot_wide = jnp.where(valid_wide, cotangent.astype(jnp.float32), 0.0)
    cot_low = cot_wide.astype(jnp.bfloat16)
    down_total = jnp.einsum("srf,sre->fe", hidden_g, cot_low, preferred_element_type=jnp.float32)
    hidden_back = from_gathered(
        jnp.einsum("sre,fe->srf", cot_low, down_mat, preferred_element_type=jnp.float32), d_rows
    )
    sigma = jax.nn.sigmoid(gate)
    gate_back = (hidden_back * upper * sigma * (1.0 + gate * (1.0 - sigma))).astype(jnp.bfloat16)
    upper_back = (hidden_back * gate * sigma).astype(jnp.bfloat16)
    gate_up_back = jnp.concatenate([gate_back, upper_back], axis=-1)
    gate_up_total = jnp.einsum(
        "srd,srf->df", normed_two_g, gate_up_back, preferred_element_type=jnp.float32
    )
    normed_two_back = jnp.einsum(
        "srf,df->srd", gate_up_back, gate_up_mat, preferred_element_type=jnp.float32
    )
    normed_two_back = from_gathered(normed_two_back, w_rows)
    middle_norm_back, midnorm_total = norm_back(
        middle, inverse_two, midnorm_full.astype(jnp.float32), normed_two_back
    )
    middle_back = cot_wide + middle_norm_back
    middle_low = middle_back.astype(jnp.bfloat16)
    out_total = jnp.einsum("srd,sre->de", mixed_low_g, middle_low, preferred_element_type=jnp.float32)

    down_share = ctx_allreduce(
        z_combine(yc_reduce_scatter(down_total.astype(jnp.bfloat16).reshape(n_fsdp, d_rows, width))),
        n_ctx,
    )
    mlp_grads = jnp.concatenate(
        [
            gate_up_total.reshape(n_fsdp, w_rows, 2 * ff),
            out_total.reshape(n_fsdp, w_rows, width),
        ],
        axis=2,
    ).astype(jnp.bfloat16)
    mlp_halves = yc_reduce_scatter(mlp_grads)

    blended_value_gradient = from_gathered(
        jnp.einsum("sre,de->srd", middle_low, out_mat, preferred_element_type=jnp.float32).astype(
            jnp.bfloat16
        ),
        w_rows,
    )
    query_rot_back, kv_back = attention_backward(
        meta, query_flat, kv_all, blended_value_gradient.reshape(rows, width), head_dim, score_scale
    )
    query_rot_back = query_rot_back.reshape(slots, rows, head_count, head_dim)
    key_value = jnp.sum(
        lax.all_to_all(kv_back.reshape(n_ctx, rows, 2 * width), CTX, 0, 0, tiled=False).astype(
            jnp.float32
        ),
        axis=0,
    )
    key_value = key_value.reshape(rows, width // HEAD_BLOCK, 2, HEAD_BLOCK)
    key_rot_back = key_value[:, :, 0, :].reshape(slots, rows, head_count, head_dim)
    value_mix_back = key_value[:, :, 1, :].reshape(slots, rows, width)
    first_grad = 0.5 * value_mix_back
    query_back = (
        rotate(query_rot_back, cos_rows, -sin_rows).reshape(slots, rows, width).astype(jnp.bfloat16)
    )
    key_back = (
        rotate(key_rot_back, cos_rows, -sin_rows).reshape(slots, rows, width).astype(jnp.bfloat16)
    )
    value_back = (0.5 * value_mix_back).astype(jnp.bfloat16)
    query_total = jnp.einsum(
        "srd,sre->de", normed_low_g, query_back, preferred_element_type=jnp.float32
    )
    key_total = jnp.einsum("srd,sre->de", normed_low_g, key_back, preferred_element_type=jnp.float32)
    value_total = jnp.einsum(
        "srd,sre->de", normed_low_g, value_back, preferred_element_type=jnp.float32
    )
    normed_back = jnp.einsum(
        "sre,de->srd", query_back, query_mat, preferred_element_type=jnp.float32
    )
    normed_back = normed_back + jnp.einsum(
        "sre,de->srd", key_back, key_mat, preferred_element_type=jnp.float32
    )
    normed_back = normed_back + jnp.einsum(
        "sre,de->srd", value_back, value_mat, preferred_element_type=jnp.float32
    )
    normed_back = from_gathered(normed_back, w_rows)
    tokens_norm_back, prenorm_total = norm_back(
        tokens_wide, inverse, prenorm_full.astype(jnp.float32), normed_back
    )
    tokens_grad = middle_back + tokens_norm_back

    attn_grads = jnp.concatenate(
        [
            query_total.reshape(n_fsdp, w_rows, width),
            key_total.reshape(n_fsdp, w_rows, width),
            value_total.reshape(n_fsdp, w_rows, width),
            gain_block(
                to_gathered(prenorm_total, g_len).reshape(n_fsdp, g_len),
                to_gathered(midnorm_total, g_len).reshape(n_fsdp, g_len),
                width,
                leading=(n_fsdp,),
            ),
        ],
        axis=1,
    ).astype(jnp.bfloat16)
    attn_grads, mlp_halves = lax.optimization_barrier((attn_grads, mlp_halves))
    mlp_share = ctx_allreduce(z_combine(mlp_halves), n_ctx)
    attn_share = fsdp_reduce_scatter(attn_grads)
    attn_share = ctx_allreduce(attn_share, n_ctx)

    def attn_grad(i):
        return attn_share[i * w_rows:(i + 1) * w_rows]

    query_grad, key_grad, value_grad = (attn_grad(i) for i in range(3))
    prenorm_grad = attn_share[3 * w_rows, 0:g_len]
    midnorm_grad = attn_share[3 * w_rows, g_len:2 * g_len]
    gate_grad = mlp_share[:, 0:ff]
    up_grad = mlp_share[:, ff:2 * ff]
    down_grad = down_share
    out_grad = mlp_share[:, 2 * ff:]
    return (
        layer_out,
        tokens_grad,
        first_grad,
        query_grad,
        key_grad,
        value_grad,
        out_grad,
        gate_grad,
        up_grad,
        down_grad,
        prenorm_grad,
        midnorm_grad,
    )


def solution(mesh):
    zh = 2
    zl = 2
    n_f, n_c = mesh.devices.shape
    fine = jax.sharding.Mesh(
        mesh.devices.reshape(zh, n_f // (2 * zh), 2, zl, n_c // zl), FSDP + CTX
    )
    placed = (
        P(FSDP, CTX, None),
        P(FSDP, CTX, None),
        P(FSDP, None),
        P(FSDP, None),
        P(FSDP, None),
        P(FSDP, None),
        P(FSDP, None),
        P(FSDP, None),
        P(FSDP, None),
        P(FSDP),
        P(FSDP),
        P(FSDP, CTX, None),
        P(),
        P(),
    )
    return jax.shard_map(
        body,
        mesh=fine,
        in_specs=placed,
        out_specs=(
            P(FSDP, CTX, None),
            P(FSDP, CTX, None),
            P(FSDP, CTX, None),
            P(FSDP, None),
            P(FSDP, None),
            P(FSDP, None),
            P(FSDP, None),
            P(FSDP, None),
            P(FSDP, None),
            P(FSDP, None),
            P(FSDP),
            P(FSDP),
        ),
        check_vma=False,
    )
```

```python
import functools
import math

import jax
import jax.numpy as jnp
from jax import lax
from jax.experimental import pallas as pl
from jax.experimental.pallas import tpu as pltpu
from jax.sharding import PartitionSpec as P

H = 16


EPS = 1e-06
MASKED = -1e30
GAIN_ROWS = 16
FSDP = ("zh", "y", "core")
CTX = ("zl", "x")
Z_CROSS = [(0, 3), (3, 0), (1, 2), (2, 1)]


HEAD_BLOCK = 128
NT_DIMS = (((1,), (1,)), ((), ()))
TN_DIMS = (((0,), (0,)), ((), ()))


def attention_shares(query, keys, first_row, slot_len, scale):
    scores = lax.dot_general(query, keys, NT_DIMS, preferred_element_type=jnp.float32) * scale
    shape = scores.shape
    query_pos = first_row + lax.broadcasted_iota(jnp.int32, shape, 0)
    key_pos = lax.broadcasted_iota(jnp.int32, shape, 1)
    allowed = (key_pos <= query_pos) & (key_pos < slot_len)
    scores = jnp.where(allowed, scores, MASKED)
    peak = jnp.max(scores, axis=-1, keepdims=True)
    raised = jnp.exp(scores - peak)
    denominator = jnp.sum(raised, axis=-1, keepdims=True)
    return raised / denominator


def attn_fwd_kernel(head_dim, scale, meta_ref, q_ref, k_ref, v_ref, o_ref):
    first_row = meta_ref[0]
    slot_len = meta_ref[1]
    for j in range(q_ref.shape[1] // head_dim):
        cols = slice(j * head_dim, (j + 1) * head_dim)
        shares = attention_shares(q_ref[:, cols], k_ref[:, cols], first_row, slot_len, scale)
        mixed = jnp.dot(
            shares.astype(jnp.bfloat16), v_ref[:, cols], preferred_element_type=jnp.float32
        )
        o_ref[:, cols] = mixed.astype(o_ref.dtype)


def attn_bwd_kernel(head_dim, scale, meta_ref, q_ref, k_ref, v_ref, do_ref, dq_ref, dkv_ref):
    first_row = meta_ref[0]
    slot_len = meta_ref[1]
    for j in range(q_ref.shape[1] // head_dim):
        cols = slice(j * head_dim, (j + 1) * head_dim)
        query = q_ref[:, cols]
        keys = k_ref[:, cols]
        back = do_ref[:, cols]
        shares = attention_shares(query, keys, first_row, slot_len, scale)
        prob_back = lax.dot_general(back, v_ref[:, cols], NT_DIMS, preferred_element_type=jnp.float32)
        inner = jnp.sum(shares * prob_back, axis=-1, keepdims=True)
        score_back = (shares * (prob_back - inner)).astype(jnp.bfloat16)
        dq_ref[:, cols] = (
            jnp.dot(score_back, keys, preferred_element_type=jnp.float32) * scale
        )
        dkv_ref[:, cols] = (
            lax.dot_general(score_back, query, TN_DIMS, preferred_element_type=jnp.float32) * scale
        ).astype(dkv_ref.dtype)
        half = q_ref.shape[1]
        dkv_ref[:, half + j * head_dim:half + (j + 1) * head_dim] = lax.dot_general(
            shares.astype(jnp.bfloat16), back, TN_DIMS, preferred_element_type=jnp.float32
        ).astype(dkv_ref.dtype)


def attention_forward(meta, query_rows, kv_rows, head_dim, scale):
    rows, width = query_rows.shape
    keys = kv_rows.shape[0]
    blocks = width // HEAD_BLOCK
    return pl.pallas_call(
        functools.partial(attn_fwd_kernel, head_dim, scale),
        out_shape=jax.ShapeDtypeStruct((rows, width), jnp.bfloat16),
        grid_spec=pltpu.PrefetchScalarGridSpec(
            num_scalar_prefetch=1,
            grid=(blocks,),
            in_specs=[
                pl.BlockSpec((rows, HEAD_BLOCK), lambda h, m: (0, h)),
                pl.BlockSpec((keys, HEAD_BLOCK), lambda h, m: (0, h)),
                pl.BlockSpec((keys, HEAD_BLOCK), lambda h, m: (0, h + blocks)),
            ],
            out_specs=pl.BlockSpec((rows, HEAD_BLOCK), lambda h, m: (0, h)),
        ),
        compiler_params=pltpu.CompilerParams(
            dimension_semantics=("arbitrary",), vmem_limit_bytes=48 * 1024 * 1024
        ),
        cost_estimate=pl.CostEstimate(
            flops=4 * rows * keys * width,
            transcendentals=rows * keys * (width // head_dim),
            bytes_accessed=2 * (2 * rows * width + 2 * keys * width),
        ),
    )(meta, query_rows, kv_rows, kv_rows)


def attention_backward(meta, query_rows, kv_rows, back_rows, head_dim, scale):
    rows, width = query_rows.shape
    keys = kv_rows.shape[0]
    blocks = width // HEAD_BLOCK
    return pl.pallas_call(
        functools.partial(attn_bwd_kernel, head_dim, scale),
        out_shape=(
            jax.ShapeDtypeStruct((rows, width), jnp.float32),
            jax.ShapeDtypeStruct((keys, 2 * width), jnp.bfloat16),
        ),
        grid_spec=pltpu.PrefetchScalarGridSpec(
            num_scalar_prefetch=1,
            grid=(blocks,),
            in_specs=[
                pl.BlockSpec((rows, HEAD_BLOCK), lambda h, m: (0, h)),
                pl.BlockSpec((keys, HEAD_BLOCK), lambda h, m: (0, h)),
                pl.BlockSpec((keys, HEAD_BLOCK), lambda h, m: (0, h + blocks)),
                pl.BlockSpec((rows, HEAD_BLOCK), lambda h, m: (0, h)),
            ],
            out_specs=[
                pl.BlockSpec((rows, HEAD_BLOCK), lambda h, m: (0, h)),
                pl.BlockSpec((keys, 2 * HEAD_BLOCK), lambda h, m: (0, h)),
            ],
        ),
        compiler_params=pltpu.CompilerParams(
            dimension_semantics=("arbitrary",), vmem_limit_bytes=48 * 1024 * 1024
        ),
        cost_estimate=pl.CostEstimate(
            flops=10 * rows * keys * width,
            transcendentals=rows * keys * (width // head_dim),
            bytes_accessed=2 * (3 * rows * width + 4 * keys * width) + 4 * rows * width,
        ),
    )(meta, query_rows, kv_rows, kv_rows, back_rows)


def rope_tables(positions, half):
    freq = jnp.exp(
        jnp.arange(half, dtype=jnp.int32).astype(jnp.float32) * (-math.log(10000.0) / half)
    )
    angle = positions.astype(jnp.float32)[:, None] * freq[None, :]
    return (jnp.cos(angle), jnp.sin(angle))


def rotate(value_rows, cosine, sine):
    half = value_rows.shape[-1] // 2
    first = value_rows[..., :half]
    second = value_rows[..., half:]
    return jnp.concatenate(
        [first * cosine - second * sine, second * cosine + first * sine], axis=-1
    )


def norm_apply(value_rows, gain):
    inverse = lax.rsqrt(jnp.mean(value_rows * value_rows, axis=-1, keepdims=True) + EPS)
    return (value_rows * inverse * gain, inverse)


def norm_back(value_rows, inverse, gain, upstream):
    scaled = upstream * gain
    gain_part = jnp.sum(upstream * value_rows * inverse, axis=(0, 1))
    inner = jnp.mean(scaled * value_rows, axis=-1, keepdims=True)
    return (inverse * scaled - value_rows * inverse * inverse * inverse * inner, gain_part)


def gain_block(first, second, width, leading=()):
    pad_cols = width - first.shape[-1] - second.shape[-1]
    row = jnp.concatenate(
        [first, second, jnp.zeros(leading + (pad_cols,), first.dtype)], axis=-1
    )
    row = row[..., None, :]
    pads = [(0, 0)] * len(leading) + [(0, GAIN_ROWS - 1), (0, 0)]
    return jnp.pad(row, pads)


def to_gathered(rows, block):
    lead = rows.shape[:-1]
    return jnp.swapaxes(rows.reshape(lead + (2, -1, block)), -3, -2).reshape(rows.shape)


def from_gathered(rows, block):
    lead = rows.shape[:-1]
    return jnp.swapaxes(rows.reshape(lead + (-1, 2, block)), -3, -2).reshape(rows.shape)


def zh_pair(mine, other):
    first = lax.axis_index("zh") == 0
    return jnp.stack([jnp.where(first, mine, other), jnp.where(first, other, mine)])


def fsdp_gather(pack):
    return yc_gather(z_exchange(pack))


def z_exchange(pack):
    return zh_pair(pack, lax.ppermute(pack, ("zh", "zl"), Z_CROSS))


def yc_gather(pair):
    both = lax.all_gather(pair, ("y", "core"), axis=0, tiled=False)
    return both.reshape((-1,) + pair.shape[1:])


def fsdp_reduce_scatter(grads):
    return z_combine(yc_reduce_scatter(grads))


def yc_reduce_scatter(grads):
    n_yc = grads.shape[0] // 2
    by_yc = grads
    block = grads.shape[1:]
    halves = lax.psum_scatter(
        by_yc.reshape((n_yc, 2 * block[0]) + block[1:]), ("y", "core"), scatter_dimension=0, tiled=False
    ).reshape((2,) + block)
    return halves


def z_combine(halves):
    zh = lax.axis_index("zh")
    mine = lax.dynamic_index_in_dim(halves, zh, axis=0, keepdims=False)
    theirs = lax.dynamic_index_in_dim(halves, 1 - zh, axis=0, keepdims=False)
    got = lax.ppermute(theirs, ("zh", "zl"), Z_CROSS)
    return (mine.astype(jnp.float32) + got.astype(jnp.float32)).astype(jnp.bfloat16)


def xor_sum(value, axes, partners):
    got = [lax.ppermute(value[k], axes, [(j, j ^ (k + 1)) for j in range(partners)]) for k in range(3)]
    wide = [v.astype(jnp.float32) for v in [value[3]] + got]
    return (wide[0] + wide[1]) + (wide[2] + wide[3])


def group_sum(halves):
    across_x = xor_sum([halves] * 4, "x", 4).astype(jnp.bfloat16)
    zh = lax.axis_index("zh")
    mine = lax.dynamic_index_in_dim(across_x, zh, axis=0, keepdims=False)
    theirs = lax.dynamic_index_in_dim(across_x, 1 - zh, axis=0, keepdims=False)
    return xor_sum([mine, theirs, theirs, mine], ("zh", "zl"), 4)


def ctx_allreduce(part, n_ctx):
    total = part
    step = 1
    while step < n_ctx:
        other = lax.ppermute(total, CTX, [(j, j ^ step) for j in range(n_ctx)])
        total = (total.astype(jnp.float32) + other.astype(jnp.float32)).astype(jnp.bfloat16)
        step *= 2
    return total.astype(jnp.float32)


def body(
    tokens,
    first_value,
    query_weight,
    key_weight,
    value_weight,
    out_weight,
    gate_weight,
    up_weight,
    down_weight,
    prenorm_gain,
    midnorm_gain,
    cotangent,
    lengths,
    assignment,
):
    slots, rows, width = tokens.shape
    assert slots == 1
    head_count = H
    head_dim = width // head_count
    score_scale = head_dim ** (-0.5)
    n_fsdp = lax.axis_size(FSDP)
    n_ctx = lax.axis_size(CTX)
    total_len = rows * n_ctx
    w_rows = query_weight.shape[0]
    g_len = prenorm_gain.shape[0]
    ff = gate_weight.shape[1]
    d_rows = down_weight.shape[0]

    slot_count = assignment.shape[0]
    chosen = assignment[:, None] == jnp.arange(slot_count, dtype=jnp.int32)[None, :]
    lengths_all = jnp.sum(jnp.where(chosen, lengths[None, :], 0), axis=1)
    slot_lengths = lax.dynamic_slice_in_dim(lengths_all, lax.axis_index(FSDP) * slots, slots)
    query_places = lax.axis_index(CTX) * rows + jnp.arange(rows, dtype=jnp.int32)
    valid = query_places[None, :] < slot_lengths[:, None]
    cosine, sine = rope_tables(query_places, head_dim // 2)
    cos_rows = cosine[None, :, None, :]
    sin_rows = sine[None, :, None, :]
    valid_wide = valid[:, :, None]

    kv_pair = z_exchange(
        jnp.concatenate(
            [key_weight, value_weight, gain_block(prenorm_gain, midnorm_gain, width)], axis=0
        )
    )
    qod_pair = z_exchange(jnp.concatenate([query_weight, out_weight, down_weight], axis=0))
    gate_up_pair = z_exchange(jnp.concatenate([gate_weight, up_weight], axis=1))
    kv_wall = yc_gather(kv_pair)
    qod_pair, gate_up_pair, kv_wall = lax.optimization_barrier((qod_pair, gate_up_pair, kv_wall))
    qod_wall = yc_gather(qod_pair)
    gate_up_mat = yc_gather(gate_up_pair).reshape(n_fsdp * w_rows, 2 * ff)

    key_mat = kv_wall[:, 0:w_rows, :].reshape(n_fsdp * w_rows, width)
    value_mat = kv_wall[:, w_rows:2 * w_rows, :].reshape(n_fsdp * w_rows, width)
    prenorm_full = from_gathered(kv_wall[:, 2 * w_rows, 0:g_len].reshape(n_fsdp * g_len), g_len)
    midnorm_full = from_gathered(
        kv_wall[:, 2 * w_rows, g_len:2 * g_len].reshape(n_fsdp * g_len), g_len
    )
    query_mat = qod_wall[:, 0:w_rows, :].reshape(n_fsdp * w_rows, width)
    out_mat = qod_wall[:, w_rows:2 * w_rows, :].reshape(n_fsdp * w_rows, width)
    down_mat = qod_wall[:, 2 * w_rows:, :].reshape(n_fsdp * d_rows, width)

    tokens_wide = tokens.astype(jnp.float32)
    first_wide = first_value.astype(jnp.float32)
    normed, inverse = norm_apply(tokens_wide, prenorm_full.astype(jnp.float32))
    normed_low = normed.astype(jnp.bfloat16)
    normed_low_g = to_gathered(normed_low, w_rows)
    keyed = jnp.dot(normed_low_g, key_mat, preferred_element_type=jnp.float32)
    own_value = jnp.dot(normed_low_g, value_mat, preferred_element_type=jnp.float32)
    heads_shape = keyed.shape[:2] + (head_count, head_dim)
    key_rot = (
        rotate(keyed.reshape(heads_shape), cos_rows, sin_rows)
        .astype(jnp.bfloat16)
        .reshape(keyed.shape)
    )
    value_mix = (0.5 * own_value + 0.5 * first_wide).astype(jnp.bfloat16)

    kv_own = jnp.concatenate([key_rot, value_mix], axis=-1).reshape(rows, 2 * width)
    kv_all = lax.all_to_all(
        jnp.broadcast_to(kv_own[None], (n_ctx, rows, 2 * width)), CTX, 0, 0, tiled=False
    ).reshape(total_len, 2 * width)
    query_in, kv_all = lax.optimization_barrier((normed_low_g, kv_all))
    query = jnp.dot(query_in, query_mat, preferred_element_type=jnp.float32)
    query_rotated_rows = rotate(query.reshape(heads_shape), cos_rows, sin_rows).astype(jnp.bfloat16)
    meta = jnp.stack([lax.axis_index(CTX) * rows, slot_lengths[0]]).astype(jnp.int32)
    query_flat = query_rotated_rows.reshape(rows, width)
    mixed_low = attention_forward(
        meta, query_flat, kv_all, head_dim, score_scale
    ).reshape(slots, rows, width)

    mixed_low_g = to_gathered(mixed_low, w_rows)
    middle = tokens_wide + jnp.dot(mixed_low_g, out_mat, preferred_element_type=jnp.float32)
    normed_two, inverse_two = norm_apply(middle, midnorm_full.astype(jnp.float32))
    normed_two = normed_two.astype(jnp.bfloat16)
    normed_two_g = to_gathered(normed_two, w_rows)
    gate_up = jnp.dot(normed_two_g, gate_up_mat, preferred_element_type=jnp.float32)
    gate = gate_up[..., :ff]
    upper = gate_up[..., ff:]
    hidden = (jax.nn.silu(gate) * upper).astype(jnp.bfloat16)
    hidden_g = to_gathered(hidden, d_rows)
    branch = jnp.dot(hidden_g, down_mat, preferred_element_type=jnp.float32)
    layer_out = jnp.where(valid_wide, middle + branch, 0.0).astype(jnp.bfloat16)

    cot_wide = jnp.where(valid_wide, cotangent.astype(jnp.float32), 0.0)
    cot_low = cot_wide.astype(jnp.bfloat16)
    down_total = jnp.einsum("srf,sre->fe", hidden_g, cot_low, preferred_element_type=jnp.float32)
    hidden_back = from_gathered(
        jnp.einsum("sre,fe->srf", cot_low, down_mat, preferred_element_type=jnp.float32), d_rows
    )
    sigma = jax.nn.sigmoid(gate)
    gate_back = (hidden_back * upper * sigma * (1.0 + gate * (1.0 - sigma))).astype(jnp.bfloat16)
    upper_back = (hidden_back * gate * sigma).astype(jnp.bfloat16)
    gate_up_back = jnp.concatenate([gate_back, upper_back], axis=-1)
    gate_up_total = jnp.einsum(
        "srd,srf->df", normed_two_g, gate_up_back, preferred_element_type=jnp.float32
    )
    normed_two_back = jnp.einsum(
        "srf,df->srd", gate_up_back, gate_up_mat, preferred_element_type=jnp.float32
    )
    normed_two_back = from_gathered(normed_two_back, w_rows)
    middle_norm_back, midnorm_total = norm_back(
        middle, inverse_two, midnorm_full.astype(jnp.float32), normed_two_back
    )
    middle_back = cot_wide + middle_norm_back
    middle_low = middle_back.astype(jnp.bfloat16)
    out_total = jnp.einsum("srd,sre->de", mixed_low_g, middle_low, preferred_element_type=jnp.float32)

    down_share = group_sum(
        yc_reduce_scatter(down_total.astype(jnp.bfloat16).reshape(n_fsdp, d_rows, width))
    )
    mlp_grads = jnp.concatenate(
        [
            gate_up_total.reshape(n_fsdp, w_rows, 2 * ff),
            out_total.reshape(n_fsdp, w_rows, width),
        ],
        axis=2,
    ).astype(jnp.bfloat16)
    mlp_halves = yc_reduce_scatter(mlp_grads)

    blended_value_gradient = from_gathered(
        jnp.einsum("sre,de->srd", middle_low, out_mat, preferred_element_type=jnp.float32).astype(
            jnp.bfloat16
        ),
        w_rows,
    )
    query_rot_back, kv_back = attention_backward(
        meta, query_flat, kv_all, blended_value_gradient.reshape(rows, width), head_dim, score_scale
    )
    query_rot_back = query_rot_back.reshape(slots, rows, head_count, head_dim)
    key_value = jnp.sum(
        lax.all_to_all(kv_back.reshape(n_ctx, rows, 2 * width), CTX, 0, 0, tiled=False).astype(
            jnp.float32
        ),
        axis=0,
    )
    key_value = key_value.reshape(rows, width // HEAD_BLOCK, 2, HEAD_BLOCK)
    key_rot_back = key_value[:, :, 0, :].reshape(slots, rows, head_count, head_dim)
    value_mix_back = key_value[:, :, 1, :].reshape(slots, rows, width)
    first_grad = 0.5 * value_mix_back
    query_back = (
        rotate(query_rot_back, cos_rows, -sin_rows).reshape(slots, rows, width).astype(jnp.bfloat16)
    )
    key_back = (
        rotate(key_rot_back, cos_rows, -sin_rows).reshape(slots, rows, width).astype(jnp.bfloat16)
    )
    value_back = (0.5 * value_mix_back).astype(jnp.bfloat16)
    query_total = jnp.einsum(
        "srd,sre->de", normed_low_g, query_back, preferred_element_type=jnp.float32
    )
    key_total = jnp.einsum("srd,sre->de", normed_low_g, key_back, preferred_element_type=jnp.float32)
    value_total = jnp.einsum(
        "srd,sre->de", normed_low_g, value_back, preferred_element_type=jnp.float32
    )
    normed_back = jnp.einsum(
        "sre,de->srd", query_back, query_mat, preferred_element_type=jnp.float32
    )
    normed_back = normed_back + jnp.einsum(
        "sre,de->srd", key_back, key_mat, preferred_element_type=jnp.float32
    )
    normed_back = normed_back + jnp.einsum(
        "sre,de->srd", value_back, value_mat, preferred_element_type=jnp.float32
    )
    normed_back = from_gathered(normed_back, w_rows)
    tokens_norm_back, prenorm_total = norm_back(
        tokens_wide, inverse, prenorm_full.astype(jnp.float32), normed_back
    )
    tokens_grad = middle_back + tokens_norm_back

    attn_grads = jnp.concatenate(
        [
            query_total.reshape(n_fsdp, w_rows, width),
            key_total.reshape(n_fsdp, w_rows, width),
            value_total.reshape(n_fsdp, w_rows, width),
            gain_block(
                to_gathered(prenorm_total, g_len).reshape(n_fsdp, g_len),
                to_gathered(midnorm_total, g_len).reshape(n_fsdp, g_len),
                width,
                leading=(n_fsdp,),
            ),
        ],
        axis=1,
    ).astype(jnp.bfloat16)
    attn_grads, mlp_halves = lax.optimization_barrier((attn_grads, mlp_halves))
    mlp_share = group_sum(mlp_halves)
    attn_share = group_sum(yc_reduce_scatter(attn_grads))

    def attn_grad(i):
        return attn_share[i * w_rows:(i + 1) * w_rows]

    query_grad, key_grad, value_grad = (attn_grad(i) for i in range(3))
    prenorm_grad = attn_share[3 * w_rows, 0:g_len]
    midnorm_grad = attn_share[3 * w_rows, g_len:2 * g_len]
    gate_grad = mlp_share[:, 0:ff]
    up_grad = mlp_share[:, ff:2 * ff]
    down_grad = down_share
    out_grad = mlp_share[:, 2 * ff:]
    return (
        layer_out,
        tokens_grad,
        first_grad,
        query_grad,
        key_grad,
        value_grad,
        out_grad,
        gate_grad,
        up_grad,
        down_grad,
        prenorm_grad,
        midnorm_grad,
    )


def solution(mesh):
    zh = 2
    zl = 2
    n_f, n_c = mesh.devices.shape
    fine = jax.sharding.Mesh(
        mesh.devices.reshape(zh, n_f // (2 * zh), 2, zl, n_c // zl), FSDP + CTX
    )
    placed = (
        P(FSDP, CTX, None),
        P(FSDP, CTX, None),
        P(FSDP, None),
        P(FSDP, None),
        P(FSDP, None),
        P(FSDP, None),
        P(FSDP, None),
        P(FSDP, None),
        P(FSDP, None),
        P(FSDP),
        P(FSDP),
        P(FSDP, CTX, None),
        P(),
        P(),
    )
    return jax.shard_map(
        body,
        mesh=fine,
        in_specs=placed,
        out_specs=(
            P(FSDP, CTX, None),
            P(FSDP, CTX, None),
            P(FSDP, CTX, None),
            P(FSDP, None),
            P(FSDP, None),
            P(FSDP, None),
            P(FSDP, None),
            P(FSDP, None),
            P(FSDP, None),
            P(FSDP, None),
            P(FSDP),
            P(FSDP),
        ),
        check_vma=False,
    )
```

```python
import functools
import math

import jax
import jax.numpy as jnp
from jax import lax
from jax.experimental import pallas as pl
from jax.experimental.pallas import tpu as pltpu
from jax.sharding import PartitionSpec as P

H = 16


EPS = 1e-06
MASKED = -1e30
GAIN_ROWS = 16
FSDP = ("zh", "y", "core")
CTX = ("zl", "x")
Z_CROSS = [(0, 3), (3, 0), (1, 2), (2, 1)]


HEAD_BLOCK = 256
NT_DIMS = (((1,), (1,)), ((), ()))
TN_DIMS = (((0,), (0,)), ((), ()))


def allowed_keys(rows, keys, first_row, slot_len):
    query_pos = first_row + lax.broadcasted_iota(jnp.int32, (rows, keys), 0)
    key_pos = lax.broadcasted_iota(jnp.int32, (rows, keys), 1)
    return (key_pos <= query_pos) & (key_pos < slot_len)


def attention_shares(query, keys, allowed, scale):
    scores = lax.dot_general(query, keys, NT_DIMS, preferred_element_type=jnp.float32) * scale
    scores = jnp.where(allowed, scores, MASKED)
    peak = jnp.max(scores, axis=-1, keepdims=True)
    raised = jnp.exp(scores - peak)
    denominator = jnp.sum(raised, axis=-1, keepdims=True)
    return raised * (1.0 / denominator)


def attn_fwd_kernel(head_dim, scale, meta_ref, q_ref, k_ref, v_ref, o_ref):
    allowed = allowed_keys(q_ref.shape[0], k_ref.shape[0], meta_ref[0], meta_ref[1])
    for j in range(q_ref.shape[1] // head_dim):
        cols = slice(j * head_dim, (j + 1) * head_dim)
        shares = attention_shares(q_ref[:, cols], k_ref[:, cols], allowed, scale)
        mixed = jnp.dot(
            shares.astype(jnp.bfloat16), v_ref[:, cols], preferred_element_type=jnp.float32
        )
        o_ref[:, cols] = mixed.astype(o_ref.dtype)


def attn_bwd_kernel(head_dim, scale, meta_ref, q_ref, k_ref, v_ref, do_ref, dq_ref, dkv_ref):
    allowed = allowed_keys(q_ref.shape[0], k_ref.shape[0], meta_ref[0], meta_ref[1])
    for j in range(q_ref.shape[1] // head_dim):
        cols = slice(j * head_dim, (j + 1) * head_dim)
        query = q_ref[:, cols]
        keys = k_ref[:, cols]
        back = do_ref[:, cols]
        shares = attention_shares(query, keys, allowed, scale)
        prob_back = lax.dot_general(back, v_ref[:, cols], NT_DIMS, preferred_element_type=jnp.float32)
        inner = jnp.sum(shares * prob_back, axis=-1, keepdims=True)
        score_back = (shares * (prob_back - inner)).astype(jnp.bfloat16)
        dq_ref[:, cols] = (
            jnp.dot(score_back, keys, preferred_element_type=jnp.float32) * scale
        )
        dkv_ref[:, cols] = (
            lax.dot_general(score_back, query, TN_DIMS, preferred_element_type=jnp.float32) * scale
        ).astype(dkv_ref.dtype)
        half = q_ref.shape[1]
        dkv_ref[:, half + j * head_dim:half + (j + 1) * head_dim] = lax.dot_general(
            shares.astype(jnp.bfloat16), back, TN_DIMS, preferred_element_type=jnp.float32
        ).astype(dkv_ref.dtype)


def attention_forward(meta, query_rows, kv_rows, head_dim, scale):
    rows, width = query_rows.shape
    keys = kv_rows.shape[0]
    blocks = width // HEAD_BLOCK
    return pl.pallas_call(
        functools.partial(attn_fwd_kernel, head_dim, scale),
        out_shape=jax.ShapeDtypeStruct((rows, width), jnp.bfloat16),
        grid_spec=pltpu.PrefetchScalarGridSpec(
            num_scalar_prefetch=1,
            grid=(blocks,),
            in_specs=[
                pl.BlockSpec((rows, HEAD_BLOCK), lambda h, m: (0, h)),
                pl.BlockSpec((keys, HEAD_BLOCK), lambda h, m: (0, h)),
                pl.BlockSpec((keys, HEAD_BLOCK), lambda h, m: (0, h + blocks)),
            ],
            out_specs=pl.BlockSpec((rows, HEAD_BLOCK), lambda h, m: (0, h)),
        ),
        compiler_params=pltpu.CompilerParams(
            dimension_semantics=("arbitrary",), vmem_limit_bytes=48 * 1024 * 1024
        ),
        cost_estimate=pl.CostEstimate(
            flops=4 * rows * keys * width,
            transcendentals=rows * keys * (width // head_dim),
            bytes_accessed=2 * (2 * rows * width + 2 * keys * width),
        ),
    )(meta, query_rows, kv_rows, kv_rows)


def attention_backward(meta, query_rows, kv_rows, back_rows, head_dim, scale):
    rows, width = query_rows.shape
    keys = kv_rows.shape[0]
    blocks = width // HEAD_BLOCK
    return pl.pallas_call(
        functools.partial(attn_bwd_kernel, head_dim, scale),
        out_shape=(
            jax.ShapeDtypeStruct((rows, width), jnp.float32),
            jax.ShapeDtypeStruct((keys, 2 * width), jnp.bfloat16),
        ),
        grid_spec=pltpu.PrefetchScalarGridSpec(
            num_scalar_prefetch=1,
            grid=(blocks,),
            in_specs=[
                pl.BlockSpec((rows, HEAD_BLOCK), lambda h, m: (0, h)),
                pl.BlockSpec((keys, HEAD_BLOCK), lambda h, m: (0, h)),
                pl.BlockSpec((keys, HEAD_BLOCK), lambda h, m: (0, h + blocks)),
                pl.BlockSpec((rows, HEAD_BLOCK), lambda h, m: (0, h)),
            ],
            out_specs=[
                pl.BlockSpec((rows, HEAD_BLOCK), lambda h, m: (0, h)),
                pl.BlockSpec((keys, 2 * HEAD_BLOCK), lambda h, m: (0, h)),
            ],
        ),
        compiler_params=pltpu.CompilerParams(
            dimension_semantics=("arbitrary",), vmem_limit_bytes=48 * 1024 * 1024
        ),
        cost_estimate=pl.CostEstimate(
            flops=10 * rows * keys * width,
            transcendentals=rows * keys * (width // head_dim),
            bytes_accessed=2 * (3 * rows * width + 4 * keys * width) + 4 * rows * width,
        ),
    )(meta, query_rows, kv_rows, kv_rows, back_rows)


def rope_tables(positions, half):
    freq = jnp.exp(
        jnp.arange(half, dtype=jnp.int32).astype(jnp.float32) * (-math.log(10000.0) / half)
    )
    angle = positions.astype(jnp.float32)[:, None] * freq[None, :]
    return (jnp.cos(angle), jnp.sin(angle))


def rotate(value_rows, cosine, sine):
    half = value_rows.shape[-1] // 2
    first = value_rows[..., :half]
    second = value_rows[..., half:]
    return jnp.concatenate(
        [first * cosine - second * sine, second * cosine + first * sine], axis=-1
    )


def norm_apply(value_rows, gain):
    inverse = lax.rsqrt(jnp.mean(value_rows * value_rows, axis=-1, keepdims=True) + EPS)
    return (value_rows * inverse * gain, inverse)


def norm_back(value_rows, inverse, gain, upstream):
    scaled = upstream * gain
    gain_part = jnp.sum(upstream * value_rows * inverse, axis=(0, 1))
    inner = jnp.mean(scaled * value_rows, axis=-1, keepdims=True)
    return (inverse * scaled - value_rows * inverse * inverse * inverse * inner, gain_part)


def gain_block(first, second, width, leading=()):
    pad_cols = width - first.shape[-1] - second.shape[-1]
    row = jnp.concatenate(
        [first, second, jnp.zeros(leading + (pad_cols,), first.dtype)], axis=-1
    )
    row = row[..., None, :]
    pads = [(0, 0)] * len(leading) + [(0, GAIN_ROWS - 1), (0, 0)]
    return jnp.pad(row, pads)


def to_gathered(rows, block):
    lead = rows.shape[:-1]
    return jnp.swapaxes(rows.reshape(lead + (2, -1, block)), -3, -2).reshape(rows.shape)


def from_gathered(rows, block):
    lead = rows.shape[:-1]
    return jnp.swapaxes(rows.reshape(lead + (-1, 2, block)), -3, -2).reshape(rows.shape)


def zh_pair(mine, other):
    first = lax.axis_index("zh") == 0
    return jnp.stack([jnp.where(first, mine, other), jnp.where(first, other, mine)])


def fsdp_gather(pack):
    return yc_gather(z_exchange(pack))


def z_exchange(pack):
    return zh_pair(pack, lax.ppermute(pack, ("zh", "zl"), Z_CROSS))


def yc_gather(pair):
    both = lax.all_gather(pair, ("y", "core"), axis=0, tiled=False)
    return both.reshape((-1,) + pair.shape[1:])


def fsdp_reduce_scatter(grads):
    return z_combine(yc_reduce_scatter(grads))


def yc_reduce_scatter(grads):
    n_yc = grads.shape[0] // 2
    by_yc = grads
    block = grads.shape[1:]
    halves = lax.psum_scatter(
        by_yc.reshape((n_yc, 2 * block[0]) + block[1:]), ("y", "core"), scatter_dimension=0, tiled=False
    ).reshape((2,) + block)
    return halves


def z_combine(halves):
    zh = lax.axis_index("zh")
    mine = lax.dynamic_index_in_dim(halves, zh, axis=0, keepdims=False)
    theirs = lax.dynamic_index_in_dim(halves, 1 - zh, axis=0, keepdims=False)
    got = lax.ppermute(theirs, ("zh", "zl"), Z_CROSS)
    return (mine.astype(jnp.float32) + got.astype(jnp.float32)).astype(jnp.bfloat16)


def ctx_allreduce(part, n_ctx):
    total = part
    step = 1
    while step < n_ctx:
        other = lax.ppermute(total, CTX, [(j, j ^ step) for j in range(n_ctx)])
        total = (total.astype(jnp.float32) + other.astype(jnp.float32)).astype(jnp.bfloat16)
        step *= 2
    return total.astype(jnp.float32)


def body(
    tokens,
    first_value,
    query_weight,
    key_weight,
    value_weight,
    out_weight,
    gate_weight,
    up_weight,
    down_weight,
    prenorm_gain,
    midnorm_gain,
    cotangent,
    lengths,
    assignment,
):
    slots, rows, width = tokens.shape
    assert slots == 1
    head_count = H
    head_dim = width // head_count
    score_scale = head_dim ** (-0.5)
    n_fsdp = lax.axis_size(FSDP)
    n_ctx = lax.axis_size(CTX)
    total_len = rows * n_ctx
    w_rows = query_weight.shape[0]
    g_len = prenorm_gain.shape[0]
    ff = gate_weight.shape[1]
    d_rows = down_weight.shape[0]

    slot_count = assignment.shape[0]
    chosen = assignment[:, None] == jnp.arange(slot_count, dtype=jnp.int32)[None, :]
    lengths_all = jnp.sum(jnp.where(chosen, lengths[None, :], 0), axis=1)
    slot_lengths = lax.dynamic_slice_in_dim(lengths_all, lax.axis_index(FSDP) * slots, slots)
    query_places = lax.axis_index(CTX) * rows + jnp.arange(rows, dtype=jnp.int32)
    valid = query_places[None, :] < slot_lengths[:, None]
    cosine, sine = rope_tables(query_places, head_dim // 2)
    cos_rows = cosine[None, :, None, :]
    sin_rows = sine[None, :, None, :]
    valid_wide = valid[:, :, None]

    kv_pair = z_exchange(
        jnp.concatenate(
            [key_weight, value_weight, gain_block(prenorm_gain, midnorm_gain, width)], axis=0
        )
    )
    qod_pair = z_exchange(jnp.concatenate([query_weight, out_weight, down_weight], axis=0))
    gate_up_pair = z_exchange(jnp.concatenate([gate_weight, up_weight], axis=1))
    kv_wall = yc_gather(kv_pair)
    qod_pair, gate_up_pair, kv_wall = lax.optimization_barrier((qod_pair, gate_up_pair, kv_wall))
    qod_wall = yc_gather(qod_pair)
    gate_up_mat = yc_gather(gate_up_pair).reshape(n_fsdp * w_rows, 2 * ff)

    key_mat = kv_wall[:, 0:w_rows, :].reshape(n_fsdp * w_rows, width)
    value_mat = kv_wall[:, w_rows:2 * w_rows, :].reshape(n_fsdp * w_rows, width)
    prenorm_full = from_gathered(kv_wall[:, 2 * w_rows, 0:g_len].reshape(n_fsdp * g_len), g_len)
    midnorm_full = from_gathered(
        kv_wall[:, 2 * w_rows, g_len:2 * g_len].reshape(n_fsdp * g_len), g_len
    )
    query_mat = qod_wall[:, 0:w_rows, :].reshape(n_fsdp * w_rows, width)
    out_mat = qod_wall[:, w_rows:2 * w_rows, :].reshape(n_fsdp * w_rows, width)
    down_mat = qod_wall[:, 2 * w_rows:, :].reshape(n_fsdp * d_rows, width)

    tokens_wide = tokens.astype(jnp.float32)
    first_wide = first_value.astype(jnp.float32)
    normed, inverse = norm_apply(tokens_wide, prenorm_full.astype(jnp.float32))
    normed_low = normed.astype(jnp.bfloat16)
    normed_low_g = to_gathered(normed_low, w_rows)
    keyed = jnp.dot(normed_low_g, key_mat, preferred_element_type=jnp.float32)
    own_value = jnp.dot(normed_low_g, value_mat, preferred_element_type=jnp.float32)
    heads_shape = keyed.shape[:2] + (head_count, head_dim)
    key_rot = (
        rotate(keyed.reshape(heads_shape), cos_rows, sin_rows)
        .astype(jnp.bfloat16)
        .reshape(keyed.shape)
    )
    value_mix = (0.5 * own_value + 0.5 * first_wide).astype(jnp.bfloat16)

    kv_own = jnp.concatenate([key_rot, value_mix], axis=-1).reshape(rows, 2 * width)
    kv_all = lax.all_to_all(
        jnp.broadcast_to(kv_own[None], (n_ctx, rows, 2 * width)), CTX, 0, 0, tiled=False
    ).reshape(total_len, 2 * width)
    query_in, kv_all = lax.optimization_barrier((normed_low_g, kv_all))
    query = jnp.dot(query_in, query_mat, preferred_element_type=jnp.float32)
    query_rotated_rows = rotate(query.reshape(heads_shape), cos_rows, sin_rows).astype(jnp.bfloat16)
    meta = jnp.stack([lax.axis_index(CTX) * rows, slot_lengths[0]]).astype(jnp.int32)
    query_flat = query_rotated_rows.reshape(rows, width)
    mixed_low = attention_forward(
        meta, query_flat, kv_all, head_dim, score_scale
    ).reshape(slots, rows, width)

    mixed_low_g = to_gathered(mixed_low, w_rows)
    middle = tokens_wide + jnp.dot(mixed_low_g, out_mat, preferred_element_type=jnp.float32)
    normed_two, inverse_two = norm_apply(middle, midnorm_full.astype(jnp.float32))
    normed_two = normed_two.astype(jnp.bfloat16)
    normed_two_g = to_gathered(normed_two, w_rows)
    gate_up = jnp.dot(normed_two_g, gate_up_mat, preferred_element_type=jnp.float32)
    gate = gate_up[..., :ff]
    upper = gate_up[..., ff:]
    hidden = (jax.nn.silu(gate) * upper).astype(jnp.bfloat16)
    hidden_g = to_gathered(hidden, d_rows)
    branch = jnp.dot(hidden_g, down_mat, preferred_element_type=jnp.float32)
    layer_out = jnp.where(valid_wide, middle + branch, 0.0).astype(jnp.bfloat16)

    cot_wide = jnp.where(valid_wide, cotangent.astype(jnp.float32), 0.0)
    cot_low = cot_wide.astype(jnp.bfloat16)
    down_total = jnp.einsum("srf,sre->fe", hidden_g, cot_low, preferred_element_type=jnp.float32)
    hidden_back = from_gathered(
        jnp.einsum("sre,fe->srf", cot_low, down_mat, preferred_element_type=jnp.float32), d_rows
    )
    sigma = jax.nn.sigmoid(gate)
    gate_back = (hidden_back * upper * sigma * (1.0 + gate * (1.0 - sigma))).astype(jnp.bfloat16)
    upper_back = (hidden_back * gate * sigma).astype(jnp.bfloat16)
    gate_up_back = jnp.concatenate([gate_back, upper_back], axis=-1)
    gate_up_total = jnp.einsum(
        "srd,srf->df", normed_two_g, gate_up_back, preferred_element_type=jnp.float32
    )
    normed_two_back = jnp.einsum(
        "srf,df->srd", gate_up_back, gate_up_mat, preferred_element_type=jnp.float32
    )
    normed_two_back = from_gathered(normed_two_back, w_rows)
    middle_norm_back, midnorm_total = norm_back(
        middle, inverse_two, midnorm_full.astype(jnp.float32), normed_two_back
    )
    middle_back = cot_wide + middle_norm_back
    middle_low = middle_back.astype(jnp.bfloat16)
    out_total = jnp.einsum("srd,sre->de", mixed_low_g, middle_low, preferred_element_type=jnp.float32)

    down_share = ctx_allreduce(
        z_combine(yc_reduce_scatter(down_total.astype(jnp.bfloat16).reshape(n_fsdp, d_rows, width))),
        n_ctx,
    )
    mlp_grads = jnp.concatenate(
        [
            gate_up_total.reshape(n_fsdp, w_rows, 2 * ff),
            out_total.reshape(n_fsdp, w_rows, width),
        ],
        axis=2,
    ).astype(jnp.bfloat16)
    mlp_halves = yc_reduce_scatter(mlp_grads)

    blended_value_gradient = from_gathered(
        jnp.einsum("sre,de->srd", middle_low, out_mat, preferred_element_type=jnp.float32).astype(
            jnp.bfloat16
        ),
        w_rows,
    )
    query_rot_back, kv_back = attention_backward(
        meta, query_flat, kv_all, blended_value_gradient.reshape(rows, width), head_dim, score_scale
    )
    query_rot_back = query_rot_back.reshape(slots, rows, head_count, head_dim)
    key_value = jnp.sum(
        lax.all_to_all(kv_back.reshape(n_ctx, rows, 2 * width), CTX, 0, 0, tiled=False).astype(
            jnp.float32
        ),
        axis=0,
    )
    key_value = key_value.reshape(rows, width // HEAD_BLOCK, 2, HEAD_BLOCK)
    key_rot_back = key_value[:, :, 0, :].reshape(slots, rows, head_count, head_dim)
    value_mix_back = key_value[:, :, 1, :].reshape(slots, rows, width)
    first_grad = 0.5 * value_mix_back
    query_back = (
        rotate(query_rot_back, cos_rows, -sin_rows).reshape(slots, rows, width).astype(jnp.bfloat16)
    )
    key_back = (
        rotate(key_rot_back, cos_rows, -sin_rows).reshape(slots, rows, width).astype(jnp.bfloat16)
    )
    value_back = (0.5 * value_mix_back).astype(jnp.bfloat16)
    query_total = jnp.einsum(
        "srd,sre->de", normed_low_g, query_back, preferred_element_type=jnp.float32
    )
    key_total = jnp.einsum("srd,sre->de", normed_low_g, key_back, preferred_element_type=jnp.float32)
    value_total = jnp.einsum(
        "srd,sre->de", normed_low_g, value_back, preferred_element_type=jnp.float32
    )
    normed_back = jnp.einsum(
        "sre,de->srd", query_back, query_mat, preferred_element_type=jnp.float32
    )
    normed_back = normed_back + jnp.einsum(
        "sre,de->srd", key_back, key_mat, preferred_element_type=jnp.float32
    )
    normed_back = normed_back + jnp.einsum(
        "sre,de->srd", value_back, value_mat, preferred_element_type=jnp.float32
    )
    normed_back = from_gathered(normed_back, w_rows)
    tokens_norm_back, prenorm_total = norm_back(
        tokens_wide, inverse, prenorm_full.astype(jnp.float32), normed_back
    )
    tokens_grad = middle_back + tokens_norm_back

    attn_grads = jnp.concatenate(
        [
            query_total.reshape(n_fsdp, w_rows, width),
            key_total.reshape(n_fsdp, w_rows, width),
            value_total.reshape(n_fsdp, w_rows, width),
            gain_block(
                to_gathered(prenorm_total, g_len).reshape(n_fsdp, g_len),
                to_gathered(midnorm_total, g_len).reshape(n_fsdp, g_len),
                width,
                leading=(n_fsdp,),
            ),
        ],
        axis=1,
    ).astype(jnp.bfloat16)
    attn_grads, mlp_halves = lax.optimization_barrier((attn_grads, mlp_halves))
    mlp_share = ctx_allreduce(z_combine(mlp_halves), n_ctx)
    attn_share = fsdp_reduce_scatter(attn_grads)
    attn_share = ctx_allreduce(attn_share, n_ctx)

    def attn_grad(i):
        return attn_share[i * w_rows:(i + 1) * w_rows]

    query_grad, key_grad, value_grad = (attn_grad(i) for i in range(3))
    prenorm_grad = attn_share[3 * w_rows, 0:g_len]
    midnorm_grad = attn_share[3 * w_rows, g_len:2 * g_len]
    gate_grad = mlp_share[:, 0:ff]
    up_grad = mlp_share[:, ff:2 * ff]
    down_grad = down_share
    out_grad = mlp_share[:, 2 * ff:]
    return (
        layer_out,
        tokens_grad,
        first_grad,
        query_grad,
        key_grad,
        value_grad,
        out_grad,
        gate_grad,
        up_grad,
        down_grad,
        prenorm_grad,
        midnorm_grad,
    )


def solution(mesh):
    zh = 2
    zl = 2
    n_f, n_c = mesh.devices.shape
    fine = jax.sharding.Mesh(
        mesh.devices.reshape(zh, n_f // (2 * zh), 2, zl, n_c // zl), FSDP + CTX
    )
    placed = (
        P(FSDP, CTX, None),
        P(FSDP, CTX, None),
        P(FSDP, None),
        P(FSDP, None),
        P(FSDP, None),
        P(FSDP, None),
        P(FSDP, None),
        P(FSDP, None),
        P(FSDP, None),
        P(FSDP),
        P(FSDP),
        P(FSDP, CTX, None),
        P(),
        P(),
    )
    return jax.shard_map(
        body,
        mesh=fine,
        in_specs=placed,
        out_specs=(
            P(FSDP, CTX, None),
            P(FSDP, CTX, None),
            P(FSDP, CTX, None),
            P(FSDP, None),
            P(FSDP, None),
            P(FSDP, None),
            P(FSDP, None),
            P(FSDP, None),
            P(FSDP, None),
            P(FSDP, None),
            P(FSDP),
            P(FSDP),
        ),
        check_vma=False,
    )
```

```python
import functools
import math

import jax
import jax.numpy as jnp
from jax import lax
from jax.experimental import pallas as pl
from jax.experimental.pallas import tpu as pltpu
from jax.sharding import PartitionSpec as P

H = 16


EPS = 1e-06
MASKED = -1e30
GAIN_ROWS = 16
FSDP = ("zh", "y", "core")
CTX = ("zl", "x")
Z_CROSS = [(0, 3), (3, 0), (1, 2), (2, 1)]


HEAD_BLOCK = 256
NT_DIMS = (((1,), (1,)), ((), ()))
TN_DIMS = (((0,), (0,)), ((), ()))


def allowed_keys(rows, keys, first_row, slot_len):
    query_pos = first_row + lax.broadcasted_iota(jnp.int32, (rows, keys), 0)
    key_pos = lax.broadcasted_iota(jnp.int32, (rows, keys), 1)
    return (key_pos <= query_pos) & (key_pos < slot_len)


def attention_shares(query, keys, allowed, scale):
    scores = lax.dot_general(query, keys, NT_DIMS, preferred_element_type=jnp.float32) * scale
    scores = jnp.where(allowed, scores, MASKED)
    peak = jnp.max(scores, axis=-1, keepdims=True)
    raised = jnp.exp(scores - peak)
    denominator = jnp.sum(raised, axis=-1, keepdims=True)
    return raised * (1.0 / denominator)


def attn_fwd_kernel(head_dim, scale, meta_ref, q_ref, k_ref, v_ref, o_ref):
    allowed = allowed_keys(q_ref.shape[0], k_ref.shape[0], meta_ref[0], meta_ref[1])
    for j in range(q_ref.shape[1] // head_dim):
        cols = slice(j * head_dim, (j + 1) * head_dim)
        shares = attention_shares(q_ref[:, cols], k_ref[:, cols], allowed, scale)
        mixed = jnp.dot(
            shares.astype(jnp.bfloat16), v_ref[:, cols], preferred_element_type=jnp.float32
        )
        o_ref[:, cols] = mixed.astype(o_ref.dtype)


def attn_bwd_kernel(head_dim, scale, meta_ref, q_ref, k_ref, v_ref, do_ref, dq_ref, dkv_ref):
    allowed = allowed_keys(q_ref.shape[0], k_ref.shape[0], meta_ref[0], meta_ref[1])
    for j in range(q_ref.shape[1] // head_dim):
        cols = slice(j * head_dim, (j + 1) * head_dim)
        query = q_ref[:, cols]
        keys = k_ref[:, cols]
        back = do_ref[:, cols]
        shares = attention_shares(query, keys, allowed, scale)
        prob_back = lax.dot_general(back, v_ref[:, cols], NT_DIMS, preferred_element_type=jnp.float32)
        inner = jnp.sum(shares * prob_back, axis=-1, keepdims=True)
        score_back = (shares * (prob_back - inner)).astype(jnp.bfloat16)
        dq_ref[:, cols] = (
            jnp.dot(score_back, keys, preferred_element_type=jnp.float32) * scale
        )
        dkv_ref[:, cols] = (
            lax.dot_general(score_back, query, TN_DIMS, preferred_element_type=jnp.float32) * scale
        ).astype(dkv_ref.dtype)
        half = q_ref.shape[1]
        dkv_ref[:, half + j * head_dim:half + (j + 1) * head_dim] = lax.dot_general(
            shares.astype(jnp.bfloat16), back, TN_DIMS, preferred_element_type=jnp.float32
        ).astype(dkv_ref.dtype)


def attention_forward(meta, query_rows, kv_rows, head_dim, scale):
    rows, width = query_rows.shape
    keys = kv_rows.shape[0]
    blocks = width // HEAD_BLOCK
    return pl.pallas_call(
        functools.partial(attn_fwd_kernel, head_dim, scale),
        out_shape=jax.ShapeDtypeStruct((rows, width), jnp.bfloat16),
        grid_spec=pltpu.PrefetchScalarGridSpec(
            num_scalar_prefetch=1,
            grid=(blocks,),
            in_specs=[
                pl.BlockSpec((rows, HEAD_BLOCK), lambda h, m: (0, h)),
                pl.BlockSpec((keys, HEAD_BLOCK), lambda h, m: (0, h)),
                pl.BlockSpec((keys, HEAD_BLOCK), lambda h, m: (0, h + blocks)),
            ],
            out_specs=pl.BlockSpec((rows, HEAD_BLOCK), lambda h, m: (0, h)),
        ),
        compiler_params=pltpu.CompilerParams(
            dimension_semantics=("arbitrary",), vmem_limit_bytes=48 * 1024 * 1024
        ),
        cost_estimate=pl.CostEstimate(
            flops=4 * rows * keys * width,
            transcendentals=rows * keys * (width // head_dim),
            bytes_accessed=2 * (2 * rows * width + 2 * keys * width),
        ),
    )(meta, query_rows, kv_rows, kv_rows)


def attention_backward(meta, query_rows, kv_rows, back_rows, head_dim, scale, first, count):
    rows, width = query_rows.shape
    keys = kv_rows.shape[0]
    blocks = width // HEAD_BLOCK
    part = count * HEAD_BLOCK
    return pl.pallas_call(
        functools.partial(attn_bwd_kernel, head_dim, scale),
        out_shape=(
            jax.ShapeDtypeStruct((rows, part), jnp.float32),
            jax.ShapeDtypeStruct((keys, 2 * part), jnp.bfloat16),
        ),
        grid_spec=pltpu.PrefetchScalarGridSpec(
            num_scalar_prefetch=1,
            grid=(count,),
            in_specs=[
                pl.BlockSpec((rows, HEAD_BLOCK), lambda h, m: (0, h + first)),
                pl.BlockSpec((keys, HEAD_BLOCK), lambda h, m: (0, h + first)),
                pl.BlockSpec((keys, HEAD_BLOCK), lambda h, m: (0, h + first + blocks)),
                pl.BlockSpec((rows, HEAD_BLOCK), lambda h, m: (0, h + first)),
            ],
            out_specs=[
                pl.BlockSpec((rows, HEAD_BLOCK), lambda h, m: (0, h)),
                pl.BlockSpec((keys, 2 * HEAD_BLOCK), lambda h, m: (0, h)),
            ],
        ),
        compiler_params=pltpu.CompilerParams(
            dimension_semantics=("arbitrary",), vmem_limit_bytes=48 * 1024 * 1024
        ),
        cost_estimate=pl.CostEstimate(
            flops=10 * rows * keys * part,
            transcendentals=rows * keys * (part // head_dim),
            bytes_accessed=2 * (3 * rows * part + 4 * keys * part) + 4 * rows * part,
        ),
    )(meta, query_rows, kv_rows, kv_rows, back_rows)


def rope_tables(positions, half):
    freq = jnp.exp(
        jnp.arange(half, dtype=jnp.int32).astype(jnp.float32) * (-math.log(10000.0) / half)
    )
    angle = positions.astype(jnp.float32)[:, None] * freq[None, :]
    return (jnp.cos(angle), jnp.sin(angle))


def rotate(value_rows, cosine, sine):
    half = value_rows.shape[-1] // 2
    first = value_rows[..., :half]
    second = value_rows[..., half:]
    return jnp.concatenate(
        [first * cosine - second * sine, second * cosine + first * sine], axis=-1
    )


def norm_apply(value_rows, gain):
    inverse = lax.rsqrt(jnp.mean(value_rows * value_rows, axis=-1, keepdims=True) + EPS)
    return (value_rows * inverse * gain, inverse)


def norm_back(value_rows, inverse, gain, upstream):
    scaled = upstream * gain
    gain_part = jnp.sum(upstream * value_rows * inverse, axis=(0, 1))
    inner = jnp.mean(scaled * value_rows, axis=-1, keepdims=True)
    return (inverse * scaled - value_rows * inverse * inverse * inverse * inner, gain_part)


def gain_block(first, second, width, leading=()):
    pad_cols = width - first.shape[-1] - second.shape[-1]
    row = jnp.concatenate(
        [first, second, jnp.zeros(leading + (pad_cols,), first.dtype)], axis=-1
    )
    row = row[..., None, :]
    pads = [(0, 0)] * len(leading) + [(0, GAIN_ROWS - 1), (0, 0)]
    return jnp.pad(row, pads)


def to_gathered(rows, block):
    lead = rows.shape[:-1]
    return jnp.swapaxes(rows.reshape(lead + (2, -1, block)), -3, -2).reshape(rows.shape)


def from_gathered(rows, block):
    lead = rows.shape[:-1]
    return jnp.swapaxes(rows.reshape(lead + (-1, 2, block)), -3, -2).reshape(rows.shape)


def zh_pair(mine, other):
    first = lax.axis_index("zh") == 0
    return jnp.stack([jnp.where(first, mine, other), jnp.where(first, other, mine)])


def fsdp_gather(pack):
    return yc_gather(z_exchange(pack))


def z_exchange(pack):
    return zh_pair(pack, lax.ppermute(pack, ("zh", "zl"), Z_CROSS))


def yc_gather(pair):
    both = lax.all_gather(pair, ("y", "core"), axis=0, tiled=False)
    return both.reshape((-1,) + pair.shape[1:])


def fsdp_reduce_scatter(grads):
    return z_combine(yc_reduce_scatter(grads))


def yc_reduce_scatter(grads):
    n_yc = grads.shape[0] // 2
    by_yc = grads
    block = grads.shape[1:]
    halves = lax.psum_scatter(
        by_yc.reshape((n_yc, 2 * block[0]) + block[1:]), ("y", "core"), scatter_dimension=0, tiled=False
    ).reshape((2,) + block)
    return halves


def z_combine(halves):
    zh = lax.axis_index("zh")
    mine = lax.dynamic_index_in_dim(halves, zh, axis=0, keepdims=False)
    theirs = lax.dynamic_index_in_dim(halves, 1 - zh, axis=0, keepdims=False)
    got = lax.ppermute(theirs, ("zh", "zl"), Z_CROSS)
    return (mine.astype(jnp.float32) + got.astype(jnp.float32)).astype(jnp.bfloat16)


def ctx_allreduce(part, n_ctx):
    total = part
    step = 1
    while step < n_ctx:
        other = lax.ppermute(total, CTX, [(j, j ^ step) for j in range(n_ctx)])
        total = (total.astype(jnp.float32) + other.astype(jnp.float32)).astype(jnp.bfloat16)
        step *= 2
    return total.astype(jnp.float32)


def body(
    tokens,
    first_value,
    query_weight,
    key_weight,
    value_weight,
    out_weight,
    gate_weight,
    up_weight,
    down_weight,
    prenorm_gain,
    midnorm_gain,
    cotangent,
    lengths,
    assignment,
):
    slots, rows, width = tokens.shape
    assert slots == 1
    head_count = H
    head_dim = width // head_count
    score_scale = head_dim ** (-0.5)
    n_fsdp = lax.axis_size(FSDP)
    n_ctx = lax.axis_size(CTX)
    total_len = rows * n_ctx
    w_rows = query_weight.shape[0]
    g_len = prenorm_gain.shape[0]
    ff = gate_weight.shape[1]
    d_rows = down_weight.shape[0]

    slot_count = assignment.shape[0]
    chosen = assignment[:, None] == jnp.arange(slot_count, dtype=jnp.int32)[None, :]
    lengths_all = jnp.sum(jnp.where(chosen, lengths[None, :], 0), axis=1)
    slot_lengths = lax.dynamic_slice_in_dim(lengths_all, lax.axis_index(FSDP) * slots, slots)
    query_places = lax.axis_index(CTX) * rows + jnp.arange(rows, dtype=jnp.int32)
    valid = query_places[None, :] < slot_lengths[:, None]
    cosine, sine = rope_tables(query_places, head_dim // 2)
    cos_rows = cosine[None, :, None, :]
    sin_rows = sine[None, :, None, :]
    valid_wide = valid[:, :, None]

    kv_pair = z_exchange(
        jnp.concatenate(
            [key_weight, value_weight, gain_block(prenorm_gain, midnorm_gain, width)], axis=0
        )
    )
    qod_pair = z_exchange(jnp.concatenate([query_weight, out_weight, down_weight], axis=0))
    gate_up_pair = z_exchange(jnp.concatenate([gate_weight, up_weight], axis=1))
    kv_wall = yc_gather(kv_pair)
    qod_pair, gate_up_pair, kv_wall = lax.optimization_barrier((qod_pair, gate_up_pair, kv_wall))
    qod_wall = yc_gather(qod_pair)
    gate_up_mat = yc_gather(gate_up_pair).reshape(n_fsdp * w_rows, 2 * ff)

    key_mat = kv_wall[:, 0:w_rows, :].reshape(n_fsdp * w_rows, width)
    value_mat = kv_wall[:, w_rows:2 * w_rows, :].reshape(n_fsdp * w_rows, width)
    prenorm_full = from_gathered(kv_wall[:, 2 * w_rows, 0:g_len].reshape(n_fsdp * g_len), g_len)
    midnorm_full = from_gathered(
        kv_wall[:, 2 * w_rows, g_len:2 * g_len].reshape(n_fsdp * g_len), g_len
    )
    query_mat = qod_wall[:, 0:w_rows, :].reshape(n_fsdp * w_rows, width)
    out_mat = qod_wall[:, w_rows:2 * w_rows, :].reshape(n_fsdp * w_rows, width)
    down_mat = qod_wall[:, 2 * w_rows:, :].reshape(n_fsdp * d_rows, width)

    tokens_wide = tokens.astype(jnp.float32)
    first_wide = first_value.astype(jnp.float32)
    normed, inverse = norm_apply(tokens_wide, prenorm_full.astype(jnp.float32))
    normed_low = normed.astype(jnp.bfloat16)
    normed_low_g = to_gathered(normed_low, w_rows)
    keyed = jnp.dot(normed_low_g, key_mat, preferred_element_type=jnp.float32)
    own_value = jnp.dot(normed_low_g, value_mat, preferred_element_type=jnp.float32)
    heads_shape = keyed.shape[:2] + (head_count, head_dim)
    key_rot = (
        rotate(keyed.reshape(heads_shape), cos_rows, sin_rows)
        .astype(jnp.bfloat16)
        .reshape(keyed.shape)
    )
    value_mix = (0.5 * own_value + 0.5 * first_wide).astype(jnp.bfloat16)

    kv_own = jnp.concatenate([key_rot, value_mix], axis=-1).reshape(rows, 2 * width)
    kv_all = lax.all_to_all(
        jnp.broadcast_to(kv_own[None], (n_ctx, rows, 2 * width)), CTX, 0, 0, tiled=False
    ).reshape(total_len, 2 * width)
    query_in, kv_all = lax.optimization_barrier((normed_low_g, kv_all))
    query = jnp.dot(query_in, query_mat, preferred_element_type=jnp.float32)
    query_rotated_rows = rotate(query.reshape(heads_shape), cos_rows, sin_rows).astype(jnp.bfloat16)
    meta = jnp.stack([lax.axis_index(CTX) * rows, slot_lengths[0]]).astype(jnp.int32)
    query_flat = query_rotated_rows.reshape(rows, width)
    mixed_low = attention_forward(
        meta, query_flat, kv_all, head_dim, score_scale
    ).reshape(slots, rows, width)

    mixed_low_g = to_gathered(mixed_low, w_rows)
    middle = tokens_wide + jnp.dot(mixed_low_g, out_mat, preferred_element_type=jnp.float32)
    normed_two, inverse_two = norm_apply(middle, midnorm_full.astype(jnp.float32))
    normed_two = normed_two.astype(jnp.bfloat16)
    normed_two_g = to_gathered(normed_two, w_rows)
    gate_up = jnp.dot(normed_two_g, gate_up_mat, preferred_element_type=jnp.float32)
    gate = gate_up[..., :ff]
    upper = gate_up[..., ff:]
    hidden = (jax.nn.silu(gate) * upper).astype(jnp.bfloat16)
    hidden_g = to_gathered(hidden, d_rows)
    branch = jnp.dot(hidden_g, down_mat, preferred_element_type=jnp.float32)
    layer_out = jnp.where(valid_wide, middle + branch, 0.0).astype(jnp.bfloat16)

    cot_wide = jnp.where(valid_wide, cotangent.astype(jnp.float32), 0.0)
    cot_low = cot_wide.astype(jnp.bfloat16)
    down_total = jnp.einsum("srf,sre->fe", hidden_g, cot_low, preferred_element_type=jnp.float32)
    hidden_back = from_gathered(
        jnp.einsum("sre,fe->srf", cot_low, down_mat, preferred_element_type=jnp.float32), d_rows
    )
    sigma = jax.nn.sigmoid(gate)
    gate_back = (hidden_back * upper * sigma * (1.0 + gate * (1.0 - sigma))).astype(jnp.bfloat16)
    upper_back = (hidden_back * gate * sigma).astype(jnp.bfloat16)
    gate_up_back = jnp.concatenate([gate_back, upper_back], axis=-1)
    gate_up_total = jnp.einsum(
        "srd,srf->df", normed_two_g, gate_up_back, preferred_element_type=jnp.float32
    )
    normed_two_back = jnp.einsum(
        "srf,df->srd", gate_up_back, gate_up_mat, preferred_element_type=jnp.float32
    )
    normed_two_back = from_gathered(normed_two_back, w_rows)
    middle_norm_back, midnorm_total = norm_back(
        middle, inverse_two, midnorm_full.astype(jnp.float32), normed_two_back
    )
    middle_back = cot_wide + middle_norm_back
    middle_low = middle_back.astype(jnp.bfloat16)
    out_total = jnp.einsum("srd,sre->de", mixed_low_g, middle_low, preferred_element_type=jnp.float32)

    down_share = ctx_allreduce(
        z_combine(yc_reduce_scatter(down_total.astype(jnp.bfloat16).reshape(n_fsdp, d_rows, width))),
        n_ctx,
    )
    mlp_grads = jnp.concatenate(
        [
            gate_up_total.reshape(n_fsdp, w_rows, 2 * ff),
            out_total.reshape(n_fsdp, w_rows, width),
        ],
        axis=2,
    ).astype(jnp.bfloat16)
    mlp_halves = yc_reduce_scatter(mlp_grads)

    blended_value_gradient = from_gathered(
        jnp.einsum("sre,de->srd", middle_low, out_mat, preferred_element_type=jnp.float32).astype(
            jnp.bfloat16
        ),
        w_rows,
    )
    n_head_blocks = width // HEAD_BLOCK
    half_blocks = n_head_blocks // 2
    back_flat = blended_value_gradient.reshape(rows, width)
    dq_parts = []
    kv_parts = []
    for first in (0, half_blocks):
        dq_part, kv_back = attention_backward(
            meta, query_flat, kv_all, back_flat, head_dim, score_scale, first, half_blocks
        )
        dq_parts.append(dq_part)
        kv_parts.append(
            jnp.sum(
                lax.all_to_all(
                    kv_back.reshape(n_ctx, rows, kv_back.shape[1]), CTX, 0, 0, tiled=False
                ).astype(jnp.float32),
                axis=0,
            ).reshape(rows, half_blocks, 2, HEAD_BLOCK)
        )
    query_rot_back = jnp.concatenate(dq_parts, axis=-1).reshape(slots, rows, head_count, head_dim)
    key_value = jnp.concatenate(kv_parts, axis=1)
    key_rot_back = key_value[:, :, 0, :].reshape(slots, rows, head_count, head_dim)
    value_mix_back = key_value[:, :, 1, :].reshape(slots, rows, width)
    first_grad = 0.5 * value_mix_back
    query_back = (
        rotate(query_rot_back, cos_rows, -sin_rows).reshape(slots, rows, width).astype(jnp.bfloat16)
    )
    key_back = (
        rotate(key_rot_back, cos_rows, -sin_rows).reshape(slots, rows, width).astype(jnp.bfloat16)
    )
    value_back = (0.5 * value_mix_back).astype(jnp.bfloat16)
    query_total = jnp.einsum(
        "srd,sre->de", normed_low_g, query_back, preferred_element_type=jnp.float32
    )
    key_total = jnp.einsum("srd,sre->de", normed_low_g, key_back, preferred_element_type=jnp.float32)
    value_total = jnp.einsum(
        "srd,sre->de", normed_low_g, value_back, preferred_element_type=jnp.float32
    )
    normed_back = jnp.einsum(
        "sre,de->srd", query_back, query_mat, preferred_element_type=jnp.float32
    )
    normed_back = normed_back + jnp.einsum(
        "sre,de->srd", key_back, key_mat, preferred_element_type=jnp.float32
    )
    normed_back = normed_back + jnp.einsum(
        "sre,de->srd", value_back, value_mat, preferred_element_type=jnp.float32
    )
    normed_back = from_gathered(normed_back, w_rows)
    tokens_norm_back, prenorm_total = norm_back(
        tokens_wide, inverse, prenorm_full.astype(jnp.float32), normed_back
    )
    tokens_grad = middle_back + tokens_norm_back

    attn_grads = jnp.concatenate(
        [
            query_total.reshape(n_fsdp, w_rows, width),
            key_total.reshape(n_fsdp, w_rows, width),
            value_total.reshape(n_fsdp, w_rows, width),
            gain_block(
                to_gathered(prenorm_total, g_len).reshape(n_fsdp, g_len),
                to_gathered(midnorm_total, g_len).reshape(n_fsdp, g_len),
                width,
                leading=(n_fsdp,),
            ),
        ],
        axis=1,
    ).astype(jnp.bfloat16)
    attn_grads, mlp_halves = lax.optimization_barrier((attn_grads, mlp_halves))
    mlp_share = ctx_allreduce(z_combine(mlp_halves), n_ctx)
    attn_share = fsdp_reduce_scatter(attn_grads)
    attn_share = ctx_allreduce(attn_share, n_ctx)

    def attn_grad(i):
        return attn_share[i * w_rows:(i + 1) * w_rows]

    query_grad, key_grad, value_grad = (attn_grad(i) for i in range(3))
    prenorm_grad = attn_share[3 * w_rows, 0:g_len]
    midnorm_grad = attn_share[3 * w_rows, g_len:2 * g_len]
    gate_grad = mlp_share[:, 0:ff]
    up_grad = mlp_share[:, ff:2 * ff]
    down_grad = down_share
    out_grad = mlp_share[:, 2 * ff:]
    return (
        layer_out,
        tokens_grad,
        first_grad,
        query_grad,
        key_grad,
        value_grad,
        out_grad,
        gate_grad,
        up_grad,
        down_grad,
        prenorm_grad,
        midnorm_grad,
    )


def solution(mesh):
    zh = 2
    zl = 2
    n_f, n_c = mesh.devices.shape
    fine = jax.sharding.Mesh(
        mesh.devices.reshape(zh, n_f // (2 * zh), 2, zl, n_c // zl), FSDP + CTX
    )
    placed = (
        P(FSDP, CTX, None),
        P(FSDP, CTX, None),
        P(FSDP, None),
        P(FSDP, None),
        P(FSDP, None),
        P(FSDP, None),
        P(FSDP, None),
        P(FSDP, None),
        P(FSDP, None),
        P(FSDP),
        P(FSDP),
        P(FSDP, CTX, None),
        P(),
        P(),
    )
    return jax.shard_map(
        body,
        mesh=fine,
        in_specs=placed,
        out_specs=(
            P(FSDP, CTX, None),
            P(FSDP, CTX, None),
            P(FSDP, CTX, None),
            P(FSDP, None),
            P(FSDP, None),
            P(FSDP, None),
            P(FSDP, None),
            P(FSDP, None),
            P(FSDP, None),
            P(FSDP, None),
            P(FSDP),
            P(FSDP),
        ),
        check_vma=False,
    )
```

```python
import functools
import math

import jax
import jax.numpy as jnp
from jax import lax
from jax.experimental import pallas as pl
from jax.experimental.pallas import tpu as pltpu
from jax.sharding import PartitionSpec as P

H = 16


EPS = 1e-06
MASKED = -1e30
GAIN_ROWS = 16
FSDP = ("zh", "y", "core")
CTX = ("zl", "x")
Z_CROSS = [(0, 3), (3, 0), (1, 2), (2, 1)]


HEAD_BLOCK = 256
NT_DIMS = (((1,), (1,)), ((), ()))
TN_DIMS = (((0,), (0,)), ((), ()))


def allowed_keys(rows, keys, first_row, slot_len):
    query_pos = first_row + lax.broadcasted_iota(jnp.int32, (rows, keys), 0)
    key_pos = lax.broadcasted_iota(jnp.int32, (rows, keys), 1)
    return (key_pos <= query_pos) & (key_pos < slot_len)


def attention_shares(query, keys, allowed, scale):
    scores = lax.dot_general(query, keys, NT_DIMS, preferred_element_type=jnp.float32) * scale
    scores = jnp.where(allowed, scores, MASKED)
    peak = jnp.max(scores, axis=-1, keepdims=True)
    raised = jnp.exp(scores - peak)
    denominator = jnp.sum(raised, axis=-1, keepdims=True)
    return raised * (1.0 / denominator)


def attn_fwd_kernel(head_dim, scale, meta_ref, q_ref, k_ref, v_ref, o_ref):
    allowed = allowed_keys(q_ref.shape[0], k_ref.shape[0], meta_ref[0], meta_ref[1])
    for j in range(q_ref.shape[1] // head_dim):
        cols = slice(j * head_dim, (j + 1) * head_dim)
        shares = attention_shares(q_ref[:, cols], k_ref[:, cols], allowed, scale)
        mixed = jnp.dot(
            shares.astype(jnp.bfloat16), v_ref[:, cols], preferred_element_type=jnp.float32
        )
        o_ref[:, cols] = mixed.astype(o_ref.dtype)


def attn_bwd_kernel(head_dim, scale, meta_ref, q_ref, k_ref, v_ref, do_ref, dq_ref, dkv_ref):
    allowed = allowed_keys(q_ref.shape[0], k_ref.shape[0], meta_ref[0], meta_ref[1])
    for j in range(q_ref.shape[1] // head_dim):
        cols = slice(j * head_dim, (j + 1) * head_dim)
        query = q_ref[:, cols]
        keys = k_ref[:, cols]
        back = do_ref[:, cols]
        shares = attention_shares(query, keys, allowed, scale)
        prob_back = lax.dot_general(back, v_ref[:, cols], NT_DIMS, preferred_element_type=jnp.float32)
        inner = jnp.sum(shares * prob_back, axis=-1, keepdims=True)
        score_back = (shares * (prob_back - inner)).astype(jnp.bfloat16)
        dq_ref[:, cols] = (
            jnp.dot(score_back, keys, preferred_element_type=jnp.float32) * scale
        )
        dkv_ref[:, cols] = (
            lax.dot_general(score_back, query, TN_DIMS, preferred_element_type=jnp.float32) * scale
        ).astype(dkv_ref.dtype)
        half = q_ref.shape[1]
        dkv_ref[:, half + j * head_dim:half + (j + 1) * head_dim] = lax.dot_general(
            shares.astype(jnp.bfloat16), back, TN_DIMS, preferred_element_type=jnp.float32
        ).astype(dkv_ref.dtype)


def attention_forward(meta, query_rows, kv_rows, head_dim, scale):
    rows, width = query_rows.shape
    keys = kv_rows.shape[0]
    blocks = width // HEAD_BLOCK
    return pl.pallas_call(
        functools.partial(attn_fwd_kernel, head_dim, scale),
        out_shape=jax.ShapeDtypeStruct((rows, width), jnp.bfloat16),
        grid_spec=pltpu.PrefetchScalarGridSpec(
            num_scalar_prefetch=1,
            grid=(blocks,),
            in_specs=[
                pl.BlockSpec((rows, HEAD_BLOCK), lambda h, m: (0, h)),
                pl.BlockSpec((keys, HEAD_BLOCK), lambda h, m: (0, h)),
                pl.BlockSpec((keys, HEAD_BLOCK), lambda h, m: (0, h + blocks)),
            ],
            out_specs=pl.BlockSpec((rows, HEAD_BLOCK), lambda h, m: (0, h)),
        ),
        compiler_params=pltpu.CompilerParams(
            dimension_semantics=("arbitrary",), vmem_limit_bytes=48 * 1024 * 1024
        ),
        cost_estimate=pl.CostEstimate(
            flops=4 * rows * keys * width,
            transcendentals=rows * keys * (width // head_dim),
            bytes_accessed=2 * (2 * rows * width + 2 * keys * width),
        ),
    )(meta, query_rows, kv_rows, kv_rows)


def attention_backward(meta, query_rows, kv_rows, back_rows, head_dim, scale, first, count):
    rows, width = query_rows.shape
    keys = kv_rows.shape[0]
    blocks = width // HEAD_BLOCK
    part = count * HEAD_BLOCK
    return pl.pallas_call(
        functools.partial(attn_bwd_kernel, head_dim, scale),
        out_shape=(
            jax.ShapeDtypeStruct((rows, part), jnp.float32),
            jax.ShapeDtypeStruct((keys, 2 * part), jnp.bfloat16),
        ),
        grid_spec=pltpu.PrefetchScalarGridSpec(
            num_scalar_prefetch=1,
            grid=(count,),
            in_specs=[
                pl.BlockSpec((rows, HEAD_BLOCK), lambda h, m: (0, h + first)),
                pl.BlockSpec((keys, HEAD_BLOCK), lambda h, m: (0, h + first)),
                pl.BlockSpec((keys, HEAD_BLOCK), lambda h, m: (0, h + first + blocks)),
                pl.BlockSpec((rows, HEAD_BLOCK), lambda h, m: (0, h + first)),
            ],
            out_specs=[
                pl.BlockSpec((rows, HEAD_BLOCK), lambda h, m: (0, h)),
                pl.BlockSpec((keys, 2 * HEAD_BLOCK), lambda h, m: (0, h)),
            ],
        ),
        compiler_params=pltpu.CompilerParams(
            dimension_semantics=("arbitrary",), vmem_limit_bytes=48 * 1024 * 1024
        ),
        cost_estimate=pl.CostEstimate(
            flops=10 * rows * keys * part,
            transcendentals=rows * keys * (part // head_dim),
            bytes_accessed=2 * (3 * rows * part + 4 * keys * part) + 4 * rows * part,
        ),
    )(meta, query_rows, kv_rows, kv_rows, back_rows)


def rope_tables(positions, half):
    freq = jnp.exp(
        jnp.arange(half, dtype=jnp.int32).astype(jnp.float32) * (-math.log(10000.0) / half)
    )
    angle = positions.astype(jnp.float32)[:, None] * freq[None, :]
    return (jnp.cos(angle), jnp.sin(angle))


def rotate(value_rows, cosine, sine):
    half = value_rows.shape[-1] // 2
    first = value_rows[..., :half]
    second = value_rows[..., half:]
    return jnp.concatenate(
        [first * cosine - second * sine, second * cosine + first * sine], axis=-1
    )


def norm_apply(value_rows, gain):
    inverse = lax.rsqrt(jnp.mean(value_rows * value_rows, axis=-1, keepdims=True) + EPS)
    return (value_rows * inverse * gain, inverse)


def norm_back(value_rows, inverse, gain, upstream):
    scaled = upstream * gain
    gain_part = jnp.sum(upstream * value_rows * inverse, axis=(0, 1))
    inner = jnp.mean(scaled * value_rows, axis=-1, keepdims=True)
    return (inverse * scaled - value_rows * inverse * inverse * inverse * inner, gain_part)


def gain_block(first, second, width, leading=()):
    pad_cols = width - first.shape[-1] - second.shape[-1]
    row = jnp.concatenate(
        [first, second, jnp.zeros(leading + (pad_cols,), first.dtype)], axis=-1
    )
    row = row[..., None, :]
    pads = [(0, 0)] * len(leading) + [(0, GAIN_ROWS - 1), (0, 0)]
    return jnp.pad(row, pads)


def to_gathered(rows, block):
    lead = rows.shape[:-1]
    return jnp.swapaxes(rows.reshape(lead + (2, -1, block)), -3, -2).reshape(rows.shape)


def from_gathered(rows, block):
    lead = rows.shape[:-1]
    return jnp.swapaxes(rows.reshape(lead + (-1, 2, block)), -3, -2).reshape(rows.shape)


def zh_pair(mine, other):
    first = lax.axis_index("zh") == 0
    return jnp.stack([jnp.where(first, mine, other), jnp.where(first, other, mine)])


def fsdp_gather(pack):
    return yc_gather(z_exchange(pack))


def z_exchange(pack):
    return zh_pair(pack, lax.ppermute(pack, ("zh", "zl"), Z_CROSS))


def yc_gather(pair):
    both = lax.all_gather(pair, ("y", "core"), axis=0, tiled=False)
    return both.reshape((-1,) + pair.shape[1:])


def fsdp_reduce_scatter(grads):
    return z_combine(yc_reduce_scatter(grads))


def yc_reduce_scatter(grads):
    n_yc = grads.shape[0] // 2
    by_yc = grads
    block = grads.shape[1:]
    halves = lax.psum_scatter(
        by_yc.reshape((n_yc, 2 * block[0]) + block[1:]), ("y", "core"), scatter_dimension=0, tiled=False
    ).reshape((2,) + block)
    return halves


def z_combine(halves):
    zh = lax.axis_index("zh")
    mine = lax.dynamic_index_in_dim(halves, zh, axis=0, keepdims=False)
    theirs = lax.dynamic_index_in_dim(halves, 1 - zh, axis=0, keepdims=False)
    got = lax.ppermute(theirs, ("zh", "zl"), Z_CROSS)
    return (mine.astype(jnp.float32) + got.astype(jnp.float32)).astype(jnp.bfloat16)


def ctx_allreduce(part, n_ctx):
    total = part
    step = 1
    while step < n_ctx:
        other = lax.ppermute(total, CTX, [(j, j ^ step) for j in range(n_ctx)])
        total = (total.astype(jnp.float32) + other.astype(jnp.float32)).astype(jnp.bfloat16)
        step *= 2
    return total.astype(jnp.float32)


def body(
    tokens,
    first_value,
    query_weight,
    key_weight,
    value_weight,
    out_weight,
    gate_weight,
    up_weight,
    down_weight,
    prenorm_gain,
    midnorm_gain,
    cotangent,
    lengths,
    assignment,
):
    slots, rows, width = tokens.shape
    assert slots == 1
    head_count = H
    head_dim = width // head_count
    score_scale = head_dim ** (-0.5)
    n_fsdp = lax.axis_size(FSDP)
    n_ctx = lax.axis_size(CTX)
    total_len = rows * n_ctx
    w_rows = query_weight.shape[0]
    g_len = prenorm_gain.shape[0]
    ff = gate_weight.shape[1]
    d_rows = down_weight.shape[0]

    slot_count = assignment.shape[0]
    chosen = assignment[:, None] == jnp.arange(slot_count, dtype=jnp.int32)[None, :]
    lengths_all = jnp.sum(jnp.where(chosen, lengths[None, :], 0), axis=1)
    slot_lengths = lax.dynamic_slice_in_dim(lengths_all, lax.axis_index(FSDP) * slots, slots)
    query_places = lax.axis_index(CTX) * rows + jnp.arange(rows, dtype=jnp.int32)
    valid = query_places[None, :] < slot_lengths[:, None]
    cosine, sine = rope_tables(query_places, head_dim // 2)
    cos_rows = cosine[None, :, None, :]
    sin_rows = sine[None, :, None, :]
    valid_wide = valid[:, :, None]

    kv_pair = z_exchange(
        jnp.concatenate(
            [key_weight, value_weight, gain_block(prenorm_gain, midnorm_gain, width)], axis=0
        )
    )
    qod_pair = z_exchange(jnp.concatenate([query_weight, out_weight, down_weight], axis=0))
    gate_up_pair = z_exchange(jnp.concatenate([gate_weight, up_weight], axis=1))
    kv_wall = yc_gather(kv_pair)
    qod_pair, gate_up_pair, kv_wall = lax.optimization_barrier((qod_pair, gate_up_pair, kv_wall))
    qod_wall = yc_gather(qod_pair)
    gate_up_mat = yc_gather(gate_up_pair).reshape(n_fsdp * w_rows, 2 * ff)

    key_mat = kv_wall[:, 0:w_rows, :].reshape(n_fsdp * w_rows, width)
    value_mat = kv_wall[:, w_rows:2 * w_rows, :].reshape(n_fsdp * w_rows, width)
    prenorm_full = from_gathered(kv_wall[:, 2 * w_rows, 0:g_len].reshape(n_fsdp * g_len), g_len)
    midnorm_full = from_gathered(
        kv_wall[:, 2 * w_rows, g_len:2 * g_len].reshape(n_fsdp * g_len), g_len
    )
    query_mat = qod_wall[:, 0:w_rows, :].reshape(n_fsdp * w_rows, width)
    out_mat = qod_wall[:, w_rows:2 * w_rows, :].reshape(n_fsdp * w_rows, width)
    down_mat = qod_wall[:, 2 * w_rows:, :].reshape(n_fsdp * d_rows, width)

    tokens_wide = tokens.astype(jnp.float32)
    first_wide = first_value.astype(jnp.float32)
    normed, inverse = norm_apply(tokens_wide, prenorm_full.astype(jnp.float32))
    normed_low = normed.astype(jnp.bfloat16)
    normed_low_g = to_gathered(normed_low, w_rows)
    keyed = jnp.dot(normed_low_g, key_mat, preferred_element_type=jnp.float32)
    own_value = jnp.dot(normed_low_g, value_mat, preferred_element_type=jnp.float32)
    heads_shape = keyed.shape[:2] + (head_count, head_dim)
    key_rot = (
        rotate(keyed.reshape(heads_shape), cos_rows, sin_rows)
        .astype(jnp.bfloat16)
        .reshape(keyed.shape)
    )
    value_mix = (0.5 * own_value + 0.5 * first_wide).astype(jnp.bfloat16)

    kv_own = jnp.concatenate([key_rot, value_mix], axis=-1).reshape(rows, 2 * width)
    kv_all = lax.all_to_all(
        jnp.broadcast_to(kv_own[None], (n_ctx, rows, 2 * width)), CTX, 0, 0, tiled=False
    ).reshape(total_len, 2 * width)
    query_in, kv_all = lax.optimization_barrier((normed_low_g, kv_all))
    query = jnp.dot(query_in, query_mat, preferred_element_type=jnp.float32)
    query_rotated_rows = rotate(query.reshape(heads_shape), cos_rows, sin_rows).astype(jnp.bfloat16)
    meta = jnp.stack([lax.axis_index(CTX) * rows, slot_lengths[0]]).astype(jnp.int32)
    query_flat = query_rotated_rows.reshape(rows, width)
    mixed_low = attention_forward(
        meta, query_flat, kv_all, head_dim, score_scale
    ).reshape(slots, rows, width)

    mixed_low_g = to_gathered(mixed_low, w_rows)
    middle = tokens_wide + jnp.dot(mixed_low_g, out_mat, preferred_element_type=jnp.float32)
    normed_two, inverse_two = norm_apply(middle, midnorm_full.astype(jnp.float32))
    normed_two = normed_two.astype(jnp.bfloat16)
    normed_two_g = to_gathered(normed_two, w_rows)
    gate_up = jnp.dot(normed_two_g, gate_up_mat, preferred_element_type=jnp.float32)
    gate = gate_up[..., :ff]
    upper = gate_up[..., ff:]
    hidden = (jax.nn.silu(gate) * upper).astype(jnp.bfloat16)
    hidden_g = to_gathered(hidden, d_rows)
    branch = jnp.dot(hidden_g, down_mat, preferred_element_type=jnp.float32)
    layer_out = jnp.where(valid_wide, middle + branch, 0.0).astype(jnp.bfloat16)

    cot_wide = jnp.where(valid_wide, cotangent.astype(jnp.float32), 0.0)
    cot_low = cot_wide.astype(jnp.bfloat16)
    down_total = jnp.einsum("srf,sre->fe", hidden_g, cot_low, preferred_element_type=jnp.float32)
    hidden_back = from_gathered(
        jnp.einsum("sre,fe->srf", cot_low, down_mat, preferred_element_type=jnp.float32), d_rows
    )
    sigma = jax.nn.sigmoid(gate)
    gate_back = (hidden_back * upper * sigma * (1.0 + gate * (1.0 - sigma))).astype(jnp.bfloat16)
    upper_back = (hidden_back * gate * sigma).astype(jnp.bfloat16)
    gate_up_back = jnp.concatenate([gate_back, upper_back], axis=-1)
    gate_up_total = jnp.einsum(
        "srd,srf->df", normed_two_g, gate_up_back, preferred_element_type=jnp.float32
    )
    normed_two_back = jnp.einsum(
        "srf,df->srd", gate_up_back, gate_up_mat, preferred_element_type=jnp.float32
    )
    normed_two_back = from_gathered(normed_two_back, w_rows)
    middle_norm_back, midnorm_total = norm_back(
        middle, inverse_two, midnorm_full.astype(jnp.float32), normed_two_back
    )
    middle_back = cot_wide + middle_norm_back
    middle_low = middle_back.astype(jnp.bfloat16)
    out_total = jnp.einsum("srd,sre->de", mixed_low_g, middle_low, preferred_element_type=jnp.float32)

    down_share = ctx_allreduce(
        z_combine(yc_reduce_scatter(down_total.astype(jnp.bfloat16).reshape(n_fsdp, d_rows, width))),
        n_ctx,
    )
    mlp_grads = jnp.concatenate(
        [
            gate_up_total.reshape(n_fsdp, w_rows, 2 * ff),
            out_total.reshape(n_fsdp, w_rows, width),
        ],
        axis=2,
    ).astype(jnp.bfloat16)
    mlp_halves = yc_reduce_scatter(mlp_grads)

    blended_value_gradient = from_gathered(
        jnp.einsum("sre,de->srd", middle_low, out_mat, preferred_element_type=jnp.float32).astype(
            jnp.bfloat16
        ),
        w_rows,
    )
    n_head_blocks = width // HEAD_BLOCK
    half_blocks = 1
    back_flat = blended_value_gradient.reshape(rows, width)
    dq_parts = []
    kv_parts = []
    for first in range(0, n_head_blocks, half_blocks):
        dq_part, kv_back = attention_backward(
            meta, query_flat, kv_all, back_flat, head_dim, score_scale, first, half_blocks
        )
        dq_parts.append(dq_part)
        kv_parts.append(
            jnp.sum(
                lax.all_to_all(
                    kv_back.reshape(n_ctx, rows, kv_back.shape[1]), CTX, 0, 0, tiled=False
                ).astype(jnp.float32),
                axis=0,
            ).reshape(rows, half_blocks, 2, HEAD_BLOCK)
        )
    query_rot_back = jnp.concatenate(dq_parts, axis=-1).reshape(slots, rows, head_count, head_dim)
    key_value = jnp.concatenate(kv_parts, axis=1)
    key_rot_back = key_value[:, :, 0, :].reshape(slots, rows, head_count, head_dim)
    value_mix_back = key_value[:, :, 1, :].reshape(slots, rows, width)
    first_grad = 0.5 * value_mix_back
    query_back = (
        rotate(query_rot_back, cos_rows, -sin_rows).reshape(slots, rows, width).astype(jnp.bfloat16)
    )
    key_back = (
        rotate(key_rot_back, cos_rows, -sin_rows).reshape(slots, rows, width).astype(jnp.bfloat16)
    )
    value_back = (0.5 * value_mix_back).astype(jnp.bfloat16)
    query_total = jnp.einsum(
        "srd,sre->de", normed_low_g, query_back, preferred_element_type=jnp.float32
    )
    key_total = jnp.einsum("srd,sre->de", normed_low_g, key_back, preferred_element_type=jnp.float32)
    value_total = jnp.einsum(
        "srd,sre->de", normed_low_g, value_back, preferred_element_type=jnp.float32
    )
    normed_back = jnp.einsum(
        "sre,de->srd", query_back, query_mat, preferred_element_type=jnp.float32
    )
    normed_back = normed_back + jnp.einsum(
        "sre,de->srd", key_back, key_mat, preferred_element_type=jnp.float32
    )
    normed_back = normed_back + jnp.einsum(
        "sre,de->srd", value_back, value_mat, preferred_element_type=jnp.float32
    )
    normed_back = from_gathered(normed_back, w_rows)
    tokens_norm_back, prenorm_total = norm_back(
        tokens_wide, inverse, prenorm_full.astype(jnp.float32), normed_back
    )
    tokens_grad = middle_back + tokens_norm_back

    attn_grads = jnp.concatenate(
        [
            query_total.reshape(n_fsdp, w_rows, width),
            key_total.reshape(n_fsdp, w_rows, width),
            value_total.reshape(n_fsdp, w_rows, width),
            gain_block(
                to_gathered(prenorm_total, g_len).reshape(n_fsdp, g_len),
                to_gathered(midnorm_total, g_len).reshape(n_fsdp, g_len),
                width,
                leading=(n_fsdp,),
            ),
        ],
        axis=1,
    ).astype(jnp.bfloat16)
    attn_grads, mlp_halves = lax.optimization_barrier((attn_grads, mlp_halves))
    mlp_share = ctx_allreduce(z_combine(mlp_halves), n_ctx)
    attn_share = fsdp_reduce_scatter(attn_grads)
    attn_share = ctx_allreduce(attn_share, n_ctx)

    def attn_grad(i):
        return attn_share[i * w_rows:(i + 1) * w_rows]

    query_grad, key_grad, value_grad = (attn_grad(i) for i in range(3))
    prenorm_grad = attn_share[3 * w_rows, 0:g_len]
    midnorm_grad = attn_share[3 * w_rows, g_len:2 * g_len]
    gate_grad = mlp_share[:, 0:ff]
    up_grad = mlp_share[:, ff:2 * ff]
    down_grad = down_share
    out_grad = mlp_share[:, 2 * ff:]
    return (
        layer_out,
        tokens_grad,
        first_grad,
        query_grad,
        key_grad,
        value_grad,
        out_grad,
        gate_grad,
        up_grad,
        down_grad,
        prenorm_grad,
        midnorm_grad,
    )


def solution(mesh):
    zh = 2
    zl = 2
    n_f, n_c = mesh.devices.shape
    fine = jax.sharding.Mesh(
        mesh.devices.reshape(zh, n_f // (2 * zh), 2, zl, n_c // zl), FSDP + CTX
    )
    placed = (
        P(FSDP, CTX, None),
        P(FSDP, CTX, None),
        P(FSDP, None),
        P(FSDP, None),
        P(FSDP, None),
        P(FSDP, None),
        P(FSDP, None),
        P(FSDP, None),
        P(FSDP, None),
        P(FSDP),
        P(FSDP),
        P(FSDP, CTX, None),
        P(),
        P(),
    )
    return jax.shard_map(
        body,
        mesh=fine,
        in_specs=placed,
        out_specs=(
            P(FSDP, CTX, None),
            P(FSDP, CTX, None),
            P(FSDP, CTX, None),
            P(FSDP, None),
            P(FSDP, None),
            P(FSDP, None),
            P(FSDP, None),
            P(FSDP, None),
            P(FSDP, None),
            P(FSDP, None),
            P(FSDP),
            P(FSDP),
        ),
        check_vma=False,
    )
```

```python
import functools
import math

import jax
import jax.numpy as jnp
from jax import lax
from jax.experimental import pallas as pl
from jax.experimental.pallas import tpu as pltpu
from jax.sharding import PartitionSpec as P

H = 16


EPS = 1e-06
MASKED = -1e30
GAIN_ROWS = 16
FSDP = ("zh", "y", "core")
CTX = ("zl", "x")
Z_CROSS = [(0, 3), (3, 0), (1, 2), (2, 1)]


HEAD_BLOCK = 256
NT_DIMS = (((1,), (1,)), ((), ()))
TN_DIMS = (((0,), (0,)), ((), ()))


def allowed_keys(rows, keys, first_row, slot_len):
    query_pos = first_row + lax.broadcasted_iota(jnp.int32, (rows, keys), 0)
    key_pos = lax.broadcasted_iota(jnp.int32, (rows, keys), 1)
    return (key_pos <= query_pos) & (key_pos < slot_len)


def attention_shares(query, keys, allowed, scale):
    scores = lax.dot_general(query, keys, NT_DIMS, preferred_element_type=jnp.float32) * scale
    scores = jnp.where(allowed, scores, MASKED)
    peak = jnp.max(scores, axis=-1, keepdims=True)
    raised = jnp.exp(scores - peak)
    denominator = jnp.sum(raised, axis=-1, keepdims=True)
    return raised * (1.0 / denominator)


def attn_fwd_kernel(head_dim, scale, meta_ref, q_ref, k_ref, v_ref, o_ref):
    allowed = allowed_keys(q_ref.shape[0], k_ref.shape[0], meta_ref[0], meta_ref[1])
    for j in range(q_ref.shape[1] // head_dim):
        cols = slice(j * head_dim, (j + 1) * head_dim)
        shares = attention_shares(q_ref[:, cols], k_ref[:, cols], allowed, scale)
        mixed = jnp.dot(
            shares.astype(jnp.bfloat16), v_ref[:, cols], preferred_element_type=jnp.float32
        )
        o_ref[:, cols] = mixed.astype(o_ref.dtype)


def attn_bwd_kernel(head_dim, scale, meta_ref, q_ref, k_ref, v_ref, do_ref, dq_ref, dkv_ref):
    allowed = allowed_keys(q_ref.shape[0], k_ref.shape[0], meta_ref[0], meta_ref[1])
    for j in range(q_ref.shape[1] // head_dim):
        cols = slice(j * head_dim, (j + 1) * head_dim)
        query = q_ref[:, cols]
        keys = k_ref[:, cols]
        back = do_ref[:, cols]
        shares = attention_shares(query, keys, allowed, scale)
        prob_back = lax.dot_general(back, v_ref[:, cols], NT_DIMS, preferred_element_type=jnp.float32)
        inner = jnp.sum(shares * prob_back, axis=-1, keepdims=True)
        score_back = (shares * (prob_back - inner)).astype(jnp.bfloat16)
        dq_ref[:, cols] = (
            jnp.dot(score_back, keys, preferred_element_type=jnp.float32) * scale
        )
        dkv_ref[:, cols] = (
            lax.dot_general(score_back, query, TN_DIMS, preferred_element_type=jnp.float32) * scale
        ).astype(dkv_ref.dtype)
        half = q_ref.shape[1]
        dkv_ref[:, half + j * head_dim:half + (j + 1) * head_dim] = lax.dot_general(
            shares.astype(jnp.bfloat16), back, TN_DIMS, preferred_element_type=jnp.float32
        ).astype(dkv_ref.dtype)


def attention_forward(meta, query_rows, kv_rows, head_dim, scale):
    rows, width = query_rows.shape
    keys = kv_rows.shape[0]
    blocks = width // HEAD_BLOCK
    return pl.pallas_call(
        functools.partial(attn_fwd_kernel, head_dim, scale),
        out_shape=jax.ShapeDtypeStruct((rows, width), jnp.bfloat16),
        grid_spec=pltpu.PrefetchScalarGridSpec(
            num_scalar_prefetch=1,
            grid=(blocks,),
            in_specs=[
                pl.BlockSpec((rows, HEAD_BLOCK), lambda h, m: (0, h)),
                pl.BlockSpec((keys, HEAD_BLOCK), lambda h, m: (0, h)),
                pl.BlockSpec((keys, HEAD_BLOCK), lambda h, m: (0, h + blocks)),
            ],
            out_specs=pl.BlockSpec((rows, HEAD_BLOCK), lambda h, m: (0, h)),
        ),
        compiler_params=pltpu.CompilerParams(
            dimension_semantics=("arbitrary",), vmem_limit_bytes=48 * 1024 * 1024
        ),
        cost_estimate=pl.CostEstimate(
            flops=4 * rows * keys * width,
            transcendentals=rows * keys * (width // head_dim),
            bytes_accessed=2 * (2 * rows * width + 2 * keys * width),
        ),
    )(meta, query_rows, kv_rows, kv_rows)


def attention_backward(meta, query_rows, kv_rows, back_rows, head_dim, scale, first, count):
    rows, width = query_rows.shape
    keys = kv_rows.shape[0]
    blocks = width // HEAD_BLOCK
    part = count * HEAD_BLOCK
    return pl.pallas_call(
        functools.partial(attn_bwd_kernel, head_dim, scale),
        out_shape=(
            jax.ShapeDtypeStruct((rows, part), jnp.float32),
            jax.ShapeDtypeStruct((keys, 2 * part), jnp.bfloat16),
        ),
        grid_spec=pltpu.PrefetchScalarGridSpec(
            num_scalar_prefetch=1,
            grid=(count,),
            in_specs=[
                pl.BlockSpec((rows, HEAD_BLOCK), lambda h, m: (0, h + first)),
                pl.BlockSpec((keys, HEAD_BLOCK), lambda h, m: (0, h + first)),
                pl.BlockSpec((keys, HEAD_BLOCK), lambda h, m: (0, h + first + blocks)),
                pl.BlockSpec((rows, HEAD_BLOCK), lambda h, m: (0, h + first)),
            ],
            out_specs=[
                pl.BlockSpec((rows, HEAD_BLOCK), lambda h, m: (0, h)),
                pl.BlockSpec((keys, 2 * HEAD_BLOCK), lambda h, m: (0, h)),
            ],
        ),
        compiler_params=pltpu.CompilerParams(
            dimension_semantics=("arbitrary",), vmem_limit_bytes=48 * 1024 * 1024
        ),
        cost_estimate=pl.CostEstimate(
            flops=10 * rows * keys * part,
            transcendentals=rows * keys * (part // head_dim),
            bytes_accessed=2 * (3 * rows * part + 4 * keys * part) + 4 * rows * part,
        ),
    )(meta, query_rows, kv_rows, kv_rows, back_rows)


def rope_tables(positions, half):
    freq = jnp.exp(
        jnp.arange(half, dtype=jnp.int32).astype(jnp.float32) * (-math.log(10000.0) / half)
    )
    angle = positions.astype(jnp.float32)[:, None] * freq[None, :]
    return (jnp.cos(angle), jnp.sin(angle))


def rotate(value_rows, cosine, sine):
    half = value_rows.shape[-1] // 2
    first = value_rows[..., :half]
    second = value_rows[..., half:]
    return jnp.concatenate(
        [first * cosine - second * sine, second * cosine + first * sine], axis=-1
    )


def norm_apply(value_rows, gain):
    inverse = lax.rsqrt(jnp.mean(value_rows * value_rows, axis=-1, keepdims=True) + EPS)
    return (value_rows * inverse * gain, inverse)


def norm_back(value_rows, inverse, gain, upstream):
    scaled = upstream * gain
    gain_part = jnp.sum(upstream * value_rows * inverse, axis=(0, 1))
    inner = jnp.mean(scaled * value_rows, axis=-1, keepdims=True)
    return (inverse * scaled - value_rows * inverse * inverse * inverse * inner, gain_part)


def gain_block(first, second, width, leading=()):
    pad_cols = width - first.shape[-1] - second.shape[-1]
    row = jnp.concatenate(
        [first, second, jnp.zeros(leading + (pad_cols,), first.dtype)], axis=-1
    )
    row = row[..., None, :]
    pads = [(0, 0)] * len(leading) + [(0, GAIN_ROWS - 1), (0, 0)]
    return jnp.pad(row, pads)


def to_gathered(rows, block):
    lead = rows.shape[:-1]
    return jnp.swapaxes(rows.reshape(lead + (2, -1, block)), -3, -2).reshape(rows.shape)


def from_gathered(rows, block):
    lead = rows.shape[:-1]
    return jnp.swapaxes(rows.reshape(lead + (-1, 2, block)), -3, -2).reshape(rows.shape)


def zh_pair(mine, other):
    first = lax.axis_index("zh") == 0
    return jnp.stack([jnp.where(first, mine, other), jnp.where(first, other, mine)])


def fsdp_gather(pack):
    return yc_gather(z_exchange(pack))


def z_exchange(pack):
    return zh_pair(pack, lax.ppermute(pack, ("zh", "zl"), Z_CROSS))


def yc_gather(pair):
    both = lax.all_gather(pair, ("y", "core"), axis=0, tiled=False)
    return both.reshape((-1,) + pair.shape[1:])


def fsdp_reduce_scatter(grads):
    return z_combine(yc_reduce_scatter(grads))


def yc_reduce_scatter(grads):
    n_yc = grads.shape[0] // 2
    by_yc = grads
    block = grads.shape[1:]
    halves = lax.psum_scatter(
        by_yc.reshape((n_yc, 2 * block[0]) + block[1:]), ("y", "core"), scatter_dimension=0, tiled=False
    ).reshape((2,) + block)
    return halves


def z_combine(halves):
    zh = lax.axis_index("zh")
    mine = lax.dynamic_index_in_dim(halves, zh, axis=0, keepdims=False)
    theirs = lax.dynamic_index_in_dim(halves, 1 - zh, axis=0, keepdims=False)
    got = lax.ppermute(theirs, ("zh", "zl"), Z_CROSS)
    return (mine.astype(jnp.float32) + got.astype(jnp.float32)).astype(jnp.bfloat16)


def ctx_allreduce(part, n_ctx):
    total = part
    step = 1
    while step < n_ctx:
        other = lax.ppermute(total, CTX, [(j, j ^ step) for j in range(n_ctx)])
        total = (total.astype(jnp.float32) + other.astype(jnp.float32)).astype(jnp.bfloat16)
        step *= 2
    return total.astype(jnp.float32)


def body(
    tokens,
    first_value,
    query_weight,
    key_weight,
    value_weight,
    out_weight,
    gate_weight,
    up_weight,
    down_weight,
    prenorm_gain,
    midnorm_gain,
    cotangent,
    lengths,
    assignment,
):
    slots, rows, width = tokens.shape
    assert slots == 1
    head_count = H
    head_dim = width // head_count
    score_scale = head_dim ** (-0.5)
    n_fsdp = lax.axis_size(FSDP)
    n_ctx = lax.axis_size(CTX)
    total_len = rows * n_ctx
    w_rows = query_weight.shape[0]
    g_len = prenorm_gain.shape[0]
    ff = gate_weight.shape[1]
    d_rows = down_weight.shape[0]

    slot_count = assignment.shape[0]
    chosen = assignment[:, None] == jnp.arange(slot_count, dtype=jnp.int32)[None, :]
    lengths_all = jnp.sum(jnp.where(chosen, lengths[None, :], 0), axis=1)
    slot_lengths = lax.dynamic_slice_in_dim(lengths_all, lax.axis_index(FSDP) * slots, slots)
    query_places = lax.axis_index(CTX) * rows + jnp.arange(rows, dtype=jnp.int32)
    valid = query_places[None, :] < slot_lengths[:, None]
    cosine, sine = rope_tables(query_places, head_dim // 2)
    cos_rows = cosine[None, :, None, :]
    sin_rows = sine[None, :, None, :]
    valid_wide = valid[:, :, None]

    kv_pair = z_exchange(
        jnp.concatenate(
            [key_weight, value_weight, gain_block(prenorm_gain, midnorm_gain, width)], axis=0
        )
    )
    qod_pair = z_exchange(jnp.concatenate([query_weight, out_weight, down_weight], axis=0))
    gate_up_pair = z_exchange(jnp.concatenate([gate_weight, up_weight], axis=1))
    kv_wall = yc_gather(kv_pair)
    qod_pair, gate_up_pair, kv_wall = lax.optimization_barrier((qod_pair, gate_up_pair, kv_wall))
    qod_wall = yc_gather(qod_pair)
    gate_up_mat = yc_gather(gate_up_pair).reshape(n_fsdp * w_rows, 2 * ff)

    key_mat = kv_wall[:, 0:w_rows, :].reshape(n_fsdp * w_rows, width)
    value_mat = kv_wall[:, w_rows:2 * w_rows, :].reshape(n_fsdp * w_rows, width)
    prenorm_full = from_gathered(kv_wall[:, 2 * w_rows, 0:g_len].reshape(n_fsdp * g_len), g_len)
    midnorm_full = from_gathered(
        kv_wall[:, 2 * w_rows, g_len:2 * g_len].reshape(n_fsdp * g_len), g_len
    )
    query_mat = qod_wall[:, 0:w_rows, :].reshape(n_fsdp * w_rows, width)
    out_mat = qod_wall[:, w_rows:2 * w_rows, :].reshape(n_fsdp * w_rows, width)
    down_mat = qod_wall[:, 2 * w_rows:, :].reshape(n_fsdp * d_rows, width)

    tokens_wide = tokens.astype(jnp.float32)
    first_wide = first_value.astype(jnp.float32)
    normed, inverse = norm_apply(tokens_wide, prenorm_full.astype(jnp.float32))
    normed_low = normed.astype(jnp.bfloat16)
    normed_low_g = to_gathered(normed_low, w_rows)
    keyed = jnp.dot(normed_low_g, key_mat, preferred_element_type=jnp.float32)
    own_value = jnp.dot(normed_low_g, value_mat, preferred_element_type=jnp.float32)
    heads_shape = keyed.shape[:2] + (head_count, head_dim)
    key_rot = (
        rotate(keyed.reshape(heads_shape), cos_rows, sin_rows)
        .astype(jnp.bfloat16)
        .reshape(keyed.shape)
    )
    value_mix = (0.5 * own_value + 0.5 * first_wide).astype(jnp.bfloat16)

    half_width = width // 2
    key_rot = key_rot.reshape(rows, width)
    value_mix = value_mix.reshape(rows, width)
    kv_halves = []
    for part in range(2):
        cols = slice(part * half_width, (part + 1) * half_width)
        kv_own = jnp.concatenate([key_rot[:, cols], value_mix[:, cols]], axis=-1)
        kv_halves.append(
            lax.all_to_all(
                jnp.broadcast_to(kv_own[None], (n_ctx, rows, width)), CTX, 0, 0, tiled=False
            ).reshape(total_len, width)
        )
    query_in, kv_halves[0] = lax.optimization_barrier((normed_low_g, kv_halves[0]))
    query = jnp.dot(query_in, query_mat, preferred_element_type=jnp.float32)
    query_rotated_rows = rotate(query.reshape(heads_shape), cos_rows, sin_rows).astype(jnp.bfloat16)
    meta = jnp.stack([lax.axis_index(CTX) * rows, slot_lengths[0]]).astype(jnp.int32)
    query_flat = query_rotated_rows.reshape(rows, width)
    query_halves = [query_flat[:, :half_width], query_flat[:, half_width:]]
    mixed_first = attention_forward(meta, query_halves[0], kv_halves[0], head_dim, score_scale)
    mixed_first, kv_halves[1] = lax.optimization_barrier((mixed_first, kv_halves[1]))
    mixed_low = jnp.concatenate(
        [
            mixed_first,
            attention_forward(meta, query_halves[1], kv_halves[1], head_dim, score_scale),
        ],
        axis=-1,
    ).reshape(slots, rows, width)

    mixed_low_g = to_gathered(mixed_low, w_rows)
    middle = tokens_wide + jnp.dot(mixed_low_g, out_mat, preferred_element_type=jnp.float32)
    normed_two, inverse_two = norm_apply(middle, midnorm_full.astype(jnp.float32))
    normed_two = normed_two.astype(jnp.bfloat16)
    normed_two_g = to_gathered(normed_two, w_rows)
    gate_up = jnp.dot(normed_two_g, gate_up_mat, preferred_element_type=jnp.float32)
    gate = gate_up[..., :ff]
    upper = gate_up[..., ff:]
    hidden = (jax.nn.silu(gate) * upper).astype(jnp.bfloat16)
    hidden_g = to_gathered(hidden, d_rows)
    branch = jnp.dot(hidden_g, down_mat, preferred_element_type=jnp.float32)
    layer_out = jnp.where(valid_wide, middle + branch, 0.0).astype(jnp.bfloat16)

    cot_wide = jnp.where(valid_wide, cotangent.astype(jnp.float32), 0.0)
    cot_low = cot_wide.astype(jnp.bfloat16)
    down_total = jnp.einsum("srf,sre->fe", hidden_g, cot_low, preferred_element_type=jnp.float32)
    hidden_back = from_gathered(
        jnp.einsum("sre,fe->srf", cot_low, down_mat, preferred_element_type=jnp.float32), d_rows
    )
    sigma = jax.nn.sigmoid(gate)
    gate_back = (hidden_back * upper * sigma * (1.0 + gate * (1.0 - sigma))).astype(jnp.bfloat16)
    upper_back = (hidden_back * gate * sigma).astype(jnp.bfloat16)
    gate_up_back = jnp.concatenate([gate_back, upper_back], axis=-1)
    gate_up_total = jnp.einsum(
        "srd,srf->df", normed_two_g, gate_up_back, preferred_element_type=jnp.float32
    )
    normed_two_back = jnp.einsum(
        "srf,df->srd", gate_up_back, gate_up_mat, preferred_element_type=jnp.float32
    )
    normed_two_back = from_gathered(normed_two_back, w_rows)
    middle_norm_back, midnorm_total = norm_back(
        middle, inverse_two, midnorm_full.astype(jnp.float32), normed_two_back
    )
    middle_back = cot_wide + middle_norm_back
    middle_low = middle_back.astype(jnp.bfloat16)
    out_total = jnp.einsum("srd,sre->de", mixed_low_g, middle_low, preferred_element_type=jnp.float32)

    down_share = ctx_allreduce(
        z_combine(yc_reduce_scatter(down_total.astype(jnp.bfloat16).reshape(n_fsdp, d_rows, width))),
        n_ctx,
    )
    mlp_grads = jnp.concatenate(
        [
            gate_up_total.reshape(n_fsdp, w_rows, 2 * ff),
            out_total.reshape(n_fsdp, w_rows, width),
        ],
        axis=2,
    ).astype(jnp.bfloat16)
    mlp_halves = yc_reduce_scatter(mlp_grads)

    blended_value_gradient = from_gathered(
        jnp.einsum("sre,de->srd", middle_low, out_mat, preferred_element_type=jnp.float32).astype(
            jnp.bfloat16
        ),
        w_rows,
    )
    n_head_blocks = width // HEAD_BLOCK
    half_blocks = n_head_blocks // 2
    back_flat = blended_value_gradient.reshape(rows, width)
    back_halves = [back_flat[:, :half_width], back_flat[:, half_width:]]
    dq_parts = []
    kv_parts = []
    for part in range(2):
        dq_part, kv_back = attention_backward(
            meta,
            query_halves[part],
            kv_halves[part],
            back_halves[part],
            head_dim,
            score_scale,
            0,
            half_blocks,
        )
        dq_parts.append(dq_part)
        kv_parts.append(
            jnp.sum(
                lax.all_to_all(
                    kv_back.reshape(n_ctx, rows, kv_back.shape[1]), CTX, 0, 0, tiled=False
                ).astype(jnp.float32),
                axis=0,
            ).reshape(rows, half_blocks, 2, HEAD_BLOCK)
        )
    query_rot_back = jnp.concatenate(dq_parts, axis=-1).reshape(slots, rows, head_count, head_dim)
    key_value = jnp.concatenate(kv_parts, axis=1)
    key_rot_back = key_value[:, :, 0, :].reshape(slots, rows, head_count, head_dim)
    value_mix_back = key_value[:, :, 1, :].reshape(slots, rows, width)
    first_grad = 0.5 * value_mix_back
    query_back = (
        rotate(query_rot_back, cos_rows, -sin_rows).reshape(slots, rows, width).astype(jnp.bfloat16)
    )
    key_back = (
        rotate(key_rot_back, cos_rows, -sin_rows).reshape(slots, rows, width).astype(jnp.bfloat16)
    )
    value_back = (0.5 * value_mix_back).astype(jnp.bfloat16)
    query_total = jnp.einsum(
        "srd,sre->de", normed_low_g, query_back, preferred_element_type=jnp.float32
    )
    key_total = jnp.einsum("srd,sre->de", normed_low_g, key_back, preferred_element_type=jnp.float32)
    value_total = jnp.einsum(
        "srd,sre->de", normed_low_g, value_back, preferred_element_type=jnp.float32
    )
    normed_back = jnp.einsum(
        "sre,de->srd", query_back, query_mat, preferred_element_type=jnp.float32
    )
    normed_back = normed_back + jnp.einsum(
        "sre,de->srd", key_back, key_mat, preferred_element_type=jnp.float32
    )
    normed_back = normed_back + jnp.einsum(
        "sre,de->srd", value_back, value_mat, preferred_element_type=jnp.float32
    )
    normed_back = from_gathered(normed_back, w_rows)
    tokens_norm_back, prenorm_total = norm_back(
        tokens_wide, inverse, prenorm_full.astype(jnp.float32), normed_back
    )
    tokens_grad = middle_back + tokens_norm_back

    attn_grads = jnp.concatenate(
        [
            query_total.reshape(n_fsdp, w_rows, width),
            key_total.reshape(n_fsdp, w_rows, width),
            value_total.reshape(n_fsdp, w_rows, width),
            gain_block(
                to_gathered(prenorm_total, g_len).reshape(n_fsdp, g_len),
                to_gathered(midnorm_total, g_len).reshape(n_fsdp, g_len),
                width,
                leading=(n_fsdp,),
            ),
        ],
        axis=1,
    ).astype(jnp.bfloat16)
    attn_grads, mlp_halves = lax.optimization_barrier((attn_grads, mlp_halves))
    mlp_share = ctx_allreduce(z_combine(mlp_halves), n_ctx)
    attn_share = fsdp_reduce_scatter(attn_grads)
    attn_share = ctx_allreduce(attn_share, n_ctx)

    def attn_grad(i):
        return attn_share[i * w_rows:(i + 1) * w_rows]

    query_grad, key_grad, value_grad = (attn_grad(i) for i in range(3))
    prenorm_grad = attn_share[3 * w_rows, 0:g_len]
    midnorm_grad = attn_share[3 * w_rows, g_len:2 * g_len]
    gate_grad = mlp_share[:, 0:ff]
    up_grad = mlp_share[:, ff:2 * ff]
    down_grad = down_share
    out_grad = mlp_share[:, 2 * ff:]
    return (
        layer_out,
        tokens_grad,
        first_grad,
        query_grad,
        key_grad,
        value_grad,
        out_grad,
        gate_grad,
        up_grad,
        down_grad,
        prenorm_grad,
        midnorm_grad,
    )


def solution(mesh):
    zh = 2
    zl = 2
    n_f, n_c = mesh.devices.shape
    fine = jax.sharding.Mesh(
        mesh.devices.reshape(zh, n_f // (2 * zh), 2, zl, n_c // zl), FSDP + CTX
    )
    placed = (
        P(FSDP, CTX, None),
        P(FSDP, CTX, None),
        P(FSDP, None),
        P(FSDP, None),
        P(FSDP, None),
        P(FSDP, None),
        P(FSDP, None),
        P(FSDP, None),
        P(FSDP, None),
        P(FSDP),
        P(FSDP),
        P(FSDP, CTX, None),
        P(),
        P(),
    )
    return jax.shard_map(
        body,
        mesh=fine,
        in_specs=placed,
        out_specs=(
            P(FSDP, CTX, None),
            P(FSDP, CTX, None),
            P(FSDP, CTX, None),
            P(FSDP, None),
            P(FSDP, None),
            P(FSDP, None),
            P(FSDP, None),
            P(FSDP, None),
            P(FSDP, None),
            P(FSDP, None),
            P(FSDP),
            P(FSDP),
        ),
        check_vma=False,
    )
```

```python
import functools
import math

import jax
import jax.numpy as jnp
from jax import lax
from jax.experimental import pallas as pl
from jax.experimental.pallas import tpu as pltpu
from jax.sharding import PartitionSpec as P

H = 16


EPS = 1e-06
MASKED = -1e30
GAIN_ROWS = 16
FSDP = ("zh", "y", "core")
CTX = ("zl", "x")
Z_CROSS = [(0, 3), (3, 0), (1, 2), (2, 1)]


HEAD_BLOCK = 256
NT_DIMS = (((1,), (1,)), ((), ()))
TN_DIMS = (((0,), (0,)), ((), ()))


def allowed_keys(rows, keys, first_row, slot_len):
    query_pos = first_row + lax.broadcasted_iota(jnp.int32, (rows, keys), 0)
    key_pos = lax.broadcasted_iota(jnp.int32, (rows, keys), 1)
    return (key_pos <= query_pos) & (key_pos < slot_len)


def attention_shares(query, keys, allowed, scale):
    scores = lax.dot_general(query, keys, NT_DIMS, preferred_element_type=jnp.float32) * scale
    scores = jnp.where(allowed, scores, MASKED)
    peak = jnp.max(scores, axis=-1, keepdims=True)
    raised = jnp.exp(scores - peak)
    denominator = jnp.sum(raised, axis=-1, keepdims=True)
    return raised * (1.0 / denominator)


def attn_fwd_kernel(head_dim, scale, meta_ref, q_ref, k_ref, v_ref, o_ref):
    allowed = allowed_keys(q_ref.shape[0], k_ref.shape[0], meta_ref[0], meta_ref[1])
    for j in range(q_ref.shape[1] // head_dim):
        cols = slice(j * head_dim, (j + 1) * head_dim)
        shares = attention_shares(q_ref[:, cols], k_ref[:, cols], allowed, scale)
        mixed = jnp.dot(
            shares.astype(jnp.bfloat16), v_ref[:, cols], preferred_element_type=jnp.float32
        )
        o_ref[:, cols] = mixed.astype(o_ref.dtype)


def attn_bwd_kernel(head_dim, scale, meta_ref, q_ref, k_ref, v_ref, do_ref, dq_ref, dkv_ref):
    allowed = allowed_keys(q_ref.shape[0], k_ref.shape[0], meta_ref[0], meta_ref[1])
    for j in range(q_ref.shape[1] // head_dim):
        cols = slice(j * head_dim, (j + 1) * head_dim)
        query = q_ref[:, cols]
        keys = k_ref[:, cols]
        back = do_ref[:, cols]
        shares = attention_shares(query, keys, allowed, scale)
        prob_back = lax.dot_general(back, v_ref[:, cols], NT_DIMS, preferred_element_type=jnp.float32)
        inner = jnp.sum(shares * prob_back, axis=-1, keepdims=True)
        score_back = (shares * (prob_back - inner)).astype(jnp.bfloat16)
        dq_ref[:, cols] = (
            jnp.dot(score_back, keys, preferred_element_type=jnp.float32) * scale
        )
        dkv_ref[:, cols] = (
            lax.dot_general(score_back, query, TN_DIMS, preferred_element_type=jnp.float32) * scale
        ).astype(dkv_ref.dtype)
        half = q_ref.shape[1]
        dkv_ref[:, half + j * head_dim:half + (j + 1) * head_dim] = lax.dot_general(
            shares.astype(jnp.bfloat16), back, TN_DIMS, preferred_element_type=jnp.float32
        ).astype(dkv_ref.dtype)


def attention_forward(meta, query_rows, kv_rows, head_dim, scale):
    rows, width = query_rows.shape
    keys = kv_rows.shape[0]
    blocks = width // HEAD_BLOCK
    return pl.pallas_call(
        functools.partial(attn_fwd_kernel, head_dim, scale),
        out_shape=jax.ShapeDtypeStruct((rows, width), jnp.bfloat16),
        grid_spec=pltpu.PrefetchScalarGridSpec(
            num_scalar_prefetch=1,
            grid=(blocks,),
            in_specs=[
                pl.BlockSpec((rows, HEAD_BLOCK), lambda h, m: (0, h)),
                pl.BlockSpec((keys, HEAD_BLOCK), lambda h, m: (0, h)),
                pl.BlockSpec((keys, HEAD_BLOCK), lambda h, m: (0, h + blocks)),
            ],
            out_specs=pl.BlockSpec((rows, HEAD_BLOCK), lambda h, m: (0, h)),
        ),
        compiler_params=pltpu.CompilerParams(
            dimension_semantics=("arbitrary",), vmem_limit_bytes=48 * 1024 * 1024
        ),
        cost_estimate=pl.CostEstimate(
            flops=4 * rows * keys * width,
            transcendentals=rows * keys * (width // head_dim),
            bytes_accessed=2 * (2 * rows * width + 2 * keys * width),
        ),
    )(meta, query_rows, kv_rows, kv_rows)


def attention_backward(meta, query_rows, kv_rows, back_rows, head_dim, scale, first, count):
    rows, width = query_rows.shape
    keys = kv_rows.shape[0]
    blocks = width // HEAD_BLOCK
    part = count * HEAD_BLOCK
    return pl.pallas_call(
        functools.partial(attn_bwd_kernel, head_dim, scale),
        out_shape=(
            jax.ShapeDtypeStruct((rows, part), jnp.float32),
            jax.ShapeDtypeStruct((keys, 2 * part), jnp.bfloat16),
        ),
        grid_spec=pltpu.PrefetchScalarGridSpec(
            num_scalar_prefetch=1,
            grid=(count,),
            in_specs=[
                pl.BlockSpec((rows, HEAD_BLOCK), lambda h, m: (0, h + first)),
                pl.BlockSpec((keys, HEAD_BLOCK), lambda h, m: (0, h + first)),
                pl.BlockSpec((keys, HEAD_BLOCK), lambda h, m: (0, h + first + blocks)),
                pl.BlockSpec((rows, HEAD_BLOCK), lambda h, m: (0, h + first)),
            ],
            out_specs=[
                pl.BlockSpec((rows, HEAD_BLOCK), lambda h, m: (0, h)),
                pl.BlockSpec((keys, 2 * HEAD_BLOCK), lambda h, m: (0, h)),
            ],
        ),
        compiler_params=pltpu.CompilerParams(
            dimension_semantics=("arbitrary",), vmem_limit_bytes=48 * 1024 * 1024
        ),
        cost_estimate=pl.CostEstimate(
            flops=10 * rows * keys * part,
            transcendentals=rows * keys * (part // head_dim),
            bytes_accessed=2 * (3 * rows * part + 4 * keys * part) + 4 * rows * part,
        ),
    )(meta, query_rows, kv_rows, kv_rows, back_rows)


def rope_tables(positions, half):
    freq = jnp.exp(
        jnp.arange(half, dtype=jnp.int32).astype(jnp.float32) * (-math.log(10000.0) / half)
    )
    angle = positions.astype(jnp.float32)[:, None] * freq[None, :]
    return (jnp.cos(angle), jnp.sin(angle))


def rotate(value_rows, cosine, sine):
    half = value_rows.shape[-1] // 2
    first = value_rows[..., :half]
    second = value_rows[..., half:]
    return jnp.concatenate(
        [first * cosine - second * sine, second * cosine + first * sine], axis=-1
    )


def norm_apply(value_rows, gain):
    inverse = lax.rsqrt(jnp.mean(value_rows * value_rows, axis=-1, keepdims=True) + EPS)
    return (value_rows * inverse * gain, inverse)


def norm_back(value_rows, inverse, gain, upstream):
    scaled = upstream * gain
    gain_part = jnp.sum(upstream * value_rows * inverse, axis=(0, 1))
    inner = jnp.mean(scaled * value_rows, axis=-1, keepdims=True)
    return (inverse * scaled - value_rows * inverse * inverse * inverse * inner, gain_part)


def gain_block(first, second, width, leading=()):
    pad_cols = width - first.shape[-1] - second.shape[-1]
    row = jnp.concatenate(
        [first, second, jnp.zeros(leading + (pad_cols,), first.dtype)], axis=-1
    )
    row = row[..., None, :]
    pads = [(0, 0)] * len(leading) + [(0, GAIN_ROWS - 1), (0, 0)]
    return jnp.pad(row, pads)


def to_gathered(rows, block):
    lead = rows.shape[:-1]
    return jnp.swapaxes(rows.reshape(lead + (2, -1, block)), -3, -2).reshape(rows.shape)


def from_gathered(rows, block):
    lead = rows.shape[:-1]
    return jnp.swapaxes(rows.reshape(lead + (-1, 2, block)), -3, -2).reshape(rows.shape)


def zh_pair(mine, other):
    first = lax.axis_index("zh") == 0
    return jnp.stack([jnp.where(first, mine, other), jnp.where(first, other, mine)])


def fsdp_gather(pack):
    return yc_gather(z_exchange(pack))


def z_exchange(pack):
    return zh_pair(pack, lax.ppermute(pack, ("zh", "zl"), Z_CROSS))


def yc_gather(pair):
    both = lax.all_gather(pair, ("y", "core"), axis=0, tiled=False)
    return both.reshape((-1,) + pair.shape[1:])


def fsdp_reduce_scatter(grads):
    return z_combine(yc_reduce_scatter(grads))


def yc_reduce_scatter(grads):
    n_yc = grads.shape[0] // 2
    by_yc = grads
    block = grads.shape[1:]
    halves = lax.psum_scatter(
        by_yc.reshape((n_yc, 2 * block[0]) + block[1:]), ("y", "core"), scatter_dimension=0, tiled=False
    ).reshape((2,) + block)
    return halves


def z_combine(halves):
    zh = lax.axis_index("zh")
    mine = lax.dynamic_index_in_dim(halves, zh, axis=0, keepdims=False)
    theirs = lax.dynamic_index_in_dim(halves, 1 - zh, axis=0, keepdims=False)
    got = lax.ppermute(theirs, ("zh", "zl"), Z_CROSS)
    return (mine.astype(jnp.float32) + got.astype(jnp.float32)).astype(jnp.bfloat16)


def ctx_allreduce(part, n_ctx):
    total = part
    step = 1
    while step < n_ctx:
        other = lax.ppermute(total, CTX, [(j, j ^ step) for j in range(n_ctx)])
        total = (total.astype(jnp.float32) + other.astype(jnp.float32)).astype(jnp.bfloat16)
        step *= 2
    return total.astype(jnp.float32)


def body(
    tokens,
    first_value,
    query_weight,
    key_weight,
    value_weight,
    out_weight,
    gate_weight,
    up_weight,
    down_weight,
    prenorm_gain,
    midnorm_gain,
    cotangent,
    lengths,
    assignment,
):
    slots, rows, width = tokens.shape
    assert slots == 1
    head_count = H
    head_dim = width // head_count
    score_scale = head_dim ** (-0.5)
    n_fsdp = lax.axis_size(FSDP)
    n_ctx = lax.axis_size(CTX)
    total_len = rows * n_ctx
    w_rows = query_weight.shape[0]
    g_len = prenorm_gain.shape[0]
    ff = gate_weight.shape[1]
    d_rows = down_weight.shape[0]

    slot_count = assignment.shape[0]
    chosen = assignment[:, None] == jnp.arange(slot_count, dtype=jnp.int32)[None, :]
    lengths_all = jnp.sum(jnp.where(chosen, lengths[None, :], 0), axis=1)
    slot_lengths = lax.dynamic_slice_in_dim(lengths_all, lax.axis_index(FSDP) * slots, slots)
    query_places = lax.axis_index(CTX) * rows + jnp.arange(rows, dtype=jnp.int32)
    valid = query_places[None, :] < slot_lengths[:, None]
    cosine, sine = rope_tables(query_places, head_dim // 2)
    cos_rows = cosine[None, :, None, :]
    sin_rows = sine[None, :, None, :]
    valid_wide = valid[:, :, None]

    kv_pair = z_exchange(
        jnp.concatenate(
            [key_weight, value_weight, gain_block(prenorm_gain, midnorm_gain, width)], axis=0
        )
    )
    qod_pair = z_exchange(jnp.concatenate([query_weight, out_weight, down_weight], axis=0))
    gate_up_pair = z_exchange(jnp.concatenate([gate_weight, up_weight], axis=1))
    kv_wall = yc_gather(kv_pair)
    qod_pair, gate_up_pair, kv_wall = lax.optimization_barrier((qod_pair, gate_up_pair, kv_wall))
    qod_wall = yc_gather(qod_pair)
    gate_up_mat = yc_gather(gate_up_pair).reshape(n_fsdp * w_rows, 2 * ff)

    key_mat = kv_wall[:, 0:w_rows, :].reshape(n_fsdp * w_rows, width)
    value_mat = kv_wall[:, w_rows:2 * w_rows, :].reshape(n_fsdp * w_rows, width)
    prenorm_full = from_gathered(kv_wall[:, 2 * w_rows, 0:g_len].reshape(n_fsdp * g_len), g_len)
    midnorm_full = from_gathered(
        kv_wall[:, 2 * w_rows, g_len:2 * g_len].reshape(n_fsdp * g_len), g_len
    )
    query_mat = qod_wall[:, 0:w_rows, :].reshape(n_fsdp * w_rows, width)
    out_mat = qod_wall[:, w_rows:2 * w_rows, :].reshape(n_fsdp * w_rows, width)
    down_mat = qod_wall[:, 2 * w_rows:, :].reshape(n_fsdp * d_rows, width)

    tokens_wide = tokens.astype(jnp.float32)
    first_wide = first_value.astype(jnp.float32)
    normed, inverse = norm_apply(tokens_wide, prenorm_full.astype(jnp.float32))
    normed_low = normed.astype(jnp.bfloat16)
    normed_low_g = to_gathered(normed_low, w_rows)
    keyed = jnp.dot(normed_low_g, key_mat, preferred_element_type=jnp.float32)
    own_value = jnp.dot(normed_low_g, value_mat, preferred_element_type=jnp.float32)
    heads_shape = keyed.shape[:2] + (head_count, head_dim)
    key_rot = (
        rotate(keyed.reshape(heads_shape), cos_rows, sin_rows)
        .astype(jnp.bfloat16)
        .reshape(keyed.shape)
    )
    value_mix = (0.5 * own_value + 0.5 * first_wide).astype(jnp.bfloat16)

    half_width = width // 2
    key_rot = key_rot.reshape(rows, width)
    value_mix = value_mix.reshape(rows, width)
    kv_halves = []
    for part in range(2):
        cols = slice(part * half_width, (part + 1) * half_width)
        kv_own = jnp.concatenate([key_rot[:, cols], value_mix[:, cols]], axis=-1)
        kv_halves.append(
            lax.all_to_all(
                jnp.broadcast_to(kv_own[None], (n_ctx, rows, width)), CTX, 0, 0, tiled=False
            ).reshape(total_len, width)
        )
    query_in, kv_halves[0] = lax.optimization_barrier((normed_low_g, kv_halves[0]))
    query = jnp.dot(query_in, query_mat, preferred_element_type=jnp.float32)
    query_rotated_rows = rotate(query.reshape(heads_shape), cos_rows, sin_rows).astype(jnp.bfloat16)
    meta = jnp.stack([lax.axis_index(CTX) * rows, slot_lengths[0]]).astype(jnp.int32)
    query_flat = query_rotated_rows.reshape(rows, width)
    query_halves = [query_flat[:, :half_width], query_flat[:, half_width:]]
    mixed_first = attention_forward(meta, query_halves[0], kv_halves[0], head_dim, score_scale)
    mixed_first, kv_halves[1] = lax.optimization_barrier((mixed_first, kv_halves[1]))
    mixed_low = jnp.concatenate(
        [
            mixed_first,
            attention_forward(meta, query_halves[1], kv_halves[1], head_dim, score_scale),
        ],
        axis=-1,
    ).reshape(slots, rows, width)

    mixed_low_g = to_gathered(mixed_low, w_rows)
    middle = tokens_wide + jnp.dot(mixed_low_g, out_mat, preferred_element_type=jnp.float32)
    normed_two, inverse_two = norm_apply(middle, midnorm_full.astype(jnp.float32))
    normed_two = normed_two.astype(jnp.bfloat16)
    normed_two_g = to_gathered(normed_two, w_rows)
    gate_up = jnp.dot(normed_two_g, gate_up_mat, preferred_element_type=jnp.float32)
    gate = gate_up[..., :ff]
    upper = gate_up[..., ff:]
    hidden = (jax.nn.silu(gate) * upper).astype(jnp.bfloat16)
    hidden_g = to_gathered(hidden, d_rows)
    branch = jnp.dot(hidden_g, down_mat, preferred_element_type=jnp.float32)
    layer_out = jnp.where(valid_wide, middle + branch, 0.0).astype(jnp.bfloat16)

    cot_wide = jnp.where(valid_wide, cotangent.astype(jnp.float32), 0.0)
    cot_low = cot_wide.astype(jnp.bfloat16)
    down_total = jnp.einsum("srf,sre->fe", hidden_g, cot_low, preferred_element_type=jnp.float32)
    hidden_back = from_gathered(
        jnp.einsum("sre,fe->srf", cot_low, down_mat, preferred_element_type=jnp.float32), d_rows
    )
    sigma = jax.nn.sigmoid(gate)
    gate_back = (hidden_back * upper * sigma * (1.0 + gate * (1.0 - sigma))).astype(jnp.bfloat16)
    upper_back = (hidden_back * gate * sigma).astype(jnp.bfloat16)
    gate_up_back = jnp.concatenate([gate_back, upper_back], axis=-1)
    gate_up_total = jnp.einsum(
        "srd,srf->df", normed_two_g, gate_up_back, preferred_element_type=jnp.float32
    )
    normed_two_back = jnp.einsum(
        "srf,df->srd", gate_up_back, gate_up_mat, preferred_element_type=jnp.float32
    )
    normed_two_back = from_gathered(normed_two_back, w_rows)
    middle_norm_back, midnorm_total = norm_back(
        middle, inverse_two, midnorm_full.astype(jnp.float32), normed_two_back
    )
    middle_back = cot_wide + middle_norm_back
    middle_low = middle_back.astype(jnp.bfloat16)
    out_total = jnp.einsum("srd,sre->de", mixed_low_g, middle_low, preferred_element_type=jnp.float32)

    down_share = ctx_allreduce(
        z_combine(yc_reduce_scatter(down_total.astype(jnp.bfloat16).reshape(n_fsdp, d_rows, width))),
        n_ctx,
    )
    mlp_grads = jnp.concatenate(
        [
            gate_up_total.reshape(n_fsdp, w_rows, 2 * ff),
            out_total.reshape(n_fsdp, w_rows, width),
        ],
        axis=2,
    ).astype(jnp.bfloat16)
    mlp_halves = yc_reduce_scatter(mlp_grads)

    blended_value_gradient = from_gathered(
        jnp.einsum("sre,de->srd", middle_low, out_mat, preferred_element_type=jnp.float32).astype(
            jnp.bfloat16
        ),
        w_rows,
    )
    n_head_blocks = width // HEAD_BLOCK
    half_blocks = n_head_blocks // 2
    back_flat = blended_value_gradient.reshape(rows, width)
    back_halves = [back_flat[:, :half_width], back_flat[:, half_width:]]
    dq_parts = []
    kv_parts = []
    for part in range(2):
        dq_part, kv_back = attention_backward(
            meta,
            query_halves[part],
            kv_halves[part],
            back_halves[part],
            head_dim,
            score_scale,
            0,
            half_blocks,
        )
        dq_parts.append(dq_part)
        kv_parts.append(
            jnp.sum(
                lax.all_to_all(
                    kv_back.reshape(n_ctx, rows, kv_back.shape[1]), CTX, 0, 0, tiled=False
                ).astype(jnp.float32),
                axis=0,
            ).reshape(rows, half_blocks, 2, HEAD_BLOCK)
        )
    query_rot_back = jnp.concatenate(dq_parts, axis=-1).reshape(slots, rows, head_count, head_dim)
    key_totals, value_totals, value_mix_backs, kv_normed_back = [], [], [], []
    for part, key_value in enumerate(kv_parts):
        cols = slice(part * half_width, (part + 1) * half_width)
        key_rot_back = key_value[:, :, 0, :].reshape(slots, rows, head_count // 2, head_dim)
        value_mix_back = key_value[:, :, 1, :].reshape(slots, rows, half_width)
        key_back = (
            rotate(key_rot_back, cos_rows, -sin_rows)
            .reshape(slots, rows, half_width)
            .astype(jnp.bfloat16)
        )
        value_back = (0.5 * value_mix_back).astype(jnp.bfloat16)
        key_totals.append(
            jnp.einsum("srd,sre->de", normed_low_g, key_back, preferred_element_type=jnp.float32)
        )
        value_totals.append(
            jnp.einsum("srd,sre->de", normed_low_g, value_back, preferred_element_type=jnp.float32)
        )
        value_mix_backs.append(value_mix_back)
        kv_normed_back.append(
            jnp.einsum("sre,de->srd", key_back, key_mat[:, cols], preferred_element_type=jnp.float32)
            + jnp.einsum(
                "sre,de->srd", value_back, value_mat[:, cols], preferred_element_type=jnp.float32
            )
        )
    first_grad = 0.5 * jnp.concatenate(value_mix_backs, axis=-1)
    query_back = (
        rotate(query_rot_back, cos_rows, -sin_rows).reshape(slots, rows, width).astype(jnp.bfloat16)
    )
    query_total = jnp.einsum(
        "srd,sre->de", normed_low_g, query_back, preferred_element_type=jnp.float32
    )
    key_total = jnp.concatenate(key_totals, axis=1)
    value_total = jnp.concatenate(value_totals, axis=1)
    normed_back = jnp.einsum(
        "sre,de->srd", query_back, query_mat, preferred_element_type=jnp.float32
    )
    normed_back = normed_back + (kv_normed_back[0] + kv_normed_back[1])
    normed_back = from_gathered(normed_back, w_rows)
    tokens_norm_back, prenorm_total = norm_back(
        tokens_wide, inverse, prenorm_full.astype(jnp.float32), normed_back
    )
    tokens_grad = middle_back + tokens_norm_back

    attn_grads = jnp.concatenate(
        [
            query_total.reshape(n_fsdp, w_rows, width),
            key_total.reshape(n_fsdp, w_rows, width),
            value_total.reshape(n_fsdp, w_rows, width),
            gain_block(
                to_gathered(prenorm_total, g_len).reshape(n_fsdp, g_len),
                to_gathered(midnorm_total, g_len).reshape(n_fsdp, g_len),
                width,
                leading=(n_fsdp,),
            ),
        ],
        axis=1,
    ).astype(jnp.bfloat16)
    attn_grads, mlp_halves = lax.optimization_barrier((attn_grads, mlp_halves))
    mlp_share = ctx_allreduce(z_combine(mlp_halves), n_ctx)
    attn_share = fsdp_reduce_scatter(attn_grads)
    attn_share = ctx_allreduce(attn_share, n_ctx)

    def attn_grad(i):
        return attn_share[i * w_rows:(i + 1) * w_rows]

    query_grad, key_grad, value_grad = (attn_grad(i) for i in range(3))
    prenorm_grad = attn_share[3 * w_rows, 0:g_len]
    midnorm_grad = attn_share[3 * w_rows, g_len:2 * g_len]
    gate_grad = mlp_share[:, 0:ff]
    up_grad = mlp_share[:, ff:2 * ff]
    down_grad = down_share
    out_grad = mlp_share[:, 2 * ff:]
    return (
        layer_out,
        tokens_grad,
        first_grad,
        query_grad,
        key_grad,
        value_grad,
        out_grad,
        gate_grad,
        up_grad,
        down_grad,
        prenorm_grad,
        midnorm_grad,
    )


def solution(mesh):
    zh = 2
    zl = 2
    n_f, n_c = mesh.devices.shape
    fine = jax.sharding.Mesh(
        mesh.devices.reshape(zh, n_f // (2 * zh), 2, zl, n_c // zl), FSDP + CTX
    )
    placed = (
        P(FSDP, CTX, None),
        P(FSDP, CTX, None),
        P(FSDP, None),
        P(FSDP, None),
        P(FSDP, None),
        P(FSDP, None),
        P(FSDP, None),
        P(FSDP, None),
        P(FSDP, None),
        P(FSDP),
        P(FSDP),
        P(FSDP, CTX, None),
        P(),
        P(),
    )
    return jax.shard_map(
        body,
        mesh=fine,
        in_specs=placed,
        out_specs=(
            P(FSDP, CTX, None),
            P(FSDP, CTX, None),
            P(FSDP, CTX, None),
            P(FSDP, None),
            P(FSDP, None),
            P(FSDP, None),
            P(FSDP, None),
            P(FSDP, None),
            P(FSDP, None),
            P(FSDP, None),
            P(FSDP),
            P(FSDP),
        ),
        check_vma=False,
    )
```

```python
import functools
import math

import jax
import jax.numpy as jnp
from jax import lax
from jax.experimental import pallas as pl
from jax.experimental.pallas import tpu as pltpu
from jax.sharding import PartitionSpec as P

H = 16


EPS = 1e-06
MASKED = -1e30
GAIN_ROWS = 16
FSDP = ("zh", "y", "core")
CTX = ("zl", "x")
Z_CROSS = [(0, 3), (3, 0), (1, 2), (2, 1)]


HEAD_BLOCK = 256
NT_DIMS = (((1,), (1,)), ((), ()))
TN_DIMS = (((0,), (0,)), ((), ()))


def allowed_keys(rows, keys, first_row, slot_len):
    query_pos = first_row + lax.broadcasted_iota(jnp.int32, (rows, keys), 0)
    key_pos = lax.broadcasted_iota(jnp.int32, (rows, keys), 1)
    return (key_pos <= query_pos) & (key_pos < slot_len)


def attention_shares(query, keys, allowed, scale):
    scores = lax.dot_general(query, keys, NT_DIMS, preferred_element_type=jnp.float32) * scale
    scores = jnp.where(allowed, scores, MASKED)
    peak = jnp.max(scores, axis=-1, keepdims=True)
    raised = jnp.exp(scores - peak)
    denominator = jnp.sum(raised, axis=-1, keepdims=True)
    return raised * (1.0 / denominator)


def attn_fwd_kernel(head_dim, scale, meta_ref, q_ref, k_ref, v_ref, o_ref):
    allowed = allowed_keys(q_ref.shape[0], k_ref.shape[0], meta_ref[0], meta_ref[1])
    for j in range(q_ref.shape[1] // head_dim):
        cols = slice(j * head_dim, (j + 1) * head_dim)
        shares = attention_shares(q_ref[:, cols], k_ref[:, cols], allowed, scale)
        mixed = jnp.dot(
            shares.astype(jnp.bfloat16), v_ref[:, cols], preferred_element_type=jnp.float32
        )
        o_ref[:, cols] = mixed.astype(o_ref.dtype)


def attn_bwd_kernel(head_dim, scale, meta_ref, q_ref, k_ref, v_ref, do_ref, dq_ref, dkv_ref):
    allowed = allowed_keys(q_ref.shape[0], k_ref.shape[0], meta_ref[0], meta_ref[1])
    for j in range(q_ref.shape[1] // head_dim):
        cols = slice(j * head_dim, (j + 1) * head_dim)
        query = q_ref[:, cols]
        keys = k_ref[:, cols]
        back = do_ref[:, cols]
        shares = attention_shares(query, keys, allowed, scale)
        prob_back = lax.dot_general(back, v_ref[:, cols], NT_DIMS, preferred_element_type=jnp.float32)
        inner = jnp.sum(shares * prob_back, axis=-1, keepdims=True)
        score_back = (shares * (prob_back - inner)).astype(jnp.bfloat16)
        dq_ref[:, cols] = (
            jnp.dot(score_back, keys, preferred_element_type=jnp.float32) * scale
        )
        dkv_ref[:, cols] = (
            lax.dot_general(score_back, query, TN_DIMS, preferred_element_type=jnp.float32) * scale
        ).astype(dkv_ref.dtype)
        half = q_ref.shape[1]
        dkv_ref[:, half + j * head_dim:half + (j + 1) * head_dim] = lax.dot_general(
            shares.astype(jnp.bfloat16), back, TN_DIMS, preferred_element_type=jnp.float32
        ).astype(dkv_ref.dtype)


def attention_forward(meta, query_rows, kv_rows, head_dim, scale):
    rows, width = query_rows.shape
    keys = kv_rows.shape[0]
    blocks = width // HEAD_BLOCK
    return pl.pallas_call(
        functools.partial(attn_fwd_kernel, head_dim, scale),
        out_shape=jax.ShapeDtypeStruct((rows, width), jnp.bfloat16),
        grid_spec=pltpu.PrefetchScalarGridSpec(
            num_scalar_prefetch=1,
            grid=(blocks,),
            in_specs=[
                pl.BlockSpec((rows, HEAD_BLOCK), lambda h, m: (0, h)),
                pl.BlockSpec((keys, HEAD_BLOCK), lambda h, m: (0, h)),
                pl.BlockSpec((keys, HEAD_BLOCK), lambda h, m: (0, h + blocks)),
            ],
            out_specs=pl.BlockSpec((rows, HEAD_BLOCK), lambda h, m: (0, h)),
        ),
        compiler_params=pltpu.CompilerParams(
            dimension_semantics=("arbitrary",), vmem_limit_bytes=48 * 1024 * 1024
        ),
        cost_estimate=pl.CostEstimate(
            flops=4 * rows * keys * width,
            transcendentals=rows * keys * (width // head_dim),
            bytes_accessed=2 * (2 * rows * width + 2 * keys * width),
        ),
    )(meta, query_rows, kv_rows, kv_rows)


def attention_backward(meta, query_rows, kv_rows, back_rows, head_dim, scale, first, count):
    rows, width = query_rows.shape
    keys = kv_rows.shape[0]
    blocks = width // HEAD_BLOCK
    part = count * HEAD_BLOCK
    return pl.pallas_call(
        functools.partial(attn_bwd_kernel, head_dim, scale),
        out_shape=(
            jax.ShapeDtypeStruct((rows, part), jnp.float32),
            jax.ShapeDtypeStruct((keys, 2 * part), jnp.bfloat16),
        ),
        grid_spec=pltpu.PrefetchScalarGridSpec(
            num_scalar_prefetch=1,
            grid=(count,),
            in_specs=[
                pl.BlockSpec((rows, HEAD_BLOCK), lambda h, m: (0, h + first)),
                pl.BlockSpec((keys, HEAD_BLOCK), lambda h, m: (0, h + first)),
                pl.BlockSpec((keys, HEAD_BLOCK), lambda h, m: (0, h + first + blocks)),
                pl.BlockSpec((rows, HEAD_BLOCK), lambda h, m: (0, h + first)),
            ],
            out_specs=[
                pl.BlockSpec((rows, HEAD_BLOCK), lambda h, m: (0, h)),
                pl.BlockSpec((keys, 2 * HEAD_BLOCK), lambda h, m: (0, h)),
            ],
        ),
        compiler_params=pltpu.CompilerParams(
            dimension_semantics=("arbitrary",), vmem_limit_bytes=48 * 1024 * 1024
        ),
        cost_estimate=pl.CostEstimate(
            flops=10 * rows * keys * part,
            transcendentals=rows * keys * (part // head_dim),
            bytes_accessed=2 * (3 * rows * part + 4 * keys * part) + 4 * rows * part,
        ),
    )(meta, query_rows, kv_rows, kv_rows, back_rows)


def rope_tables(positions, half):
    freq = jnp.exp(
        jnp.arange(half, dtype=jnp.int32).astype(jnp.float32) * (-math.log(10000.0) / half)
    )
    angle = positions.astype(jnp.float32)[:, None] * freq[None, :]
    return (jnp.cos(angle), jnp.sin(angle))


def rotate(value_rows, cosine, sine):
    half = value_rows.shape[-1] // 2
    first = value_rows[..., :half]
    second = value_rows[..., half:]
    return jnp.concatenate(
        [first * cosine - second * sine, second * cosine + first * sine], axis=-1
    )


def norm_apply(value_rows, gain):
    inverse = lax.rsqrt(jnp.mean(value_rows * value_rows, axis=-1, keepdims=True) + EPS)
    return (value_rows * inverse * gain, inverse)


def norm_back(value_rows, inverse, gain, upstream):
    scaled = upstream * gain
    gain_part = jnp.sum(upstream * value_rows * inverse, axis=(0, 1))
    inner = jnp.mean(scaled * value_rows, axis=-1, keepdims=True)
    return (inverse * scaled - value_rows * inverse * inverse * inverse * inner, gain_part)


def gain_block(first, second, width, leading=()):
    pad_cols = width - first.shape[-1] - second.shape[-1]
    row = jnp.concatenate(
        [first, second, jnp.zeros(leading + (pad_cols,), first.dtype)], axis=-1
    )
    row = row[..., None, :]
    pads = [(0, 0)] * len(leading) + [(0, GAIN_ROWS - 1), (0, 0)]
    return jnp.pad(row, pads)


def to_gathered(rows, block):
    lead = rows.shape[:-1]
    return jnp.swapaxes(rows.reshape(lead + (2, -1, block)), -3, -2).reshape(rows.shape)


def from_gathered(rows, block):
    lead = rows.shape[:-1]
    return jnp.swapaxes(rows.reshape(lead + (-1, 2, block)), -3, -2).reshape(rows.shape)


def zh_pair(mine, other):
    first = lax.axis_index("zh") == 0
    return jnp.stack([jnp.where(first, mine, other), jnp.where(first, other, mine)])


def fsdp_gather(pack):
    return yc_gather(z_exchange(pack))


def z_exchange(pack):
    return zh_pair(pack, lax.ppermute(pack, ("zh", "zl"), Z_CROSS))


def yc_gather(pair):
    both = lax.all_gather(pair, ("y", "core"), axis=0, tiled=False)
    return both.reshape((-1,) + pair.shape[1:])


def fsdp_reduce_scatter(grads):
    return z_combine(yc_reduce_scatter(grads))


def yc_reduce_scatter(grads):
    n_yc = grads.shape[0] // 2
    by_yc = grads
    block = grads.shape[1:]
    halves = lax.psum_scatter(
        by_yc.reshape((n_yc, 2 * block[0]) + block[1:]), ("y", "core"), scatter_dimension=0, tiled=False
    ).reshape((2,) + block)
    return halves


def z_combine(halves):
    zh = lax.axis_index("zh")
    mine = lax.dynamic_index_in_dim(halves, zh, axis=0, keepdims=False)
    theirs = lax.dynamic_index_in_dim(halves, 1 - zh, axis=0, keepdims=False)
    got = lax.ppermute(theirs, ("zh", "zl"), Z_CROSS)
    return (mine.astype(jnp.float32) + got.astype(jnp.float32)).astype(jnp.bfloat16)


def ctx_allreduce(part, n_ctx):
    total = part
    step = 1
    while step < n_ctx:
        other = lax.ppermute(total, CTX, [(j, j ^ step) for j in range(n_ctx)])
        total = (total.astype(jnp.float32) + other.astype(jnp.float32)).astype(jnp.bfloat16)
        step *= 2
    return total.astype(jnp.float32)


def body(
    tokens,
    first_value,
    query_weight,
    key_weight,
    value_weight,
    out_weight,
    gate_weight,
    up_weight,
    down_weight,
    prenorm_gain,
    midnorm_gain,
    cotangent,
    lengths,
    assignment,
):
    slots, rows, width = tokens.shape
    assert slots == 1
    head_count = H
    head_dim = width // head_count
    score_scale = head_dim ** (-0.5)
    n_fsdp = lax.axis_size(FSDP)
    n_ctx = lax.axis_size(CTX)
    total_len = rows * n_ctx
    w_rows = query_weight.shape[0]
    g_len = prenorm_gain.shape[0]
    ff = gate_weight.shape[1]
    d_rows = down_weight.shape[0]

    slot_count = assignment.shape[0]
    chosen = assignment[:, None] == jnp.arange(slot_count, dtype=jnp.int32)[None, :]
    lengths_all = jnp.sum(jnp.where(chosen, lengths[None, :], 0), axis=1)
    slot_lengths = lax.dynamic_slice_in_dim(lengths_all, lax.axis_index(FSDP) * slots, slots)
    query_places = lax.axis_index(CTX) * rows + jnp.arange(rows, dtype=jnp.int32)
    valid = query_places[None, :] < slot_lengths[:, None]
    cosine, sine = rope_tables(query_places, head_dim // 2)
    cos_rows = cosine[None, :, None, :]
    sin_rows = sine[None, :, None, :]
    valid_wide = valid[:, :, None]

    kv_pair = z_exchange(
        jnp.concatenate(
            [key_weight, value_weight, gain_block(prenorm_gain, midnorm_gain, width)], axis=0
        )
    )
    qod_pair = z_exchange(jnp.concatenate([query_weight, out_weight, down_weight], axis=0))
    gate_up_pair = z_exchange(jnp.concatenate([gate_weight, up_weight], axis=1))
    kv_wall = yc_gather(kv_pair)
    qod_pair, gate_up_pair, kv_wall = lax.optimization_barrier((qod_pair, gate_up_pair, kv_wall))
    qod_wall = yc_gather(qod_pair)
    gate_up_mat = yc_gather(gate_up_pair).reshape(n_fsdp * w_rows, 2 * ff)

    key_mat = kv_wall[:, 0:w_rows, :].reshape(n_fsdp * w_rows, width)
    value_mat = kv_wall[:, w_rows:2 * w_rows, :].reshape(n_fsdp * w_rows, width)
    prenorm_full = from_gathered(kv_wall[:, 2 * w_rows, 0:g_len].reshape(n_fsdp * g_len), g_len)
    midnorm_full = from_gathered(
        kv_wall[:, 2 * w_rows, g_len:2 * g_len].reshape(n_fsdp * g_len), g_len
    )
    query_mat = qod_wall[:, 0:w_rows, :].reshape(n_fsdp * w_rows, width)
    out_mat = qod_wall[:, w_rows:2 * w_rows, :].reshape(n_fsdp * w_rows, width)
    down_mat = qod_wall[:, 2 * w_rows:, :].reshape(n_fsdp * d_rows, width)

    tokens_wide = tokens.astype(jnp.float32)
    first_wide = first_value.astype(jnp.float32)
    normed, inverse = norm_apply(tokens_wide, prenorm_full.astype(jnp.float32))
    normed_low = normed.astype(jnp.bfloat16)
    normed_low_g = to_gathered(normed_low, w_rows)
    heads_shape = (slots, rows, head_count, head_dim)

    half_width = width // 2
    kv_halves = []
    for part in range(2):
        cols = slice(part * half_width, (part + 1) * half_width)
        keyed = jnp.dot(normed_low_g, key_mat[:, cols], preferred_element_type=jnp.float32)
        own_value = jnp.dot(normed_low_g, value_mat[:, cols], preferred_element_type=jnp.float32)
        key_rot = (
            rotate(keyed.reshape(slots, rows, head_count // 2, head_dim), cos_rows, sin_rows)
            .astype(jnp.bfloat16)
            .reshape(rows, half_width)
        )
        value_mix = (0.5 * own_value + 0.5 * first_wide[..., cols]).astype(jnp.bfloat16)
        kv_own = jnp.concatenate([key_rot, value_mix.reshape(rows, half_width)], axis=-1)
        kv_halves.append(
            lax.all_to_all(
                jnp.broadcast_to(kv_own[None], (n_ctx, rows, width)), CTX, 0, 0, tiled=False
            ).reshape(total_len, width)
        )
    query_in, kv_halves[0] = lax.optimization_barrier((normed_low_g, kv_halves[0]))
    query = jnp.dot(query_in, query_mat, preferred_element_type=jnp.float32)
    query_rotated_rows = rotate(query.reshape(heads_shape), cos_rows, sin_rows).astype(jnp.bfloat16)
    meta = jnp.stack([lax.axis_index(CTX) * rows, slot_lengths[0]]).astype(jnp.int32)
    query_flat = query_rotated_rows.reshape(rows, width)
    query_halves = [query_flat[:, :half_width], query_flat[:, half_width:]]
    mixed_first = attention_forward(meta, query_halves[0], kv_halves[0], head_dim, score_scale)
    mixed_first, kv_halves[1] = lax.optimization_barrier((mixed_first, kv_halves[1]))
    mixed_low = jnp.concatenate(
        [
            mixed_first,
            attention_forward(meta, query_halves[1], kv_halves[1], head_dim, score_scale),
        ],
        axis=-1,
    ).reshape(slots, rows, width)

    mixed_low_g = to_gathered(mixed_low, w_rows)
    middle = tokens_wide + jnp.dot(mixed_low_g, out_mat, preferred_element_type=jnp.float32)
    normed_two, inverse_two = norm_apply(middle, midnorm_full.astype(jnp.float32))
    normed_two = normed_two.astype(jnp.bfloat16)
    normed_two_g = to_gathered(normed_two, w_rows)
    gate_up = jnp.dot(normed_two_g, gate_up_mat, preferred_element_type=jnp.float32)
    gate = gate_up[..., :ff]
    upper = gate_up[..., ff:]
    hidden = (jax.nn.silu(gate) * upper).astype(jnp.bfloat16)
    hidden_g = to_gathered(hidden, d_rows)
    branch = jnp.dot(hidden_g, down_mat, preferred_element_type=jnp.float32)
    layer_out = jnp.where(valid_wide, middle + branch, 0.0).astype(jnp.bfloat16)

    cot_wide = jnp.where(valid_wide, cotangent.astype(jnp.float32), 0.0)
    cot_low = cot_wide.astype(jnp.bfloat16)
    down_total = jnp.einsum("srf,sre->fe", hidden_g, cot_low, preferred_element_type=jnp.float32)
    hidden_back = from_gathered(
        jnp.einsum("sre,fe->srf", cot_low, down_mat, preferred_element_type=jnp.float32), d_rows
    )
    sigma = jax.nn.sigmoid(gate)
    gate_back = (hidden_back * upper * sigma * (1.0 + gate * (1.0 - sigma))).astype(jnp.bfloat16)
    upper_back = (hidden_back * gate * sigma).astype(jnp.bfloat16)
    gate_up_back = jnp.concatenate([gate_back, upper_back], axis=-1)
    gate_up_total = jnp.einsum(
        "srd,srf->df", normed_two_g, gate_up_back, preferred_element_type=jnp.float32
    )
    normed_two_back = jnp.einsum(
        "srf,df->srd", gate_up_back, gate_up_mat, preferred_element_type=jnp.float32
    )
    normed_two_back = from_gathered(normed_two_back, w_rows)
    middle_norm_back, midnorm_total = norm_back(
        middle, inverse_two, midnorm_full.astype(jnp.float32), normed_two_back
    )
    middle_back = cot_wide + middle_norm_back
    middle_low = middle_back.astype(jnp.bfloat16)
    out_total = jnp.einsum("srd,sre->de", mixed_low_g, middle_low, preferred_element_type=jnp.float32)

    down_share = ctx_allreduce(
        z_combine(yc_reduce_scatter(down_total.astype(jnp.bfloat16).reshape(n_fsdp, d_rows, width))),
        n_ctx,
    )
    mlp_grads = jnp.concatenate(
        [
            gate_up_total.reshape(n_fsdp, w_rows, 2 * ff),
            out_total.reshape(n_fsdp, w_rows, width),
        ],
        axis=2,
    ).astype(jnp.bfloat16)
    mlp_halves = yc_reduce_scatter(mlp_grads)

    blended_value_gradient = from_gathered(
        jnp.einsum("sre,de->srd", middle_low, out_mat, preferred_element_type=jnp.float32).astype(
            jnp.bfloat16
        ),
        w_rows,
    )
    n_head_blocks = width // HEAD_BLOCK
    half_blocks = n_head_blocks // 2
    back_flat = blended_value_gradient.reshape(rows, width)
    back_halves = [back_flat[:, :half_width], back_flat[:, half_width:]]
    dq_parts = []
    kv_parts = []
    for part in range(2):
        dq_part, kv_back = attention_backward(
            meta,
            query_halves[part],
            kv_halves[part],
            back_halves[part],
            head_dim,
            score_scale,
            0,
            half_blocks,
        )
        dq_parts.append(dq_part)
        kv_parts.append(
            jnp.sum(
                lax.all_to_all(
                    kv_back.reshape(n_ctx, rows, kv_back.shape[1]), CTX, 0, 0, tiled=False
                ).astype(jnp.float32),
                axis=0,
            ).reshape(rows, half_blocks, 2, HEAD_BLOCK)
        )
    query_rot_back = jnp.concatenate(dq_parts, axis=-1).reshape(slots, rows, head_count, head_dim)
    key_value = jnp.concatenate(kv_parts, axis=1)
    key_rot_back = key_value[:, :, 0, :].reshape(slots, rows, head_count, head_dim)
    value_mix_back = key_value[:, :, 1, :].reshape(slots, rows, width)
    first_grad = 0.5 * value_mix_back
    query_back = (
        rotate(query_rot_back, cos_rows, -sin_rows).reshape(slots, rows, width).astype(jnp.bfloat16)
    )
    key_back = (
        rotate(key_rot_back, cos_rows, -sin_rows).reshape(slots, rows, width).astype(jnp.bfloat16)
    )
    value_back = (0.5 * value_mix_back).astype(jnp.bfloat16)
    query_total = jnp.einsum(
        "srd,sre->de", normed_low_g, query_back, preferred_element_type=jnp.float32
    )
    key_total = jnp.einsum("srd,sre->de", normed_low_g, key_back, preferred_element_type=jnp.float32)
    value_total = jnp.einsum(
        "srd,sre->de", normed_low_g, value_back, preferred_element_type=jnp.float32
    )
    normed_back = jnp.einsum(
        "sre,de->srd", query_back, query_mat, preferred_element_type=jnp.float32
    )
    normed_back = normed_back + jnp.einsum(
        "sre,de->srd", key_back, key_mat, preferred_element_type=jnp.float32
    )
    normed_back = normed_back + jnp.einsum(
        "sre,de->srd", value_back, value_mat, preferred_element_type=jnp.float32
    )
    normed_back = from_gathered(normed_back, w_rows)
    tokens_norm_back, prenorm_total = norm_back(
        tokens_wide, inverse, prenorm_full.astype(jnp.float32), normed_back
    )
    tokens_grad = middle_back + tokens_norm_back

    attn_grads = jnp.concatenate(
        [
            query_total.reshape(n_fsdp, w_rows, width),
            key_total.reshape(n_fsdp, w_rows, width),
            value_total.reshape(n_fsdp, w_rows, width),
            gain_block(
                to_gathered(prenorm_total, g_len).reshape(n_fsdp, g_len),
                to_gathered(midnorm_total, g_len).reshape(n_fsdp, g_len),
                width,
                leading=(n_fsdp,),
            ),
        ],
        axis=1,
    ).astype(jnp.bfloat16)
    attn_grads, mlp_halves = lax.optimization_barrier((attn_grads, mlp_halves))
    mlp_share = ctx_allreduce(z_combine(mlp_halves), n_ctx)
    attn_share = fsdp_reduce_scatter(attn_grads)
    attn_share = ctx_allreduce(attn_share, n_ctx)

    def attn_grad(i):
        return attn_share[i * w_rows:(i + 1) * w_rows]

    query_grad, key_grad, value_grad = (attn_grad(i) for i in range(3))
    prenorm_grad = attn_share[3 * w_rows, 0:g_len]
    midnorm_grad = attn_share[3 * w_rows, g_len:2 * g_len]
    gate_grad = mlp_share[:, 0:ff]
    up_grad = mlp_share[:, ff:2 * ff]
    down_grad = down_share
    out_grad = mlp_share[:, 2 * ff:]
    return (
        layer_out,
        tokens_grad,
        first_grad,
        query_grad,
        key_grad,
        value_grad,
        out_grad,
        gate_grad,
        up_grad,
        down_grad,
        prenorm_grad,
        midnorm_grad,
    )


def solution(mesh):
    zh = 2
    zl = 2
    n_f, n_c = mesh.devices.shape
    fine = jax.sharding.Mesh(
        mesh.devices.reshape(zh, n_f // (2 * zh), 2, zl, n_c // zl), FSDP + CTX
    )
    placed = (
        P(FSDP, CTX, None),
        P(FSDP, CTX, None),
        P(FSDP, None),
        P(FSDP, None),
        P(FSDP, None),
        P(FSDP, None),
        P(FSDP, None),
        P(FSDP, None),
        P(FSDP, None),
        P(FSDP),
        P(FSDP),
        P(FSDP, CTX, None),
        P(),
        P(),
    )
    return jax.shard_map(
        body,
        mesh=fine,
        in_specs=placed,
        out_specs=(
            P(FSDP, CTX, None),
            P(FSDP, CTX, None),
            P(FSDP, CTX, None),
            P(FSDP, None),
            P(FSDP, None),
            P(FSDP, None),
            P(FSDP, None),
            P(FSDP, None),
            P(FSDP, None),
            P(FSDP, None),
            P(FSDP),
            P(FSDP),
        ),
        check_vma=False,
    )
```
